32 devices in a mesh: clip: 8 (over y, x, core), head: 4 (over z).
Axes of the slice: x: 2, y: 2, z: 4, core: 2. Of those that a mesh axis runs over, the one named last changes fastest.
Arguments:
- tokens: bfloat16 [40960, 1024], P(('clip', 'head')), may hold values from -6 to 6
- d_out: bfloat16 [40960, 1024], P(('clip', 'head')), may hold values from -6 to 6
- modulation: float32 [8, 12, 1024], P('clip'), may hold values from -1.5 to 1.5
- frame_counts: int32 [8], P('clip'), may hold values from 2 to 5, as said below
- w_qkv: bfloat16 [2, 3, 1024, 1024], P(None, None, None, 'head'), may hold values from -0.1875 to 0.1875
- w_out: bfloat16 [2, 1024, 1024], P(None, 'head'), may hold values from -0.75 to 0.75
- w_up: bfloat16 [2, 1024, 4096], P(None, None, 'head'), may hold values from -0.1875 to 0.1875
- w_down: bfloat16 [2, 4096, 1024], P(None, 'head'), may hold values from -0.09375 to 0.09375
- table_s: float32 [16, 961], P('head'), may hold values from -4 to 4
- table_t: float32 [16, 2025], P('head'), may hold values from -4 to 4
Outputs:
- output: bfloat16 [40960, 1024], P(('clip', 'head'))
- grad_tokens: float32 [40960, 1024], P(('clip', 'head'))
- grad_modulation: float32 [8, 12, 1024], P('clip')
- grad_qkv: float32 [2, 3, 1024, 1024], P(None, None, None, 'head')
- grad_out: float32 [2, 1024, 1024], P(None, 'head')
- grad_up: float32 [2, 1024, 4096], P(None, None, 'head')
- grad_down: float32 [2, 4096, 1024], P(None, 'head')
- grad_table_s: float32 [16, 961], P('head')
- grad_table_t: float32 [16, 2025], P('head')
The draws below stay inside these ranges and needn't reach their ends.
Inputs may be any that keep to these rules, and one draw needn't show every extreme that they name: `frame_counts`: every clip has 2 to 5 live frames; in every draw some clip has 5 and some has 2.
All inputs are finite; a program needn't handle non-finite values.
Results may differ from the reference program's by a relative error of at most 0.04.
Values may be sent and summed in bfloat16 or wider, within the bound.
A program may use at most 512 MiB of HBM per device.

```python
import jax
import jax.numpy as jnp
from jax import lax

D = 1024
HEADS = 16
HD = 64
FF = 4096
FH = 32
FW = 32
SWIN = 16
TWIN = 8
PADF = 5
CLIPS = 8
TOKENS = 40960
NREL_S = 961
NREL_T = 2025


def draw_frame_counts(key, part):
    choices_table = jnp.array([2, 2, 2, 2, 2, 2, 2, 3, 3, 3, 3, 4, 4, 4, 5, 5], dtype=jnp.int32)
    picks = jax.random.randint(jax.random.fold_in(key, 11), (CLIPS,), 0, 16)
    counts = jnp.minimum(choices_table[picks], PADF)
    longest = jax.random.randint(jax.random.fold_in(key, 12), (), 0, CLIPS)
    counts = counts.at[longest].set(PADF)
    counts = counts.at[(longest + 1) % CLIPS].set(2)
    return counts


def shard_levels(key, shape, cuts, least, largest):
    gain = 1.0
    for dim, shards_of in cuts:
        heights = jax.random.uniform(jax.random.fold_in(jax.random.fold_in(key, 6), dim), (shards_of,), jnp.float32, least / len(cuts), largest / len(cuts))
        gain = gain * jnp.repeat(jnp.exp(heights), shape[dim] // shards_of).reshape((-1,) + (1,) * (len(shape) - 1 - dim))
    return gain


def bell_draw(key, shape, scale, bound, shards=(), kind=jnp.bfloat16):
    drawn = jax.random.normal(key, shape, jnp.float32) * scale
    if len(shards) > 0:
        drawn = shard_levels(key, shape, shards, -0.22, 0.18) * drawn
    return jnp.clip(drawn, min=-bound, max=bound).astype(kind)


def setup_inputs(seed: int = 0) -> dict:
    arg_keys = jax.random.split(jax.random.key(seed), 11)
    return {
        "tokens": bell_draw(arg_keys[0], (TOKENS, D), 1.0, 6.0, ((0, 32),)),
        "d_out": bell_draw(arg_keys[1], (TOKENS, D), 1.0, 6.0, ((0, 32),)),
        "modulation": bell_draw(arg_keys[2], (CLIPS, 12, D), 0.3, 1.5, ((0, 8),), jnp.float32),
        "frame_counts": draw_frame_counts(jax.random.fold_in(arg_keys[10], 71), 0),
        "w_qkv": bell_draw(arg_keys[4], (2, 3, D, D), D ** -0.5, 0.1875, ((3, 4),)),
        "w_out": bell_draw(arg_keys[5], (2, D, D), HD ** -0.5, 0.75, ((1, 4),)),
        "w_up": bell_draw(arg_keys[6], (2, D, FF), D ** -0.5, 0.1875, ((2, 4),)),
        "w_down": bell_draw(arg_keys[7], (2, FF, D), FF ** -0.5, 0.09375, ((1, 4),)),
        "table_s": bell_draw(arg_keys[8], (HEADS, NREL_S), 0.7, 4.0, ((0, 4),), jnp.float32),
        "table_t": bell_draw(arg_keys[9], (HEADS, NREL_T), 0.7, 4.0, ((0, 4),), jnp.float32),
    }


EPS = 1e-06
HIGHEST_PRECISION = lax.Precision.HIGHEST
NEGATIVE = -1e+30

@jax.custom_vjp
def low(v):
    return lax.optimization_barrier(v.astype(jnp.bfloat16)).astype(jnp.float32)

@jax.custom_vjp
def low_back(v):
    return v

def low_keep(v):
    return (low(v), None)

def low_pass(kept, grad):
    return (grad,)

def back_keep(v):
    return (v, None)

def back_low(kept, grad):
    return (low(grad),)
low.defvjp(low_keep, low_pass)
low_back.defvjp(back_keep, back_low)

def layer_norm(values, shift_row, scale_row):
    average = lax.optimization_barrier(jnp.mean(values, axis=-1, keepdims=True))
    centred = values - average
    spread = lax.optimization_barrier(jnp.mean(centred * centred, axis=-1, keepdims=True))
    return centred * lax.rsqrt(spread + EPS) * (1.0 + scale_row) + shift_row

def window_index(side_t, side_len):
    window_size = side_t * side_len * side_len
    places = jnp.arange(window_size, dtype=jnp.int32)
    time_pos = places // (side_len * side_len)
    height_pos = places // side_len % side_len
    width_pos = places % side_len
    span_len = 2 * side_len - 1
    return (time_pos[:, None] - time_pos[None, :] + side_t - 1) * span_len * span_len + (height_pos[:, None] - height_pos[None, :] + side_len - 1) * span_len + (width_pos[:, None] - width_pos[None, :] + side_len - 1)

def to_windows(values, side_t, side_len):
    tail_shape = values.shape[1:]
    frames = values.shape[0] // (FH * FW)
    shaped = values.reshape((frames // side_t, side_t, FH // side_len, side_len, FW // side_len, side_len) + tail_shape)
    axis_order = (0, 2, 4, 1, 3, 5) + tuple(range(6, 6 + len(tail_shape)))
    shaped = shaped.transpose(axis_order)
    return shaped.reshape((-1, side_t * side_len * side_len) + tail_shape)

def from_windows(values, side_t, side_len):
    tail_shape = values.shape[2:]
    blocks_high = FH // side_len
    blocks_wide = FW // side_len
    frame_groups = values.shape[0] // (blocks_high * blocks_wide)
    shaped = values.reshape((frame_groups, blocks_high, blocks_wide, side_t, side_len, side_len) + tail_shape)
    axis_order = (0, 3, 1, 4, 2, 5) + tuple(range(6, 6 + len(tail_shape)))
    return shaped.transpose(axis_order).reshape((frame_groups * side_t * FH * FW,) + tail_shape)

def attention(normed, weight_in, weight_out, table_arg, keep_mask, side_t, side_len):
    projected = jnp.einsum('ld,cde->lce', normed, weight_in, precision=HIGHEST_PRECISION)
    projected = low(low_back(projected))
    head_width = weight_in.shape[-1]
    head_count = head_width // HD
    windows = to_windows(projected, side_t, side_len)
    window_size = side_t * side_len * side_len
    windows = windows.reshape(windows.shape[0], window_size, 3, head_count, HD)
    queries = windows[:, :, 0]
    key_rows = windows[:, :, 1]
    value_rows = windows[:, :, 2]
    rel_index = window_index(side_t, side_len)
    logits = jnp.einsum('wqhe,wkhe->whqk', queries, key_rows, precision=HIGHEST_PRECISION) * HD ** (-0.5)
    logits = logits + table_arg[:, rel_index][None]
    if keep_mask is not None:
        keep_win = to_windows(keep_mask[:, None], side_t, side_len)[:, :, 0]
        logits = jnp.where(keep_win[:, None, None, :], logits, NEGATIVE)
    logits = low_back(logits)
    probs = low(jax.nn.softmax(logits, axis=-1))
    attended = jnp.einsum('whqk,wkhe->wqhe', probs, value_rows, precision=HIGHEST_PRECISION)
    attended = from_windows(attended.reshape(attended.shape[0], window_size, head_width), side_t, side_len)
    attended = low(low_back(attended))
    return low_back(jnp.dot(attended, weight_out, precision=HIGHEST_PRECISION))

def layer_clip(params, clip_tokens, clip_mods, frame_count):
    w_qkv, w_out, w_up, w_down, table_s, table_t = params
    frame_of = jnp.arange(PADF * FH * FW, dtype=jnp.int32) // (FH * FW)
    keep_mask = frame_of < frame_count
    hidden = clip_tokens
    for block_id in range(2):
        slots = clip_mods[6 * block_id:6 * block_id + 6]
        normed = low(layer_norm(hidden, slots[0], slots[1]))
        if block_id == 0:
            branch = attention(normed, w_qkv[0], w_out[0], table_s, None, 1, SWIN)
        else:
            branch = attention(normed, w_qkv[1], w_out[1], table_t, keep_mask, PADF, TWIN)
        hidden = hidden + slots[2] * branch
        shifted = low(layer_norm(hidden, slots[3], slots[4]))
        pre_gelu = low_back(jnp.dot(shifted, w_up[block_id], precision=HIGHEST_PRECISION))
        activated = low(jax.nn.gelu(pre_gelu, approximate=True))
        feed_out = low_back(jnp.dot(activated, w_down[block_id], precision=HIGHEST_PRECISION))
        hidden = hidden + slots[5] * feed_out
    return hidden * keep_mask.astype(jnp.float32)[:, None]

def reference(tokens, d_out, modulation, frame_counts, w_qkv, w_out, w_up, w_down, table_s, table_t):
    clip_len = PADF * FH * FW
    params = (w_qkv.astype(jnp.float32), w_out.astype(jnp.float32), w_up.astype(jnp.float32), w_down.astype(jnp.float32), table_s.astype(jnp.float32), table_t.astype(jnp.float32))
    inputs = tokens.astype(jnp.float32).reshape(CLIPS, clip_len, D)

    def forward(weights, clip_inputs, clip_mods):

        def one_clip(clip_item):
            return layer_clip(weights, clip_item[0], clip_item[1], clip_item[2])
        return lax.map(jax.checkpoint(one_clip), (clip_inputs, clip_mods, frame_counts))
    result, pull_back = jax.vjp(forward, params, inputs, modulation)
    grad_params, grad_inputs, grad_mods = pull_back(d_out.astype(jnp.float32).reshape(CLIPS, clip_len, D))
    return (result.reshape(TOKENS, D).astype(jnp.bfloat16), grad_inputs.reshape(TOKENS, D), grad_mods, grad_params[0], grad_params[1], grad_params[2], grad_params[3], grad_params[4], grad_params[5])
```

```python
import jax
import jax.numpy as jnp
from jax import lax
from jax.experimental import pallas as pl
from jax.experimental.pallas import tpu as pltpu
from jax.sharding import PartitionSpec as P

HD = 64
FH = 32
FW = 32
SWIN = 16
TWIN = 8
PADF = 5


EPS = 1e-06
HIGHEST_PRECISION = lax.Precision.HIGHEST
NEGATIVE = -1e30


def layer_norm(values, shift_row, scale_row):
    average = jnp.mean(values, axis=-1, keepdims=True)
    centred = values - average
    spread = jnp.mean(centred * centred, axis=-1, keepdims=True)
    return centred * lax.rsqrt(spread + EPS) * (1.0 + scale_row) + shift_row


def gelu_tanh(values):
    return jax.nn.gelu(values, approximate=True)


def window_index(side_t, side_len):
    window_size = side_t * side_len * side_len
    places = jnp.arange(window_size, dtype=jnp.int32)
    time_pos = places // (side_len * side_len)
    height_pos = places // side_len % side_len
    width_pos = places % side_len
    span_len = 2 * side_len - 1
    return (
        (time_pos[:, None] - time_pos[None, :] + side_t - 1) * span_len * span_len
        + (height_pos[:, None] - height_pos[None, :] + side_len - 1) * span_len
        + (width_pos[:, None] - width_pos[None, :] + side_len - 1)
    )


def to_windows(values, side_t, side_len):
    tail_shape = values.shape[1:]
    frames = values.shape[0] // (FH * FW)
    shaped = values.reshape(
        (frames // side_t, side_t, FH // side_len, side_len, FW // side_len, side_len) + tail_shape
    )
    axis_order = (0, 2, 4, 1, 3, 5) + tuple(range(6, 6 + len(tail_shape)))
    shaped = shaped.transpose(axis_order)
    return shaped.reshape((-1, side_t * side_len * side_len) + tail_shape)


def from_windows(values, side_t, side_len):
    tail_shape = values.shape[2:]
    blocks_high = FH // side_len
    blocks_wide = FW // side_len
    frame_groups = values.shape[0] // (blocks_high * blocks_wide)
    shaped = values.reshape(
        (frame_groups, blocks_high, blocks_wide, side_t, side_len, side_len) + tail_shape
    )
    axis_order = (0, 3, 1, 4, 2, 5) + tuple(range(6, 6 + len(tail_shape)))
    return shaped.transpose(axis_order).reshape((frame_groups * side_t * FH * FW,) + tail_shape)


def on_device(
    tokens, d_out, modulation, frame_counts, w_qkv, w_out, w_up, w_down, table_s, table_t
):
    local_rows = tokens.shape[0]
    clip_len = PADF * FH * FW
    group_clips = modulation.shape[0]
    group_rows = group_clips * clip_len
    scale_dot = HD ** (-0.5)
    my_index = lax.axis_index("head")
    first_row = my_index * local_rows
    row_ids = first_row + jnp.arange(local_rows, dtype=jnp.int32)
    clip_slots = jnp.arange(group_clips, dtype=jnp.int32)
    row_onehot = ((row_ids // clip_len)[:, None] == clip_slots[None, :]).astype(jnp.float32)
    count_float = frame_counts.astype(jnp.float32)
    row_frames = jnp.dot(row_onehot, count_float, precision=HIGHEST_PRECISION)
    row_keep = ((row_ids % clip_len // (FH * FW)).astype(jnp.float32) < row_frames).astype(
        jnp.float32
    )[:, None]
    group_ids = jnp.arange(group_rows, dtype=jnp.int32)
    group_onehot = ((group_ids // clip_len)[:, None] == clip_slots[None, :]).astype(jnp.float32)
    group_frames = jnp.dot(group_onehot, count_float, precision=HIGHEST_PRECISION)
    group_keep = (group_ids % clip_len // (FH * FW)).astype(jnp.float32) < group_frames

    def block_shape(block_id):
        if block_id == 0:
            return (1, SWIN)
        return (PADF, TWIN)

    def mod_row(slot):
        return jnp.dot(row_onehot, modulation[:, slot, :], precision=HIGHEST_PRECISION)

    def rows_in(values):
        return lax.all_gather(values, "head", axis=0, tiled=True)

    def grads_in(values):
        return lax.all_gather(values, "head", axis=0, tiled=True)

    def rows_out(full_rows, weight):
        return lax.psum_scatter(
            jnp.dot(full_rows, weight, preferred_element_type=jnp.float32).astype(jnp.bfloat16),
            "head",
            scatter_dimension=0,
            tiled=True,
        ).astype(jnp.float32)

    def grads_out(full_rows, weight, einsum_form):
        return lax.psum_scatter(
            jnp.einsum(einsum_form, full_rows, weight, preferred_element_type=jnp.float32).astype(
                jnp.bfloat16
            ),
            "head",
            scatter_dimension=0,
            tiled=True,
        ).astype(jnp.float32)

    def rows_keep(block_id):
        if block_id == 0:
            return None
        return to_windows(group_keep[:, None], PADF, TWIN)[:, :, 0]

    def shape_windows(projected, side_t, side_len):
        head_count = projected.shape[-1] // HD
        window_size = side_t * side_len * side_len
        windows = to_windows(projected, side_t, side_len)
        return windows.reshape(windows.shape[0], window_size, 3, head_count, HD)

    def shape_grad(grad_attended, side_t, side_len):
        head_count = grad_attended.shape[-1] // HD
        window_size = side_t * side_len * side_len
        windows = to_windows(grad_attended, side_t, side_len)
        return windows.reshape(windows.shape[0], window_size, head_count, HD)

    def flat_rows(windowed, side_t, side_len):
        return from_windows(windowed, side_t, side_len)

    def logits_of(queries, key_rows, table_arg, rel_index, keep_win):
        logits = (
            jnp.einsum("wqhe,wkhe->whqk", queries, key_rows, preferred_element_type=jnp.float32)
            * scale_dot
        )
        logits = logits + table_arg[:, rel_index][None]
        if keep_win is not None:
            logits = jnp.where(keep_win[:, None, None, :], logits, NEGATIVE)
        return logits

    def attend(windows, table_arg, rel_index, keep_win):
        logits = logits_of(windows[:, :, 0], windows[:, :, 1], table_arg, rel_index, keep_win)
        row_max = jnp.max(logits, axis=-1, keepdims=True)
        exponent = jnp.exp(logits - row_max)
        row_total = jnp.sum(exponent, axis=-1, keepdims=True)
        probs = exponent / row_total
        log_total = row_max + jnp.log(row_total)
        attended = jnp.einsum(
            "whqk,wkhe->wqhe",
            probs.astype(jnp.bfloat16),
            windows[:, :, 2],
            preferred_element_type=jnp.float32,
        )
        return (attended.reshape(attended.shape[0], attended.shape[1], -1), log_total)

    def attend_back(windows, grad_windows, log_total, table_arg, rel_index, keep_win):
        queries = windows[:, :, 0]
        key_rows = windows[:, :, 1]
        value_rows = windows[:, :, 2]
        logits = logits_of(queries, key_rows, table_arg, rel_index, keep_win)
        probs = jnp.exp(logits - log_total)
        grad_probs = jnp.einsum(
            "wqhe,wkhe->whqk", grad_windows, value_rows, preferred_element_type=jnp.float32
        )
        grad_values = jnp.einsum(
            "whqk,wqhe->wkhe",
            probs.astype(jnp.bfloat16),
            grad_windows,
            preferred_element_type=jnp.float32,
        )
        grad_logits = (
            probs * (grad_probs - jnp.sum(grad_probs * probs, axis=-1, keepdims=True))
        ).astype(jnp.bfloat16)
        head_count = queries.shape[2]
        table_terms = jnp.sum(grad_logits.astype(jnp.float32), axis=0).reshape(head_count, -1)
        grad_table = jax.ops.segment_sum(
            table_terms.T, rel_index.reshape(-1), num_segments=table_arg.shape[1]
        ).T
        grad_queries = (
            jnp.einsum("whqk,wkhe->wqhe", grad_logits, key_rows, preferred_element_type=jnp.float32)
            * scale_dot
        )
        grad_keys = (
            jnp.einsum("whqk,wqhe->wkhe", grad_logits, queries, preferred_element_type=jnp.float32)
            * scale_dot
        )
        grad_stack = jnp.stack([grad_queries, grad_keys, grad_values], axis=2)
        return (
            grad_stack.reshape(grad_stack.shape[0], grad_stack.shape[1], 3, head_count * HD),
            grad_table,
        )

    def forward_block(hidden, block_id):
        side_t, side_len = block_shape(block_id)
        table_local = table_s if block_id == 0 else table_t
        rel_index = window_index(side_t, side_len)
        normed = layer_norm(hidden, mod_row(6 * block_id), mod_row(6 * block_id + 1)).astype(
            jnp.bfloat16
        )
        plan = None
        normed_in = rows_in(normed)
        qkv_use, out_use, table_use = (w_qkv[block_id], w_out[block_id], table_local)
        keep_win = rows_keep(block_id)
        projected = jnp.einsum(
            "gd,cde->gce", normed_in, qkv_use, preferred_element_type=jnp.float32
        ).astype(jnp.bfloat16)
        windows = shape_windows(projected, side_t, side_len)
        attended_win, log_total = attend(windows, table_use, rel_index, keep_win)
        attended = flat_rows(attended_win, side_t, side_len).astype(jnp.bfloat16)
        branch = rows_out(attended, out_use)
        middle = hidden + mod_row(6 * block_id + 2) * branch
        shifted = layer_norm(middle, mod_row(6 * block_id + 3), mod_row(6 * block_id + 4)).astype(
            jnp.bfloat16
        )
        up_full, down_full = (
            lax.all_gather(w_up[block_id], "head", axis=1, tiled=True),
            lax.all_gather(w_down[block_id], "head", axis=0, tiled=True),
        )
        pre_gelu = jnp.dot(shifted, up_full, preferred_element_type=jnp.float32)
        activated = gelu_tanh(pre_gelu).astype(jnp.bfloat16)
        feed_out = jnp.dot(activated, down_full, preferred_element_type=jnp.float32)
        mlp_state = (shifted, pre_gelu, activated, up_full, down_full)
        result = middle + mod_row(6 * block_id + 5) * feed_out
        attn_state = (
            normed_in,
            projected,
            log_total,
            attended,
            qkv_use,
            out_use,
            table_use,
            keep_win,
            plan,
        )
        saved_state = (hidden, attn_state, branch, middle, feed_out, mlp_state)
        return (saved_state, result)

    def backward_block(saved_state, grad_result, block_id):
        hidden, attn_state, branch, middle, feed_out, mlp_state = saved_state
        normed_in, projected, log_total, attended, qkv_use, out_use, table_use, keep_win, plan = (
            attn_state
        )
        shifted_in, pre_gelu, activated, up_weight, down_weight = mlp_state
        side_t, side_len = block_shape(block_id)
        rel_index = window_index(side_t, side_len)
        grad_feed = (grad_result * mod_row(6 * block_id + 5)).astype(jnp.bfloat16)
        grad_gate_mlp = grad_result * feed_out
        grad_down = jnp.einsum(
            "gf,gd->fd", activated, grad_feed, preferred_element_type=jnp.float32
        )
        grad_activated = jnp.einsum(
            "gd,fd->gf", grad_feed, down_weight, preferred_element_type=jnp.float32
        )
        grad_pre = jax.vjp(gelu_tanh, pre_gelu)[1](grad_activated)[0].astype(jnp.bfloat16)
        grad_up = jnp.einsum("gd,gf->df", shifted_in, grad_pre, preferred_element_type=jnp.float32)
        grad_shifted = jnp.einsum(
            "gf,df->gd", grad_pre, up_weight, preferred_element_type=jnp.float32
        )
        grad_up, grad_down = (
            lax.psum_scatter(
                grad_up.astype(jnp.bfloat16), "head", scatter_dimension=1, tiled=True
            ).astype(jnp.float32),
            lax.psum_scatter(
                grad_down.astype(jnp.bfloat16), "head", scatter_dimension=0, tiled=True
            ).astype(jnp.float32),
        )
        unused_mid, pull_second = jax.vjp(
            layer_norm, middle, mod_row(6 * block_id + 3), mod_row(6 * block_id + 4)
        )
        grad_mid_norm, grad_shift_mlp, grad_scale_mlp = pull_second(grad_shifted)
        grad_middle = grad_result + grad_mid_norm
        grad_branch = (grad_middle * mod_row(6 * block_id + 2)).astype(jnp.bfloat16)
        grad_gate_att = grad_middle * branch
        branch_in = grads_in(grad_branch)
        grad_wout = jnp.einsum("ge,gd->ed", attended, branch_in, preferred_element_type=jnp.float32)
        grad_attended = jnp.einsum(
            "gd,ed->ge", branch_in, out_use, preferred_element_type=jnp.float32
        ).astype(jnp.bfloat16)
        windows = shape_windows(projected, side_t, side_len)
        grad_windows = shape_grad(grad_attended, side_t, side_len)
        grad_stack, grad_table = attend_back(
            windows, grad_windows, log_total, table_use, rel_index, keep_win
        )
        grad_projected = flat_rows(grad_stack, side_t, side_len).astype(jnp.bfloat16)
        grad_qkv = jnp.einsum(
            "gd,gce->cde", normed_in, grad_projected, preferred_element_type=jnp.float32
        )
        grad_normed = grads_out(grad_projected, qkv_use, "gce,cde->gd")
        unused_hid, pull_first = jax.vjp(
            layer_norm, hidden, mod_row(6 * block_id), mod_row(6 * block_id + 1)
        )
        grad_hid_norm, grad_shift_att, grad_scale_att = pull_first(grad_normed)
        grad_hidden = grad_middle + grad_hid_norm
        mod_terms = jnp.stack(
            [
                grad_shift_att,
                grad_scale_att,
                grad_gate_att,
                grad_shift_mlp,
                grad_scale_mlp,
                grad_gate_mlp,
            ],
            axis=1,
        )
        grad_mods = jnp.einsum("rc,rke->cke", row_onehot, mod_terms, precision=HIGHEST_PRECISION)
        return (grad_hidden, grad_mods, (grad_qkv, grad_wout, grad_up, grad_down, grad_table))

    hidden_first = tokens.astype(jnp.float32)
    saved_first, hidden_second = forward_block(hidden_first, 0)
    saved_second, hidden_last = forward_block(hidden_second, 1)
    output = (hidden_last * row_keep).astype(jnp.bfloat16)
    grad_second, mods_second, weights_second = backward_block(
        saved_second, d_out.astype(jnp.float32) * row_keep, 1
    )
    grad_first, mods_first, weights_first = backward_block(saved_first, grad_second, 0)
    grad_modulation = lax.psum(
        jnp.concatenate([mods_first, mods_second], axis=1).astype(jnp.bfloat16), "head"
    ).astype(jnp.float32)
    summed = (
        lax.psum(
            jnp.stack([weights_first[0], weights_second[0]]).astype(jnp.bfloat16), "clip"
        ).astype(jnp.float32),
        lax.psum(
            jnp.stack([weights_first[1], weights_second[1]]).astype(jnp.bfloat16), "clip"
        ).astype(jnp.float32),
        lax.psum(
            jnp.stack([weights_first[2], weights_second[2]]).astype(jnp.bfloat16), "clip"
        ).astype(jnp.float32),
        lax.psum(
            jnp.stack([weights_first[3], weights_second[3]]).astype(jnp.bfloat16), "clip"
        ).astype(jnp.float32),
        lax.psum(weights_first[4].astype(jnp.bfloat16), "clip").astype(jnp.float32),
        lax.psum(weights_second[4].astype(jnp.bfloat16), "clip").astype(jnp.float32),
    )
    return (
        output,
        grad_first,
        grad_modulation,
        summed[0],
        summed[1],
        summed[2],
        summed[3],
        summed[4],
        summed[5],
    )


F32 = jnp.float32
BF16 = jnp.bfloat16
VMEM_LIMIT = 58 * 1024 * 1024
NZ = 4
D = 1024
HPZ = 4
CONST = pl.Buffered(1)


def dot_nn(a, b):
    return lax.dot_general(a, b, (((1,), (0,)), ((), ())), preferred_element_type=F32)


def dot_nt(a, b):
    return lax.dot_general(a, b, (((1,), (1,)), ((), ())), preferred_element_type=F32)


def dot_tn(a, b):
    return lax.dot_general(a, b, (((0,), (0,)), ((), ())), preferred_element_type=F32)


def call(kernel, name, grid, in_specs, out_specs, out_shape, scratch, flops, nbytes):
    return pl.pallas_call(
        kernel,
        name=name,
        grid=grid,
        in_specs=in_specs,
        out_specs=out_specs,
        out_shape=out_shape,
        scratch_shapes=scratch,
        compiler_params=pltpu.CompilerParams(
            dimension_semantics=("arbitrary",) * len(grid), vmem_limit_bytes=VMEM_LIMIT
        ),
        cost_estimate=pl.CostEstimate(flops=flops, bytes_accessed=nbytes, transcendentals=0),
    )


def full(shape):
    return pl.BlockSpec(shape, lambda *ids: (0,) * len(shape), pipeline_mode=CONST)


def chunk_rows(i, size):
    return pl.ds(pl.multiple_of(i * size, size), size)


def ln_stats(x):
    mean = jnp.mean(x, axis=-1, keepdims=True)
    centred = x - mean
    rstd = lax.rsqrt(jnp.mean(centred * centred, axis=-1, keepdims=True) + EPS)
    return centred * rstd, rstd


def ln_back(grad, hat, rstd, scale):
    gh = grad * (1.0 + scale)
    m1 = jnp.mean(gh, axis=-1, keepdims=True)
    m2 = jnp.mean(gh * hat, axis=-1, keepdims=True)
    return rstd * (gh - m1 - hat * m2)


def piece_specs(k, row, count):
    tail = (count, D)
    return [
        pl.BlockSpec((2, 4) + tail, lambda d: (0, 0, row, 0), pipeline_mode=CONST),
        pl.BlockSpec((4, 1) + tail, lambda d: (0, jnp.maximum(d - 1, 0), row, 0)),
        pl.BlockSpec((4, 1) + tail, lambda d: (0, jnp.maximum(d - 1, 0), row, 0)),
    ]


def by_offset(d, body, local_ref, own_ref, other_ref):
    @pl.when(d == 0)
    def _():
        body(lambda m, r, n: local_ref[0, m, r : r + n, :], lambda m, r, n: local_ref[1, m, r : r + n, :])

    @pl.when(d > 0)
    def _():
        body(lambda m, r, n: own_ref[m, 0, r : r + n, :], lambda m, r, n: other_ref[m, 0, r : r + n, :])


def head_rows(own, other, row):
    parts = []
    for m in range(4):
        parts += [own(m, row, 32), other(m, row, 32)]
    return jnp.concatenate(parts, axis=0)


def unit_rows(get, row, count):
    return jnp.concatenate([get(m, row, count) for m in range(4)], axis=0)


def ln_qkv(hidden, mods, weights, base):
    rows = hidden.shape[0]
    step = 256

    def kernel(h_ref, m_ref, l_ref, w_ref, v_ref, normed_ref, qkv_ref):
        d = pl.program_id(0)

        @pl.when(d == 0)
        def _():
            def body(i, carry):
                sl = chunk_rows(i, step)
                hat, _ = ln_stats(h_ref[sl, :].astype(F32))
                normed_ref[sl, :] = (
                    hat * (1.0 + m_ref[base + 1 : base + 2, :]) + m_ref[base : base + 1, :]
                ).astype(BF16)
                return carry

            lax.fori_loop(0, rows // step, body, 0)

        def work(own, other):
            for t in range(3):
                qkv_ref[:, t * 256 : (t + 1) * 256] = dot_nt(
                    normed_ref[...], head_rows(own, other, t * 32)
                ).astype(BF16)

        by_offset(d, work, l_ref, w_ref, v_ref)

    return call(
        kernel,
        "ln_qkv",
        (NZ,),
        [full((rows, D)), full((12, D))] + piece_specs(128, 0, 96),
        [full((rows, D)), pl.BlockSpec((rows, 768), lambda z: (0, z))],
        [jax.ShapeDtypeStruct((rows, D), BF16), jax.ShapeDtypeStruct((rows, 3 * D), BF16)],
        [],
        2 * rows * D * 3 * D,
        rows * D * 12 + 6 * D * D,
    )(hidden, mods, *weights)


def build_bias(base_ref, bias_ref, fc_ref, slides, width, lanes_step):
    rows_step = width // slides
    for h in range(HPZ):
        for s in range(slides):
            off = (slides - 1 - s) * lanes_step
            tile = base_ref[h, :, off : off + width]
            if fc_ref is not None:
                tile = jnp.where(s < fc_ref[0], tile, NEGATIVE)
            bias_ref[h, s * rows_step : (s + 1) * rows_step, :] = tile


def attn_fwd(qkv, base, fc, slides, width, lanes_step, masked):
    rows = qkv.shape[0]
    windows = rows // width
    r_step, lanes = base.shape[1], base.shape[2]

    def kernel(x_ref, b_ref, fc_ref, o_ref, bias_ref):
        @pl.when(pl.program_id(1) == 0)
        def _():
            build_bias(b_ref, bias_ref, fc_ref if masked else None, slides, width, lanes_step)

        for h in range(HPZ):
            q = x_ref[:, h * HD : (h + 1) * HD] * 0.125
            k = x_ref[:, 256 + h * HD : 256 + (h + 1) * HD]
            v = x_ref[:, 512 + h * HD : 512 + (h + 1) * HD]
            score = dot_nt(k, q) + bias_ref[h]
            expo = jnp.exp(score - jnp.max(score, axis=0, keepdims=True))
            inv = 1.0 / jnp.sum(expo, axis=0, keepdims=True)
            probs = (expo * inv).astype(BF16)
            o_ref[:, h * HD : (h + 1) * HD] = dot_tn(probs, v).astype(BF16)

    return call(
        kernel,
        "attn_fwd",
        (NZ, windows),
        [
            pl.BlockSpec((width, 768), lambda z, w: (w, z)),
            pl.BlockSpec((HPZ, r_step, lanes), lambda z, w: (z, 0, 0)),
            pl.BlockSpec(memory_space=pltpu.SMEM),
        ],
        pl.BlockSpec((width, 256), lambda z, w: (w, z)),
        jax.ShapeDtypeStruct((rows, D), BF16),
        [pltpu.VMEM((HPZ, width, width), F32)],
        windows * 16 * width * width * HD * 16,
        rows * D * 8,
    )(qkv, base, fc)


def attn_bwd(qkv, grad_att, base, fc, slides, width, lanes_step, masked):
    rows = qkv.shape[0]
    windows = rows // width
    r_step, lanes = base.shape[1], base.shape[2]

    def kernel(x_ref, d_ref, b_ref, fc_ref, o_ref, gb_ref, bias_ref, acc_ref):
        @pl.when(pl.program_id(1) == 0)
        def _():
            build_bias(b_ref, bias_ref, fc_ref if masked else None, slides, width, lanes_step)
            acc_ref[...] = jnp.zeros_like(acc_ref)

        for h in range(HPZ):
            q = x_ref[:, h * HD : (h + 1) * HD] * 0.125
            k = x_ref[:, 256 + h * HD : 256 + (h + 1) * HD]
            v = x_ref[:, 512 + h * HD : 512 + (h + 1) * HD]
            da = d_ref[:, h * HD : (h + 1) * HD]
            score = dot_nt(k, q) + bias_ref[h]
            expo = jnp.exp(score - jnp.max(score, axis=0, keepdims=True))
            inv = 1.0 / jnp.sum(expo, axis=0, keepdims=True)
            probs = expo * inv
            dp = dot_nt(v, da)
            row = jnp.sum(dp * probs, axis=0, keepdims=True)
            dl = (probs * (dp - row)).astype(BF16)
            acc_ref[h] += dl.astype(F32)
            o_ref[:, h * HD : (h + 1) * HD] = (dot_tn(dl, k) * 0.125).astype(BF16)
            o_ref[:, 256 + h * HD : 256 + (h + 1) * HD] = dot_nn(dl, q).astype(BF16)
            o_ref[:, 512 + h * HD : 512 + (h + 1) * HD] = dot_nn(probs.astype(BF16), da).astype(
                BF16
            )

        @pl.when(pl.program_id(1) == windows - 1)
        def _():
            gb_ref[...] = jnp.zeros_like(gb_ref)
            for h in range(HPZ):
                for s in range(slides):
                    off = (slides - 1 - s) * lanes_step
                    gb_ref[h, :, off : off + width] += acc_ref[h, s * r_step : (s + 1) * r_step, :]

    return call(
        kernel,
        "attn_bwd",
        (NZ, windows),
        [
            pl.BlockSpec((width, 768), lambda z, w: (w, z)),
            pl.BlockSpec((width, 256), lambda z, w: (w, z)),
            pl.BlockSpec((HPZ, r_step, lanes), lambda z, w: (z, 0, 0)),
            pl.BlockSpec(memory_space=pltpu.SMEM),
        ],
        [
            pl.BlockSpec((width, 768), lambda z, w: (w, z)),
            pl.BlockSpec((HPZ, r_step, lanes), lambda z, w: (z, 0, 0)),
        ],
        [
            jax.ShapeDtypeStruct((rows, 3 * D), BF16),
            jax.ShapeDtypeStruct(base.shape, F32),
        ],
        [pltpu.VMEM((HPZ, width, width), F32), pltpu.VMEM((HPZ, width, width), F32)],
        windows * 16 * width * width * HD * 40,
        rows * D * 16,
    )(qkv, grad_att, base, fc)


def out_specs_of(row_block):
    return [
        pl.BlockSpec((2, 4, 32, D), lambda i: (0, 0, row_block, 0), pipeline_mode=CONST),
        pl.BlockSpec((4, 3, 32, D), lambda i: (0, 0, row_block, 0), pipeline_mode=CONST),
        pl.BlockSpec((4, 3, 32, D), lambda i: (0, 0, row_block, 0), pipeline_mode=CONST),
    ]


def out_rows(d, l_ref, w_ref, v_ref):
    if d == 0:
        return head_rows(
            lambda m, r, n: l_ref[0, m, :, :], lambda m, r, n: l_ref[1, m, :, :], 0
        )
    return head_rows(
        lambda m, r, n: w_ref[m, d - 1, :, :], lambda m, r, n: v_ref[m, d - 1, :, :], 0
    )


def out_proj(attended, weights, hidden, mods, base):
    rows = attended.shape[0]
    step = 256

    def kernel(a_ref, l_ref, w_ref, v_ref, h_ref, m_ref, br_ref, mid_ref, sh_ref):
        branch = jnp.zeros((step, D), F32)
        for d in range(NZ):
            branch += dot_nn(a_ref[:, d * 256 : (d + 1) * 256], out_rows(d, l_ref, w_ref, v_ref))
        br_ref[...] = branch.astype(BF16)
        middle = h_ref[...].astype(F32) + m_ref[base + 2 : base + 3, :] * branch
        mid_ref[...] = middle
        hat, _ = ln_stats(middle)
        sh_ref[...] = (
            hat * (1.0 + m_ref[base + 4 : base + 5, :]) + m_ref[base + 3 : base + 4, :]
        ).astype(BF16)

    tile = pl.BlockSpec((step, D), lambda i: (i, 0))
    return call(
        kernel,
        "out_proj",
        (rows // step,),
        [tile] + out_specs_of(3) + [tile, full((12, D))],
        [tile, tile, tile],
        [
            jax.ShapeDtypeStruct((rows, D), BF16),
            jax.ShapeDtypeStruct((rows, D), F32),
            jax.ShapeDtypeStruct((rows, D), BF16),
        ],
        [],
        2 * rows * D * D,
        rows * D * 14 + 2 * D * D,
    )(attended, *weights, hidden, mods)


GELU_C = 0.7978845608028654
GELU_A = 0.044715


def gelu_of(x):
    return 0.5 * x * (1.0 + jnp.tanh(GELU_C * (x + GELU_A * x * x * x)))


def gelu_both(x):
    x2 = x * x
    th = jnp.tanh(GELU_C * (x + GELU_A * x * x2))
    half = 0.5 * (1.0 + th)
    slope = half + 0.5 * x * (1.0 - th * th) * (GELU_C * (1.0 + 3.0 * GELU_A * x2))
    return x * half, slope


def ffn_fwd(shifted, weights, middle, mods, base):
    rows = shifted.shape[0]
    step = 256

    def kernel(x_ref, l_ref, w_ref, v_ref, mid_ref, m_ref, pre_ref, feed_ref, nx_ref, acc_ref):
        z = pl.program_id(0)

        def work(own, other):
            halves = (own, other)

            def body(i, carry):
                sl = chunk_rows(i, step)
                part = jnp.zeros((step, D), F32)
                for j, get in enumerate(halves):
                    pre = dot_nt(x_ref[sl, :], unit_rows(get, 0, 128))
                    pre_ref[sl, j * 512 : (j + 1) * 512] = pre.astype(BF16)
                    part += dot_nn(gelu_of(pre).astype(BF16), unit_rows(get, 128, 128))

                @pl.when(z == 0)
                def _():
                    acc_ref[sl, :] = part

                @pl.when((z > 0) & (z < NZ - 1))
                def _():
                    acc_ref[sl, :] += part

                @pl.when(z == NZ - 1)
                def _():
                    feed = acc_ref[sl, :] + part
                    feed_ref[sl, :] = feed.astype(BF16)
                    nx_ref[sl, :] = (
                        mid_ref[sl, :] + m_ref[base + 5 : base + 6, :] * feed
                    ).astype(BF16)

                return carry

            lax.fori_loop(0, rows // step, body, 0)

        by_offset(z, work, l_ref, w_ref, v_ref)

    return call(
        kernel,
        "ffn_fwd",
        (NZ,),
        [full((rows, D))] + piece_specs(256, 0, 256) + [full((rows, D)), full((12, D))],
        [pl.BlockSpec((rows, D), lambda z: (0, z)), full((rows, D)), full((rows, D))],
        [
            jax.ShapeDtypeStruct((rows, 4 * D), BF16),
            jax.ShapeDtypeStruct((rows, D), BF16),
            jax.ShapeDtypeStruct((rows, D), BF16),
        ],
        [pltpu.VMEM((rows, D), F32)],
        16 * rows * D * D,
        rows * D * 20 + 16 * D * D,
    )(shifted, *weights, middle, mods)


def ffn_bwd(grad, pre, shifted, weights, mods, base):
    rows = grad.shape[0]
    step = 256

    def kernel(
        g_ref, p_ref, x_ref, l_ref, w_ref, v_ref, m_ref, keep_ref, send_ref, gs_ref, gf_ref, act_ref, gp_ref
    ):
        z = pl.program_id(0)

        @pl.when(z == 0)
        def _():
            def body(i, carry):
                sl = chunk_rows(i, step)
                gf_ref[sl, :] = (
                    g_ref[sl, :].astype(F32) * m_ref[base + 5 : base + 6, :]
                ).astype(BF16)
                gs_ref[sl, :] = jnp.zeros((step, D), F32)
                return carry

            lax.fori_loop(0, rows // step, body, 0)

        def work(own, other):
            halves = (own, other)

            def body(i, carry):
                sl = chunk_rows(i, step)
                part = jnp.zeros((step, D), F32)
                for j, get in enumerate(halves):
                    cols = slice(j * 512, (j + 1) * 512)
                    act, slope = gelu_both(p_ref[sl, cols].astype(F32))
                    act_ref[sl, cols] = act.astype(BF16)
                    gpre = (dot_nt(gf_ref[sl, :], unit_rows(get, 128, 128)) * slope).astype(BF16)
                    gp_ref[sl, cols] = gpre
                    part += dot_nn(gpre, unit_rows(get, 0, 128))
                gs_ref[sl, :] += part
                return carry

            lax.fori_loop(0, rows // step, body, 0)

        by_offset(z, work, l_ref, w_ref, v_ref)
        for j, out_ref in enumerate((keep_ref, send_ref)):
            for i in range(2):
                cols = slice(j * 512 + i * 256, j * 512 + (i + 1) * 256)
                gd = dot_tn(act_ref[:, cols], gf_ref[...]).astype(BF16)
                gu = dot_tn(gp_ref[:, cols], x_ref[...]).astype(BF16)
                out_ref[2 * i : 2 * i + 2, 0, 0:128] = gu.reshape(2, 128, D)
                out_ref[2 * i : 2 * i + 2, 0, 128:256] = gd.reshape(2, 128, D)

    gspec = pl.BlockSpec((4, 1, 256, D), lambda z: (0, z, 0, 0))
    gshape = jax.ShapeDtypeStruct((4, NZ, 256, D), BF16)
    return call(
        kernel,
        "ffn_bwd",
        (NZ,),
        [
            full((rows, D)),
            pl.BlockSpec((rows, D), lambda z: (0, z)),
            full((rows, D)),
        ]
        + piece_specs(256, 0, 256)
        + [full((12, D))],
        [gspec, gspec, full((rows, D))],
        [gshape, gshape, jax.ShapeDtypeStruct((rows, D), F32)],
        [pltpu.VMEM((rows, D), BF16)] * 3,
        32 * rows * D * D,
        rows * D * 16 + 32 * D * D,
    )(grad, pre, shifted, *weights, mods)


def split_heads(value, keep_ref, send_ref, d, row):
    for m in range(4):
        keep_ref[m, d, row : row + 32] = value[m * 64 : m * 64 + 32]
        send_ref[m, d, row : row + 32] = value[m * 64 + 32 : m * 64 + 64]


def out_bwd(grad, grad_shifted, middle, feed, branch, attended, weights, mods, base):
    rows = grad.shape[0]
    step = 256
    steps = rows // step

    def kernel(
        g_ref, gs_ref, mid_ref, f_ref, b_ref, a_ref, l_ref, w_ref, v_ref, m_ref, gm_ref, ga_ref,
        keep_ref, send_ref, s_ref, gb_ref,
    ):
        i = pl.program_id(0)

        @pl.when(i == 0)
        def _():
            s_ref[...] = jnp.zeros_like(s_ref)

        g = g_ref[...].astype(F32)
        gs = gs_ref[...]
        hat, rstd = ln_stats(mid_ref[...])
        gm = g + ln_back(gs, hat, rstd, m_ref[base + 4 : base + 5, :])
        gm_ref[...] = gm
        s_ref[0:1, :] += jnp.sum(gs, axis=0, keepdims=True)
        s_ref[1:2, :] += jnp.sum(gs * hat, axis=0, keepdims=True)
        s_ref[2:3, :] += jnp.sum(gm * b_ref[...].astype(F32), axis=0, keepdims=True)
        s_ref[3:4, :] += jnp.sum(g * f_ref[...].astype(F32), axis=0, keepdims=True)
        gb = (gm * m_ref[base + 2 : base + 3, :]).astype(BF16)
        gb_ref[chunk_rows(i, step), :] = gb
        for d in range(NZ):
            ga_ref[:, d * 256 : (d + 1) * 256] = dot_nt(
                gb, out_rows(d, l_ref, w_ref, v_ref)
            ).astype(BF16)

        @pl.when(i == steps - 1)
        def _():
            for d in range(NZ):
                gw = dot_tn(a_ref[:, d * 256 : (d + 1) * 256], gb_ref[...]).astype(BF16)
                split_heads(gw, keep_ref, send_ref, d, 0)

    tile = pl.BlockSpec((step, D), lambda i: (i, 0))
    gshape = jax.ShapeDtypeStruct((4, NZ, 32, D), BF16)
    return call(
        kernel,
        "out_bwd",
        (steps,),
        [tile, tile, tile, tile, tile, full((rows, D))] + out_specs_of(3) + [full((12, D))],
        [tile, tile, full(gshape.shape), full(gshape.shape), full((8, D))],
        [
            jax.ShapeDtypeStruct((rows, D), F32),
            jax.ShapeDtypeStruct((rows, D), BF16),
            gshape,
            gshape,
            jax.ShapeDtypeStruct((8, D), F32),
        ],
        [pltpu.VMEM((rows, D), BF16)],
        4 * rows * D * D,
        rows * D * 24 + 4 * D * D,
    )(grad, grad_shifted, middle, feed, branch, attended, *weights, mods)


def qkv_bwd(
    grad_proj, normed, weights, out_keep, out_send, table_rows, hidden, grad_middle, mods, base, out_dtype
):
    rows = normed.shape[0]
    step = 256

    def kernel(
        p_ref, n_ref, l_ref, w_ref, v_ref, ok_ref, os_ref, t_ref, h_ref, gm_ref, m_ref, keep_ref,
        send_ref, gh_ref, s_ref, acc_ref,
    ):
        z = pl.program_id(0)
        for t in range(3):
            gw = dot_tn(p_ref[:, t * 256 : (t + 1) * 256], n_ref[...]).astype(BF16)
            split_heads(gw, keep_ref, send_ref, 0, t * 32)
        keep_ref[:, :, 96:128] = ok_ref[...]
        send_ref[:, :, 96:128] = os_ref[...]
        keep_ref[:, :, 128:144] = t_ref[...]
        send_ref[:, :, 128:144] = t_ref[...]

        @pl.when(z == 0)
        def _():
            acc_ref[...] = jnp.zeros_like(acc_ref)
            s_ref[...] = jnp.zeros_like(s_ref)

        def work(own, other):
            def body(i, carry):
                sl = chunk_rows(i, step)
                part = jnp.zeros((step, D), F32)
                for t in range(3):
                    part += dot_nn(
                        p_ref[sl, t * 256 : (t + 1) * 256], head_rows(own, other, t * 32)
                    )
                acc_ref[sl, :] += part
                return carry

            lax.fori_loop(0, rows // step, body, 0)

        by_offset(z, work, l_ref, w_ref, v_ref)

        @pl.when(z == NZ - 1)
        def _():
            def tail(i, carry):
                sl = chunk_rows(i, step)
                gn = acc_ref[sl, :]
                hat, rstd = ln_stats(h_ref[sl, :].astype(F32))
                gh = gm_ref[sl, :] + ln_back(gn, hat, rstd, m_ref[base + 1 : base + 2, :])
                gh_ref[sl, :] = gh.astype(out_dtype)
                s_ref[0:1, :] += jnp.sum(gn, axis=0, keepdims=True)
                s_ref[1:2, :] += jnp.sum(gn * hat, axis=0, keepdims=True)
                return carry

            lax.fori_loop(0, rows // step, tail, 0)

    gspec = pl.BlockSpec((4, 1, 144, D), lambda z: (0, z, 0, 0))
    ospec = pl.BlockSpec((4, 1, 32, D), lambda z: (0, z, 0, 0))
    tspec = pl.BlockSpec((4, 1, 16, D), lambda z: (0, z, 0, 0))
    gshape = jax.ShapeDtypeStruct((4, NZ, 144, D), BF16)
    return call(
        kernel,
        "qkv_bwd",
        (NZ,),
        [pl.BlockSpec((rows, 768), lambda z: (0, z)), full((rows, D))]
        + piece_specs(128, 0, 96)
        + [ospec, ospec, tspec, full((rows, D)), full((rows, D)), full((12, D))],
        [gspec, gspec, full((rows, D)), full((8, D))],
        [
            gshape,
            gshape,
            jax.ShapeDtypeStruct((rows, D), out_dtype),
            jax.ShapeDtypeStruct((8, D), F32),
        ],
        [pltpu.VMEM((rows, D), F32)],
        12 * rows * D * D,
        rows * D * 20 + 12 * D * D,
    )(grad_proj, normed, *weights, out_keep, out_send, table_rows, hidden, grad_middle, mods)


def partner(values):
    return lax.ppermute(values, "head", [(i, i ^ 1) for i in range(NZ)])


def rows_to_spatial(rows, odd):
    cols = rows.shape[1]
    whole = lax.dynamic_slice(rows, (256 * odd, 0), (1024, cols))
    part = lax.dynamic_slice(rows, (1024 * (1 - odd), 0), (256, cols)).reshape(8, 2, 16, cols)
    wins = whole.reshape(2, 16, 2, 16, cols).transpose(0, 2, 1, 3, 4).reshape(1024, cols)
    left, right = part[:, 0].reshape(128, cols), part[:, 1].reshape(128, cols)
    keep = jnp.where(odd == 0, left, right)
    got = partner(jnp.where(odd == 0, right, left))
    top, bottom = jnp.where(odd == 0, keep, got), jnp.where(odd == 0, got, keep)
    return jnp.concatenate([wins, top, bottom], axis=0)


def spatial_to_rows(wins, odd):
    cols = wins.shape[1]
    whole = wins[:1024].reshape(2, 2, 16, 16, cols).transpose(0, 2, 1, 3, 4).reshape(1024, cols)
    top, bottom = wins[1024:1152], wins[1152:]
    keep = jnp.where(odd == 0, top, bottom)
    got = partner(jnp.where(odd == 0, bottom, top))
    left, right = jnp.where(odd == 0, keep, got), jnp.where(odd == 0, got, keep)
    part = jnp.stack([left.reshape(8, 16, cols), right.reshape(8, 16, cols)], axis=1)
    part = part.reshape(256, cols)
    return jnp.where(
        odd == 0,
        jnp.concatenate([whole, part], axis=0),
        jnp.concatenate([part, whole], axis=0),
    )


def block_order():
    places = {}
    for z in range(NZ):
        first = 5 * (z // 2)
        halves = (first, first + 1) if z % 2 == 0 else (first + 3, first + 4)
        listed = [(h, x) for h in halves for x in (0, 1)] + [(first + 2, z % 2)]
        for k, item in enumerate(listed):
            places[item] = z * 5 + k
    return [places[(2 * t + wy, wx)] for wy in (0, 1) for wx in (0, 1) for t in range(PADF)]


def exchange(values):
    return lax.all_to_all(values, "head", 0, 0, tiled=True)


def spatial_to_tubes(wins):
    cols = wins.shape[1]
    quads = wins.reshape(5, 2, 8, 2, 8, cols).transpose(1, 3, 0, 2, 4, 5).reshape(1280, cols)
    got = exchange(quads)
    return jnp.concatenate([got[64 * b : 64 * (b + 1)] for b in block_order()], axis=0)


def tubes_to_spatial(tubes):
    cols = tubes.shape[1]
    order = block_order()
    back = [order.index(b) for b in range(20)]
    got = exchange(jnp.concatenate([tubes[64 * b : 64 * (b + 1)] for b in back], axis=0))
    quads = got.reshape(2, 2, 5, 8, 8, cols).transpose(2, 0, 3, 1, 4, 5)
    return quads.reshape(1280, cols)


def toeplitz(side):
    span = 2 * side - 1
    b = lax.broadcasted_iota(jnp.int32, (span, side, side), 0)
    j = lax.broadcasted_iota(jnp.int32, (span, side, side), 1)
    i = lax.broadcasted_iota(jnp.int32, (span, side, side), 2)
    return (b == i - j + side - 1).astype(F32)


def toeplitz_pair(side):
    span = 2 * side - 1
    shape = (span * span, side * side, side * side)
    r = lax.broadcasted_iota(jnp.int32, shape, 0)
    j = lax.broadcasted_iota(jnp.int32, shape, 1)
    i = lax.broadcasted_iota(jnp.int32, shape, 2)
    dy = i // side - j // side + side - 1
    dx = i % side - j % side + side - 1
    return (r == dy * span + dx).astype(F32)


CORE, ROW_X, ROW_Y = 1, 2, 4


def swap(values, bit):
    return lax.ppermute(values, "clip", [(i, i ^ bit) for i in range(8)])


def from_z(values, d):
    return lax.ppermute(values, "head", [((i + d) % NZ, i) for i in range(NZ)])


def to_z(values, d):
    return lax.ppermute(values, "head", [(i, (i + d) % NZ) for i in range(NZ)])


def sync(*values):
    return lax.optimization_barrier(values)


def add(first, second):
    return (first.astype(F32) + second.astype(F32)).astype(BF16)


def line_stage(piece):
    return jnp.stack([from_z(piece, d) for d in (1, 2, 3)])


def cross_stage(own):
    return own, swap(own, ROW_X), swap(own, ROW_Y)


def corner_stage(crossed, axis):
    own, by_x, by_y = crossed
    half = own.shape[axis] // 2
    first = swap(lax.slice_in_dim(by_x, 0, half, axis=axis), ROW_Y)
    second = swap(lax.slice_in_dim(by_y, half, 2 * half, axis=axis), ROW_X)
    return jnp.stack([own, by_x, by_y, jnp.concatenate([first, second], axis=axis)])


def sum_core(pair):
    return add(pair[0], swap(pair[1], CORE))


def sum_cross(total):
    k = total.shape[2]
    total = total.reshape(2, 2, NZ, k, D)
    first, second = total[:, :, :, : k // 2], total[:, :, :, k // 2 :]
    first = add(first[:, 0], swap(first[:, 1], ROW_X))
    second = add(second[0], swap(second[1], ROW_Y))
    return first, second


def sum_corner(halves):
    first, second = halves
    first = add(first[0], swap(first[1], ROW_Y))
    second = add(second[0], swap(second[1], ROW_X))
    return first, second


def sum_line(halves):
    first, second = halves
    mine = jnp.concatenate([first[0], second[0]], axis=0).astype(F32)
    for d in (1, 2, 3):
        part = to_z(jnp.concatenate([first[d], second[d]], axis=0), d)
        mine = mine + part.astype(F32)
    return mine.astype(BF16)


def sum_z(values):
    total = values
    for d in (1, 2, 3):
        total = total + from_z(values, d)
    return total


def by_place(blocks, c):
    return jnp.concatenate(
        [lax.dynamic_slice_in_dim(blocks, c ^ i, 1, axis=0) for i in range(8)], axis=0
    )


def on_device_windows(
    tokens, d_out, modulation, frame_counts, w_qkv, w_out, w_up, w_down, table_s, table_t
):
    z = lax.axis_index("head")
    c = lax.axis_index("clip")
    chip = c // 2
    odd = z % 2
    mods = modulation[0]
    n_s, n_t = table_s.shape[1], table_t.shape[1]
    hot_s, hot_t = toeplitz(SWIN), toeplitz_pair(TWIN)

    def own_pieces(b):
        qkv = lax.dynamic_slice_in_dim(w_qkv[b], c * 32, 32, 2).transpose(0, 2, 1)
        out = lax.dynamic_slice_in_dim(w_out[b], c * 32, 32, 0)
        up = lax.dynamic_slice_in_dim(w_up[b], c * 128, 128, 1).T
        down = lax.dynamic_slice_in_dim(w_down[b], c * 128, 128, 0)
        return (
            jnp.concatenate([qkv.reshape(96, D), out], axis=0),
            jnp.concatenate([up, down], axis=0),
        )

    def local_pieces(qkv, out, up, down):
        up = up.T.reshape(8, 128, D)
        down = down.reshape(8, 128, D)
        qkv = qkv.transpose(0, 2, 1).reshape(3, 8, 32, D).transpose(1, 0, 2, 3)
        attn = jnp.concatenate([qkv.reshape(8, 96, D), out.reshape(8, 32, D)], axis=1)
        feed = jnp.concatenate([up, down], axis=1)
        moved = [by_place(value, c) for value in (attn, feed)]
        return [v.reshape((4, 2) + v.shape[1:]).transpose(1, 0, 2, 3) for v in moved]

    def spatial_base(tables):
        base = jnp.einsum(
            "hab,bji->hjai", tables[:, :n_s].reshape(16, 31, 31), hot_s, precision=HIGHEST_PRECISION
        ).reshape(16, 16, 496)
        return jnp.pad(base, ((0, 0), (0, 0), (0, 16)))

    def tube_base(tables):
        base = jnp.einsum(
            "htr,rjk->hjtk", tables[:, n_s:].reshape(16, 9, 225), hot_t, precision=HIGHEST_PRECISION
        ).reshape(16, 64, 576)
        return jnp.pad(base, ((0, 0), (0, 0), (0, 64)))

    def table_rows(values):
        values = jnp.pad(values, ((0, 0), (0, 16 * D - values.shape[1]))).astype(BF16)
        return values.reshape(NZ, 4, 16, D).transpose(1, 0, 2, 3)

    kinds = ((16, 256, 16, False), (5, 320, 64, True))

    piece_a0, piece_f0 = own_pieces(0)
    line_a0 = line_stage(piece_a0)
    table_piece = jnp.concatenate([table_s, table_t], axis=1)
    tables = jnp.stack([table_piece] + [from_z(table_piece, d) for d in (1, 2, 3)])
    line_a0, piece_f0, tables = sync(line_a0, piece_f0, tables)
    line_f0 = line_stage(piece_f0)
    own_a0 = corner_stage(cross_stage(line_a0), 1)
    other_a0 = swap(own_a0, CORE)
    tables = jnp.concatenate(
        [lax.dynamic_slice_in_dim(tables, chip ^ m, 1, axis=1) for m in range(4)], axis=1
    ).reshape(16, n_s + n_t)
    base_s = spatial_base(tables)
    hidden0 = rows_to_spatial(tokens, odd)
    local_a0, local_f0 = local_pieces(w_qkv[0], w_out[0], w_up[0], w_down[0])
    own_a0, other_a0, line_f0, base_s, hidden0, local_a0, local_f0, tables = sync(
        own_a0, other_a0, line_f0, base_s, hidden0, local_a0, local_f0, tables
    )
    weights_a0 = (local_a0, own_a0, other_a0)
    cross_f0 = cross_stage(line_f0)
    piece_a1, piece_f1 = own_pieces(1)
    line_a1 = line_stage(piece_a1)
    normed0, qkv0 = ln_qkv(hidden0, mods, weights_a0, 0)
    attended0 = attn_fwd(qkv0, base_s, frame_counts, *kinds[0])
    attended0, cross_f0, line_a1, piece_f1 = sync(attended0, cross_f0, line_a1, piece_f1)
    own_f0 = corner_stage(cross_f0, 1)
    other_f0 = swap(own_f0, CORE)
    branch0, middle0, shifted0 = out_proj(attended0, weights_a0, hidden0, mods, 0)
    shifted0, own_f0, other_f0, line_a1, piece_f1 = sync(
        shifted0, own_f0, other_f0, line_a1, piece_f1
    )
    weights_f0 = (local_f0, own_f0, other_f0)
    line_f1 = line_stage(piece_f1)
    cross_a1 = cross_stage(line_a1)
    pre0, feed0, hidden1 = ffn_fwd(shifted0, weights_f0, middle0, mods, 0)
    hidden1, line_f1, cross_a1, tables, d_out, w_qkv, w_out, w_up, w_down = sync(
        hidden1, line_f1, cross_a1, tables, d_out, w_qkv, w_out, w_up, w_down
    )
    tubes1 = spatial_to_tubes(hidden1)
    own_a1 = corner_stage(cross_a1, 1)
    other_a1 = swap(own_a1, CORE)
    cross_f1 = cross_stage(line_f1)
    local_a1, local_f1 = local_pieces(w_qkv[1], w_out[1], w_up[1], w_down[1])
    base_t = tube_base(tables)
    spatial_d = rows_to_spatial(d_out, odd)
    tubes1, own_a1, other_a1, cross_f1, local_a1, local_f1, base_t, spatial_d = sync(
        tubes1, own_a1, other_a1, cross_f1, local_a1, local_f1, base_t, spatial_d
    )
    weights_a1 = (local_a1, own_a1, other_a1)
    own_f1 = corner_stage(cross_f1, 1)
    tubes_d = spatial_to_tubes(spatial_d)
    normed1, qkv1 = ln_qkv(tubes1, mods, weights_a1, 6)
    qkv1, own_f1 = sync(qkv1, own_f1)
    other_f1 = swap(own_f1, CORE)
    attended1 = attn_fwd(qkv1, base_t, frame_counts, *kinds[1])
    branch1, middle1, shifted1 = out_proj(attended1, weights_a1, tubes1, mods, 6)
    shifted1, other_f1 = sync(shifted1, other_f1)
    weights_f1 = (local_f1, own_f1, other_f1)
    pre1, feed1, hidden2 = ffn_fwd(shifted1, weights_f1, middle1, mods, 6)
    frame = lax.broadcasted_iota(jnp.int32, (1280, 1), 0) % 320 // 64
    live = frame < frame_counts[0]
    grad2 = jnp.where(live, tubes_d, 0)
    hidden2, grad2 = sync(hidden2, grad2)
    out_wins = tubes_to_spatial(jnp.where(live, hidden2, 0))
    f1_keep, f1_send, g_shift1 = ffn_bwd(grad2, pre1, shifted1, weights_f1, mods, 6)
    f1_keep, f1_send, g_shift1, out_wins = sync(f1_keep, f1_send, g_shift1, out_wins)
    total_f1 = sum_core((f1_keep, f1_send))
    g_mid1, g_att1, o1_keep, o1_send, sums_o1 = out_bwd(
        grad2, g_shift1, middle1, feed1, branch1, attended1, weights_a1, mods, 6
    )
    g_att1, total_f1, out_wins = sync(g_att1, total_f1, out_wins)
    half_f1 = sum_cross(total_f1)
    g_proj1, g_base1 = attn_bwd(qkv1, g_att1, base_t, frame_counts, *kinds[1])
    g_proj1, g_base1, half_f1 = sync(g_proj1, g_base1, half_f1)
    half_f1 = sum_corner(half_f1)
    gt_t = jnp.einsum(
        "hjtk,rjk->htr",
        g_base1[:, :, :576].reshape(16, 64, 9, 64),
        hot_t,
        precision=HIGHEST_PRECISION,
    ).reshape(16, n_t)
    a1_keep, a1_send, g_hid1, sums_q1 = qkv_bwd(
        g_proj1, normed1, weights_a1, o1_keep, o1_send, table_rows(gt_t), tubes1, g_mid1, mods, 6, BF16
    )
    a1_keep, a1_send, g_hid1, half_f1 = sync(a1_keep, a1_send, g_hid1, half_f1)
    grad1 = tubes_to_spatial(g_hid1)
    half_a1 = sum_corner(sum_cross(sum_core((a1_keep, a1_send))))
    mod1 = jnp.concatenate([sums_q1[0:2], sums_o1[2:3], sums_o1[0:2], sums_o1[3:4]], axis=0)
    output = spatial_to_rows(out_wins, odd)
    grad1, half_a1, half_f1, output = sync(grad1, half_a1, half_f1, output)
    mine_f1, mine_a1 = sum_line(half_f1), sum_line(half_a1)
    f0_keep, f0_send, g_shift0 = ffn_bwd(grad1, pre0, shifted0, weights_f0, mods, 0)
    f0_keep, f0_send, g_shift0, mine_f1, mine_a1 = sync(
        f0_keep, f0_send, g_shift0, mine_f1, mine_a1
    )
    total_f0 = sum_core((f0_keep, f0_send))
    cross1 = cross_stage(jnp.concatenate([mine_f1, mine_a1], axis=0))
    g_mid0, g_att0, o0_keep, o0_send, sums_o0 = out_bwd(
        grad1, g_shift0, middle0, feed0, branch0, attended0, weights_a0, mods, 0
    )
    g_att0, total_f0, cross1 = sync(g_att0, total_f0, cross1)
    half_f0 = sum_cross(total_f0)
    g_proj0, g_base0 = attn_bwd(qkv0, g_att0, base_s, frame_counts, *kinds[0])
    g_proj0, g_base0, half_f0, cross1 = sync(g_proj0, g_base0, half_f0, cross1)
    half_f0 = sum_corner(half_f0)
    plane1 = corner_stage(cross1, 0)
    gt_s = jnp.einsum(
        "hjai,bji->hab",
        g_base0[:, :, :496].reshape(16, 16, 31, 16),
        hot_s,
        precision=HIGHEST_PRECISION,
    ).reshape(16, n_s)
    a0_keep, a0_send, grad0, sums_q0 = qkv_bwd(
        g_proj0, normed0, weights_a0, o0_keep, o0_send, table_rows(gt_s), hidden0, g_mid0, mods, 0, F32
    )
    a0_keep, a0_send, grad0, half_f0, plane1, sums_q0 = sync(
        a0_keep, a0_send, grad0, half_f0, plane1, sums_q0
    )
    mod0 = jnp.concatenate([sums_q0[0:2], sums_o0[2:3], sums_o0[0:2], sums_o0[3:4]], axis=0)
    grad_tokens = spatial_to_rows(grad0, odd)
    grad_mods = sum_z(jnp.concatenate([mod0, mod1], axis=0))[None]
    mine_f0 = sum_line(half_f0)
    mine_a0 = sum_line(sum_corner(sum_cross(sum_core((a0_keep, a0_send)))))
    plane0f = corner_stage(cross_stage(mine_f0), 0)
    plane0a = corner_stage(cross_stage(mine_a0), 0)

    def placed(plane):
        both = jnp.stack([plane, swap(plane, CORE)], axis=1)
        return by_place(both.reshape((8,) + plane.shape[1:]), c)

    done1 = placed(plane1)
    pairs = ((placed(plane0f), placed(plane0a)), (done1[:, :256], done1[:, 256:]))
    g_qkv, g_out, g_up, g_down = [], [], [], []
    for feed, attn in pairs:
        g_qkv.append(
            attn[:, :96].reshape(8, 3, 32, D).transpose(1, 3, 0, 2).reshape(3, D, 256).astype(F32)
        )
        g_out.append(attn[:, 96:128].reshape(256, D).astype(F32))
        g_up.append(feed[:, :128].reshape(D, D).T.astype(F32))
        g_down.append(feed[:, 128:].reshape(D, D).astype(F32))

    def table_of(attn, size):
        return attn[::2, 128:144].reshape(4, 16 * D)[:, :size].astype(F32)

    return (
        output,
        grad_tokens,
        grad_mods,
        jnp.stack(g_qkv),
        jnp.stack(g_out),
        jnp.stack(g_up),
        jnp.stack(g_down),
        table_of(pairs[0][1], n_s),
        table_of(pairs[1][1], n_t),
    )


def solution(mesh):
    if mesh.shape["head"] == NZ and mesh.shape["clip"] == 8:
        body = on_device_windows
    else:
        body = on_device
    return jax.shard_map(
        body,
        mesh=mesh,
        in_specs=(
            P(("clip", "head"), None),
            P(("clip", "head"), None),
            P("clip", None, None),
            P("clip"),
            P(None, None, None, "head"),
            P(None, "head", None),
            P(None, None, "head"),
            P(None, "head", None),
            P("head", None),
            P("head", None),
        ),
        out_specs=(
            P(("clip", "head"), None),
            P(("clip", "head"), None),
            P("clip", None, None),
            P(None, None, None, "head"),
            P(None, "head", None),
            P(None, None, "head"),
            P(None, "head", None),
            P("head", None),
            P("head", None),
        ),
        check_vma=False,
    )
```

```python
import jax
import jax.numpy as jnp
from jax import lax
from jax.experimental import pallas as pl
from jax.experimental.pallas import tpu as pltpu
from jax.sharding import PartitionSpec as P

HD = 64
FH = 32
FW = 32
SWIN = 16
TWIN = 8
PADF = 5


EPS = 1e-06
HIGHEST_PRECISION = lax.Precision.HIGHEST
NEGATIVE = -1e30


def layer_norm(values, shift_row, scale_row):
    average = jnp.mean(values, axis=-1, keepdims=True)
    centred = values - average
    spread = jnp.mean(centred * centred, axis=-1, keepdims=True)
    return centred * lax.rsqrt(spread + EPS) * (1.0 + scale_row) + shift_row


def gelu_tanh(values):
    return jax.nn.gelu(values, approximate=True)


def window_index(side_t, side_len):
    window_size = side_t * side_len * side_len
    places = jnp.arange(window_size, dtype=jnp.int32)
    time_pos = places // (side_len * side_len)
    height_pos = places // side_len % side_len
    width_pos = places % side_len
    span_len = 2 * side_len - 1
    return (
        (time_pos[:, None] - time_pos[None, :] + side_t - 1) * span_len * span_len
        + (height_pos[:, None] - height_pos[None, :] + side_len - 1) * span_len
        + (width_pos[:, None] - width_pos[None, :] + side_len - 1)
    )


def to_windows(values, side_t, side_len):
    tail_shape = values.shape[1:]
    frames = values.shape[0] // (FH * FW)
    shaped = values.reshape(
        (frames // side_t, side_t, FH // side_len, side_len, FW // side_len, side_len) + tail_shape
    )
    axis_order = (0, 2, 4, 1, 3, 5) + tuple(range(6, 6 + len(tail_shape)))
    shaped = shaped.transpose(axis_order)
    return shaped.reshape((-1, side_t * side_len * side_len) + tail_shape)


def from_windows(values, side_t, side_len):
    tail_shape = values.shape[2:]
    blocks_high = FH // side_len
    blocks_wide = FW // side_len
    frame_groups = values.shape[0] // (blocks_high * blocks_wide)
    shaped = values.reshape(
        (frame_groups, blocks_high, blocks_wide, side_t, side_len, side_len) + tail_shape
    )
    axis_order = (0, 3, 1, 4, 2, 5) + tuple(range(6, 6 + len(tail_shape)))
    return shaped.transpose(axis_order).reshape((frame_groups * side_t * FH * FW,) + tail_shape)


def on_device(
    tokens, d_out, modulation, frame_counts, w_qkv, w_out, w_up, w_down, table_s, table_t
):
    local_rows = tokens.shape[0]
    clip_len = PADF * FH * FW
    group_clips = modulation.shape[0]
    group_rows = group_clips * clip_len
    scale_dot = HD ** (-0.5)
    my_index = lax.axis_index("head")
    first_row = my_index * local_rows
    row_ids = first_row + jnp.arange(local_rows, dtype=jnp.int32)
    clip_slots = jnp.arange(group_clips, dtype=jnp.int32)
    row_onehot = ((row_ids // clip_len)[:, None] == clip_slots[None, :]).astype(jnp.float32)
    count_float = frame_counts.astype(jnp.float32)
    row_frames = jnp.dot(row_onehot, count_float, precision=HIGHEST_PRECISION)
    row_keep = ((row_ids % clip_len // (FH * FW)).astype(jnp.float32) < row_frames).astype(
        jnp.float32
    )[:, None]
    group_ids = jnp.arange(group_rows, dtype=jnp.int32)
    group_onehot = ((group_ids // clip_len)[:, None] == clip_slots[None, :]).astype(jnp.float32)
    group_frames = jnp.dot(group_onehot, count_float, precision=HIGHEST_PRECISION)
    group_keep = (group_ids % clip_len // (FH * FW)).astype(jnp.float32) < group_frames

    def block_shape(block_id):
        if block_id == 0:
            return (1, SWIN)
        return (PADF, TWIN)

    def mod_row(slot):
        return jnp.dot(row_onehot, modulation[:, slot, :], precision=HIGHEST_PRECISION)

    def rows_in(values):
        return lax.all_gather(values, "head", axis=0, tiled=True)

    def grads_in(values):
        return lax.all_gather(values, "head", axis=0, tiled=True)

    def rows_out(full_rows, weight):
        return lax.psum_scatter(
            jnp.dot(full_rows, weight, preferred_element_type=jnp.float32).astype(jnp.bfloat16),
            "head",
            scatter_dimension=0,
            tiled=True,
        ).astype(jnp.float32)

    def grads_out(full_rows, weight, einsum_form):
        return lax.psum_scatter(
            jnp.einsum(einsum_form, full_rows, weight, preferred_element_type=jnp.float32).astype(
                jnp.bfloat16
            ),
            "head",
            scatter_dimension=0,
            tiled=True,
        ).astype(jnp.float32)

    def rows_keep(block_id):
        if block_id == 0:
            return None
        return to_windows(group_keep[:, None], PADF, TWIN)[:, :, 0]

    def shape_windows(projected, side_t, side_len):
        head_count = projected.shape[-1] // HD
        window_size = side_t * side_len * side_len
        windows = to_windows(projected, side_t, side_len)
        return windows.reshape(windows.shape[0], window_size, 3, head_count, HD)

    def shape_grad(grad_attended, side_t, side_len):
        head_count = grad_attended.shape[-1] // HD
        window_size = side_t * side_len * side_len
        windows = to_windows(grad_attended, side_t, side_len)
        return windows.reshape(windows.shape[0], window_size, head_count, HD)

    def flat_rows(windowed, side_t, side_len):
        return from_windows(windowed, side_t, side_len)

    def logits_of(queries, key_rows, table_arg, rel_index, keep_win):
        logits = (
            jnp.einsum("wqhe,wkhe->whqk", queries, key_rows, preferred_element_type=jnp.float32)
            * scale_dot
        )
        logits = logits + table_arg[:, rel_index][None]
        if keep_win is not None:
            logits = jnp.where(keep_win[:, None, None, :], logits, NEGATIVE)
        return logits

    def attend(windows, table_arg, rel_index, keep_win):
        logits = logits_of(windows[:, :, 0], windows[:, :, 1], table_arg, rel_index, keep_win)
        row_max = jnp.max(logits, axis=-1, keepdims=True)
        exponent = jnp.exp(logits - row_max)
        row_total = jnp.sum(exponent, axis=-1, keepdims=True)
        probs = exponent / row_total
        log_total = row_max + jnp.log(row_total)
        attended = jnp.einsum(
            "whqk,wkhe->wqhe",
            probs.astype(jnp.bfloat16),
            windows[:, :, 2],
            preferred_element_type=jnp.float32,
        )
        return (attended.reshape(attended.shape[0], attended.shape[1], -1), log_total)

    def attend_back(windows, grad_windows, log_total, table_arg, rel_index, keep_win):
        queries = windows[:, :, 0]
        key_rows = windows[:, :, 1]
        value_rows = windows[:, :, 2]
        logits = logits_of(queries, key_rows, table_arg, rel_index, keep_win)
        probs = jnp.exp(logits - log_total)
        grad_probs = jnp.einsum(
            "wqhe,wkhe->whqk", grad_windows, value_rows, preferred_element_type=jnp.float32
        )
        grad_values = jnp.einsum(
            "whqk,wqhe->wkhe",
            probs.astype(jnp.bfloat16),
            grad_windows,
            preferred_element_type=jnp.float32,
        )
        grad_logits = (
            probs * (grad_probs - jnp.sum(grad_probs * probs, axis=-1, keepdims=True))
        ).astype(jnp.bfloat16)
        head_count = queries.shape[2]
        table_terms = jnp.sum(grad_logits.astype(jnp.float32), axis=0).reshape(head_count, -1)
        grad_table = jax.ops.segment_sum(
            table_terms.T, rel_index.reshape(-1), num_segments=table_arg.shape[1]
        ).T
        grad_queries = (
            jnp.einsum("whqk,wkhe->wqhe", grad_logits, key_rows, preferred_element_type=jnp.float32)
            * scale_dot
        )
        grad_keys = (
            jnp.einsum("whqk,wqhe->wkhe", grad_logits, queries, preferred_element_type=jnp.float32)
            * scale_dot
        )
        grad_stack = jnp.stack([grad_queries, grad_keys, grad_values], axis=2)
        return (
            grad_stack.reshape(grad_stack.shape[0], grad_stack.shape[1], 3, head_count * HD),
            grad_table,
        )

    def forward_block(hidden, block_id):
        side_t, side_len = block_shape(block_id)
        table_local = table_s if block_id == 0 else table_t
        rel_index = window_index(side_t, side_len)
        normed = layer_norm(hidden, mod_row(6 * block_id), mod_row(6 * block_id + 1)).astype(
            jnp.bfloat16
        )
        plan = None
        normed_in = rows_in(normed)
        qkv_use, out_use, table_use = (w_qkv[block_id], w_out[block_id], table_local)
        keep_win = rows_keep(block_id)
        projected = jnp.einsum(
            "gd,cde->gce", normed_in, qkv_use, preferred_element_type=jnp.float32
        ).astype(jnp.bfloat16)
        windows = shape_windows(projected, side_t, side_len)
        attended_win, log_total = attend(windows, table_use, rel_index, keep_win)
        attended = flat_rows(attended_win, side_t, side_len).astype(jnp.bfloat16)
        branch = rows_out(attended, out_use)
        middle = hidden + mod_row(6 * block_id + 2) * branch
        shifted = layer_norm(middle, mod_row(6 * block_id + 3), mod_row(6 * block_id + 4)).astype(
            jnp.bfloat16
        )
        up_full, down_full = (
            lax.all_gather(w_up[block_id], "head", axis=1, tiled=True),
            lax.all_gather(w_down[block_id], "head", axis=0, tiled=True),
        )
        pre_gelu = jnp.dot(shifted, up_full, preferred_element_type=jnp.float32)
        activated = gelu_tanh(pre_gelu).astype(jnp.bfloat16)
        feed_out = jnp.dot(activated, down_full, preferred_element_type=jnp.float32)
        mlp_state = (shifted, pre_gelu, activated, up_full, down_full)
        result = middle + mod_row(6 * block_id + 5) * feed_out
        attn_state = (
            normed_in,
            projected,
            log_total,
            attended,
            qkv_use,
            out_use,
            table_use,
            keep_win,
            plan,
        )
        saved_state = (hidden, attn_state, branch, middle, feed_out, mlp_state)
        return (saved_state, result)

    def backward_block(saved_state, grad_result, block_id):
        hidden, attn_state, branch, middle, feed_out, mlp_state = saved_state
        normed_in, projected, log_total, attended, qkv_use, out_use, table_use, keep_win, plan = (
            attn_state
        )
        shifted_in, pre_gelu, activated, up_weight, down_weight = mlp_state
        side_t, side_len = block_shape(block_id)
        rel_index = window_index(side_t, side_len)
        grad_feed = (grad_result * mod_row(6 * block_id + 5)).astype(jnp.bfloat16)
        grad_gate_mlp = grad_result * feed_out
        grad_down = jnp.einsum(
            "gf,gd->fd", activated, grad_feed, preferred_element_type=jnp.float32
        )
        grad_activated = jnp.einsum(
            "gd,fd->gf", grad_feed, down_weight, preferred_element_type=jnp.float32
        )
        grad_pre = jax.vjp(gelu_tanh, pre_gelu)[1](grad_activated)[0].astype(jnp.bfloat16)
        grad_up = jnp.einsum("gd,gf->df", shifted_in, grad_pre, preferred_element_type=jnp.float32)
        grad_shifted = jnp.einsum(
            "gf,df->gd", grad_pre, up_weight, preferred_element_type=jnp.float32
        )
        grad_up, grad_down = (
            lax.psum_scatter(
                grad_up.astype(jnp.bfloat16), "head", scatter_dimension=1, tiled=True
            ).astype(jnp.float32),
            lax.psum_scatter(
                grad_down.astype(jnp.bfloat16), "head", scatter_dimension=0, tiled=True
            ).astype(jnp.float32),
        )
        unused_mid, pull_second = jax.vjp(
            layer_norm, middle, mod_row(6 * block_id + 3), mod_row(6 * block_id + 4)
        )
        grad_mid_norm, grad_shift_mlp, grad_scale_mlp = pull_second(grad_shifted)
        grad_middle = grad_result + grad_mid_norm
        grad_branch = (grad_middle * mod_row(6 * block_id + 2)).astype(jnp.bfloat16)
        grad_gate_att = grad_middle * branch
        branch_in = grads_in(grad_branch)
        grad_wout = jnp.einsum("ge,gd->ed", attended, branch_in, preferred_element_type=jnp.float32)
        grad_attended = jnp.einsum(
            "gd,ed->ge", branch_in, out_use, preferred_element_type=jnp.float32
        ).astype(jnp.bfloat16)
        windows = shape_windows(projected, side_t, side_len)
        grad_windows = shape_grad(grad_attended, side_t, side_len)
        grad_stack, grad_table = attend_back(
            windows, grad_windows, log_total, table_use, rel_index, keep_win
        )
        grad_projected = flat_rows(grad_stack, side_t, side_len).astype(jnp.bfloat16)
        grad_qkv = jnp.einsum(
            "gd,gce->cde", normed_in, grad_projected, preferred_element_type=jnp.float32
        )
        grad_normed = grads_out(grad_projected, qkv_use, "gce,cde->gd")
        unused_hid, pull_first = jax.vjp(
            layer_norm, hidden, mod_row(6 * block_id), mod_row(6 * block_id + 1)
        )
        grad_hid_norm, grad_shift_att, grad_scale_att = pull_first(grad_normed)
        grad_hidden = grad_middle + grad_hid_norm
        mod_terms = jnp.stack(
            [
                grad_shift_att,
                grad_scale_att,
                grad_gate_att,
                grad_shift_mlp,
                grad_scale_mlp,
                grad_gate_mlp,
            ],
            axis=1,
        )
        grad_mods = jnp.einsum("rc,rke->cke", row_onehot, mod_terms, precision=HIGHEST_PRECISION)
        return (grad_hidden, grad_mods, (grad_qkv, grad_wout, grad_up, grad_down, grad_table))

    hidden_first = tokens.astype(jnp.float32)
    saved_first, hidden_second = forward_block(hidden_first, 0)
    saved_second, hidden_last = forward_block(hidden_second, 1)
    output = (hidden_last * row_keep).astype(jnp.bfloat16)
    grad_second, mods_second, weights_second = backward_block(
        saved_second, d_out.astype(jnp.float32) * row_keep, 1
    )
    grad_first, mods_first, weights_first = backward_block(saved_first, grad_second, 0)
    grad_modulation = lax.psum(
        jnp.concatenate([mods_first, mods_second], axis=1).astype(jnp.bfloat16), "head"
    ).astype(jnp.float32)
    summed = (
        lax.psum(
            jnp.stack([weights_first[0], weights_second[0]]).astype(jnp.bfloat16), "clip"
        ).astype(jnp.float32),
        lax.psum(
            jnp.stack([weights_first[1], weights_second[1]]).astype(jnp.bfloat16), "clip"
        ).astype(jnp.float32),
        lax.psum(
            jnp.stack([weights_first[2], weights_second[2]]).astype(jnp.bfloat16), "clip"
        ).astype(jnp.float32),
        lax.psum(
            jnp.stack([weights_first[3], weights_second[3]]).astype(jnp.bfloat16), "clip"
        ).astype(jnp.float32),
        lax.psum(weights_first[4].astype(jnp.bfloat16), "clip").astype(jnp.float32),
        lax.psum(weights_second[4].astype(jnp.bfloat16), "clip").astype(jnp.float32),
    )
    return (
        output,
        grad_first,
        grad_modulation,
        summed[0],
        summed[1],
        summed[2],
        summed[3],
        summed[4],
        summed[5],
    )


F32 = jnp.float32
BF16 = jnp.bfloat16
VMEM_LIMIT = 58 * 1024 * 1024
NZ = 4
D = 1024
HPZ = 4
CONST = pl.Buffered(1)


def dot_nn(a, b):
    return lax.dot_general(a, b, (((1,), (0,)), ((), ())), preferred_element_type=F32)


def dot_nt(a, b):
    return lax.dot_general(a, b, (((1,), (1,)), ((), ())), preferred_element_type=F32)


def dot_tn(a, b):
    return lax.dot_general(a, b, (((0,), (0,)), ((), ())), preferred_element_type=F32)


def call(kernel, name, grid, in_specs, out_specs, out_shape, scratch, flops, nbytes):
    return pl.pallas_call(
        kernel,
        name=name,
        grid=grid,
        in_specs=in_specs,
        out_specs=out_specs,
        out_shape=out_shape,
        scratch_shapes=scratch,
        compiler_params=pltpu.CompilerParams(
            dimension_semantics=("arbitrary",) * len(grid), vmem_limit_bytes=VMEM_LIMIT
        ),
        cost_estimate=pl.CostEstimate(
            flops=flops // 4, bytes_accessed=nbytes // 4, transcendentals=0
        ),
    )


def full(shape):
    return pl.BlockSpec(shape, lambda *ids: (0,) * len(shape), pipeline_mode=CONST)


def chunk_rows(i, size):
    return pl.ds(pl.multiple_of(i * size, size), size)


def ln_stats(x):
    mean = jnp.mean(x, axis=-1, keepdims=True)
    centred = x - mean
    rstd = lax.rsqrt(jnp.mean(centred * centred, axis=-1, keepdims=True) + EPS)
    return centred * rstd, rstd


def ln_back(grad, hat, rstd, scale):
    gh = grad * (1.0 + scale)
    m1 = jnp.mean(gh, axis=-1, keepdims=True)
    m2 = jnp.mean(gh * hat, axis=-1, keepdims=True)
    return rstd * (gh - m1 - hat * m2)


def piece_specs(k, row, count):
    tail = (count, D)
    return [
        pl.BlockSpec((2, 4) + tail, lambda d: (0, 0, row, 0), pipeline_mode=CONST),
        pl.BlockSpec((4, 1) + tail, lambda d: (0, jnp.maximum(d - 1, 0), row, 0)),
        pl.BlockSpec((4, 1) + tail, lambda d: (0, jnp.maximum(d - 1, 0), row, 0)),
    ]


def by_offset(d, body, local_ref, own_ref, other_ref):
    @pl.when(d == 0)
    def _():
        body(lambda m, r, n: local_ref[0, m, r : r + n, :], lambda m, r, n: local_ref[1, m, r : r + n, :])

    @pl.when(d > 0)
    def _():
        body(lambda m, r, n: own_ref[m, 0, r : r + n, :], lambda m, r, n: other_ref[m, 0, r : r + n, :])


def head_rows(own, other, row):
    parts = []
    for m in range(4):
        parts += [own(m, row, 32), other(m, row, 32)]
    return jnp.concatenate(parts, axis=0)


def pair_rows(first, second):
    return jnp.concatenate([get(m) for get in (first, second) for m in range(4)], axis=0)


def feed_specs(down_block):
    def spec(block):
        return pl.BlockSpec((4, 1, 128, D), lambda d: (0, jnp.maximum(d - 1, 0), block, 0))

    return [full((2, 4, 256, D)), spec(0), spec(0), spec(down_block), spec(down_block)]


def feed_by_offset(d, body, l_ref, wu_ref, vu_ref, wd_ref, vd_ref):
    @pl.when(d == 0)
    def _():
        body(
            lambda: pair_rows(lambda m: l_ref[0, m, 0:128], lambda m: l_ref[1, m, 0:128]),
            lambda: pair_rows(lambda m: l_ref[0, m, 128:256], lambda m: l_ref[1, m, 128:256]),
        )

    @pl.when(d > 0)
    def _():
        body(
            lambda: pair_rows(lambda m: wu_ref[m, 0], lambda m: vu_ref[m, 0]),
            lambda: pair_rows(lambda m: wd_ref[m, 0], lambda m: vd_ref[m, 0]),
        )


def ln_qkv(hidden, mods, weights, base):
    rows = hidden.shape[0]
    step = 640

    def kernel(h_ref, m_ref, l_ref, w_ref, v_ref, normed_ref, qkv_ref):
        d = pl.program_id(0)

        @pl.when(d == 0)
        def _():
            def body(i, carry):
                sl = chunk_rows(i, step)
                hat, _ = ln_stats(h_ref[sl, :].astype(F32))
                normed_ref[sl, :] = (
                    hat * (1.0 + m_ref[base + 1 : base + 2, :]) + m_ref[base : base + 1, :]
                ).astype(BF16)
                return carry

            lax.fori_loop(0, rows // step, body, 0)

        def work(own, other):
            for t in range(3):
                qkv_ref[:, t * 256 : (t + 1) * 256] = dot_nt(
                    normed_ref[...], head_rows(own, other, t * 32)
                ).astype(BF16)

        by_offset(d, work, l_ref, w_ref, v_ref)

    return call(
        kernel,
        "ln_qkv",
        (NZ,),
        [full((rows, D)), full((12, D))] + piece_specs(128, 0, 96),
        [full((rows, D)), pl.BlockSpec((rows, 768), lambda z: (0, z))],
        [jax.ShapeDtypeStruct((rows, D), BF16), jax.ShapeDtypeStruct((rows, 3 * D), BF16)],
        [],
        2 * rows * D * 3 * D,
        rows * D * 12 + 6 * D * D,
    )(hidden, mods, *weights)


def build_bias(base_ref, bias_ref, fc_ref, slides, width, lanes_step):
    rows_step = width // slides
    for h in range(HPZ):
        for s in range(slides):
            off = (slides - 1 - s) * lanes_step
            tile = base_ref[h, :, off : off + width]
            if fc_ref is not None:
                tile = jnp.where(s < fc_ref[0], tile, NEGATIVE)
            bias_ref[h, s * rows_step : (s + 1) * rows_step, :] = tile


def window_view(values, kind):
    parts, count, size = kind[0]
    return values.reshape(parts, count, size, values.shape[-1])


def attn_fwd(qkv, base, fc, kind):
    (parts, count, size), slides, lanes_step, masked = kind
    rows, width = qkv.shape[0], parts * size
    r_step, lanes = base.shape[1], base.shape[2]

    def kernel(x_ref, b_ref, fc_ref, o_ref, bias_ref):
        build_bias(b_ref, bias_ref, fc_ref if masked else None, slides, width, lanes_step)

        def one(w, carry):
            def cut(col):
                return x_ref[:, w, :, col : col + HD].reshape(width, HD)

            scores, probs = [], []
            for h in range(HPZ):
                scores.append(dot_nt(cut(256 + h * HD), cut(h * HD) * 0.125) + bias_ref[h])
            for h in range(HPZ):
                expo = jnp.exp(scores[h] - jnp.max(scores[h], axis=0, keepdims=True))
                inv = 1.0 / jnp.sum(expo, axis=0, keepdims=True)
                probs.append((expo * inv).astype(BF16))
            for h in range(HPZ):
                got = dot_tn(probs[h], cut(512 + h * HD)).astype(BF16)
                o_ref[:, w, :, h * HD : (h + 1) * HD] = got.reshape(parts, size, HD)
            return carry

        lax.fori_loop(0, count, one, 0)

    return call(
        kernel,
        "attn_fwd",
        (NZ,),
        [
            pl.BlockSpec((parts, count, size, 768), lambda z: (0, 0, 0, z)),
            pl.BlockSpec((HPZ, r_step, lanes), lambda z: (z, 0, 0)),
            pl.BlockSpec(memory_space=pltpu.SMEM),
        ],
        pl.BlockSpec((parts, count, size, 256), lambda z: (0, 0, 0, z)),
        jax.ShapeDtypeStruct((parts, count, size, D), BF16),
        [pltpu.VMEM((HPZ, width, width), F32)],
        count * 16 * width * width * HD * 16,
        rows * D * 8,
    )(window_view(qkv, kind), base, fc).reshape(rows, D)


def attn_bwd(qkv, grad_att, base, fc, kind):
    (parts, count, size), slides, lanes_step, masked = kind
    rows, width = qkv.shape[0], parts * size
    r_step, lanes = base.shape[1], base.shape[2]

    def kernel(x_ref, d_ref, b_ref, fc_ref, o_ref, gb_ref, bias_ref, acc_ref):
        build_bias(b_ref, bias_ref, fc_ref if masked else None, slides, width, lanes_step)
        acc_ref[...] = jnp.zeros_like(acc_ref)

        def one(w, carry):
            def cut(ref, col):
                return ref[:, w, :, col : col + HD].reshape(width, HD)

            def put(col, value):
                o_ref[:, w, :, col : col + HD] = value.astype(BF16).reshape(parts, size, HD)

            q = [cut(x_ref, h * HD) * 0.125 for h in range(HPZ)]
            k = [cut(x_ref, 256 + h * HD) for h in range(HPZ)]
            da = [cut(d_ref, h * HD) for h in range(HPZ)]
            score = [dot_nt(k[h], q[h]) + bias_ref[h] for h in range(HPZ)]
            dp = [dot_nt(cut(x_ref, 512 + h * HD), da[h]) for h in range(HPZ)]
            probs, dl = [], []
            for h in range(HPZ):
                expo = jnp.exp(score[h] - jnp.max(score[h], axis=0, keepdims=True))
                inv = 1.0 / jnp.sum(expo, axis=0, keepdims=True)
                p = expo * inv
                row = jnp.sum(dp[h] * p, axis=0, keepdims=True)
                g = (p * (dp[h] - row)).astype(BF16)
                acc_ref[h] += g.astype(F32)
                probs.append(p.astype(BF16))
                dl.append(g)
            for h in range(HPZ):
                put(h * HD, dot_tn(dl[h], k[h]) * 0.125)
                put(256 + h * HD, dot_nn(dl[h], q[h]))
                put(512 + h * HD, dot_nn(probs[h], da[h]))
            return carry

        lax.fori_loop(0, count, one, 0)
        gb_ref[...] = jnp.zeros_like(gb_ref)
        for h in range(HPZ):
            for s in range(slides):
                off = (slides - 1 - s) * lanes_step
                gb_ref[h, :, off : off + width] += acc_ref[h, s * r_step : (s + 1) * r_step, :]

    xspec = pl.BlockSpec((parts, count, size, 768), lambda z: (0, 0, 0, z))
    bspec = pl.BlockSpec((HPZ, r_step, lanes), lambda z: (z, 0, 0))
    proj, strips = call(
        kernel,
        "attn_bwd",
        (NZ,),
        [
            xspec,
            pl.BlockSpec((parts, count, size, 256), lambda z: (0, 0, 0, z)),
            bspec,
            pl.BlockSpec(memory_space=pltpu.SMEM),
        ],
        [xspec, bspec],
        [
            jax.ShapeDtypeStruct((parts, count, size, 3 * D), BF16),
            jax.ShapeDtypeStruct(base.shape, F32),
        ],
        [pltpu.VMEM((HPZ, width, width), F32), pltpu.VMEM((HPZ, width, width), F32)],
        count * 16 * width * width * HD * 40,
        rows * D * 16,
    )(window_view(qkv, kind), window_view(grad_att, kind), base, fc)
    return proj.reshape(rows, 3 * D), strips


def out_specs_of(row_block):
    return [
        pl.BlockSpec((2, 4, 32, D), lambda i: (0, 0, row_block, 0), pipeline_mode=CONST),
        pl.BlockSpec((4, 3, 32, D), lambda i: (0, 0, row_block, 0), pipeline_mode=CONST),
        pl.BlockSpec((4, 3, 32, D), lambda i: (0, 0, row_block, 0), pipeline_mode=CONST),
    ]


def out_rows(d, l_ref, w_ref, v_ref):
    if d == 0:
        return head_rows(
            lambda m, r, n: l_ref[0, m, :, :], lambda m, r, n: l_ref[1, m, :, :], 0
        )
    return head_rows(
        lambda m, r, n: w_ref[m, d - 1, :, :], lambda m, r, n: v_ref[m, d - 1, :, :], 0
    )


def out_proj(attended, weights, hidden, mods, base):
    rows = attended.shape[0]
    step = 256

    def kernel(a_ref, l_ref, w_ref, v_ref, h_ref, m_ref, br_ref, mid_ref, sh_ref):
        branch = jnp.zeros((step, D), F32)
        for d in range(NZ):
            branch += dot_nn(a_ref[:, d * 256 : (d + 1) * 256], out_rows(d, l_ref, w_ref, v_ref))
        br_ref[...] = branch.astype(BF16)
        middle = h_ref[...].astype(F32) + m_ref[base + 2 : base + 3, :] * branch
        mid_ref[...] = middle
        hat, _ = ln_stats(middle)
        sh_ref[...] = (
            hat * (1.0 + m_ref[base + 4 : base + 5, :]) + m_ref[base + 3 : base + 4, :]
        ).astype(BF16)

    tile = pl.BlockSpec((step, D), lambda i: (i, 0))
    return call(
        kernel,
        "out_proj",
        (rows // step,),
        [tile] + out_specs_of(3) + [tile, full((12, D))],
        [tile, tile, tile],
        [
            jax.ShapeDtypeStruct((rows, D), BF16),
            jax.ShapeDtypeStruct((rows, D), F32),
            jax.ShapeDtypeStruct((rows, D), BF16),
        ],
        [],
        2 * rows * D * D,
        rows * D * 14 + 2 * D * D,
    )(attended, *weights, hidden, mods)


GELU_C = 0.7978845608028654
GELU_A = 0.044715


def gelu_of(x):
    return 0.5 * x * (1.0 + jnp.tanh(GELU_C * (x + GELU_A * x * x * x)))


def gelu_both(x):
    x2 = x * x
    th = jnp.tanh(GELU_C * (x + GELU_A * x * x2))
    half = 0.5 * (1.0 + th)
    slope = half + 0.5 * x * (1.0 - th * th) * (GELU_C * (1.0 + 3.0 * GELU_A * x2))
    return x * half, slope


def ffn_fwd(shifted, weights, down_block, middle, mods, base):
    rows = shifted.shape[0]
    step = 640

    def kernel(x_ref, *refs):
        parts, (mid_ref, m_ref, pre_ref, feed_ref, nx_ref, acc_ref) = refs[:5], refs[5:]
        z = pl.program_id(0)

        def work(up, down):
            def body(i, carry):
                sl = chunk_rows(i, step)
                pre = dot_nt(x_ref[sl, :], up())
                pre_ref[sl, :] = pre.astype(BF16)
                part = dot_nn(gelu_of(pre).astype(BF16), down())

                @pl.when(z == 0)
                def _():
                    acc_ref[sl, :] = part

                @pl.when((z > 0) & (z < NZ - 1))
                def _():
                    acc_ref[sl, :] += part

                @pl.when(z == NZ - 1)
                def _():
                    feed = acc_ref[sl, :] + part
                    feed_ref[sl, :] = feed.astype(BF16)
                    nx_ref[sl, :] = (
                        mid_ref[sl, :] + m_ref[base + 5 : base + 6, :] * feed
                    ).astype(BF16)

                return carry

            lax.fori_loop(0, rows // step, body, 0)

        feed_by_offset(z, work, *parts)

    return call(
        kernel,
        "ffn_fwd",
        (NZ,),
        [full((rows, D))] + feed_specs(down_block) + [full((rows, D)), full((12, D))],
        [pl.BlockSpec((rows, D), lambda z: (0, z)), full((rows, D)), full((rows, D))],
        [
            jax.ShapeDtypeStruct((rows, 4 * D), BF16),
            jax.ShapeDtypeStruct((rows, D), BF16),
            jax.ShapeDtypeStruct((rows, D), BF16),
        ],
        [pltpu.VMEM((rows, D), F32)],
        16 * rows * D * D,
        rows * D * 20 + 16 * D * D,
    )(shifted, *weights, middle, mods)


def ffn_bwd(grad, pre, shifted, weights, down_block, mods, base):
    rows = grad.shape[0]
    step = 640

    def kernel(g_ref, p_ref, x_ref, *refs):
        parts, refs = refs[:5], refs[5:]
        m_ref, keep_ref, send_ref, gs_ref, gf_ref, act_ref, gp_ref = refs
        z = pl.program_id(0)

        @pl.when(z == 0)
        def _():
            def body(i, carry):
                sl = chunk_rows(i, step)
                gf_ref[sl, :] = (
                    g_ref[sl, :].astype(F32) * m_ref[base + 5 : base + 6, :]
                ).astype(BF16)
                gs_ref[sl, :] = jnp.zeros((step, D), F32)
                return carry

            lax.fori_loop(0, rows // step, body, 0)

        def work(up, down):
            def body(i, carry):
                sl = chunk_rows(i, step)
                back = dot_nt(gf_ref[sl, :], down())
                act, slope = gelu_both(p_ref[sl, :].astype(F32))
                act_ref[sl, :] = act.astype(BF16)
                gpre = (back * slope).astype(BF16)
                gp_ref[sl, :] = gpre
                part = dot_nn(gpre, up())
                gs_ref[sl, :] += part
                return carry

            lax.fori_loop(0, rows // step, body, 0)

        feed_by_offset(z, work, *parts)
        for j, out_ref in enumerate((keep_ref, send_ref)):
            cols = slice(j * 512, (j + 1) * 512)
            gd = dot_tn(act_ref[:, cols], gf_ref[...]).astype(BF16)
            gu = dot_tn(gp_ref[:, cols], x_ref[...]).astype(BF16)
            out_ref[:, 0, 0:128] = gu.reshape(4, 128, D)
            out_ref[:, 0, 128:256] = gd.reshape(4, 128, D)

    gspec = pl.BlockSpec((4, 1, 256, D), lambda z: (0, z, 0, 0))
    gshape = jax.ShapeDtypeStruct((4, NZ, 256, D), BF16)
    return call(
        kernel,
        "ffn_bwd",
        (NZ,),
        [
            full((rows, D)),
            pl.BlockSpec((rows, D), lambda z: (0, z)),
            full((rows, D)),
        ]
        + feed_specs(down_block)
        + [full((12, D))],
        [gspec, gspec, full((rows, D))],
        [gshape, gshape, jax.ShapeDtypeStruct((rows, D), F32)],
        [pltpu.VMEM((rows, D), BF16)] * 3,
        32 * rows * D * D,
        rows * D * 16 + 32 * D * D,
    )(grad, pre, shifted, *weights, mods)


def split_heads(value, keep_ref, send_ref, d, row):
    for m in range(4):
        keep_ref[m, d, row : row + 32] = value[m * 64 : m * 64 + 32]
        send_ref[m, d, row : row + 32] = value[m * 64 + 32 : m * 64 + 64]


def out_bwd(grad, grad_shifted, middle, feed, branch, attended, weights, mods, base):
    rows = grad.shape[0]
    step = 256
    steps = rows // step

    def kernel(
        g_ref, gs_ref, mid_ref, f_ref, b_ref, a_ref, l_ref, w_ref, v_ref, m_ref, gm_ref, ga_ref,
        keep_ref, send_ref, s_ref, gb_ref,
    ):
        i = pl.program_id(0)

        @pl.when(i == 0)
        def _():
            s_ref[...] = jnp.zeros_like(s_ref)

        g = g_ref[...].astype(F32)
        gs = gs_ref[...]
        hat, rstd = ln_stats(mid_ref[...])
        gm = g + ln_back(gs, hat, rstd, m_ref[base + 4 : base + 5, :])
        gm_ref[...] = gm
        s_ref[0:1, :] += jnp.sum(gs, axis=0, keepdims=True)
        s_ref[1:2, :] += jnp.sum(gs * hat, axis=0, keepdims=True)
        s_ref[2:3, :] += jnp.sum(gm * b_ref[...].astype(F32), axis=0, keepdims=True)
        s_ref[3:4, :] += jnp.sum(g * f_ref[...].astype(F32), axis=0, keepdims=True)
        gb = (gm * m_ref[base + 2 : base + 3, :]).astype(BF16)
        gb_ref[chunk_rows(i, step), :] = gb
        for d in range(NZ):
            ga_ref[:, d * 256 : (d + 1) * 256] = dot_nt(
                gb, out_rows(d, l_ref, w_ref, v_ref)
            ).astype(BF16)

        @pl.when(i == steps - 1)
        def _():
            for d in range(NZ):
                gw = dot_tn(a_ref[:, d * 256 : (d + 1) * 256], gb_ref[...]).astype(BF16)
                split_heads(gw, keep_ref, send_ref, d, 0)

    tile = pl.BlockSpec((step, D), lambda i: (i, 0))
    gshape = jax.ShapeDtypeStruct((4, NZ, 32, D), BF16)
    return call(
        kernel,
        "out_bwd",
        (steps,),
        [tile, tile, tile, tile, tile, full((rows, D))] + out_specs_of(3) + [full((12, D))],
        [tile, tile, full(gshape.shape), full(gshape.shape), full((8, D))],
        [
            jax.ShapeDtypeStruct((rows, D), F32),
            jax.ShapeDtypeStruct((rows, D), BF16),
            gshape,
            gshape,
            jax.ShapeDtypeStruct((8, D), F32),
        ],
        [pltpu.VMEM((rows, D), BF16)],
        4 * rows * D * D,
        rows * D * 24 + 4 * D * D,
    )(grad, grad_shifted, middle, feed, branch, attended, *weights, mods)


def qkv_back(grad_proj, weights, hidden, grad_middle, mods, base, out_dtype, pieces):
    rows = hidden.shape[0]
    step = 640

    cols = D // pieces

    def kernel(p_ref, l_ref, w_ref, v_ref, h_ref, gm_ref, m_ref, *refs):
        gh_refs, (s_ref, acc_ref) = refs[:pieces], refs[pieces:]
        z = pl.program_id(0)

        @pl.when(z == 0)
        def _():
            acc_ref[...] = jnp.zeros_like(acc_ref)
            s_ref[...] = jnp.zeros_like(s_ref)

        def work(own, other):
            def body(i, carry):
                sl = chunk_rows(i, step)
                rows_of = jnp.concatenate([head_rows(own, other, t * 32) for t in range(3)], axis=0)
                acc_ref[sl, :] += dot_nn(p_ref[sl, :], rows_of)
                return carry

            lax.fori_loop(0, rows // step, body, 0)

        by_offset(z, work, l_ref, w_ref, v_ref)

        @pl.when(z == NZ - 1)
        def _():
            def tail(n, carry):
                sl = chunk_rows(n, 256)
                gn = acc_ref[sl, :]
                hat, rstd = ln_stats(h_ref[sl, :].astype(F32))
                gh = gm_ref[sl, :] + ln_back(gn, hat, rstd, m_ref[base + 1 : base + 2, :])
                for i, gh_ref in enumerate(gh_refs):
                    gh_ref[sl, :] = gh[:, i * cols : (i + 1) * cols].astype(out_dtype)
                s_ref[0:1, :] += jnp.sum(gn, axis=0, keepdims=True)
                s_ref[1:2, :] += jnp.sum(gn * hat, axis=0, keepdims=True)
                return carry

            lax.fori_loop(0, rows // 256, tail, 0)

    return call(
        kernel,
        "qkv_back",
        (NZ,),
        [pl.BlockSpec((rows, 768), lambda z: (0, z))]
        + piece_specs(128, 0, 96)
        + [full((rows, D)), full((rows, D)), full((12, D))],
        [full((rows, cols))] * pieces + [full((8, D))],
        [jax.ShapeDtypeStruct((rows, cols), out_dtype)] * pieces
        + [jax.ShapeDtypeStruct((8, D), F32)],
        [pltpu.VMEM((rows, D), F32)],
        6 * rows * D * D,
        rows * D * 20 + 6 * D * D,
    )(grad_proj, *weights, hidden, grad_middle, mods)


def qkv_grad(grad_proj, normed, out_keep, out_send, table_rows):
    rows = normed.shape[0]
    k = 128 if table_rows is None else 144

    def kernel(p_ref, n_ref, ok_ref, os_ref, *rest):
        keep_ref, send_ref = rest[-2:]
        for t in range(3):
            gw = dot_tn(p_ref[:, t * 256 : (t + 1) * 256], n_ref[...]).astype(BF16)
            split_heads(gw, keep_ref, send_ref, 0, t * 32)
        keep_ref[:, :, 96:128] = ok_ref[...]
        send_ref[:, :, 96:128] = os_ref[...]
        if table_rows is not None:
            keep_ref[:, :, 128:144] = rest[0][...]
            send_ref[:, :, 128:144] = rest[0][...]

    gspec = pl.BlockSpec((4, 1, k, D), lambda z: (0, z, 0, 0))
    ospec = pl.BlockSpec((4, 1, 32, D), lambda z: (0, z, 0, 0))
    tspec = pl.BlockSpec((4, 1, 16, D), lambda z: (0, z, 0, 0))
    gshape = jax.ShapeDtypeStruct((4, NZ, k, D), BF16)
    extra = () if table_rows is None else (table_rows,)
    return call(
        kernel,
        "qkv_grad",
        (NZ,),
        [pl.BlockSpec((rows, 768), lambda z: (0, z)), full((rows, D)), ospec, ospec]
        + [tspec] * len(extra),
        [gspec, gspec],
        [gshape, gshape],
        [],
        6 * rows * D * D,
        rows * D * 8 + 8 * D * D,
    )(grad_proj, normed, out_keep, out_send, *extra)


def place_call(kernel, name, in_specs, out_specs, out_shape, scratch, nbytes, aliases):
    return pl.pallas_call(
        kernel,
        name=name,
        grid_spec=pltpu.PrefetchScalarGridSpec(
            num_scalar_prefetch=1,
            grid=(8,),
            in_specs=in_specs,
            out_specs=out_specs,
            scratch_shapes=scratch,
        ),
        out_shape=out_shape,
        input_output_aliases=aliases,
        compiler_params=pltpu.CompilerParams(
            dimension_semantics=("arbitrary",), vmem_limit_bytes=VMEM_LIMIT
        ),
        cost_estimate=pl.CostEstimate(flops=0, bytes_accessed=nbytes, transcendentals=0),
    )


def rows_at(place):
    return pl.ds(pl.multiple_of(place * 32, 32), 32)


def prep_attn(place, w_qkv, w_out, b):
    def kernel(c_ref, q_ref, o_ref, out_ref, t_ref):
        r = pl.program_id(0)

        @pl.when(r == 0)
        def _():
            for t in range(3):
                t_ref[t] = q_ref[0, t].T

        at = rows_at(c_ref[0] ^ r)
        for t in range(3):
            out_ref[0, 0, t * 32 : (t + 1) * 32, :] = t_ref[t, at, :]
        out_ref[0, 0, 96:128, :] = o_ref[0, at, :]

    return place_call(
        kernel,
        "prep_attn",
        [
            pl.BlockSpec((1, 3, D, 256), lambda r, c: (b, 0, 0, 0)),
            pl.BlockSpec((1, 256, D), lambda r, c: (b, 0, 0)),
        ],
        pl.BlockSpec((1, 1, 128, D), lambda r, c: (r % 2, r // 2, 0, 0)),
        jax.ShapeDtypeStruct((2, 4, 128, D), BF16),
        [pltpu.VMEM((3, 256, D), BF16)],
        4 * D * D,
        {},
    )(place, w_qkv, w_out)


def prep_feed(place, w_up, w_down, b):
    def kernel(c_ref, u_ref, d_ref, out_ref):
        out_ref[0, 0, 0:128, :] = u_ref[0].T
        out_ref[0, 0, 128:256, :] = d_ref[0]

    return place_call(
        kernel,
        "prep_feed",
        [
            pl.BlockSpec((1, D, 128), lambda r, c: (b, 0, c[0] ^ r)),
            pl.BlockSpec((1, 128, D), lambda r, c: (b, c[0] ^ r, 0)),
        ],
        pl.BlockSpec((1, 1, 256, D), lambda r, c: (r % 2, r // 2, 0, 0)),
        jax.ShapeDtypeStruct((2, 4, 256, D), BF16),
        [],
        8 * D * D,
        {},
    )(place, w_up, w_down)


def finish_attn(place, own, other, b, earlier, block):

    def kernel(c_ref, own_ref, oth_ref, *rest):
        gq_ref, go_ref, t_ref = rest[-3:]
        r = pl.program_id(0)
        at = rows_at(c_ref[0] ^ r)

        def store(ref):
            for t in range(3):
                t_ref[t, at, :] = ref[0, t * 32 : (t + 1) * 32, :]
            go_ref[0, at, :] = ref[0, 96:128, :].astype(F32)

        @pl.when(r % 2 == 0)
        def _():
            store(own_ref)

        @pl.when(r % 2 == 1)
        def _():
            store(oth_ref)

        @pl.when(r == 7)
        def _():
            for t in range(3):
                gq_ref[0, t] = t_ref[t].T.astype(F32)

    piece = pl.BlockSpec((1, 128, D), lambda r, c: (r // 2, block, 0))
    anywhere = pl.BlockSpec(memory_space=pl.ANY)
    return place_call(
        kernel,
        "finish_attn",
        [piece, piece] + [anywhere] * len(earlier),
        [
            pl.BlockSpec((1, 3, D, 256), lambda r, c: (b, 0, 0, 0)),
            pl.BlockSpec((1, 256, D), lambda r, c: (b, 0, 0)),
        ],
        [
            jax.ShapeDtypeStruct((2, 3, D, 256), F32),
            jax.ShapeDtypeStruct((2, 256, D), F32),
        ],
        [pltpu.VMEM((3, 256, D), BF16)],
        6 * D * D,
        {3 + i: i for i in range(len(earlier))},
    )(place, own, other, *earlier)


def finish_feed(place, own, other, b, earlier):
    def kernel(c_ref, own_ref, oth_ref, *rest):
        gu_ref, gd_ref = rest[-2:]
        r = pl.program_id(0)

        def store(ref):
            gu_ref[0] = ref[0, 0:128, :].T.astype(F32)
            gd_ref[0] = ref[0, 128:256, :].astype(F32)

        @pl.when(r % 2 == 0)
        def _():
            store(own_ref)

        @pl.when(r % 2 == 1)
        def _():
            store(oth_ref)

    piece = pl.BlockSpec((1, 256, D), lambda r, c: (r // 2, 0, 0))
    anywhere = pl.BlockSpec(memory_space=pl.ANY)
    return place_call(
        kernel,
        "finish_feed",
        [piece, piece] + [anywhere] * len(earlier),
        [
            pl.BlockSpec((1, D, 128), lambda r, c: (b, 0, c[0] ^ r)),
            pl.BlockSpec((1, 128, D), lambda r, c: (b, c[0] ^ r, 0)),
        ],
        [jax.ShapeDtypeStruct((2, D, D), F32), jax.ShapeDtypeStruct((2, D, D), F32)],
        [],
        12 * D * D,
        {3 + i: i for i in range(len(earlier))},
    )(place, own, other, *earlier)


def partner(values):
    return lax.ppermute(values, "head", [(i, i ^ 1) for i in range(NZ)])


def rows_to_spatial(rows, odd):
    cols = rows.shape[1]
    whole = lax.dynamic_slice(rows, (256 * odd, 0), (1024, cols))
    part = lax.dynamic_slice(rows, (1024 * (1 - odd), 0), (256, cols)).reshape(8, 2, 16, cols)
    wins = whole.reshape(2, 16, 2, 16, cols).transpose(0, 2, 1, 3, 4).reshape(1024, cols)
    left, right = part[:, 0].reshape(128, cols), part[:, 1].reshape(128, cols)
    keep = jnp.where(odd == 0, left, right)
    got = partner(jnp.where(odd == 0, right, left))
    top, bottom = jnp.where(odd == 0, keep, got), jnp.where(odd == 0, got, keep)
    part = jnp.concatenate([top, bottom], axis=0)
    return jnp.where(
        odd == 0,
        jnp.concatenate([wins, part], axis=0),
        jnp.concatenate([part, wins], axis=0),
    )


def spatial_to_rows(wins, odd):
    cols = wins.shape[1]
    whole = lax.dynamic_slice(wins, (256 * odd, 0), (1024, cols))
    part = lax.dynamic_slice(wins, (1024 * (1 - odd), 0), (256, cols))
    whole = whole.reshape(2, 2, 16, 16, cols).transpose(0, 2, 1, 3, 4).reshape(1024, cols)
    keep = jnp.where(odd == 0, part[:128], part[128:])
    got = partner(jnp.where(odd == 0, part[128:], part[:128]))
    left, right = jnp.where(odd == 0, keep, got), jnp.where(odd == 0, got, keep)
    part = jnp.stack([left.reshape(8, 16, cols), right.reshape(8, 16, cols)], axis=1)
    part = part.reshape(256, cols)
    return jnp.where(
        odd == 0,
        jnp.concatenate([whole, part], axis=0),
        jnp.concatenate([part, whole], axis=0),
    )


def exchange(values):
    return lax.all_to_all(values, "head", 0, 0, tiled=True)


def spatial_to_tubes(wins):
    cols = wins.shape[1]
    return exchange(
        wins.reshape(5, 2, 8, 2, 8, cols).transpose(1, 3, 0, 2, 4, 5).reshape(1280, cols)
    )


def from_quads(quads):
    cols = quads.shape[1]
    return quads.reshape(2, 2, 5, 8, 8, cols).transpose(2, 0, 3, 1, 4, 5).reshape(1280, cols)


def toeplitz(side):
    span = 2 * side - 1
    b = lax.broadcasted_iota(jnp.int32, (span, side, side), 0)
    j = lax.broadcasted_iota(jnp.int32, (span, side, side), 1)
    i = lax.broadcasted_iota(jnp.int32, (span, side, side), 2)
    return (b == i - j + side - 1).astype(F32)


def toeplitz_pair(side):
    span = 2 * side - 1
    shape = (span * span, side * side, side * side)
    r = lax.broadcasted_iota(jnp.int32, shape, 0)
    j = lax.broadcasted_iota(jnp.int32, shape, 1)
    i = lax.broadcasted_iota(jnp.int32, shape, 2)
    dy = i // side - j // side + side - 1
    dx = i % side - j % side + side - 1
    return (r == dy * span + dx).astype(F32)


CORE, ROW_X, ROW_Y = 1, 2, 4


def swap(values, bit):
    return lax.ppermute(values, "clip", [(i, i ^ bit) for i in range(8)])


def from_z(values, d):
    return lax.ppermute(values, "head", [((i + d) % NZ, i) for i in range(NZ)])


def sync(*values):
    return lax.optimization_barrier(values)


def add(first, second):
    return (first.astype(F32) + second.astype(F32)).astype(BF16)


def line_stage(piece):
    return [from_z(piece, d) for d in (1, 2, 3)]


def others(by_z, z):
    return [lax.dynamic_index_in_dim(by_z, (z + d) % NZ, 0, keepdims=False) for d in (1, 2, 3)]


def cross_stage(own):
    return [own] + [swap(own, m * 2) for m in (1, 2, 3)]


def sum_core(keep, got):
    return [add(keep[m], got[m]) for m in range(4)]


def send_plane(totals, offsets):
    return [swap(totals[m], m * 2) for m in offsets]


def to_places(total, z):
    twice = jnp.concatenate([total, total[: NZ - 1]], axis=0)
    return lax.dynamic_slice_in_dim(twice, (NZ - z) % NZ, NZ, axis=0)


def sum_plane(totals, got, z):
    total = totals[0].astype(F32)
    for value in got:
        total = total + value.astype(F32)
    return to_places(total.astype(BF16), z)


def send_cross(totals):
    half = totals[0].shape[1] // 2
    first = [t[:, :half] for t in totals]
    second = [t[:, half:] for t in totals]
    by_x = swap(jnp.stack([first[1], first[3]]), ROW_X)
    by_y = swap(jnp.stack([second[2], second[3]]), ROW_Y)
    return by_x, by_y


def sum_cross(totals, got):
    half = totals[0].shape[1] // 2
    by_x, by_y = got
    first = [add(totals[0][:, :half], by_x[0]), add(totals[2][:, :half], by_x[1])]
    second = [add(totals[0][:, half:], by_y[0]), add(totals[1][:, half:], by_y[1])]
    return first, second


def send_corner(halves):
    return swap(halves[0][1], ROW_Y), swap(halves[1][1], ROW_X)


def sum_corner(halves, got, z):
    first = add(halves[0][0], got[0])
    second = add(halves[1][0], got[1])
    return to_places(jnp.concatenate([first, second], axis=1), z)


def sum_line(by_z):
    return lax.psum_scatter(by_z, "head", scatter_dimension=0)


def on_device_windows(
    tokens, d_out, modulation, frame_counts, w_qkv, w_out, w_up, w_down, table_s, table_t
):
    z = lax.axis_index("head")
    c = lax.axis_index("clip")
    place = c.astype(jnp.int32).reshape(1)
    chip = c // 2
    odd = z % 2
    mods = modulation[0]
    n_s, n_t = table_s.shape[1], table_t.shape[1]
    hot_s, hot_t = toeplitz(SWIN), toeplitz_pair(TWIN)
    fc = frame_counts

    def spatial_base(tables):
        base = jnp.einsum(
            "hab,bji->hjai", tables[:, :n_s].reshape(16, 31, 31), hot_s, precision=HIGHEST_PRECISION
        ).reshape(16, 16, 496)
        return jnp.pad(base, ((0, 0), (0, 0), (0, 16)))

    def tube_base(tables):
        base = jnp.einsum(
            "htr,rjk->hjtk", tables[:, n_s:].reshape(16, 9, 225), hot_t, precision=HIGHEST_PRECISION
        ).reshape(16, 64, 576)
        return jnp.pad(base, ((0, 0), (0, 0), (0, 64)))

    def table_rows(first, second):
        first = jnp.pad(first, ((0, 0), (0, D - n_s)))
        second = jnp.pad(second, ((0, 0), (0, 15 * D - n_t)))
        values = jnp.concatenate([first, second], axis=1).astype(BF16)
        return values.reshape(NZ, 4, 16, D).transpose(1, 0, 2, 3)

    spatial = ((1, 5, 256), 16, 16, False)
    tube = ((5, 4, 64), 5, 64, True)

    local_a0 = prep_attn(place, w_qkv, w_out, 0)
    line_a0 = line_stage(local_a0[0, 0])
    table_piece = jnp.concatenate([table_s, table_t], axis=1)
    tables = [from_z(table_piece, d) for d in (1, 2)]
    local_f0 = prep_feed(place, w_up, w_down, 0)
    local_a1 = prep_attn(place, w_qkv, w_out, 1)
    local_f1 = prep_feed(place, w_up, w_down, 1)
    line_a0, local_f0, local_a1, local_f1, tables, tokens, table_piece = sync(
        line_a0, local_f0, local_a1, local_f1, tables, tokens, table_piece
    )
    own_a0 = cross_stage(jnp.stack(line_a0))
    z_u0 = lax.all_gather(local_f0[0, 0, :128], "head")
    z_d0 = lax.all_gather(local_f0[0, 0, 128:], "head")
    tables = jnp.stack([table_piece] + tables + [from_z(table_piece, 3)])
    tables = jnp.concatenate(
        [lax.dynamic_slice_in_dim(tables, chip ^ m, 1, axis=1) for m in range(4)], axis=1
    ).reshape(16, n_s + n_t)
    base_s = spatial_base(tables)
    hidden0 = rows_to_spatial(tokens, odd)
    own_a0, hidden0, tables, base_s, z_u0 = sync(own_a0, hidden0, tables, base_s, z_u0)
    own_a0 = jnp.stack(own_a0)
    other_a0 = swap(own_a0, CORE)
    own_u0 = cross_stage(jnp.stack(others(z_u0, z)))
    own_a0, other_a0 = sync(own_a0, other_a0)
    weights_a0 = (local_a0, own_a0, other_a0)
    normed0, qkv0 = ln_qkv(hidden0, mods, weights_a0, 0)
    qkv0, own_u0, z_d0 = sync(qkv0, own_u0, z_d0)
    own_d0 = cross_stage(jnp.stack(others(z_d0, z)))
    own_u0 = jnp.stack(own_u0)
    other_u0 = swap(own_u0, CORE)
    z_a1 = lax.all_gather(local_a1[0, 0], "head")
    attended0 = attn_fwd(qkv0, base_s, fc, spatial)
    branch0, middle0, shifted0 = out_proj(attended0, weights_a0, hidden0, mods, 0)
    shifted0, own_d0, other_u0, z_a1 = sync(shifted0, own_d0, other_u0, z_a1)
    own_d0 = jnp.stack(own_d0)
    other_d0 = swap(own_d0, CORE)
    z_f1 = lax.all_gather(local_f1[0, 0], "head")
    own_a1 = jnp.stack(others(z_a1, z))
    shifted0, other_d0, own_a1 = sync(shifted0, other_d0, own_a1)
    own_a1 = cross_stage(own_a1)
    weights_f0 = (local_f0, own_u0, other_u0, own_d0, other_d0)
    pre0, feed0, hidden1 = ffn_fwd(shifted0, weights_f0, 0, middle0, mods, 0)
    hidden1, z_f1, own_a1, tables, d_out = sync(hidden1, z_f1, own_a1, tables, d_out)
    tubes1 = spatial_to_tubes(hidden1)
    own_a1 = jnp.stack(own_a1)
    other_a1 = swap(own_a1, CORE)
    own_f1 = cross_stage(jnp.stack(others(z_f1, z)))
    base_t = tube_base(tables)
    spatial_d = rows_to_spatial(d_out, odd)
    tubes1, other_a1, base_t, spatial_d = sync(tubes1, other_a1, base_t, spatial_d)
    weights_a1 = (local_a1, own_a1, other_a1)
    tubes_d = spatial_to_tubes(spatial_d)
    normed1, qkv1 = ln_qkv(tubes1, mods, weights_a1, 6)
    qkv1, own_f1 = sync(qkv1, own_f1)
    own_f1 = jnp.stack(own_f1)
    other_f1 = swap(own_f1, CORE)
    attended1 = attn_fwd(qkv1, base_t, fc, tube)
    branch1, middle1, shifted1 = out_proj(attended1, weights_a1, tubes1, mods, 6)
    shifted1, other_f1 = sync(shifted1, other_f1)
    weights_f1 = (local_f1, own_f1, other_f1, own_f1, other_f1)
    pre1, feed1, hidden2 = ffn_fwd(shifted1, weights_f1, 1, middle1, mods, 6)
    hidden2, tubes_d = sync(hidden2, tubes_d)
    live = lax.broadcasted_iota(jnp.int32, (1280, 1), 0) // 256 < fc[0]
    grad2 = jnp.where(live, tubes_d, 0)
    out_wins = exchange(jnp.where(live, hidden2, 0))
    f1_keep, f1_send, g_shift1 = ffn_bwd(grad2, pre1, shifted1, weights_f1, 1, mods, 6)
    f1_keep, f1_send, g_shift1, out_wins = sync(f1_keep, f1_send, g_shift1, out_wins)
    f1_got = swap(f1_send, CORE)
    g_mid1, g_att1, o1_keep, o1_send, sums_o1 = out_bwd(
        grad2, g_shift1, middle1, feed1, branch1, attended1, weights_a1, mods, 6
    )
    g_att1, f1_got = sync(g_att1, f1_got)
    total_f1 = sum_core(f1_keep, f1_got)
    g_att1, total_f1 = sync(g_att1, total_f1)
    got_f1 = send_plane(total_f1, (1, 2))
    g_proj1, g_base1 = attn_bwd(qkv1, g_att1, base_t, fc, tube)
    g_proj1, g_base1, got_f1 = sync(g_proj1, g_base1, got_f1)
    g_hid1a, g_hid1b, sums_q1 = qkv_back(
        g_proj1, weights_a1, tubes1, g_mid1, mods, 6, BF16, 2
    )
    g_hid1a, g_hid1b, g_proj1, out_wins, g_base1 = sync(
        g_hid1a, g_hid1b, g_proj1, out_wins, g_base1
    )
    grad1a = exchange(g_hid1a)
    corner_a = swap(total_f1[3][:, :128], ROW_X + ROW_Y)
    a1_keep, a1_send = qkv_grad(g_proj1, normed1, o1_keep, o1_send, None)
    gt_t = jnp.einsum(
        "hjtk,rjk->htr",
        g_base1[:, :, :576].reshape(16, 64, 9, 64),
        hot_t,
        precision=HIGHEST_PRECISION,
    ).reshape(16, n_t)
    grad1a, corner_a, a1_keep, a1_send, gt_t, g_hid1b, out_wins = sync(
        grad1a, corner_a, a1_keep, a1_send, gt_t, g_hid1b, out_wins
    )
    grad1b = exchange(g_hid1b)
    corner_b = swap(total_f1[3][:, 128:], ROW_X + ROW_Y)
    a1_got = swap(a1_send, CORE)
    output = spatial_to_rows(from_quads(out_wins), odd)
    grad1b, a1_got, corner_b, output = sync(grad1b, a1_got, corner_b, output)
    grad1 = from_quads(jnp.concatenate([grad1a, grad1b], axis=1))
    got_f1 = got_f1 + [jnp.concatenate([corner_a, corner_b], axis=1)]
    z_f1 = sum_plane(total_f1, got_f1, z)
    total_a1 = sum_core(a1_keep, a1_got)
    grad1, z_f1, total_a1 = sync(grad1, z_f1, total_a1)
    mine_f1 = sum_line(z_f1)
    got_a1 = send_plane(total_a1, (1, 2, 3))
    f0_keep, f0_send, g_shift0 = ffn_bwd(grad1, pre0, shifted0, weights_f0, 0, mods, 0)
    f0_keep, f0_send, g_shift0, mine_f1, got_a1 = sync(f0_keep, f0_send, g_shift0, mine_f1, got_a1)
    f0_got = swap(f0_send, CORE)
    own_gf1 = cross_stage(mine_f1)
    mine_a1 = sum_line(sum_plane(total_a1, got_a1, z))
    g_mid0, g_att0, o0_keep, o0_send, sums_o0 = out_bwd(
        grad1, g_shift0, middle0, feed0, branch0, attended0, weights_a0, mods, 0
    )
    g_att0, f0_got, own_gf1 = sync(g_att0, f0_got, own_gf1)
    total_f0 = sum_core(f0_keep, f0_got)
    own_gf1 = jnp.stack(own_gf1)
    g_att0, total_f0, own_gf1 = sync(g_att0, total_f0, own_gf1)
    got_f0 = send_cross(total_f0)
    other_gf1 = swap(own_gf1, CORE)
    g_proj0, g_base0 = attn_bwd(qkv0, g_att0, base_s, fc, spatial)
    gt_s = jnp.einsum(
        "hjai,bji->hab",
        g_base0[:, :, :496].reshape(16, 16, 31, 16),
        hot_s,
        precision=HIGHEST_PRECISION,
    ).reshape(16, n_s)
    a0_keep, a0_send = qkv_grad(g_proj0, normed0, o0_keep, o0_send, table_rows(gt_s, gt_t))
    a0_keep, a0_send, got_f0, mine_a1, other_gf1, g_proj0 = sync(
        a0_keep, a0_send, got_f0, mine_a1, other_gf1, g_proj0
    )
    a0_got = swap(a0_send, CORE)
    half_f0 = sum_cross(total_f0, got_f0)
    got_f0 = send_corner(half_f0)
    g_feed = finish_feed(place, own_gf1, other_gf1, 1, ())
    half_f0, got_f0, a0_got, g_feed, g_proj0 = sync(half_f0, got_f0, a0_got, g_feed, g_proj0)
    total_a0 = sum_core(a0_keep, a0_got)
    z_f0 = sum_corner(half_f0, got_f0, z)
    total_a0, z_f0, g_proj0 = sync(total_a0, z_f0, g_proj0)
    got_a0 = send_cross(total_a0)
    mine_f0 = sum_line(z_f0)
    grad0, sums_q0 = qkv_back(g_proj0, weights_a0, hidden0, g_mid0, mods, 0, F32, 1)
    grad0, sums_q0, got_a0 = sync(grad0, sums_q0, got_a0)
    half_a0 = sum_cross(total_a0, got_a0)
    half_a0, grad0, sums_q0 = sync(half_a0, grad0, sums_q0)
    got_a0 = send_corner(half_a0)
    grad_tokens = spatial_to_rows(grad0, odd)
    mod_rows = jnp.concatenate(
        [
            sums_q0[0:2], sums_o0[2:3], sums_o0[0:2], sums_o0[3:4],
            sums_q1[0:2], sums_o1[2:3], sums_o1[0:2], sums_o1[3:4],
        ],
        axis=0,
    )
    got_a0, mine_f0, mod_rows, grad_tokens = sync(got_a0, mine_f0, mod_rows, grad_tokens)
    mine_a0 = sum_line(sum_corner(half_a0, got_a0, z))
    crossed = cross_stage(jnp.concatenate([mine_f0, mine_a1], axis=0))
    mod_got = [from_z(mod_rows, 1), from_z(mod_rows, 2)]
    mine_a0, crossed, mod_got = sync(mine_a0, crossed, mod_got)
    own_ga0 = cross_stage(mine_a0)
    crossed = jnp.stack(crossed)
    other_crossed = swap(crossed, CORE)
    mod_got = mod_got + [from_z(mod_rows, 3)]
    own_ga0, other_crossed, mod_got = sync(own_ga0, other_crossed, mod_got)
    own_ga0 = jnp.stack(own_ga0)
    other_ga0 = swap(own_ga0, CORE)
    g_feed = finish_feed(place, crossed, other_crossed, 0, g_feed)
    g_attn = finish_attn(place, crossed, other_crossed, 1, (), 2)
    other_ga0, g_feed, g_attn = sync(other_ga0, g_feed, g_attn)
    g_attn = finish_attn(place, own_ga0, other_ga0, 0, g_attn, 0)
    tab = jnp.concatenate(
        [lax.dynamic_slice_in_dim(own_ga0, chip ^ m, 1, axis=0) for m in range(4)], axis=0
    )
    tab = tab[:, 128:144].reshape(4, 16 * D).astype(F32)
    return (
        output,
        grad_tokens,
        (mod_rows + mod_got[0] + mod_got[1] + mod_got[2])[None],
        g_attn[0],
        g_attn[1],
        g_feed[0],
        g_feed[1],
        tab[:, :n_s],
        tab[:, D : D + n_t],
    )


def solution(mesh):
    if mesh.shape["head"] == NZ and mesh.shape["clip"] == 8:
        body = on_device_windows
    else:
        body = on_device
    return jax.shard_map(
        body,
        mesh=mesh,
        in_specs=(
            P(("clip", "head"), None),
            P(("clip", "head"), None),
            P("clip", None, None),
            P("clip"),
            P(None, None, None, "head"),
            P(None, "head", None),
            P(None, None, "head"),
            P(None, "head", None),
            P("head", None),
            P("head", None),
        ),
        out_specs=(
            P(("clip", "head"), None),
            P(("clip", "head"), None),
            P("clip", None, None),
            P(None, None, None, "head"),
            P(None, "head", None),
            P(None, None, "head"),
            P(None, "head", None),
            P("head", None),
            P("head", None),
        ),
        check_vma=False,
    )
```

```python
import jax
import jax.numpy as jnp
from jax import lax
from jax.experimental import pallas as pl
from jax.experimental.pallas import tpu as pltpu
from jax.sharding import PartitionSpec as P

HD = 64
FH = 32
FW = 32
SWIN = 16
TWIN = 8
PADF = 5


EPS = 1e-06
HIGHEST_PRECISION = lax.Precision.HIGHEST
NEGATIVE = -1e30


def layer_norm(values, shift_row, scale_row):
    average = jnp.mean(values, axis=-1, keepdims=True)
    centred = values - average
    spread = jnp.mean(centred * centred, axis=-1, keepdims=True)
    return centred * lax.rsqrt(spread + EPS) * (1.0 + scale_row) + shift_row


def gelu_tanh(values):
    return jax.nn.gelu(values, approximate=True)


def window_index(side_t, side_len):
    window_size = side_t * side_len * side_len
    places = jnp.arange(window_size, dtype=jnp.int32)
    time_pos = places // (side_len * side_len)
    height_pos = places // side_len % side_len
    width_pos = places % side_len
    span_len = 2 * side_len - 1
    return (
        (time_pos[:, None] - time_pos[None, :] + side_t - 1) * span_len * span_len
        + (height_pos[:, None] - height_pos[None, :] + side_len - 1) * span_len
        + (width_pos[:, None] - width_pos[None, :] + side_len - 1)
    )


def to_windows(values, side_t, side_len):
    tail_shape = values.shape[1:]
    frames = values.shape[0] // (FH * FW)
    shaped = values.reshape(
        (frames // side_t, side_t, FH // side_len, side_len, FW // side_len, side_len) + tail_shape
    )
    axis_order = (0, 2, 4, 1, 3, 5) + tuple(range(6, 6 + len(tail_shape)))
    shaped = shaped.transpose(axis_order)
    return shaped.reshape((-1, side_t * side_len * side_len) + tail_shape)


def from_windows(values, side_t, side_len):
    tail_shape = values.shape[2:]
    blocks_high = FH // side_len
    blocks_wide = FW // side_len
    frame_groups = values.shape[0] // (blocks_high * blocks_wide)
    shaped = values.reshape(
        (frame_groups, blocks_high, blocks_wide, side_t, side_len, side_len) + tail_shape
    )
    axis_order = (0, 3, 1, 4, 2, 5) + tuple(range(6, 6 + len(tail_shape)))
    return shaped.transpose(axis_order).reshape((frame_groups * side_t * FH * FW,) + tail_shape)


def on_device(
    tokens, d_out, modulation, frame_counts, w_qkv, w_out, w_up, w_down, table_s, table_t
):
    local_rows = tokens.shape[0]
    clip_len = PADF * FH * FW
    group_clips = modulation.shape[0]
    group_rows = group_clips * clip_len
    scale_dot = HD ** (-0.5)
    my_index = lax.axis_index("head")
    first_row = my_index * local_rows
    row_ids = first_row + jnp.arange(local_rows, dtype=jnp.int32)
    clip_slots = jnp.arange(group_clips, dtype=jnp.int32)
    row_onehot = ((row_ids // clip_len)[:, None] == clip_slots[None, :]).astype(jnp.float32)
    count_float = frame_counts.astype(jnp.float32)
    row_frames = jnp.dot(row_onehot, count_float, precision=HIGHEST_PRECISION)
    row_keep = ((row_ids % clip_len // (FH * FW)).astype(jnp.float32) < row_frames).astype(
        jnp.float32
    )[:, None]
    group_ids = jnp.arange(group_rows, dtype=jnp.int32)
    group_onehot = ((group_ids // clip_len)[:, None] == clip_slots[None, :]).astype(jnp.float32)
    group_frames = jnp.dot(group_onehot, count_float, precision=HIGHEST_PRECISION)
    group_keep = (group_ids % clip_len // (FH * FW)).astype(jnp.float32) < group_frames

    def block_shape(block_id):
        if block_id == 0:
            return (1, SWIN)
        return (PADF, TWIN)

    def mod_row(slot):
        return jnp.dot(row_onehot, modulation[:, slot, :], precision=HIGHEST_PRECISION)

    def rows_in(values):
        return lax.all_gather(values, "head", axis=0, tiled=True)

    def grads_in(values):
        return lax.all_gather(values, "head", axis=0, tiled=True)

    def rows_out(full_rows, weight):
        return lax.psum_scatter(
            jnp.dot(full_rows, weight, preferred_element_type=jnp.float32).astype(jnp.bfloat16),
            "head",
            scatter_dimension=0,
            tiled=True,
        ).astype(jnp.float32)

    def grads_out(full_rows, weight, einsum_form):
        return lax.psum_scatter(
            jnp.einsum(einsum_form, full_rows, weight, preferred_element_type=jnp.float32).astype(
                jnp.bfloat16
            ),
            "head",
            scatter_dimension=0,
            tiled=True,
        ).astype(jnp.float32)

    def rows_keep(block_id):
        if block_id == 0:
            return None
        return to_windows(group_keep[:, None], PADF, TWIN)[:, :, 0]

    def shape_windows(projected, side_t, side_len):
        head_count = projected.shape[-1] // HD
        window_size = side_t * side_len * side_len
        windows = to_windows(projected, side_t, side_len)
        return windows.reshape(windows.shape[0], window_size, 3, head_count, HD)

    def shape_grad(grad_attended, side_t, side_len):
        head_count = grad_attended.shape[-1] // HD
        window_size = side_t * side_len * side_len
        windows = to_windows(grad_attended, side_t, side_len)
        return windows.reshape(windows.shape[0], window_size, head_count, HD)

    def flat_rows(windowed, side_t, side_len):
        return from_windows(windowed, side_t, side_len)

    def logits_of(queries, key_rows, table_arg, rel_index, keep_win):
        logits = (
            jnp.einsum("wqhe,wkhe->whqk", queries, key_rows, preferred_element_type=jnp.float32)
            * scale_dot
        )
        logits = logits + table_arg[:, rel_index][None]
        if keep_win is not None:
            logits = jnp.where(keep_win[:, None, None, :], logits, NEGATIVE)
        return logits

    def attend(windows, table_arg, rel_index, keep_win):
        logits = logits_of(windows[:, :, 0], windows[:, :, 1], table_arg, rel_index, keep_win)
        row_max = jnp.max(logits, axis=-1, keepdims=True)
        exponent = jnp.exp(logits - row_max)
        row_total = jnp.sum(exponent, axis=-1, keepdims=True)
        probs = exponent / row_total
        log_total = row_max + jnp.log(row_total)
        attended = jnp.einsum(
            "whqk,wkhe->wqhe",
            probs.astype(jnp.bfloat16),
            windows[:, :, 2],
            preferred_element_type=jnp.float32,
        )
        return (attended.reshape(attended.shape[0], attended.shape[1], -1), log_total)

    def attend_back(windows, grad_windows, log_total, table_arg, rel_index, keep_win):
        queries = windows[:, :, 0]
        key_rows = windows[:, :, 1]
        value_rows = windows[:, :, 2]
        logits = logits_of(queries, key_rows, table_arg, rel_index, keep_win)
        probs = jnp.exp(logits - log_total)
        grad_probs = jnp.einsum(
            "wqhe,wkhe->whqk", grad_windows, value_rows, preferred_element_type=jnp.float32
        )
        grad_values = jnp.einsum(
            "whqk,wqhe->wkhe",
            probs.astype(jnp.bfloat16),
            grad_windows,
            preferred_element_type=jnp.float32,
        )
        grad_logits = (
            probs * (grad_probs - jnp.sum(grad_probs * probs, axis=-1, keepdims=True))
        ).astype(jnp.bfloat16)
        head_count = queries.shape[2]
        table_terms = jnp.sum(grad_logits.astype(jnp.float32), axis=0).reshape(head_count, -1)
        grad_table = jax.ops.segment_sum(
            table_terms.T, rel_index.reshape(-1), num_segments=table_arg.shape[1]
        ).T
        grad_queries = (
            jnp.einsum("whqk,wkhe->wqhe", grad_logits, key_rows, preferred_element_type=jnp.float32)
            * scale_dot
        )
        grad_keys = (
            jnp.einsum("whqk,wqhe->wkhe", grad_logits, queries, preferred_element_type=jnp.float32)
            * scale_dot
        )
        grad_stack = jnp.stack([grad_queries, grad_keys, grad_values], axis=2)
        return (
            grad_stack.reshape(grad_stack.shape[0], grad_stack.shape[1], 3, head_count * HD),
            grad_table,
        )

    def forward_block(hidden, block_id):
        side_t, side_len = block_shape(block_id)
        table_local = table_s if block_id == 0 else table_t
        rel_index = window_index(side_t, side_len)
        normed = layer_norm(hidden, mod_row(6 * block_id), mod_row(6 * block_id + 1)).astype(
            jnp.bfloat16
        )
        plan = None
        normed_in = rows_in(normed)
        qkv_use, out_use, table_use = (w_qkv[block_id], w_out[block_id], table_local)
        keep_win = rows_keep(block_id)
        projected = jnp.einsum(
            "gd,cde->gce", normed_in, qkv_use, preferred_element_type=jnp.float32
        ).astype(jnp.bfloat16)
        windows = shape_windows(projected, side_t, side_len)
        attended_win, log_total = attend(windows, table_use, rel_index, keep_win)
        attended = flat_rows(attended_win, side_t, side_len).astype(jnp.bfloat16)
        branch = rows_out(attended, out_use)
        middle = hidden + mod_row(6 * block_id + 2) * branch
        shifted = layer_norm(middle, mod_row(6 * block_id + 3), mod_row(6 * block_id + 4)).astype(
            jnp.bfloat16
        )
        up_full, down_full = (
            lax.all_gather(w_up[block_id], "head", axis=1, tiled=True),
            lax.all_gather(w_down[block_id], "head", axis=0, tiled=True),
        )
        pre_gelu = jnp.dot(shifted, up_full, preferred_element_type=jnp.float32)
        activated = gelu_tanh(pre_gelu).astype(jnp.bfloat16)
        feed_out = jnp.dot(activated, down_full, preferred_element_type=jnp.float32)
        mlp_state = (shifted, pre_gelu, activated, up_full, down_full)
        result = middle + mod_row(6 * block_id + 5) * feed_out
        attn_state = (
            normed_in,
            projected,
            log_total,
            attended,
            qkv_use,
            out_use,
            table_use,
            keep_win,
            plan,
        )
        saved_state = (hidden, attn_state, branch, middle, feed_out, mlp_state)
        return (saved_state, result)

    def backward_block(saved_state, grad_result, block_id):
        hidden, attn_state, branch, middle, feed_out, mlp_state = saved_state
        normed_in, projected, log_total, attended, qkv_use, out_use, table_use, keep_win, plan = (
            attn_state
        )
        shifted_in, pre_gelu, activated, up_weight, down_weight = mlp_state
        side_t, side_len = block_shape(block_id)
        rel_index = window_index(side_t, side_len)
        grad_feed = (grad_result * mod_row(6 * block_id + 5)).astype(jnp.bfloat16)
        grad_gate_mlp = grad_result * feed_out
        grad_down = jnp.einsum(
            "gf,gd->fd", activated, grad_feed, preferred_element_type=jnp.float32
        )
        grad_activated = jnp.einsum(
            "gd,fd->gf", grad_feed, down_weight, preferred_element_type=jnp.float32
        )
        grad_pre = jax.vjp(gelu_tanh, pre_gelu)[1](grad_activated)[0].astype(jnp.bfloat16)
        grad_up = jnp.einsum("gd,gf->df", shifted_in, grad_pre, preferred_element_type=jnp.float32)
        grad_shifted = jnp.einsum(
            "gf,df->gd", grad_pre, up_weight, preferred_element_type=jnp.float32
        )
        grad_up, grad_down = (
            lax.psum_scatter(
                grad_up.astype(jnp.bfloat16), "head", scatter_dimension=1, tiled=True
            ).astype(jnp.float32),
            lax.psum_scatter(
                grad_down.astype(jnp.bfloat16), "head", scatter_dimension=0, tiled=True
            ).astype(jnp.float32),
        )
        unused_mid, pull_second = jax.vjp(
            layer_norm, middle, mod_row(6 * block_id + 3), mod_row(6 * block_id + 4)
        )
        grad_mid_norm, grad_shift_mlp, grad_scale_mlp = pull_second(grad_shifted)
        grad_middle = grad_result + grad_mid_norm
        grad_branch = (grad_middle * mod_row(6 * block_id + 2)).astype(jnp.bfloat16)
        grad_gate_att = grad_middle * branch
        branch_in = grads_in(grad_branch)
        grad_wout = jnp.einsum("ge,gd->ed", attended, branch_in, preferred_element_type=jnp.float32)
        grad_attended = jnp.einsum(
            "gd,ed->ge", branch_in, out_use, preferred_element_type=jnp.float32
        ).astype(jnp.bfloat16)
        windows = shape_windows(projected, side_t, side_len)
        grad_windows = shape_grad(grad_attended, side_t, side_len)
        grad_stack, grad_table = attend_back(
            windows, grad_windows, log_total, table_use, rel_index, keep_win
        )
        grad_projected = flat_rows(grad_stack, side_t, side_len).astype(jnp.bfloat16)
        grad_qkv = jnp.einsum(
            "gd,gce->cde", normed_in, grad_projected, preferred_element_type=jnp.float32
        )
        grad_normed = grads_out(grad_projected, qkv_use, "gce,cde->gd")
        unused_hid, pull_first = jax.vjp(
            layer_norm, hidden, mod_row(6 * block_id), mod_row(6 * block_id + 1)
        )
        grad_hid_norm, grad_shift_att, grad_scale_att = pull_first(grad_normed)
        grad_hidden = grad_middle + grad_hid_norm
        mod_terms = jnp.stack(
            [
                grad_shift_att,
                grad_scale_att,
                grad_gate_att,
                grad_shift_mlp,
                grad_scale_mlp,
                grad_gate_mlp,
            ],
            axis=1,
        )
        grad_mods = jnp.einsum("rc,rke->cke", row_onehot, mod_terms, precision=HIGHEST_PRECISION)
        return (grad_hidden, grad_mods, (grad_qkv, grad_wout, grad_up, grad_down, grad_table))

    hidden_first = tokens.astype(jnp.float32)
    saved_first, hidden_second = forward_block(hidden_first, 0)
    saved_second, hidden_last = forward_block(hidden_second, 1)
    output = (hidden_last * row_keep).astype(jnp.bfloat16)
    grad_second, mods_second, weights_second = backward_block(
        saved_second, d_out.astype(jnp.float32) * row_keep, 1
    )
    grad_first, mods_first, weights_first = backward_block(saved_first, grad_second, 0)
    grad_modulation = lax.psum(
        jnp.concatenate([mods_first, mods_second], axis=1).astype(jnp.bfloat16), "head"
    ).astype(jnp.float32)
    summed = (
        lax.psum(
            jnp.stack([weights_first[0], weights_second[0]]).astype(jnp.bfloat16), "clip"
        ).astype(jnp.float32),
        lax.psum(
            jnp.stack([weights_first[1], weights_second[1]]).astype(jnp.bfloat16), "clip"
        ).astype(jnp.float32),
        lax.psum(
            jnp.stack([weights_first[2], weights_second[2]]).astype(jnp.bfloat16), "clip"
        ).astype(jnp.float32),
        lax.psum(
            jnp.stack([weights_first[3], weights_second[3]]).astype(jnp.bfloat16), "clip"
        ).astype(jnp.float32),
        lax.psum(weights_first[4].astype(jnp.bfloat16), "clip").astype(jnp.float32),
        lax.psum(weights_second[4].astype(jnp.bfloat16), "clip").astype(jnp.float32),
    )
    return (
        output,
        grad_first,
        grad_modulation,
        summed[0],
        summed[1],
        summed[2],
        summed[3],
        summed[4],
        summed[5],
    )


F32 = jnp.float32
BF16 = jnp.bfloat16
VMEM_LIMIT = 58 * 1024 * 1024
NZ = 4
D = 1024
HPZ = 4
CONST = pl.Buffered(1)


def dot_nn(a, b):
    return lax.dot_general(a, b, (((1,), (0,)), ((), ())), preferred_element_type=F32)


def dot_nt(a, b):
    return lax.dot_general(a, b, (((1,), (1,)), ((), ())), preferred_element_type=F32)


def dot_tn(a, b):
    return lax.dot_general(a, b, (((0,), (0,)), ((), ())), preferred_element_type=F32)


def call(kernel, name, grid, in_specs, out_specs, out_shape, scratch, flops, nbytes):
    return pl.pallas_call(
        kernel,
        name=name,
        grid=grid,
        in_specs=in_specs,
        out_specs=out_specs,
        out_shape=out_shape,
        scratch_shapes=scratch,
        compiler_params=pltpu.CompilerParams(
            dimension_semantics=("arbitrary",) * len(grid), vmem_limit_bytes=VMEM_LIMIT
        ),
        cost_estimate=pl.CostEstimate(
            flops=flops // 4, bytes_accessed=nbytes // 4, transcendentals=0
        ),
    )


def full(shape):
    return pl.BlockSpec(shape, lambda *ids: (0,) * len(shape), pipeline_mode=CONST)


def chunk_rows(i, size):
    return pl.ds(pl.multiple_of(i * size, size), size)


def ln_stats(x):
    mean = jnp.mean(x, axis=-1, keepdims=True)
    centred = x - mean
    rstd = lax.rsqrt(jnp.mean(centred * centred, axis=-1, keepdims=True) + EPS)
    return centred * rstd, rstd


def ln_back(grad, hat, rstd, scale):
    gh = grad * (1.0 + scale)
    m1 = jnp.mean(gh, axis=-1, keepdims=True)
    m2 = jnp.mean(gh * hat, axis=-1, keepdims=True)
    return rstd * (gh - m1 - hat * m2)


def piece_specs(k, row, count):
    tail = (count, D)
    return [
        pl.BlockSpec((2, 4) + tail, lambda d: (0, 0, row, 0), pipeline_mode=CONST),
        pl.BlockSpec((4, 1) + tail, lambda d: (0, jnp.maximum(d - 1, 0), row, 0)),
        pl.BlockSpec((4, 1) + tail, lambda d: (0, jnp.maximum(d - 1, 0), row, 0)),
    ]


def by_offset(d, body, local_ref, own_ref, other_ref):
    @pl.when(d == 0)
    def _():
        body(lambda m, r, n: local_ref[0, m, r : r + n, :], lambda m, r, n: local_ref[1, m, r : r + n, :])

    @pl.when(d > 0)
    def _():
        body(lambda m, r, n: own_ref[m, 0, r : r + n, :], lambda m, r, n: other_ref[m, 0, r : r + n, :])


def head_rows(own, other, row):
    parts = []
    for m in range(4):
        parts += [own(m, row, 32), other(m, row, 32)]
    return jnp.concatenate(parts, axis=0)


def pair_rows(first, second):
    return jnp.concatenate([get(m) for get in (first, second) for m in range(4)], axis=0)


def feed_specs(down_block):
    def spec(block):
        return pl.BlockSpec((4, 1, 128, D), lambda d: (0, jnp.maximum(d - 1, 0), block, 0))

    return [full((2, 4, 256, D)), spec(0), spec(0), spec(down_block), spec(down_block)]


def feed_by_offset(d, body, l_ref, wu_ref, vu_ref, wd_ref, vd_ref):
    @pl.when(d == 0)
    def _():
        body(
            lambda: pair_rows(lambda m: l_ref[0, m, 0:128], lambda m: l_ref[1, m, 0:128]),
            lambda: pair_rows(lambda m: l_ref[0, m, 128:256], lambda m: l_ref[1, m, 128:256]),
        )

    @pl.when(d > 0)
    def _():
        body(
            lambda: pair_rows(lambda m: wu_ref[m, 0], lambda m: vu_ref[m, 0]),
            lambda: pair_rows(lambda m: wd_ref[m, 0], lambda m: vd_ref[m, 0]),
        )


def ln_qkv(hidden, mods, weights, base):
    rows = hidden.shape[0]
    step = 640

    def kernel(h_ref, m_ref, l_ref, w_ref, v_ref, normed_ref, qkv_ref):
        d = pl.program_id(0)

        @pl.when(d == 0)
        def _():
            def body(i, carry):
                sl = chunk_rows(i, step)
                hat, _ = ln_stats(h_ref[sl, :].astype(F32))
                normed_ref[sl, :] = (
                    hat * (1.0 + m_ref[base + 1 : base + 2, :]) + m_ref[base : base + 1, :]
                ).astype(BF16)
                return carry

            lax.fori_loop(0, rows // step, body, 0)

        def work(own, other):
            for t in range(3):
                qkv_ref[:, t * 256 : (t + 1) * 256] = dot_nt(
                    normed_ref[...], head_rows(own, other, t * 32)
                ).astype(BF16)

        by_offset(d, work, l_ref, w_ref, v_ref)

    return call(
        kernel,
        "ln_qkv",
        (NZ,),
        [full((rows, D)), full((12, D))] + piece_specs(128, 0, 96),
        [full((rows, D)), pl.BlockSpec((rows, 768), lambda z: (0, z))],
        [jax.ShapeDtypeStruct((rows, D), BF16), jax.ShapeDtypeStruct((rows, 3 * D), BF16)],
        [],
        2 * rows * D * 3 * D,
        rows * D * 12 + 6 * D * D,
    )(hidden, mods, *weights)


def build_bias(base_ref, bias_ref, fc_ref, slides, width, lanes_step):
    rows_step = width // slides
    for h in range(HPZ):
        for s in range(slides):
            off = (slides - 1 - s) * lanes_step
            tile = base_ref[h, :, off : off + width]
            if fc_ref is not None:
                tile = jnp.where(s < fc_ref[0], tile, NEGATIVE)
            bias_ref[h, s * rows_step : (s + 1) * rows_step, :] = tile


def window_view(values, kind):
    parts, count, size = kind[0]
    return values.reshape(parts, count, size, values.shape[-1])


def attn_fwd(qkv, base, fc, kind):
    (parts, count, size), slides, lanes_step, masked = kind
    rows, width = qkv.shape[0], parts * size
    r_step, lanes = base.shape[1], base.shape[2]

    def kernel(x_ref, b_ref, fc_ref, o_ref, bias_ref):
        build_bias(b_ref, bias_ref, fc_ref if masked else None, slides, width, lanes_step)

        def one(w, carry):
            def cut(col):
                return x_ref[:, w, :, col : col + HD].reshape(width, HD)

            scores, probs = [], []
            for h in range(HPZ):
                scores.append(dot_nt(cut(256 + h * HD), cut(h * HD) * 0.125) + bias_ref[h])
            for h in range(HPZ):
                expo = jnp.exp(scores[h] - jnp.max(scores[h], axis=0, keepdims=True))
                inv = 1.0 / jnp.sum(expo, axis=0, keepdims=True)
                probs.append((expo * inv).astype(BF16))
            for h in range(HPZ):
                got = dot_tn(probs[h], cut(512 + h * HD)).astype(BF16)
                o_ref[:, w, :, h * HD : (h + 1) * HD] = got.reshape(parts, size, HD)
            return carry

        lax.fori_loop(0, count, one, 0)

    return call(
        kernel,
        "attn_fwd",
        (NZ,),
        [
            pl.BlockSpec((parts, count, size, 768), lambda z: (0, 0, 0, z)),
            pl.BlockSpec((HPZ, r_step, lanes), lambda z: (z, 0, 0)),
            pl.BlockSpec(memory_space=pltpu.SMEM),
        ],
        pl.BlockSpec((parts, count, size, 256), lambda z: (0, 0, 0, z)),
        jax.ShapeDtypeStruct((parts, count, size, D), BF16),
        [pltpu.VMEM((HPZ, width, width), F32)],
        count * 16 * width * width * HD * 16,
        rows * D * 8,
    )(window_view(qkv, kind), base, fc).reshape(rows, D)


def attn_bwd(qkv, grad_att, base, fc, kind):
    (parts, count, size), slides, lanes_step, masked = kind
    rows, width = qkv.shape[0], parts * size
    r_step, lanes = base.shape[1], base.shape[2]

    def kernel(x_ref, d_ref, b_ref, fc_ref, o_ref, gb_ref, bias_ref, acc_ref):
        build_bias(b_ref, bias_ref, fc_ref if masked else None, slides, width, lanes_step)
        acc_ref[...] = jnp.zeros_like(acc_ref)

        def one(w, carry):
            def cut(ref, col):
                return ref[:, w, :, col : col + HD].reshape(width, HD)

            def put(col, value):
                o_ref[:, w, :, col : col + HD] = value.astype(BF16).reshape(parts, size, HD)

            q = [cut(x_ref, h * HD) * 0.125 for h in range(HPZ)]
            k = [cut(x_ref, 256 + h * HD) for h in range(HPZ)]
            da = [cut(d_ref, h * HD) for h in range(HPZ)]
            score = [dot_nt(k[h], q[h]) + bias_ref[h] for h in range(HPZ)]
            dp = [dot_nt(cut(x_ref, 512 + h * HD), da[h]) for h in range(HPZ)]
            probs, dl = [], []
            for h in range(HPZ):
                expo = jnp.exp(score[h] - jnp.max(score[h], axis=0, keepdims=True))
                inv = 1.0 / jnp.sum(expo, axis=0, keepdims=True)
                p = expo * inv
                row = jnp.sum(dp[h] * p, axis=0, keepdims=True)
                g = (p * (dp[h] - row)).astype(BF16)
                acc_ref[h] += g.astype(F32)
                probs.append(p.astype(BF16))
                dl.append(g)
            for h in range(HPZ):
                put(h * HD, dot_tn(dl[h], k[h]) * 0.125)
                put(256 + h * HD, dot_nn(dl[h], q[h]))
                put(512 + h * HD, dot_nn(probs[h], da[h]))
            return carry

        lax.fori_loop(0, count, one, 0)
        gb_ref[...] = jnp.zeros_like(gb_ref)
        for h in range(HPZ):
            for s in range(slides):
                off = (slides - 1 - s) * lanes_step
                gb_ref[h, :, off : off + width] += acc_ref[h, s * r_step : (s + 1) * r_step, :]

    xspec = pl.BlockSpec((parts, count, size, 768), lambda z: (0, 0, 0, z))
    bspec = pl.BlockSpec((HPZ, r_step, lanes), lambda z: (z, 0, 0))
    proj, strips = call(
        kernel,
        "attn_bwd",
        (NZ,),
        [
            xspec,
            pl.BlockSpec((parts, count, size, 256), lambda z: (0, 0, 0, z)),
            bspec,
            pl.BlockSpec(memory_space=pltpu.SMEM),
        ],
        [xspec, bspec],
        [
            jax.ShapeDtypeStruct((parts, count, size, 3 * D), BF16),
            jax.ShapeDtypeStruct(base.shape, F32),
        ],
        [pltpu.VMEM((HPZ, width, width), F32), pltpu.VMEM((HPZ, width, width), F32)],
        count * 16 * width * width * HD * 40,
        rows * D * 16,
    )(window_view(qkv, kind), window_view(grad_att, kind), base, fc)
    return proj.reshape(rows, 3 * D), strips


def out_specs_of(row_block):
    return [
        pl.BlockSpec((2, 4, 32, D), lambda i: (0, 0, row_block, 0), pipeline_mode=CONST),
        pl.BlockSpec((4, 3, 32, D), lambda i: (0, 0, row_block, 0), pipeline_mode=CONST),
        pl.BlockSpec((4, 3, 32, D), lambda i: (0, 0, row_block, 0), pipeline_mode=CONST),
    ]


def out_rows(d, l_ref, w_ref, v_ref):
    if d == 0:
        return head_rows(
            lambda m, r, n: l_ref[0, m, :, :], lambda m, r, n: l_ref[1, m, :, :], 0
        )
    return head_rows(
        lambda m, r, n: w_ref[m, d - 1, :, :], lambda m, r, n: v_ref[m, d - 1, :, :], 0
    )


def out_proj(attended, weights, hidden, mods, base):
    rows = attended.shape[0]
    step = 256

    def kernel(a_ref, l_ref, w_ref, v_ref, h_ref, m_ref, br_ref, mid_ref, sh_ref):
        branch = jnp.zeros((step, D), F32)
        for d in range(NZ):
            branch += dot_nn(a_ref[:, d * 256 : (d + 1) * 256], out_rows(d, l_ref, w_ref, v_ref))
        br_ref[...] = branch.astype(BF16)
        middle = h_ref[...].astype(F32) + m_ref[base + 2 : base + 3, :] * branch
        mid_ref[...] = middle
        hat, _ = ln_stats(middle)
        sh_ref[...] = (
            hat * (1.0 + m_ref[base + 4 : base + 5, :]) + m_ref[base + 3 : base + 4, :]
        ).astype(BF16)

    tile = pl.BlockSpec((step, D), lambda i: (i, 0))
    return call(
        kernel,
        "out_proj",
        (rows // step,),
        [tile] + out_specs_of(3) + [tile, full((12, D))],
        [tile, tile, tile],
        [
            jax.ShapeDtypeStruct((rows, D), BF16),
            jax.ShapeDtypeStruct((rows, D), F32),
            jax.ShapeDtypeStruct((rows, D), BF16),
        ],
        [],
        2 * rows * D * D,
        rows * D * 14 + 2 * D * D,
    )(attended, *weights, hidden, mods)


GELU_C = 0.7978845608028654
GELU_A = 0.044715


def gelu_of(x):
    return 0.5 * x * (1.0 + jnp.tanh(GELU_C * (x + GELU_A * x * x * x)))


def gelu_both(x):
    x2 = x * x
    th = jnp.tanh(GELU_C * (x + GELU_A * x * x2))
    half = 0.5 * (1.0 + th)
    slope = half + 0.5 * x * (1.0 - th * th) * (GELU_C * (1.0 + 3.0 * GELU_A * x2))
    return x * half, slope


def ffn_fwd(shifted, weights, down_block, middle, mods, base):
    rows = shifted.shape[0]
    step = 640

    def kernel(x_ref, *refs):
        parts, (mid_ref, m_ref, pre_ref, feed_ref, nx_ref, acc_ref) = refs[:5], refs[5:]
        z = pl.program_id(0)

        def work(up, down):
            def body(i, carry):
                sl = chunk_rows(i, step)
                pre = dot_nt(x_ref[sl, :], up())
                pre_ref[sl, :] = pre.astype(BF16)
                part = dot_nn(gelu_of(pre).astype(BF16), down())

                @pl.when(z == 0)
                def _():
                    acc_ref[sl, :] = part

                @pl.when((z > 0) & (z < NZ - 1))
                def _():
                    acc_ref[sl, :] += part

                @pl.when(z == NZ - 1)
                def _():
                    feed = acc_ref[sl, :] + part
                    feed_ref[sl, :] = feed.astype(BF16)
                    nx_ref[sl, :] = (
                        mid_ref[sl, :] + m_ref[base + 5 : base + 6, :] * feed
                    ).astype(BF16)

                return carry

            lax.fori_loop(0, rows // step, body, 0)

        feed_by_offset(z, work, *parts)

    return call(
        kernel,
        "ffn_fwd",
        (NZ,),
        [full((rows, D))] + feed_specs(down_block) + [full((rows, D)), full((12, D))],
        [pl.BlockSpec((rows, D), lambda z: (0, z)), full((rows, D)), full((rows, D))],
        [
            jax.ShapeDtypeStruct((rows, 4 * D), BF16),
            jax.ShapeDtypeStruct((rows, D), BF16),
            jax.ShapeDtypeStruct((rows, D), BF16),
        ],
        [pltpu.VMEM((rows, D), F32)],
        16 * rows * D * D,
        rows * D * 20 + 16 * D * D,
    )(shifted, *weights, middle, mods)


def ffn_bwd(grad, pre, shifted, weights, down_block, mods, base):
    rows = grad.shape[0]
    step = 640

    def kernel(g_ref, p_ref, x_ref, *refs):
        parts, refs = refs[:5], refs[5:]
        m_ref, keep_ref, send_ref, gs_ref, gf_ref, act_ref, gp_ref = refs
        z = pl.program_id(0)

        @pl.when(z == 0)
        def _():
            def body(i, carry):
                sl = chunk_rows(i, step)
                gf_ref[sl, :] = (
                    g_ref[sl, :].astype(F32) * m_ref[base + 5 : base + 6, :]
                ).astype(BF16)
                gs_ref[sl, :] = jnp.zeros((step, D), F32)
                return carry

            lax.fori_loop(0, rows // step, body, 0)

        def work(up, down):
            def body(i, carry):
                sl = chunk_rows(i, step)
                back = dot_nt(gf_ref[sl, :], down())
                act, slope = gelu_both(p_ref[sl, :].astype(F32))
                act_ref[sl, :] = act.astype(BF16)
                gpre = (back * slope).astype(BF16)
                gp_ref[sl, :] = gpre
                part = dot_nn(gpre, up())
                gs_ref[sl, :] += part
                return carry

            lax.fori_loop(0, rows // step, body, 0)

        feed_by_offset(z, work, *parts)
        for j, out_ref in enumerate((keep_ref, send_ref)):
            cols = slice(j * 512, (j + 1) * 512)
            gd = dot_tn(act_ref[:, cols], gf_ref[...]).astype(BF16)
            gu = dot_tn(gp_ref[:, cols], x_ref[...]).astype(BF16)
            out_ref[:, 0, 0:128] = gu.reshape(4, 128, D)
            out_ref[:, 0, 128:256] = gd.reshape(4, 128, D)

    gspec = pl.BlockSpec((4, 1, 256, D), lambda z: (0, z, 0, 0))
    gshape = jax.ShapeDtypeStruct((4, NZ, 256, D), BF16)
    return call(
        kernel,
        "ffn_bwd",
        (NZ,),
        [
            full((rows, D)),
            pl.BlockSpec((rows, D), lambda z: (0, z)),
            full((rows, D)),
        ]
        + feed_specs(down_block)
        + [full((12, D))],
        [gspec, gspec, full((rows, D))],
        [gshape, gshape, jax.ShapeDtypeStruct((rows, D), F32)],
        [pltpu.VMEM((rows, D), BF16)] * 3,
        32 * rows * D * D,
        rows * D * 16 + 32 * D * D,
    )(grad, pre, shifted, *weights, mods)


def split_heads(value, keep_ref, send_ref, d, row):
    for m in range(4):
        keep_ref[m, d, row : row + 32] = value[m * 64 : m * 64 + 32]
        send_ref[m, d, row : row + 32] = value[m * 64 + 32 : m * 64 + 64]


def out_bwd(grad, grad_shifted, middle, feed, branch, attended, weights, mods, base):
    rows = grad.shape[0]
    step = 256
    steps = rows // step

    def kernel(
        g_ref, gs_ref, mid_ref, f_ref, b_ref, a_ref, l_ref, w_ref, v_ref, m_ref, gm_ref, ga_ref,
        keep_ref, send_ref, s_ref, gb_ref,
    ):
        i = pl.program_id(0)

        @pl.when(i == 0)
        def _():
            s_ref[...] = jnp.zeros_like(s_ref)

        g = g_ref[...].astype(F32)
        gs = gs_ref[...]
        hat, rstd = ln_stats(mid_ref[...])
        gm = g + ln_back(gs, hat, rstd, m_ref[base + 4 : base + 5, :])
        gm_ref[...] = gm
        s_ref[0:1, :] += jnp.sum(gs, axis=0, keepdims=True)
        s_ref[1:2, :] += jnp.sum(gs * hat, axis=0, keepdims=True)
        s_ref[2:3, :] += jnp.sum(gm * b_ref[...].astype(F32), axis=0, keepdims=True)
        s_ref[3:4, :] += jnp.sum(g * f_ref[...].astype(F32), axis=0, keepdims=True)
        gb = (gm * m_ref[base + 2 : base + 3, :]).astype(BF16)
        gb_ref[chunk_rows(i, step), :] = gb
        for d in range(NZ):
            ga_ref[:, d * 256 : (d + 1) * 256] = dot_nt(
                gb, out_rows(d, l_ref, w_ref, v_ref)
            ).astype(BF16)

        @pl.when(i == steps - 1)
        def _():
            for d in range(NZ):
                gw = dot_tn(a_ref[:, d * 256 : (d + 1) * 256], gb_ref[...]).astype(BF16)
                split_heads(gw, keep_ref, send_ref, d, 0)

    tile = pl.BlockSpec((step, D), lambda i: (i, 0))
    gshape = jax.ShapeDtypeStruct((4, NZ, 32, D), BF16)
    return call(
        kernel,
        "out_bwd",
        (steps,),
        [tile, tile, tile, tile, tile, full((rows, D))] + out_specs_of(3) + [full((12, D))],
        [tile, tile, full(gshape.shape), full(gshape.shape), full((8, D))],
        [
            jax.ShapeDtypeStruct((rows, D), F32),
            jax.ShapeDtypeStruct((rows, D), BF16),
            gshape,
            gshape,
            jax.ShapeDtypeStruct((8, D), F32),
        ],
        [pltpu.VMEM((rows, D), BF16)],
        4 * rows * D * D,
        rows * D * 24 + 4 * D * D,
    )(grad, grad_shifted, middle, feed, branch, attended, *weights, mods)


def qkv_back(grad_proj, weights, hidden, grad_middle, mods, base, out_dtype, pieces):
    rows = hidden.shape[0]
    step = 640

    cols = D // pieces

    def kernel(p_ref, l_ref, w_ref, v_ref, h_ref, gm_ref, m_ref, *refs):
        gh_refs, (s_ref, acc_ref) = refs[:pieces], refs[pieces:]
        z = pl.program_id(0)

        @pl.when(z == 0)
        def _():
            acc_ref[...] = jnp.zeros_like(acc_ref)
            s_ref[...] = jnp.zeros_like(s_ref)

        def work(own, other):
            def body(i, carry):
                sl = chunk_rows(i, step)
                rows_of = jnp.concatenate([head_rows(own, other, t * 32) for t in range(3)], axis=0)
                acc_ref[sl, :] += dot_nn(p_ref[sl, :], rows_of)
                return carry

            lax.fori_loop(0, rows // step, body, 0)

        by_offset(z, work, l_ref, w_ref, v_ref)

        @pl.when(z == NZ - 1)
        def _():
            def tail(n, carry):
                sl = chunk_rows(n, 256)
                gn = acc_ref[sl, :]
                hat, rstd = ln_stats(h_ref[sl, :].astype(F32))
                gh = gm_ref[sl, :] + ln_back(gn, hat, rstd, m_ref[base + 1 : base + 2, :])
                for i, gh_ref in enumerate(gh_refs):
                    gh_ref[sl, :] = gh[:, i * cols : (i + 1) * cols].astype(out_dtype)
                s_ref[0:1, :] += jnp.sum(gn, axis=0, keepdims=True)
                s_ref[1:2, :] += jnp.sum(gn * hat, axis=0, keepdims=True)
                return carry

            lax.fori_loop(0, rows // 256, tail, 0)

    return call(
        kernel,
        "qkv_back",
        (NZ,),
        [pl.BlockSpec((rows, 768), lambda z: (0, z))]
        + piece_specs(128, 0, 96)
        + [full((rows, D)), full((rows, D)), full((12, D))],
        [full((rows, cols))] * pieces + [full((8, D))],
        [jax.ShapeDtypeStruct((rows, cols), out_dtype)] * pieces
        + [jax.ShapeDtypeStruct((8, D), F32)],
        [pltpu.VMEM((rows, D), F32)],
        6 * rows * D * D,
        rows * D * 20 + 6 * D * D,
    )(grad_proj, *weights, hidden, grad_middle, mods)


def qkv_grad(grad_proj, normed, out_keep, out_send, table_rows):
    rows = normed.shape[0]
    k = 128 if table_rows is None else 144

    def kernel(p_ref, n_ref, ok_ref, os_ref, *rest):
        keep_ref, send_ref = rest[-2:]
        for t in range(3):
            gw = dot_tn(p_ref[:, t * 256 : (t + 1) * 256], n_ref[...]).astype(BF16)
            split_heads(gw, keep_ref, send_ref, 0, t * 32)
        keep_ref[:, :, 96:128] = ok_ref[...]
        send_ref[:, :, 96:128] = os_ref[...]
        if table_rows is not None:
            keep_ref[:, :, 128:144] = rest[0][...]
            send_ref[:, :, 128:144] = rest[0][...]

    gspec = pl.BlockSpec((4, 1, k, D), lambda z: (0, z, 0, 0))
    ospec = pl.BlockSpec((4, 1, 32, D), lambda z: (0, z, 0, 0))
    tspec = pl.BlockSpec((4, 1, 16, D), lambda z: (0, z, 0, 0))
    gshape = jax.ShapeDtypeStruct((4, NZ, k, D), BF16)
    extra = () if table_rows is None else (table_rows,)
    return call(
        kernel,
        "qkv_grad",
        (NZ,),
        [pl.BlockSpec((rows, 768), lambda z: (0, z)), full((rows, D)), ospec, ospec]
        + [tspec] * len(extra),
        [gspec, gspec],
        [gshape, gshape],
        [],
        6 * rows * D * D,
        rows * D * 8 + 8 * D * D,
    )(grad_proj, normed, out_keep, out_send, *extra)


def place_call(kernel, name, in_specs, out_specs, out_shape, scratch, nbytes, aliases):
    return pl.pallas_call(
        kernel,
        name=name,
        grid_spec=pltpu.PrefetchScalarGridSpec(
            num_scalar_prefetch=1,
            grid=(8,),
            in_specs=in_specs,
            out_specs=out_specs,
            scratch_shapes=scratch,
        ),
        out_shape=out_shape,
        input_output_aliases=aliases,
        compiler_params=pltpu.CompilerParams(
            dimension_semantics=("arbitrary",), vmem_limit_bytes=VMEM_LIMIT
        ),
        cost_estimate=pl.CostEstimate(flops=0, bytes_accessed=nbytes, transcendentals=0),
    )


def rows_at(place):
    return pl.ds(pl.multiple_of(place * 32, 32), 32)


def prep_attn(place, w_qkv, w_out, b):
    def kernel(c_ref, q_ref, o_ref, out_ref, t_ref):
        r = pl.program_id(0)

        @pl.when(r == 0)
        def _():
            for t in range(3):
                t_ref[t] = q_ref[0, t].T

        at = rows_at(c_ref[0] ^ r)
        for t in range(3):
            out_ref[0, 0, t * 32 : (t + 1) * 32, :] = t_ref[t, at, :]
        out_ref[0, 0, 96:128, :] = o_ref[0, at, :]

    return place_call(
        kernel,
        "prep_attn",
        [
            pl.BlockSpec((1, 3, D, 256), lambda r, c: (b, 0, 0, 0)),
            pl.BlockSpec((1, 256, D), lambda r, c: (b, 0, 0)),
        ],
        pl.BlockSpec((1, 1, 128, D), lambda r, c: (r % 2, r // 2, 0, 0)),
        jax.ShapeDtypeStruct((2, 4, 128, D), BF16),
        [pltpu.VMEM((3, 256, D), BF16)],
        4 * D * D,
        {},
    )(place, w_qkv, w_out)


def prep_feed(place, w_up, w_down, b):
    def kernel(c_ref, u_ref, d_ref, out_ref):
        out_ref[0, 0, 0:128, :] = u_ref[0].T
        out_ref[0, 0, 128:256, :] = d_ref[0]

    return place_call(
        kernel,
        "prep_feed",
        [
            pl.BlockSpec((1, D, 128), lambda r, c: (b, 0, c[0] ^ r)),
            pl.BlockSpec((1, 128, D), lambda r, c: (b, c[0] ^ r, 0)),
        ],
        pl.BlockSpec((1, 1, 256, D), lambda r, c: (r % 2, r // 2, 0, 0)),
        jax.ShapeDtypeStruct((2, 4, 256, D), BF16),
        [],
        8 * D * D,
        {},
    )(place, w_up, w_down)


def finish_attn(place, own, other, b, earlier, block):

    def kernel(c_ref, own_ref, oth_ref, *rest):
        gq_ref, go_ref, t_ref = rest[-3:]
        r = pl.program_id(0)
        at = rows_at(c_ref[0] ^ r)

        def store(ref):
            for t in range(3):
                t_ref[t, at, :] = ref[0, t * 32 : (t + 1) * 32, :]
            go_ref[0, at, :] = ref[0, 96:128, :].astype(F32)

        @pl.when(r % 2 == 0)
        def _():
            store(own_ref)

        @pl.when(r % 2 == 1)
        def _():
            store(oth_ref)

        @pl.when(r == 7)
        def _():
            for t in range(3):
                gq_ref[0, t] = t_ref[t].T.astype(F32)

    piece = pl.BlockSpec((1, 128, D), lambda r, c: (r // 2, block, 0))
    anywhere = pl.BlockSpec(memory_space=pl.ANY)
    return place_call(
        kernel,
        "finish_attn",
        [piece, piece] + [anywhere] * len(earlier),
        [
            pl.BlockSpec((1, 3, D, 256), lambda r, c: (b, 0, 0, 0)),
            pl.BlockSpec((1, 256, D), lambda r, c: (b, 0, 0)),
        ],
        [
            jax.ShapeDtypeStruct((2, 3, D, 256), F32),
            jax.ShapeDtypeStruct((2, 256, D), F32),
        ],
        [pltpu.VMEM((3, 256, D), BF16)],
        6 * D * D,
        {3 + i: i for i in range(len(earlier))},
    )(place, own, other, *earlier)


def finish_feed(place, own, other, b, earlier):
    def kernel(c_ref, own_ref, oth_ref, *rest):
        gu_ref, gd_ref = rest[-2:]
        r = pl.program_id(0)

        def store(ref):
            gu_ref[0] = ref[0, 0:128, :].T.astype(F32)
            gd_ref[0] = ref[0, 128:256, :].astype(F32)

        @pl.when(r % 2 == 0)
        def _():
            store(own_ref)

        @pl.when(r % 2 == 1)
        def _():
            store(oth_ref)

    piece = pl.BlockSpec((1, 256, D), lambda r, c: (r // 2, 0, 0))
    anywhere = pl.BlockSpec(memory_space=pl.ANY)
    return place_call(
        kernel,
        "finish_feed",
        [piece, piece] + [anywhere] * len(earlier),
        [
            pl.BlockSpec((1, D, 128), lambda r, c: (b, 0, c[0] ^ r)),
            pl.BlockSpec((1, 128, D), lambda r, c: (b, c[0] ^ r, 0)),
        ],
        [jax.ShapeDtypeStruct((2, D, D), F32), jax.ShapeDtypeStruct((2, D, D), F32)],
        [],
        12 * D * D,
        {3 + i: i for i in range(len(earlier))},
    )(place, own, other, *earlier)


def partner(values):
    return lax.ppermute(values, "head", [(i, i ^ 1) for i in range(NZ)])


def rows_to_spatial(rows, odd):
    cols = rows.shape[1]
    whole = lax.dynamic_slice(rows, (256 * odd, 0), (1024, cols))
    part = lax.dynamic_slice(rows, (1024 * (1 - odd), 0), (256, cols)).reshape(8, 2, 16, cols)
    wins = whole.reshape(2, 16, 2, 16, cols).transpose(0, 2, 1, 3, 4).reshape(1024, cols)
    left, right = part[:, 0].reshape(128, cols), part[:, 1].reshape(128, cols)
    keep = jnp.where(odd == 0, left, right)
    got = partner(jnp.where(odd == 0, right, left))
    top, bottom = jnp.where(odd == 0, keep, got), jnp.where(odd == 0, got, keep)
    part = jnp.concatenate([top, bottom], axis=0)
    return jnp.where(
        odd == 0,
        jnp.concatenate([wins, part], axis=0),
        jnp.concatenate([part, wins], axis=0),
    )


def spatial_to_rows(wins, odd):
    cols = wins.shape[1]
    whole = lax.dynamic_slice(wins, (256 * odd, 0), (1024, cols))
    part = lax.dynamic_slice(wins, (1024 * (1 - odd), 0), (256, cols))
    whole = whole.reshape(2, 2, 16, 16, cols).transpose(0, 2, 1, 3, 4).reshape(1024, cols)
    keep = jnp.where(odd == 0, part[:128], part[128:])
    got = partner(jnp.where(odd == 0, part[128:], part[:128]))
    left, right = jnp.where(odd == 0, keep, got), jnp.where(odd == 0, got, keep)
    part = jnp.stack([left.reshape(8, 16, cols), right.reshape(8, 16, cols)], axis=1)
    part = part.reshape(256, cols)
    return jnp.where(
        odd == 0,
        jnp.concatenate([whole, part], axis=0),
        jnp.concatenate([part, whole], axis=0),
    )


def exchange(values):
    return lax.all_to_all(values, "head", 0, 0, tiled=True)


def spatial_to_tubes(wins):
    cols = wins.shape[1]
    return exchange(
        wins.reshape(5, 2, 8, 2, 8, cols).transpose(1, 3, 0, 2, 4, 5).reshape(1280, cols)
    )


def from_quads(quads):
    cols = quads.shape[1]
    return quads.reshape(2, 2, 5, 8, 8, cols).transpose(2, 0, 3, 1, 4, 5).reshape(1280, cols)


def toeplitz(side):
    span = 2 * side - 1
    b = lax.broadcasted_iota(jnp.int32, (span, side, side), 0)
    j = lax.broadcasted_iota(jnp.int32, (span, side, side), 1)
    i = lax.broadcasted_iota(jnp.int32, (span, side, side), 2)
    return (b == i - j + side - 1).astype(F32)


def toeplitz_pair(side):
    span = 2 * side - 1
    shape = (span * span, side * side, side * side)
    r = lax.broadcasted_iota(jnp.int32, shape, 0)
    j = lax.broadcasted_iota(jnp.int32, shape, 1)
    i = lax.broadcasted_iota(jnp.int32, shape, 2)
    dy = i // side - j // side + side - 1
    dx = i % side - j % side + side - 1
    return (r == dy * span + dx).astype(F32)


CORE, ROW_X, ROW_Y = 1, 2, 4


def swap(values, bit):
    return lax.ppermute(values, "clip", [(i, i ^ bit) for i in range(8)])


def from_z(values, d):
    return lax.ppermute(values, "head", [((i + d) % NZ, i) for i in range(NZ)])


def sync(*values):
    return lax.optimization_barrier(values)


def add(first, second):
    return (first.astype(F32) + second.astype(F32)).astype(BF16)


def line_stage(piece):
    return [from_z(piece, d) for d in (1, 2, 3)]


def others(by_z, z):
    return [lax.dynamic_index_in_dim(by_z, (z + d) % NZ, 0, keepdims=False) for d in (1, 2, 3)]


def cross_stage(own):
    return [own] + [swap(own, m * 2) for m in (1, 2, 3)]


def sides_stage(own):
    return [own, swap(own, ROW_X), swap(own, ROW_Y)]


def corner_stage(sides):
    half = sides[0].shape[1] // 2
    return [swap(sides[1][:, :half], ROW_Y), swap(sides[2][:, half:], ROW_X)]


def joined(sides, corner):
    return jnp.stack(sides + [jnp.concatenate(corner, axis=1)])


def sum_core(keep, got):
    return [add(keep[m], got[m]) for m in range(4)]


def send_plane(totals, offsets):
    return [swap(totals[m], m * 2) for m in offsets]


def to_places(total, z):
    twice = jnp.concatenate([total, total[: NZ - 1]], axis=0)
    return lax.dynamic_slice_in_dim(twice, (NZ - z) % NZ, NZ, axis=0)


def sum_plane(totals, got, z):
    total = totals[0].astype(F32)
    for value in got:
        total = total + value.astype(F32)
    return to_places(total.astype(BF16), z)


def send_cross(totals):
    half = totals[0].shape[1] // 2
    first = [t[:, :half] for t in totals]
    second = [t[:, half:] for t in totals]
    by_x = swap(jnp.stack([first[1], first[3]]), ROW_X)
    by_y = swap(jnp.stack([second[2], second[3]]), ROW_Y)
    return by_x, by_y


def sum_cross(totals, got):
    half = totals[0].shape[1] // 2
    by_x, by_y = got
    first = [add(totals[0][:, :half], by_x[0]), add(totals[2][:, :half], by_x[1])]
    second = [add(totals[0][:, half:], by_y[0]), add(totals[1][:, half:], by_y[1])]
    return first, second


def send_corner(halves):
    return swap(halves[0][1], ROW_Y), swap(halves[1][1], ROW_X)


def sum_corner(halves, got, z):
    first = add(halves[0][0], got[0])
    second = add(halves[1][0], got[1])
    return to_places(jnp.concatenate([first, second], axis=1), z)


def sum_line(by_z):
    return lax.psum_scatter(by_z, "head", scatter_dimension=0)


def on_device_windows(
    tokens, d_out, modulation, frame_counts, w_qkv, w_out, w_up, w_down, table_s, table_t
):
    z = lax.axis_index("head")
    c = lax.axis_index("clip")
    place = c.astype(jnp.int32).reshape(1)
    chip = c // 2
    odd = z % 2
    mods = modulation[0]
    n_s, n_t = table_s.shape[1], table_t.shape[1]
    hot_s, hot_t = toeplitz(SWIN), toeplitz_pair(TWIN)
    fc = frame_counts

    def spatial_base(tables):
        base = jnp.einsum(
            "hab,bji->hjai", tables[:, :n_s].reshape(16, 31, 31), hot_s, precision=HIGHEST_PRECISION
        ).reshape(16, 16, 496)
        return jnp.pad(base, ((0, 0), (0, 0), (0, 16)))

    def tube_base(tables):
        base = jnp.einsum(
            "htr,rjk->hjtk", tables[:, n_s:].reshape(16, 9, 225), hot_t, precision=HIGHEST_PRECISION
        ).reshape(16, 64, 576)
        return jnp.pad(base, ((0, 0), (0, 0), (0, 64)))

    def table_rows(first, second):
        first = jnp.pad(first, ((0, 0), (0, D - n_s)))
        second = jnp.pad(second, ((0, 0), (0, 15 * D - n_t)))
        values = jnp.concatenate([first, second], axis=1).astype(BF16)
        return values.reshape(NZ, 4, 16, D).transpose(1, 0, 2, 3)

    spatial = ((1, 5, 256), 16, 16, False)
    tube = ((5, 4, 64), 5, 64, True)

    local_a0 = prep_attn(place, w_qkv, w_out, 0)
    line_a0 = line_stage(local_a0[0, 0])
    table_piece = jnp.concatenate([table_s, table_t], axis=1)
    tables = [from_z(table_piece, d) for d in (1, 2)]
    local_f0 = prep_feed(place, w_up, w_down, 0)
    local_a1 = prep_attn(place, w_qkv, w_out, 1)
    local_f1 = prep_feed(place, w_up, w_down, 1)
    line_a0, local_f0, local_a1, local_f1, tables, tokens, table_piece = sync(
        line_a0, local_f0, local_a1, local_f1, tables, tokens, table_piece
    )
    own_a0 = cross_stage(jnp.stack(line_a0))
    z_u0 = lax.all_gather(local_f0[0, 0, :128], "head")
    z_d0 = lax.all_gather(local_f0[0, 0, 128:], "head")
    tables = jnp.stack([table_piece] + tables + [from_z(table_piece, 3)])
    tables = jnp.concatenate(
        [lax.dynamic_slice_in_dim(tables, chip ^ m, 1, axis=1) for m in range(4)], axis=1
    ).reshape(16, n_s + n_t)
    base_s = spatial_base(tables)
    hidden0 = rows_to_spatial(tokens, odd)
    own_a0, hidden0, tables, base_s, z_u0 = sync(own_a0, hidden0, tables, base_s, z_u0)
    own_a0 = jnp.stack(own_a0)
    other_a0 = swap(own_a0, CORE)
    own_u0 = sides_stage(jnp.stack(others(z_u0, z)))
    own_a0, other_a0 = sync(own_a0, other_a0)
    weights_a0 = (local_a0, own_a0, other_a0)
    normed0, qkv0 = ln_qkv(hidden0, mods, weights_a0, 0)
    qkv0, own_u0, z_d0 = sync(qkv0, own_u0, z_d0)
    corner_u0 = corner_stage(own_u0)
    own_d0 = sides_stage(jnp.stack(others(z_d0, z)))
    z_a1 = lax.all_gather(local_a1[0, 0], "head")
    attended0 = attn_fwd(qkv0, base_s, fc, spatial)
    attended0, corner_u0, own_d0 = sync(attended0, corner_u0, own_d0)
    corner_d0 = corner_stage(own_d0)
    own_u0 = joined(own_u0, corner_u0)
    other_u0 = swap(own_u0, CORE)
    branch0, middle0, shifted0 = out_proj(attended0, weights_a0, hidden0, mods, 0)
    shifted0, corner_d0, other_u0, z_a1 = sync(shifted0, corner_d0, other_u0, z_a1)
    own_d0 = joined(own_d0, corner_d0)
    other_d0 = swap(own_d0, CORE)
    z_f1 = lax.all_gather(local_f1[0, 0], "head")
    own_a1 = jnp.stack(others(z_a1, z))
    shifted0, other_d0, own_a1 = sync(shifted0, other_d0, own_a1)
    own_a1 = cross_stage(own_a1)
    weights_f0 = (local_f0, own_u0, other_u0, own_d0, other_d0)
    pre0, feed0, hidden1 = ffn_fwd(shifted0, weights_f0, 0, middle0, mods, 0)
    hidden1, z_f1, own_a1, tables, d_out = sync(hidden1, z_f1, own_a1, tables, d_out)
    tubes1 = spatial_to_tubes(hidden1)
    own_a1 = jnp.stack(own_a1)
    other_a1 = swap(own_a1, CORE)
    own_f1 = cross_stage(jnp.stack(others(z_f1, z)))
    base_t = tube_base(tables)
    spatial_d = rows_to_spatial(d_out, odd)
    tubes1, other_a1, base_t, spatial_d = sync(tubes1, other_a1, base_t, spatial_d)
    weights_a1 = (local_a1, own_a1, other_a1)
    tubes_d = spatial_to_tubes(spatial_d)
    normed1, qkv1 = ln_qkv(tubes1, mods, weights_a1, 6)
    qkv1, own_f1 = sync(qkv1, own_f1)
    own_f1 = jnp.stack(own_f1)
    other_f1 = swap(own_f1, CORE)
    attended1 = attn_fwd(qkv1, base_t, fc, tube)
    branch1, middle1, shifted1 = out_proj(attended1, weights_a1, tubes1, mods, 6)
    shifted1, other_f1 = sync(shifted1, other_f1)
    weights_f1 = (local_f1, own_f1, other_f1, own_f1, other_f1)
    pre1, feed1, hidden2 = ffn_fwd(shifted1, weights_f1, 1, middle1, mods, 6)
    hidden2, tubes_d = sync(hidden2, tubes_d)
    live = lax.broadcasted_iota(jnp.int32, (1280, 1), 0) // 256 < fc[0]
    grad2 = jnp.where(live, tubes_d, 0)
    out_wins = exchange(jnp.where(live, hidden2, 0))
    f1_keep, f1_send, g_shift1 = ffn_bwd(grad2, pre1, shifted1, weights_f1, 1, mods, 6)
    f1_keep, f1_send, g_shift1, out_wins = sync(f1_keep, f1_send, g_shift1, out_wins)
    f1_got = swap(f1_send, CORE)
    g_mid1, g_att1, o1_keep, o1_send, sums_o1 = out_bwd(
        grad2, g_shift1, middle1, feed1, branch1, attended1, weights_a1, mods, 6
    )
    g_att1, f1_got = sync(g_att1, f1_got)
    total_f1 = sum_core(f1_keep, f1_got)
    g_att1, total_f1 = sync(g_att1, total_f1)
    got_f1 = send_cross(total_f1)
    g_proj1, g_base1 = attn_bwd(qkv1, g_att1, base_t, fc, tube)
    g_proj1, g_base1, got_f1 = sync(g_proj1, g_base1, got_f1)
    half_f1 = sum_cross(total_f1, got_f1)
    half_f1, g_proj1 = sync(half_f1, g_proj1)
    got_f1 = send_corner(half_f1)
    g_hid1a, g_hid1b, sums_q1 = qkv_back(
        g_proj1, weights_a1, tubes1, g_mid1, mods, 6, BF16, 2
    )
    g_hid1a, g_hid1b, g_proj1, out_wins, g_base1, got_f1 = sync(
        g_hid1a, g_hid1b, g_proj1, out_wins, g_base1, got_f1
    )
    grad1a = exchange(g_hid1a)
    z_f1 = sum_corner(half_f1, got_f1, z)
    a1_keep, a1_send = qkv_grad(g_proj1, normed1, o1_keep, o1_send, None)
    gt_t = jnp.einsum(
        "hjtk,rjk->htr",
        g_base1[:, :, :576].reshape(16, 64, 9, 64),
        hot_t,
        precision=HIGHEST_PRECISION,
    ).reshape(16, n_t)
    grad1a, z_f1, a1_keep, a1_send, gt_t, g_hid1b, out_wins = sync(
        grad1a, z_f1, a1_keep, a1_send, gt_t, g_hid1b, out_wins
    )
    grad1b = exchange(g_hid1b)
    total_a1 = sum_core(a1_keep, swap(a1_send, CORE))
    output = spatial_to_rows(from_quads(out_wins), odd)
    grad1b, total_a1, output, z_f1 = sync(grad1b, total_a1, output, z_f1)
    grad1 = from_quads(jnp.concatenate([grad1a, grad1b], axis=1))
    mine_f1 = sum_line(z_f1)
    got_a1 = send_plane(total_a1, (1, 2, 3))
    f0_keep, f0_send, g_shift0 = ffn_bwd(grad1, pre0, shifted0, weights_f0, 0, mods, 0)
    f0_keep, f0_send, g_shift0, mine_f1, got_a1 = sync(f0_keep, f0_send, g_shift0, mine_f1, got_a1)
    f0_got = swap(f0_send, CORE)
    own_gf1 = cross_stage(mine_f1)
    mine_a1 = sum_line(sum_plane(total_a1, got_a1, z))
    g_mid0, g_att0, o0_keep, o0_send, sums_o0 = out_bwd(
        grad1, g_shift0, middle0, feed0, branch0, attended0, weights_a0, mods, 0
    )
    g_att0, f0_got, own_gf1, mine_a1 = sync(g_att0, f0_got, own_gf1, mine_a1)
    total_f0 = sum_core(f0_keep, f0_got)
    own_gf1 = jnp.stack(own_gf1)
    g_att0, total_f0, own_gf1 = sync(g_att0, total_f0, own_gf1)
    got_f0 = send_cross(total_f0)
    own_ga1 = cross_stage(mine_a1)
    g_proj0, g_base0 = attn_bwd(qkv0, g_att0, base_s, fc, spatial)
    gt_s = jnp.einsum(
        "hjai,bji->hab",
        g_base0[:, :, :496].reshape(16, 16, 31, 16),
        hot_s,
        precision=HIGHEST_PRECISION,
    ).reshape(16, n_s)
    a0_keep, a0_send = qkv_grad(g_proj0, normed0, o0_keep, o0_send, table_rows(gt_s, gt_t))
    a0_keep, a0_send, got_f0, own_ga1, g_proj0 = sync(a0_keep, a0_send, got_f0, own_ga1, g_proj0)
    a0_got = swap(a0_send, CORE)
    half_f0 = sum_cross(total_f0, got_f0)
    got_f0 = send_corner(half_f0)
    own_ga1 = jnp.stack(own_ga1)
    other_gf1, other_ga1 = swap(own_gf1, CORE), swap(own_ga1, CORE)
    g_feed = finish_feed(place, own_gf1, other_gf1, 1, ())
    g_attn = finish_attn(place, own_ga1, other_ga1, 1, (), 0)
    half_f0, got_f0, a0_got, g_feed, g_attn, g_proj0 = sync(
        half_f0, got_f0, a0_got, g_feed, g_attn, g_proj0
    )
    total_a0 = sum_core(a0_keep, a0_got)
    z_f0 = sum_corner(half_f0, got_f0, z)
    total_a0, z_f0, g_proj0 = sync(total_a0, z_f0, g_proj0)
    got_a0 = send_cross(total_a0)
    mine_f0 = sum_line(z_f0)
    grad0, sums_q0 = qkv_back(g_proj0, weights_a0, hidden0, g_mid0, mods, 0, F32, 1)
    grad0, sums_q0, got_a0 = sync(grad0, sums_q0, got_a0)
    half_a0 = sum_cross(total_a0, got_a0)
    half_a0, grad0, sums_q0 = sync(half_a0, grad0, sums_q0)
    got_a0 = send_corner(half_a0)
    grad_tokens = spatial_to_rows(grad0, odd)
    mod_rows = jnp.concatenate(
        [
            sums_q0[0:2], sums_o0[2:3], sums_o0[0:2], sums_o0[3:4],
            sums_q1[0:2], sums_o1[2:3], sums_o1[0:2], sums_o1[3:4],
        ],
        axis=0,
    )
    got_a0, mine_f0, mod_rows, grad_tokens = sync(got_a0, mine_f0, mod_rows, grad_tokens)
    mine_a0 = sum_line(sum_corner(half_a0, got_a0, z))
    own_gf0 = cross_stage(mine_f0)
    mod_got = [from_z(mod_rows, 1), from_z(mod_rows, 2)]
    mine_a0, own_gf0, mod_got = sync(mine_a0, own_gf0, mod_got)
    own_ga0 = cross_stage(mine_a0)
    own_gf0 = jnp.stack(own_gf0)
    other_gf0 = swap(own_gf0, CORE)
    mod_got = mod_got + [from_z(mod_rows, 3)]
    g_feed = finish_feed(place, own_gf0, other_gf0, 0, g_feed)
    own_ga0, g_feed, mod_got = sync(own_ga0, g_feed, mod_got)
    own_ga0 = jnp.stack(own_ga0)
    other_ga0 = swap(own_ga0, CORE)
    g_attn = finish_attn(place, own_ga0, other_ga0, 0, g_attn, 0)
    tab = jnp.concatenate(
        [lax.dynamic_slice_in_dim(own_ga0, chip ^ m, 1, axis=0) for m in range(4)], axis=0
    )
    tab = tab[:, 128:144].reshape(4, 16 * D).astype(F32)
    return (
        output,
        grad_tokens,
        (mod_rows + mod_got[0] + mod_got[1] + mod_got[2])[None],
        g_attn[0],
        g_attn[1],
        g_feed[0],
        g_feed[1],
        tab[:, :n_s],
        tab[:, D : D + n_t],
    )


def solution(mesh):
    if mesh.shape["head"] == NZ and mesh.shape["clip"] == 8:
        body = on_device_windows
    else:
        body = on_device
    return jax.shard_map(
        body,
        mesh=mesh,
        in_specs=(
            P(("clip", "head"), None),
            P(("clip", "head"), None),
            P("clip", None, None),
            P("clip"),
            P(None, None, None, "head"),
            P(None, "head", None),
            P(None, None, "head"),
            P(None, "head", None),
            P("head", None),
            P("head", None),
        ),
        out_specs=(
            P(("clip", "head"), None),
            P(("clip", "head"), None),
            P("clip", None, None),
            P(None, None, None, "head"),
            P(None, "head", None),
            P(None, None, "head"),
            P(None, "head", None),
            P("head", None),
            P("head", None),
        ),
        check_vma=False,
    )
```

```python
import jax
import jax.numpy as jnp
from jax import lax
from jax.experimental import pallas as pl
from jax.experimental.pallas import tpu as pltpu
from jax.sharding import PartitionSpec as P

HD = 64
FH = 32
FW = 32
SWIN = 16
TWIN = 8
PADF = 5


EPS = 1e-06
HIGHEST_PRECISION = lax.Precision.HIGHEST
NEGATIVE = -1e30


def layer_norm(values, shift_row, scale_row):
    average = jnp.mean(values, axis=-1, keepdims=True)
    centred = values - average
    spread = jnp.mean(centred * centred, axis=-1, keepdims=True)
    return centred * lax.rsqrt(spread + EPS) * (1.0 + scale_row) + shift_row


def gelu_tanh(values):
    return jax.nn.gelu(values, approximate=True)


def window_index(side_t, side_len):
    window_size = side_t * side_len * side_len
    places = jnp.arange(window_size, dtype=jnp.int32)
    time_pos = places // (side_len * side_len)
    height_pos = places // side_len % side_len
    width_pos = places % side_len
    span_len = 2 * side_len - 1
    return (
        (time_pos[:, None] - time_pos[None, :] + side_t - 1) * span_len * span_len
        + (height_pos[:, None] - height_pos[None, :] + side_len - 1) * span_len
        + (width_pos[:, None] - width_pos[None, :] + side_len - 1)
    )


def to_windows(values, side_t, side_len):
    tail_shape = values.shape[1:]
    frames = values.shape[0] // (FH * FW)
    shaped = values.reshape(
        (frames // side_t, side_t, FH // side_len, side_len, FW // side_len, side_len) + tail_shape
    )
    axis_order = (0, 2, 4, 1, 3, 5) + tuple(range(6, 6 + len(tail_shape)))
    shaped = shaped.transpose(axis_order)
    return shaped.reshape((-1, side_t * side_len * side_len) + tail_shape)


def from_windows(values, side_t, side_len):
    tail_shape = values.shape[2:]
    blocks_high = FH // side_len
    blocks_wide = FW // side_len
    frame_groups = values.shape[0] // (blocks_high * blocks_wide)
    shaped = values.reshape(
        (frame_groups, blocks_high, blocks_wide, side_t, side_len, side_len) + tail_shape
    )
    axis_order = (0, 3, 1, 4, 2, 5) + tuple(range(6, 6 + len(tail_shape)))
    return shaped.transpose(axis_order).reshape((frame_groups * side_t * FH * FW,) + tail_shape)


def on_device(
    tokens, d_out, modulation, frame_counts, w_qkv, w_out, w_up, w_down, table_s, table_t
):
    local_rows = tokens.shape[0]
    clip_len = PADF * FH * FW
    group_clips = modulation.shape[0]
    group_rows = group_clips * clip_len
    scale_dot = HD ** (-0.5)
    my_index = lax.axis_index("head")
    first_row = my_index * local_rows
    row_ids = first_row + jnp.arange(local_rows, dtype=jnp.int32)
    clip_slots = jnp.arange(group_clips, dtype=jnp.int32)
    row_onehot = ((row_ids // clip_len)[:, None] == clip_slots[None, :]).astype(jnp.float32)
    count_float = frame_counts.astype(jnp.float32)
    row_frames = jnp.dot(row_onehot, count_float, precision=HIGHEST_PRECISION)
    row_keep = ((row_ids % clip_len // (FH * FW)).astype(jnp.float32) < row_frames).astype(
        jnp.float32
    )[:, None]
    group_ids = jnp.arange(group_rows, dtype=jnp.int32)
    group_onehot = ((group_ids // clip_len)[:, None] == clip_slots[None, :]).astype(jnp.float32)
    group_frames = jnp.dot(group_onehot, count_float, precision=HIGHEST_PRECISION)
    group_keep = (group_ids % clip_len // (FH * FW)).astype(jnp.float32) < group_frames

    def block_shape(block_id):
        if block_id == 0:
            return (1, SWIN)
        return (PADF, TWIN)

    def mod_row(slot):
        return jnp.dot(row_onehot, modulation[:, slot, :], precision=HIGHEST_PRECISION)

    def rows_in(values):
        return lax.all_gather(values, "head", axis=0, tiled=True)

    def grads_in(values):
        return lax.all_gather(values, "head", axis=0, tiled=True)

    def rows_out(full_rows, weight):
        return lax.psum_scatter(
            jnp.dot(full_rows, weight, preferred_element_type=jnp.float32).astype(jnp.bfloat16),
            "head",
            scatter_dimension=0,
            tiled=True,
        ).astype(jnp.float32)

    def grads_out(full_rows, weight, einsum_form):
        return lax.psum_scatter(
            jnp.einsum(einsum_form, full_rows, weight, preferred_element_type=jnp.float32).astype(
                jnp.bfloat16
            ),
            "head",
            scatter_dimension=0,
            tiled=True,
        ).astype(jnp.float32)

    def rows_keep(block_id):
        if block_id == 0:
            return None
        return to_windows(group_keep[:, None], PADF, TWIN)[:, :, 0]

    def shape_windows(projected, side_t, side_len):
        head_count = projected.shape[-1] // HD
        window_size = side_t * side_len * side_len
        windows = to_windows(projected, side_t, side_len)
        return windows.reshape(windows.shape[0], window_size, 3, head_count, HD)

    def shape_grad(grad_attended, side_t, side_len):
        head_count = grad_attended.shape[-1] // HD
        window_size = side_t * side_len * side_len
        windows = to_windows(grad_attended, side_t, side_len)
        return windows.reshape(windows.shape[0], window_size, head_count, HD)

    def flat_rows(windowed, side_t, side_len):
        return from_windows(windowed, side_t, side_len)

    def logits_of(queries, key_rows, table_arg, rel_index, keep_win):
        logits = (
            jnp.einsum("wqhe,wkhe->whqk", queries, key_rows, preferred_element_type=jnp.float32)
            * scale_dot
        )
        logits = logits + table_arg[:, rel_index][None]
        if keep_win is not None:
            logits = jnp.where(keep_win[:, None, None, :], logits, NEGATIVE)
        return logits

    def attend(windows, table_arg, rel_index, keep_win):
        logits = logits_of(windows[:, :, 0], windows[:, :, 1], table_arg, rel_index, keep_win)
        row_max = jnp.max(logits, axis=-1, keepdims=True)
        exponent = jnp.exp(logits - row_max)
        row_total = jnp.sum(exponent, axis=-1, keepdims=True)
        probs = exponent / row_total
        log_total = row_max + jnp.log(row_total)
        attended = jnp.einsum(
            "whqk,wkhe->wqhe",
            probs.astype(jnp.bfloat16),
            windows[:, :, 2],
            preferred_element_type=jnp.float32,
        )
        return (attended.reshape(attended.shape[0], attended.shape[1], -1), log_total)

    def attend_back(windows, grad_windows, log_total, table_arg, rel_index, keep_win):
        queries = windows[:, :, 0]
        key_rows = windows[:, :, 1]
        value_rows = windows[:, :, 2]
        logits = logits_of(queries, key_rows, table_arg, rel_index, keep_win)
        probs = jnp.exp(logits - log_total)
        grad_probs = jnp.einsum(
            "wqhe,wkhe->whqk", grad_windows, value_rows, preferred_element_type=jnp.float32
        )
        grad_values = jnp.einsum(
            "whqk,wqhe->wkhe",
            probs.astype(jnp.bfloat16),
            grad_windows,
            preferred_element_type=jnp.float32,
        )
        grad_logits = (
            probs * (grad_probs - jnp.sum(grad_probs * probs, axis=-1, keepdims=True))
        ).astype(jnp.bfloat16)
        head_count = queries.shape[2]
        table_terms = jnp.sum(grad_logits.astype(jnp.float32), axis=0).reshape(head_count, -1)
        grad_table = jax.ops.segment_sum(
            table_terms.T, rel_index.reshape(-1), num_segments=table_arg.shape[1]
        ).T
        grad_queries = (
            jnp.einsum("whqk,wkhe->wqhe", grad_logits, key_rows, preferred_element_type=jnp.float32)
            * scale_dot
        )
        grad_keys = (
            jnp.einsum("whqk,wqhe->wkhe", grad_logits, queries, preferred_element_type=jnp.float32)
            * scale_dot
        )
        grad_stack = jnp.stack([grad_queries, grad_keys, grad_values], axis=2)
        return (
            grad_stack.reshape(grad_stack.shape[0], grad_stack.shape[1], 3, head_count * HD),
            grad_table,
        )

    def forward_block(hidden, block_id):
        side_t, side_len = block_shape(block_id)
        table_local = table_s if block_id == 0 else table_t
        rel_index = window_index(side_t, side_len)
        normed = layer_norm(hidden, mod_row(6 * block_id), mod_row(6 * block_id + 1)).astype(
            jnp.bfloat16
        )
        plan = None
        normed_in = rows_in(normed)
        qkv_use, out_use, table_use = (w_qkv[block_id], w_out[block_id], table_local)
        keep_win = rows_keep(block_id)
        projected = jnp.einsum(
            "gd,cde->gce", normed_in, qkv_use, preferred_element_type=jnp.float32
        ).astype(jnp.bfloat16)
        windows = shape_windows(projected, side_t, side_len)
        attended_win, log_total = attend(windows, table_use, rel_index, keep_win)
        attended = flat_rows(attended_win, side_t, side_len).astype(jnp.bfloat16)
        branch = rows_out(attended, out_use)
        middle = hidden + mod_row(6 * block_id + 2) * branch
        shifted = layer_norm(middle, mod_row(6 * block_id + 3), mod_row(6 * block_id + 4)).astype(
            jnp.bfloat16
        )
        up_full, down_full = (
            lax.all_gather(w_up[block_id], "head", axis=1, tiled=True),
            lax.all_gather(w_down[block_id], "head", axis=0, tiled=True),
        )
        pre_gelu = jnp.dot(shifted, up_full, preferred_element_type=jnp.float32)
        activated = gelu_tanh(pre_gelu).astype(jnp.bfloat16)
        feed_out = jnp.dot(activated, down_full, preferred_element_type=jnp.float32)
        mlp_state = (shifted, pre_gelu, activated, up_full, down_full)
        result = middle + mod_row(6 * block_id + 5) * feed_out
        attn_state = (
            normed_in,
            projected,
            log_total,
            attended,
            qkv_use,
            out_use,
            table_use,
            keep_win,
            plan,
        )
        saved_state = (hidden, attn_state, branch, middle, feed_out, mlp_state)
        return (saved_state, result)

    def backward_block(saved_state, grad_result, block_id):
        hidden, attn_state, branch, middle, feed_out, mlp_state = saved_state
        normed_in, projected, log_total, attended, qkv_use, out_use, table_use, keep_win, plan = (
            attn_state
        )
        shifted_in, pre_gelu, activated, up_weight, down_weight = mlp_state
        side_t, side_len = block_shape(block_id)
        rel_index = window_index(side_t, side_len)
        grad_feed = (grad_result * mod_row(6 * block_id + 5)).astype(jnp.bfloat16)
        grad_gate_mlp = grad_result * feed_out
        grad_down = jnp.einsum(
            "gf,gd->fd", activated, grad_feed, preferred_element_type=jnp.float32
        )
        grad_activated = jnp.einsum(
            "gd,fd->gf", grad_feed, down_weight, preferred_element_type=jnp.float32
        )
        grad_pre = jax.vjp(gelu_tanh, pre_gelu)[1](grad_activated)[0].astype(jnp.bfloat16)
        grad_up = jnp.einsum("gd,gf->df", shifted_in, grad_pre, preferred_element_type=jnp.float32)
        grad_shifted = jnp.einsum(
            "gf,df->gd", grad_pre, up_weight, preferred_element_type=jnp.float32
        )
        grad_up, grad_down = (
            lax.psum_scatter(
                grad_up.astype(jnp.bfloat16), "head", scatter_dimension=1, tiled=True
            ).astype(jnp.float32),
            lax.psum_scatter(
                grad_down.astype(jnp.bfloat16), "head", scatter_dimension=0, tiled=True
            ).astype(jnp.float32),
        )
        unused_mid, pull_second = jax.vjp(
            layer_norm, middle, mod_row(6 * block_id + 3), mod_row(6 * block_id + 4)
        )
        grad_mid_norm, grad_shift_mlp, grad_scale_mlp = pull_second(grad_shifted)
        grad_middle = grad_result + grad_mid_norm
        grad_branch = (grad_middle * mod_row(6 * block_id + 2)).astype(jnp.bfloat16)
        grad_gate_att = grad_middle * branch
        branch_in = grads_in(grad_branch)
        grad_wout = jnp.einsum("ge,gd->ed", attended, branch_in, preferred_element_type=jnp.float32)
        grad_attended = jnp.einsum(
            "gd,ed->ge", branch_in, out_use, preferred_element_type=jnp.float32
        ).astype(jnp.bfloat16)
        windows = shape_windows(projected, side_t, side_len)
        grad_windows = shape_grad(grad_attended, side_t, side_len)
        grad_stack, grad_table = attend_back(
            windows, grad_windows, log_total, table_use, rel_index, keep_win
        )
        grad_projected = flat_rows(grad_stack, side_t, side_len).astype(jnp.bfloat16)
        grad_qkv = jnp.einsum(
            "gd,gce->cde", normed_in, grad_projected, preferred_element_type=jnp.float32
        )
        grad_normed = grads_out(grad_projected, qkv_use, "gce,cde->gd")
        unused_hid, pull_first = jax.vjp(
            layer_norm, hidden, mod_row(6 * block_id), mod_row(6 * block_id + 1)
        )
        grad_hid_norm, grad_shift_att, grad_scale_att = pull_first(grad_normed)
        grad_hidden = grad_middle + grad_hid_norm
        mod_terms = jnp.stack(
            [
                grad_shift_att,
                grad_scale_att,
                grad_gate_att,
                grad_shift_mlp,
                grad_scale_mlp,
                grad_gate_mlp,
            ],
            axis=1,
        )
        grad_mods = jnp.einsum("rc,rke->cke", row_onehot, mod_terms, precision=HIGHEST_PRECISION)
        return (grad_hidden, grad_mods, (grad_qkv, grad_wout, grad_up, grad_down, grad_table))

    hidden_first = tokens.astype(jnp.float32)
    saved_first, hidden_second = forward_block(hidden_first, 0)
    saved_second, hidden_last = forward_block(hidden_second, 1)
    output = (hidden_last * row_keep).astype(jnp.bfloat16)
    grad_second, mods_second, weights_second = backward_block(
        saved_second, d_out.astype(jnp.float32) * row_keep, 1
    )
    grad_first, mods_first, weights_first = backward_block(saved_first, grad_second, 0)
    grad_modulation = lax.psum(
        jnp.concatenate([mods_first, mods_second], axis=1).astype(jnp.bfloat16), "head"
    ).astype(jnp.float32)
    summed = (
        lax.psum(
            jnp.stack([weights_first[0], weights_second[0]]).astype(jnp.bfloat16), "clip"
        ).astype(jnp.float32),
        lax.psum(
            jnp.stack([weights_first[1], weights_second[1]]).astype(jnp.bfloat16), "clip"
        ).astype(jnp.float32),
        lax.psum(
            jnp.stack([weights_first[2], weights_second[2]]).astype(jnp.bfloat16), "clip"
        ).astype(jnp.float32),
        lax.psum(
            jnp.stack([weights_first[3], weights_second[3]]).astype(jnp.bfloat16), "clip"
        ).astype(jnp.float32),
        lax.psum(weights_first[4].astype(jnp.bfloat16), "clip").astype(jnp.float32),
        lax.psum(weights_second[4].astype(jnp.bfloat16), "clip").astype(jnp.float32),
    )
    return (
        output,
        grad_first,
        grad_modulation,
        summed[0],
        summed[1],
        summed[2],
        summed[3],
        summed[4],
        summed[5],
    )


F32 = jnp.float32
BF16 = jnp.bfloat16
VMEM_LIMIT = 58 * 1024 * 1024
NZ = 4
D = 1024
HPZ = 4
CONST = pl.Buffered(1)


def dot_nn(a, b):
    return lax.dot_general(a, b, (((1,), (0,)), ((), ())), preferred_element_type=F32)


def dot_nt(a, b):
    return lax.dot_general(a, b, (((1,), (1,)), ((), ())), preferred_element_type=F32)


def dot_tn(a, b):
    return lax.dot_general(a, b, (((0,), (0,)), ((), ())), preferred_element_type=F32)


def call(kernel, name, grid, in_specs, out_specs, out_shape, scratch, flops, nbytes):
    return pl.pallas_call(
        kernel,
        name=name,
        grid=grid,
        in_specs=in_specs,
        out_specs=out_specs,
        out_shape=out_shape,
        scratch_shapes=scratch,
        compiler_params=pltpu.CompilerParams(
            dimension_semantics=("arbitrary",) * len(grid), vmem_limit_bytes=VMEM_LIMIT
        ),
        cost_estimate=pl.CostEstimate(
            flops=flops // 4, bytes_accessed=nbytes // 4, transcendentals=0
        ),
    )


def full(shape):
    return pl.BlockSpec(shape, lambda *ids: (0,) * len(shape), pipeline_mode=CONST)


def chunk_rows(i, size):
    return pl.ds(pl.multiple_of(i * size, size), size)


def ln_stats(x):
    mean = jnp.mean(x, axis=-1, keepdims=True)
    centred = x - mean
    rstd = lax.rsqrt(jnp.mean(centred * centred, axis=-1, keepdims=True) + EPS)
    return centred * rstd, rstd


def ln_back(grad, hat, rstd, scale):
    gh = grad * (1.0 + scale)
    m1 = jnp.mean(gh, axis=-1, keepdims=True)
    m2 = jnp.mean(gh * hat, axis=-1, keepdims=True)
    return rstd * (gh - m1 - hat * m2)


def piece_specs(k, row, count):
    tail = (count, D)
    return [
        pl.BlockSpec((2, 4) + tail, lambda d: (0, 0, row, 0), pipeline_mode=CONST),
        pl.BlockSpec((4, 1) + tail, lambda d: (0, jnp.maximum(d - 1, 0), row, 0)),
        pl.BlockSpec((4, 1) + tail, lambda d: (0, jnp.maximum(d - 1, 0), row, 0)),
    ]


def by_offset(d, body, local_ref, own_ref, other_ref):
    @pl.when(d == 0)
    def _():
        body(lambda m, r, n: local_ref[0, m, r : r + n, :], lambda m, r, n: local_ref[1, m, r : r + n, :])

    @pl.when(d > 0)
    def _():
        body(lambda m, r, n: own_ref[m, 0, r : r + n, :], lambda m, r, n: other_ref[m, 0, r : r + n, :])


def head_rows(own, other, row):
    parts = []
    for m in range(4):
        parts += [own(m, row, 32), other(m, row, 32)]
    return jnp.concatenate(parts, axis=0)


def pair_rows(first, second):
    return jnp.concatenate([get(m) for get in (first, second) for m in range(4)], axis=0)


def feed_specs(down_block):
    def spec(block):
        return pl.BlockSpec((4, 1, 128, D), lambda d: (0, jnp.maximum(d - 1, 0), block, 0))

    return [full((2, 4, 256, D)), spec(0), spec(0), spec(down_block), spec(down_block)]


def feed_by_offset(d, body, l_ref, wu_ref, vu_ref, wd_ref, vd_ref):
    @pl.when(d == 0)
    def _():
        body(
            lambda: pair_rows(lambda m: l_ref[0, m, 0:128], lambda m: l_ref[1, m, 0:128]),
            lambda: pair_rows(lambda m: l_ref[0, m, 128:256], lambda m: l_ref[1, m, 128:256]),
        )

    @pl.when(d > 0)
    def _():
        body(
            lambda: pair_rows(lambda m: wu_ref[m, 0], lambda m: vu_ref[m, 0]),
            lambda: pair_rows(lambda m: wd_ref[m, 0], lambda m: vd_ref[m, 0]),
        )


def ln_qkv(hidden, mods, weights, base):
    rows = hidden.shape[0]
    step = 640

    def kernel(h_ref, m_ref, l_ref, w_ref, v_ref, normed_ref, qkv_ref):
        d = pl.program_id(0)

        @pl.when(d == 0)
        def _():
            def body(i, carry):
                sl = chunk_rows(i, step)
                hat, _ = ln_stats(h_ref[sl, :].astype(F32))
                normed_ref[sl, :] = (
                    hat * (1.0 + m_ref[base + 1 : base + 2, :]) + m_ref[base : base + 1, :]
                ).astype(BF16)
                return carry

            lax.fori_loop(0, rows // step, body, 0)

        def work(own, other):
            for t in range(3):
                qkv_ref[:, t * 256 : (t + 1) * 256] = dot_nt(
                    normed_ref[...], head_rows(own, other, t * 32)
                ).astype(BF16)

        by_offset(d, work, l_ref, w_ref, v_ref)

    return call(
        kernel,
        "ln_qkv",
        (NZ,),
        [full((rows, D)), full((12, D))] + piece_specs(128, 0, 96),
        [full((rows, D)), pl.BlockSpec((rows, 768), lambda z: (0, z))],
        [jax.ShapeDtypeStruct((rows, D), BF16), jax.ShapeDtypeStruct((rows, 3 * D), BF16)],
        [],
        2 * rows * D * 3 * D,
        rows * D * 12 + 6 * D * D,
    )(hidden, mods, *weights)


def build_bias(base_ref, bias_ref, fc_ref, slides, width, lanes_step):
    rows_step = width // slides
    for h in range(HPZ):
        for s in range(slides):
            off = (slides - 1 - s) * lanes_step
            tile = base_ref[h, :, off : off + width]
            if fc_ref is not None:
                tile = jnp.where(s < fc_ref[0], tile, NEGATIVE)
            bias_ref[h, s * rows_step : (s + 1) * rows_step, :] = tile


def window_view(values, kind):
    parts, count, size = kind[0]
    return values.reshape(parts, count, size, values.shape[-1])


def attn_fwd(qkv, base, fc, kind):
    (parts, count, size), slides, lanes_step, masked = kind
    rows, width = qkv.shape[0], parts * size
    r_step, lanes = base.shape[1], base.shape[2]

    def kernel(x_ref, b_ref, fc_ref, o_ref, bias_ref):
        build_bias(b_ref, bias_ref, fc_ref if masked else None, slides, width, lanes_step)

        def one(w, carry):
            def cut(col):
                return x_ref[:, w, :, col : col + HD].reshape(width, HD)

            scores, probs = [], []
            for h in range(HPZ):
                scores.append(dot_nt(cut(256 + h * HD), cut(h * HD) * 0.125) + bias_ref[h])
            for h in range(HPZ):
                expo = jnp.exp(scores[h] - jnp.max(scores[h], axis=0, keepdims=True))
                inv = 1.0 / jnp.sum(expo, axis=0, keepdims=True)
                probs.append((expo * inv).astype(BF16))
            for h in range(HPZ):
                got = dot_tn(probs[h], cut(512 + h * HD)).astype(BF16)
                o_ref[:, w, :, h * HD : (h + 1) * HD] = got.reshape(parts, size, HD)
            return carry

        lax.fori_loop(0, count, one, 0)

    return call(
        kernel,
        "attn_fwd",
        (NZ,),
        [
            pl.BlockSpec((parts, count, size, 768), lambda z: (0, 0, 0, z)),
            pl.BlockSpec((HPZ, r_step, lanes), lambda z: (z, 0, 0)),
            pl.BlockSpec(memory_space=pltpu.SMEM),
        ],
        pl.BlockSpec((parts, count, size, 256), lambda z: (0, 0, 0, z)),
        jax.ShapeDtypeStruct((parts, count, size, D), BF16),
        [pltpu.VMEM((HPZ, width, width), F32)],
        count * 16 * width * width * HD * 16,
        rows * D * 8,
    )(window_view(qkv, kind), base, fc).reshape(rows, D)


def attn_bwd(qkv, grad_att, base, fc, kind):
    (parts, count, size), slides, lanes_step, masked = kind
    rows, width = qkv.shape[0], parts * size
    r_step, lanes = base.shape[1], base.shape[2]

    def kernel(x_ref, d_ref, b_ref, fc_ref, o_ref, gb_ref, bias_ref, acc_ref):
        build_bias(b_ref, bias_ref, fc_ref if masked else None, slides, width, lanes_step)
        acc_ref[...] = jnp.zeros_like(acc_ref)

        def one(w, carry):
            def cut(ref, col):
                return ref[:, w, :, col : col + HD].reshape(width, HD)

            def put(col, value):
                o_ref[:, w, :, col : col + HD] = value.astype(BF16).reshape(parts, size, HD)

            q = [cut(x_ref, h * HD) * 0.125 for h in range(HPZ)]
            k = [cut(x_ref, 256 + h * HD) for h in range(HPZ)]
            da = [cut(d_ref, h * HD) for h in range(HPZ)]
            score = [dot_nt(k[h], q[h]) + bias_ref[h] for h in range(HPZ)]
            dp = [dot_nt(cut(x_ref, 512 + h * HD), da[h]) for h in range(HPZ)]
            probs, dl = [], []
            for h in range(HPZ):
                expo = jnp.exp(score[h] - jnp.max(score[h], axis=0, keepdims=True))
                inv = 1.0 / jnp.sum(expo, axis=0, keepdims=True)
                p = expo * inv
                row = jnp.sum(dp[h] * p, axis=0, keepdims=True)
                g = (p * (dp[h] - row)).astype(BF16)
                acc_ref[h] += g.astype(F32)
                probs.append(p.astype(BF16))
                dl.append(g)
            for h in range(HPZ):
                put(h * HD, dot_tn(dl[h], k[h]) * 0.125)
                put(256 + h * HD, dot_nn(dl[h], q[h]))
                put(512 + h * HD, dot_nn(probs[h], da[h]))
            return carry

        lax.fori_loop(0, count, one, 0)
        gb_ref[...] = jnp.zeros_like(gb_ref)
        for h in range(HPZ):
            for s in range(slides):
                off = (slides - 1 - s) * lanes_step
                gb_ref[h, :, off : off + width] += acc_ref[h, s * r_step : (s + 1) * r_step, :]

    xspec = pl.BlockSpec((parts, count, size, 768), lambda z: (0, 0, 0, z))
    bspec = pl.BlockSpec((HPZ, r_step, lanes), lambda z: (z, 0, 0))
    proj, strips = call(
        kernel,
        "attn_bwd",
        (NZ,),
        [
            xspec,
            pl.BlockSpec((parts, count, size, 256), lambda z: (0, 0, 0, z)),
            bspec,
            pl.BlockSpec(memory_space=pltpu.SMEM),
        ],
        [xspec, bspec],
        [
            jax.ShapeDtypeStruct((parts, count, size, 3 * D), BF16),
            jax.ShapeDtypeStruct(base.shape, F32),
        ],
        [pltpu.VMEM((HPZ, width, width), F32), pltpu.VMEM((HPZ, width, width), F32)],
        count * 16 * width * width * HD * 40,
        rows * D * 16,
    )(window_view(qkv, kind), window_view(grad_att, kind), base, fc)
    return proj.reshape(rows, 3 * D), strips


def out_specs_of(row_block):
    return [
        pl.BlockSpec((2, 4, 32, D), lambda i: (0, 0, row_block, 0), pipeline_mode=CONST),
        pl.BlockSpec((4, 3, 32, D), lambda i: (0, 0, row_block, 0), pipeline_mode=CONST),
        pl.BlockSpec((4, 3, 32, D), lambda i: (0, 0, row_block, 0), pipeline_mode=CONST),
    ]


def out_rows(d, l_ref, w_ref, v_ref):
    if d == 0:
        return head_rows(
            lambda m, r, n: l_ref[0, m, :, :], lambda m, r, n: l_ref[1, m, :, :], 0
        )
    return head_rows(
        lambda m, r, n: w_ref[m, d - 1, :, :], lambda m, r, n: v_ref[m, d - 1, :, :], 0
    )


def out_proj(attended, weights, hidden, mods, base):
    rows = attended.shape[0]
    step = 256

    def kernel(a_ref, l_ref, w_ref, v_ref, h_ref, m_ref, br_ref, mid_ref, sh_ref):
        branch = jnp.zeros((step, D), F32)
        for d in range(NZ):
            branch += dot_nn(a_ref[:, d * 256 : (d + 1) * 256], out_rows(d, l_ref, w_ref, v_ref))
        br_ref[...] = branch.astype(BF16)
        middle = h_ref[...].astype(F32) + m_ref[base + 2 : base + 3, :] * branch
        mid_ref[...] = middle
        hat, _ = ln_stats(middle)
        sh_ref[...] = (
            hat * (1.0 + m_ref[base + 4 : base + 5, :]) + m_ref[base + 3 : base + 4, :]
        ).astype(BF16)

    tile = pl.BlockSpec((step, D), lambda i: (i, 0))
    return call(
        kernel,
        "out_proj",
        (rows // step,),
        [tile] + out_specs_of(3) + [tile, full((12, D))],
        [tile, tile, tile],
        [
            jax.ShapeDtypeStruct((rows, D), BF16),
            jax.ShapeDtypeStruct((rows, D), F32),
            jax.ShapeDtypeStruct((rows, D), BF16),
        ],
        [],
        2 * rows * D * D,
        rows * D * 14 + 2 * D * D,
    )(attended, *weights, hidden, mods)


GELU_C = 0.7978845608028654
GELU_A = 0.044715


def gelu_of(x):
    return 0.5 * x * (1.0 + jnp.tanh(GELU_C * (x + GELU_A * x * x * x)))


def gelu_both(x):
    x2 = x * x
    th = jnp.tanh(GELU_C * (x + GELU_A * x * x2))
    half = 0.5 * (1.0 + th)
    slope = half + 0.5 * x * (1.0 - th * th) * (GELU_C * (1.0 + 3.0 * GELU_A * x2))
    return x * half, slope


def ffn_fwd(shifted, weights, down_block, middle, mods, base):
    rows = shifted.shape[0]
    step = 640

    def kernel(x_ref, *refs):
        parts, (mid_ref, m_ref, pre_ref, feed_ref, nx_ref, acc_ref) = refs[:5], refs[5:]
        z = pl.program_id(0)

        def work(up, down):
            def body(i, carry):
                sl = chunk_rows(i, step)
                pre = dot_nt(x_ref[sl, :], up())
                pre_ref[sl, :] = pre.astype(BF16)
                part = dot_nn(gelu_of(pre).astype(BF16), down())

                @pl.when(z == 0)
                def _():
                    acc_ref[sl, :] = part

                @pl.when((z > 0) & (z < NZ - 1))
                def _():
                    acc_ref[sl, :] += part

                @pl.when(z == NZ - 1)
                def _():
                    feed = acc_ref[sl, :] + part
                    feed_ref[sl, :] = feed.astype(BF16)
                    nx_ref[sl, :] = (
                        mid_ref[sl, :] + m_ref[base + 5 : base + 6, :] * feed
                    ).astype(BF16)

                return carry

            lax.fori_loop(0, rows // step, body, 0)

        feed_by_offset(z, work, *parts)

    return call(
        kernel,
        "ffn_fwd",
        (NZ,),
        [full((rows, D))] + feed_specs(down_block) + [full((rows, D)), full((12, D))],
        [pl.BlockSpec((rows, D), lambda z: (0, z)), full((rows, D)), full((rows, D))],
        [
            jax.ShapeDtypeStruct((rows, 4 * D), BF16),
            jax.ShapeDtypeStruct((rows, D), BF16),
            jax.ShapeDtypeStruct((rows, D), BF16),
        ],
        [pltpu.VMEM((rows, D), F32)],
        16 * rows * D * D,
        rows * D * 20 + 16 * D * D,
    )(shifted, *weights, middle, mods)


def ffn_bwd(grad, pre, shifted, weights, down_block, mods, base):
    rows = grad.shape[0]
    step = 640

    def kernel(g_ref, p_ref, x_ref, *refs):
        parts, refs = refs[:5], refs[5:]
        m_ref, keep_ref, send_ref, gs_ref, gf_ref, act_ref, gp_ref = refs
        z = pl.program_id(0)

        @pl.when(z == 0)
        def _():
            def body(i, carry):
                sl = chunk_rows(i, step)
                gf_ref[sl, :] = (
                    g_ref[sl, :].astype(F32) * m_ref[base + 5 : base + 6, :]
                ).astype(BF16)
                gs_ref[sl, :] = jnp.zeros((step, D), F32)
                return carry

            lax.fori_loop(0, rows // step, body, 0)

        def work(up, down):
            def body(i, carry):
                sl = chunk_rows(i, step)
                back = dot_nt(gf_ref[sl, :], down())
                act, slope = gelu_both(p_ref[sl, :].astype(F32))
                act_ref[sl, :] = act.astype(BF16)
                gpre = (back * slope).astype(BF16)
                gp_ref[sl, :] = gpre
                part = dot_nn(gpre, up())
                gs_ref[sl, :] += part
                return carry

            lax.fori_loop(0, rows // step, body, 0)

        feed_by_offset(z, work, *parts)
        for j, out_ref in enumerate((keep_ref, send_ref)):
            cols = slice(j * 512, (j + 1) * 512)
            gd = dot_tn(act_ref[:, cols], gf_ref[...]).astype(BF16)
            gu = dot_tn(gp_ref[:, cols], x_ref[...]).astype(BF16)
            out_ref[:, 0, 0:128] = gu.reshape(4, 128, D)
            out_ref[:, 0, 128:256] = gd.reshape(4, 128, D)

    gspec = pl.BlockSpec((4, 1, 256, D), lambda z: (0, z, 0, 0))
    gshape = jax.ShapeDtypeStruct((4, NZ, 256, D), BF16)
    return call(
        kernel,
        "ffn_bwd",
        (NZ,),
        [
            full((rows, D)),
            pl.BlockSpec((rows, D), lambda z: (0, z)),
            full((rows, D)),
        ]
        + feed_specs(down_block)
        + [full((12, D))],
        [gspec, gspec, full((rows, D))],
        [gshape, gshape, jax.ShapeDtypeStruct((rows, D), F32)],
        [pltpu.VMEM((rows, D), BF16)] * 3,
        32 * rows * D * D,
        rows * D * 16 + 32 * D * D,
    )(grad, pre, shifted, *weights, mods)


def split_heads(value, keep_ref, send_ref, d, row):
    for m in range(4):
        keep_ref[m, d, row : row + 32] = value[m * 64 : m * 64 + 32]
        send_ref[m, d, row : row + 32] = value[m * 64 + 32 : m * 64 + 64]


def out_bwd(grad, grad_shifted, middle, feed, branch, attended, weights, mods, base):
    rows = grad.shape[0]
    step = 256
    steps = rows // step

    def kernel(
        g_ref, gs_ref, mid_ref, f_ref, b_ref, a_ref, l_ref, w_ref, v_ref, m_ref, gm_ref, ga_ref,
        keep_ref, send_ref, s_ref, gb_ref,
    ):
        i = pl.program_id(0)

        @pl.when(i == 0)
        def _():
            s_ref[...] = jnp.zeros_like(s_ref)

        g = g_ref[...].astype(F32)
        gs = gs_ref[...]
        hat, rstd = ln_stats(mid_ref[...])
        gm = g + ln_back(gs, hat, rstd, m_ref[base + 4 : base + 5, :])
        gm_ref[...] = gm
        s_ref[0:1, :] += jnp.sum(gs, axis=0, keepdims=True)
        s_ref[1:2, :] += jnp.sum(gs * hat, axis=0, keepdims=True)
        s_ref[2:3, :] += jnp.sum(gm * b_ref[...].astype(F32), axis=0, keepdims=True)
        s_ref[3:4, :] += jnp.sum(g * f_ref[...].astype(F32), axis=0, keepdims=True)
        gb = (gm * m_ref[base + 2 : base + 3, :]).astype(BF16)
        gb_ref[chunk_rows(i, step), :] = gb
        for d in range(NZ):
            ga_ref[:, d * 256 : (d + 1) * 256] = dot_nt(
                gb, out_rows(d, l_ref, w_ref, v_ref)
            ).astype(BF16)

        @pl.when(i == steps - 1)
        def _():
            for d in range(NZ):
                gw = dot_tn(a_ref[:, d * 256 : (d + 1) * 256], gb_ref[...]).astype(BF16)
                split_heads(gw, keep_ref, send_ref, d, 0)

    tile = pl.BlockSpec((step, D), lambda i: (i, 0))
    gshape = jax.ShapeDtypeStruct((4, NZ, 32, D), BF16)
    return call(
        kernel,
        "out_bwd",
        (steps,),
        [tile, tile, tile, tile, tile, full((rows, D))] + out_specs_of(3) + [full((12, D))],
        [tile, tile, full(gshape.shape), full(gshape.shape), full((8, D))],
        [
            jax.ShapeDtypeStruct((rows, D), F32),
            jax.ShapeDtypeStruct((rows, D), BF16),
            gshape,
            gshape,
            jax.ShapeDtypeStruct((8, D), F32),
        ],
        [pltpu.VMEM((rows, D), BF16)],
        4 * rows * D * D,
        rows * D * 24 + 4 * D * D,
    )(grad, grad_shifted, middle, feed, branch, attended, *weights, mods)


def qkv_back(grad_proj, weights, hidden, grad_middle, mods, base, out_dtype, pieces):
    rows = hidden.shape[0]
    step = 640

    cols = D // pieces

    def kernel(p_ref, l_ref, w_ref, v_ref, h_ref, gm_ref, m_ref, *refs):
        gh_refs, (s_ref, acc_ref) = refs[:pieces], refs[pieces:]
        z = pl.program_id(0)

        @pl.when(z == 0)
        def _():
            acc_ref[...] = jnp.zeros_like(acc_ref)
            s_ref[...] = jnp.zeros_like(s_ref)

        def work(own, other):
            def body(i, carry):
                sl = chunk_rows(i, step)
                rows_of = jnp.concatenate([head_rows(own, other, t * 32) for t in range(3)], axis=0)
                acc_ref[sl, :] += dot_nn(p_ref[sl, :], rows_of)
                return carry

            lax.fori_loop(0, rows // step, body, 0)

        by_offset(z, work, l_ref, w_ref, v_ref)

        @pl.when(z == NZ - 1)
        def _():
            def tail(n, carry):
                sl = chunk_rows(n, 256)
                gn = acc_ref[sl, :]
                hat, rstd = ln_stats(h_ref[sl, :].astype(F32))
                gh = gm_ref[sl, :] + ln_back(gn, hat, rstd, m_ref[base + 1 : base + 2, :])
                for i, gh_ref in enumerate(gh_refs):
                    gh_ref[sl, :] = gh[:, i * cols : (i + 1) * cols].astype(out_dtype)
                s_ref[0:1, :] += jnp.sum(gn, axis=0, keepdims=True)
                s_ref[1:2, :] += jnp.sum(gn * hat, axis=0, keepdims=True)
                return carry

            lax.fori_loop(0, rows // 256, tail, 0)

    return call(
        kernel,
        "qkv_back",
        (NZ,),
        [pl.BlockSpec((rows, 768), lambda z: (0, z))]
        + piece_specs(128, 0, 96)
        + [full((rows, D)), full((rows, D)), full((12, D))],
        [full((rows, cols))] * pieces + [full((8, D))],
        [jax.ShapeDtypeStruct((rows, cols), out_dtype)] * pieces
        + [jax.ShapeDtypeStruct((8, D), F32)],
        [pltpu.VMEM((rows, D), F32)],
        6 * rows * D * D,
        rows * D * 20 + 6 * D * D,
    )(grad_proj, *weights, hidden, grad_middle, mods)


def qkv_grad(grad_proj, normed, out_keep, out_send, table_rows):
    rows = normed.shape[0]
    k = 128 if table_rows is None else 144

    def kernel(p_ref, n_ref, ok_ref, os_ref, *rest):
        keep_ref, send_ref = rest[-2:]
        for t in range(3):
            gw = dot_tn(p_ref[:, t * 256 : (t + 1) * 256], n_ref[...]).astype(BF16)
            split_heads(gw, keep_ref, send_ref, 0, t * 32)
        keep_ref[:, :, 96:128] = ok_ref[...]
        send_ref[:, :, 96:128] = os_ref[...]
        if table_rows is not None:
            keep_ref[:, :, 128:144] = rest[0][...]
            send_ref[:, :, 128:144] = rest[0][...]

    gspec = pl.BlockSpec((4, 1, k, D), lambda z: (0, z, 0, 0))
    ospec = pl.BlockSpec((4, 1, 32, D), lambda z: (0, z, 0, 0))
    tspec = pl.BlockSpec((4, 1, 16, D), lambda z: (0, z, 0, 0))
    gshape = jax.ShapeDtypeStruct((4, NZ, k, D), BF16)
    extra = () if table_rows is None else (table_rows,)
    return call(
        kernel,
        "qkv_grad",
        (NZ,),
        [pl.BlockSpec((rows, 768), lambda z: (0, z)), full((rows, D)), ospec, ospec]
        + [tspec] * len(extra),
        [gspec, gspec],
        [gshape, gshape],
        [],
        6 * rows * D * D,
        rows * D * 8 + 8 * D * D,
    )(grad_proj, normed, out_keep, out_send, *extra)


def place_call(kernel, name, in_specs, out_specs, out_shape, scratch, nbytes, aliases):
    return pl.pallas_call(
        kernel,
        name=name,
        grid_spec=pltpu.PrefetchScalarGridSpec(
            num_scalar_prefetch=1,
            grid=(8,),
            in_specs=in_specs,
            out_specs=out_specs,
            scratch_shapes=scratch,
        ),
        out_shape=out_shape,
        input_output_aliases=aliases,
        compiler_params=pltpu.CompilerParams(
            dimension_semantics=("arbitrary",), vmem_limit_bytes=VMEM_LIMIT
        ),
        cost_estimate=pl.CostEstimate(flops=0, bytes_accessed=nbytes, transcendentals=0),
    )


def rows_at(place):
    return pl.ds(pl.multiple_of(place * 32, 32), 32)


def prep_attn(place, w_qkv, w_out, b):
    def kernel(c_ref, q_ref, o_ref, out_ref, t_ref):
        r = pl.program_id(0)

        @pl.when(r == 0)
        def _():
            for t in range(3):
                t_ref[t] = q_ref[0, t].T

        at = rows_at(c_ref[0] ^ r)
        for t in range(3):
            out_ref[0, 0, t * 32 : (t + 1) * 32, :] = t_ref[t, at, :]
        out_ref[0, 0, 96:128, :] = o_ref[0, at, :]

    return place_call(
        kernel,
        "prep_attn",
        [
            pl.BlockSpec((1, 3, D, 256), lambda r, c: (b, 0, 0, 0)),
            pl.BlockSpec((1, 256, D), lambda r, c: (b, 0, 0)),
        ],
        pl.BlockSpec((1, 1, 128, D), lambda r, c: (r % 2, r // 2, 0, 0)),
        jax.ShapeDtypeStruct((2, 4, 128, D), BF16),
        [pltpu.VMEM((3, 256, D), BF16)],
        4 * D * D,
        {},
    )(place, w_qkv, w_out)


def prep_feed(place, w_up, w_down, b):
    def kernel(c_ref, u_ref, d_ref, out_ref):
        out_ref[0, 0, 0:128, :] = u_ref[0].T
        out_ref[0, 0, 128:256, :] = d_ref[0]

    return place_call(
        kernel,
        "prep_feed",
        [
            pl.BlockSpec((1, D, 128), lambda r, c: (b, 0, c[0] ^ r)),
            pl.BlockSpec((1, 128, D), lambda r, c: (b, c[0] ^ r, 0)),
        ],
        pl.BlockSpec((1, 1, 256, D), lambda r, c: (r % 2, r // 2, 0, 0)),
        jax.ShapeDtypeStruct((2, 4, 256, D), BF16),
        [],
        8 * D * D,
        {},
    )(place, w_up, w_down)


def finish_attn(place, own, other):
    def kernel(c_ref, own_ref, oth_ref, gq_ref, go_ref, t_ref):
        r = pl.program_id(0)
        at = rows_at(c_ref[0] ^ r)

        def store(ref):
            for b in range(2):
                row = 128 * b
                for t in range(3):
                    t_ref[b, t, at, :] = ref[0, row + t * 32 : row + (t + 1) * 32, :]
                go_ref[b, at, :] = ref[0, row + 96 : row + 128, :].astype(F32)

        @pl.when(r % 2 == 0)
        def _():
            store(own_ref)

        @pl.when(r % 2 == 1)
        def _():
            store(oth_ref)

        @pl.when(r == 7)
        def _():
            for b in range(2):
                for t in range(3):
                    gq_ref[b, t] = t_ref[b, t].T.astype(F32)

    piece = pl.BlockSpec((1, 256, D), lambda r, c: (r // 2, 0, 0))
    return place_call(
        kernel,
        "finish_attn",
        [piece, piece],
        [
            pl.BlockSpec((2, 3, D, 256), lambda r, c: (0, 0, 0, 0), pipeline_mode=CONST),
            pl.BlockSpec((2, 256, D), lambda r, c: (0, 0, 0), pipeline_mode=CONST),
        ],
        [
            jax.ShapeDtypeStruct((2, 3, D, 256), F32),
            jax.ShapeDtypeStruct((2, 256, D), F32),
        ],
        [pltpu.VMEM((2, 3, 256, D), BF16)],
        12 * D * D,
        {},
    )(place, own, other)


def finish_feed(place, own, other, b, earlier):
    def kernel(c_ref, own_ref, oth_ref, *rest):
        gu_ref, gd_ref = rest[-2:]
        r = pl.program_id(0)

        def store(ref):
            gu_ref[0] = ref[0, 0:128, :].T.astype(F32)
            gd_ref[0] = ref[0, 128:256, :].astype(F32)

        @pl.when(r % 2 == 0)
        def _():
            store(own_ref)

        @pl.when(r % 2 == 1)
        def _():
            store(oth_ref)

    piece = pl.BlockSpec((1, 256, D), lambda r, c: (r // 2, 0, 0))
    anywhere = pl.BlockSpec(memory_space=pl.ANY)
    return place_call(
        kernel,
        "finish_feed",
        [piece, piece] + [anywhere] * len(earlier),
        [
            pl.BlockSpec((1, D, 128), lambda r, c: (b, 0, c[0] ^ r)),
            pl.BlockSpec((1, 128, D), lambda r, c: (b, c[0] ^ r, 0)),
        ],
        [jax.ShapeDtypeStruct((2, D, D), F32), jax.ShapeDtypeStruct((2, D, D), F32)],
        [],
        12 * D * D,
        {3 + i: i for i in range(len(earlier))},
    )(place, own, other, *earlier)


def partner(values):
    return lax.ppermute(values, "head", [(i, i ^ 1) for i in range(NZ)])


def rows_to_spatial(rows, odd):
    cols = rows.shape[1]
    whole = lax.dynamic_slice(rows, (256 * odd, 0), (1024, cols))
    part = lax.dynamic_slice(rows, (1024 * (1 - odd), 0), (256, cols)).reshape(8, 2, 16, cols)
    wins = whole.reshape(2, 16, 2, 16, cols).transpose(0, 2, 1, 3, 4).reshape(1024, cols)
    left, right = part[:, 0].reshape(128, cols), part[:, 1].reshape(128, cols)
    keep = jnp.where(odd == 0, left, right)
    got = partner(jnp.where(odd == 0, right, left))
    top, bottom = jnp.where(odd == 0, keep, got), jnp.where(odd == 0, got, keep)
    part = jnp.concatenate([top, bottom], axis=0)
    return jnp.where(
        odd == 0,
        jnp.concatenate([wins, part], axis=0),
        jnp.concatenate([part, wins], axis=0),
    )


def spatial_to_rows(wins, odd):
    cols = wins.shape[1]
    whole = lax.dynamic_slice(wins, (256 * odd, 0), (1024, cols))
    part = lax.dynamic_slice(wins, (1024 * (1 - odd), 0), (256, cols))
    whole = whole.reshape(2, 2, 16, 16, cols).transpose(0, 2, 1, 3, 4).reshape(1024, cols)
    keep = jnp.where(odd == 0, part[:128], part[128:])
    got = partner(jnp.where(odd == 0, part[128:], part[:128]))
    left, right = jnp.where(odd == 0, keep, got), jnp.where(odd == 0, got, keep)
    part = jnp.stack([left.reshape(8, 16, cols), right.reshape(8, 16, cols)], axis=1)
    part = part.reshape(256, cols)
    return jnp.where(
        odd == 0,
        jnp.concatenate([whole, part], axis=0),
        jnp.concatenate([part, whole], axis=0),
    )


def exchange(values):
    return lax.all_to_all(values, "head", 0, 0, tiled=True)


def spatial_to_tubes(wins):
    cols = wins.shape[1]
    return exchange(
        wins.reshape(5, 2, 8, 2, 8, cols).transpose(1, 3, 0, 2, 4, 5).reshape(1280, cols)
    )


def from_quads(quads):
    cols = quads.shape[1]
    return quads.reshape(2, 2, 5, 8, 8, cols).transpose(2, 0, 3, 1, 4, 5).reshape(1280, cols)


def toeplitz(side):
    span = 2 * side - 1
    b = lax.broadcasted_iota(jnp.int32, (span, side, side), 0)
    j = lax.broadcasted_iota(jnp.int32, (span, side, side), 1)
    i = lax.broadcasted_iota(jnp.int32, (span, side, side), 2)
    return (b == i - j + side - 1).astype(F32)


def toeplitz_pair(side):
    span = 2 * side - 1
    shape = (span * span, side * side, side * side)
    r = lax.broadcasted_iota(jnp.int32, shape, 0)
    j = lax.broadcasted_iota(jnp.int32, shape, 1)
    i = lax.broadcasted_iota(jnp.int32, shape, 2)
    dy = i // side - j // side + side - 1
    dx = i % side - j % side + side - 1
    return (r == dy * span + dx).astype(F32)


CORE, ROW_X, ROW_Y = 1, 2, 4


def swap(values, bit):
    return lax.ppermute(values, "clip", [(i, i ^ bit) for i in range(8)])


def from_z(values, d):
    return lax.ppermute(values, "head", [((i + d) % NZ, i) for i in range(NZ)])


def sync(*values):
    return lax.optimization_barrier(values)


def add(first, second):
    return (first.astype(F32) + second.astype(F32)).astype(BF16)


def line_stage(piece):
    return [from_z(piece, d) for d in (1, 2, 3)]


def others(by_z, z):
    return [lax.dynamic_index_in_dim(by_z, (z + d) % NZ, 0, keepdims=False) for d in (1, 2, 3)]


def cross_stage(own):
    return [own] + [swap(own, m * 2) for m in (1, 2, 3)]


def sides_stage(own):
    return [own, swap(own, ROW_X), swap(own, ROW_Y)]


def corner_stage(sides):
    half = sides[0].shape[1] // 2
    return [swap(sides[1][:, :half], ROW_Y), swap(sides[2][:, half:], ROW_X)]


def joined(sides, corner):
    return jnp.stack(sides + [jnp.concatenate(corner, axis=1)])


def sum_core(keep, got):
    return [add(keep[m], got[m]) for m in range(4)]


def send_plane(totals, offsets):
    return [swap(totals[m], m * 2) for m in offsets]


def to_places(total, z):
    twice = jnp.concatenate([total, total[: NZ - 1]], axis=0)
    return lax.dynamic_slice_in_dim(twice, (NZ - z) % NZ, NZ, axis=0)


def sum_plane(totals, got, z):
    total = totals[0].astype(F32)
    for value in got:
        total = total + value.astype(F32)
    return to_places(total.astype(BF16), z)


def send_cross(totals):
    half = totals[0].shape[1] // 2
    first = [t[:, :half] for t in totals]
    second = [t[:, half:] for t in totals]
    by_x = swap(jnp.stack([first[1], first[3]]), ROW_X)
    by_y = swap(jnp.stack([second[2], second[3]]), ROW_Y)
    return by_x, by_y


def sum_cross(totals, got):
    half = totals[0].shape[1] // 2
    by_x, by_y = got
    first = [add(totals[0][:, :half], by_x[0]), add(totals[2][:, :half], by_x[1])]
    second = [add(totals[0][:, half:], by_y[0]), add(totals[1][:, half:], by_y[1])]
    return first, second


def send_corner(halves):
    return swap(halves[0][1], ROW_Y), swap(halves[1][1], ROW_X)


def sum_corner(halves, got, z):
    first = add(halves[0][0], got[0])
    second = add(halves[1][0], got[1])
    return to_places(jnp.concatenate([first, second], axis=1), z)


def sum_line(by_z):
    return lax.psum_scatter(by_z, "head", scatter_dimension=0)


def on_device_windows(
    tokens, d_out, modulation, frame_counts, w_qkv, w_out, w_up, w_down, table_s, table_t
):
    z = lax.axis_index("head")
    c = lax.axis_index("clip")
    place = c.astype(jnp.int32).reshape(1)
    chip = c // 2
    odd = z % 2
    mods = modulation[0]
    n_s, n_t = table_s.shape[1], table_t.shape[1]
    hot_s, hot_t = toeplitz(SWIN), toeplitz_pair(TWIN)
    fc = frame_counts

    def spatial_base(tables):
        base = jnp.einsum(
            "hab,bji->hjai", tables[:, :n_s].reshape(16, 31, 31), hot_s, precision=HIGHEST_PRECISION
        ).reshape(16, 16, 496)
        return jnp.pad(base, ((0, 0), (0, 0), (0, 16)))

    def tube_base(tables):
        base = jnp.einsum(
            "htr,rjk->hjtk", tables[:, n_s:].reshape(16, 9, 225), hot_t, precision=HIGHEST_PRECISION
        ).reshape(16, 64, 576)
        return jnp.pad(base, ((0, 0), (0, 0), (0, 64)))

    def table_rows(first, second):
        first = jnp.pad(first, ((0, 0), (0, D - n_s)))
        second = jnp.pad(second, ((0, 0), (0, 15 * D - n_t)))
        values = jnp.concatenate([first, second], axis=1).astype(BF16)
        return values.reshape(NZ, 4, 16, D).transpose(1, 0, 2, 3)

    spatial = ((1, 5, 256), 16, 16, False)
    tube = ((5, 4, 64), 5, 64, True)

    local_a0 = prep_attn(place, w_qkv, w_out, 0)
    line_a0 = line_stage(local_a0[0, 0])
    table_piece = jnp.concatenate([table_s, table_t], axis=1)
    tables = [from_z(table_piece, d) for d in (1, 2)]
    local_f0 = prep_feed(place, w_up, w_down, 0)
    local_a1 = prep_attn(place, w_qkv, w_out, 1)
    local_f1 = prep_feed(place, w_up, w_down, 1)
    line_a0, local_f0, local_a1, local_f1, tables, tokens, table_piece = sync(
        line_a0, local_f0, local_a1, local_f1, tables, tokens, table_piece
    )
    own_a0 = cross_stage(jnp.stack(line_a0))
    z_u0 = lax.all_gather(local_f0[0, 0, :128], "head")
    z_d0 = lax.all_gather(local_f0[0, 0, 128:], "head")
    tables = jnp.stack([table_piece] + tables + [from_z(table_piece, 3)])
    tables = jnp.concatenate(
        [lax.dynamic_slice_in_dim(tables, chip ^ m, 1, axis=1) for m in range(4)], axis=1
    ).reshape(16, n_s + n_t)
    base_s = spatial_base(tables)
    hidden0 = rows_to_spatial(tokens, odd)
    own_a0, hidden0, tables, base_s, z_u0 = sync(own_a0, hidden0, tables, base_s, z_u0)
    own_a0 = jnp.stack(own_a0)
    other_a0 = swap(own_a0, CORE)
    own_u0 = sides_stage(jnp.stack(others(z_u0, z)))
    own_a0, other_a0 = sync(own_a0, other_a0)
    weights_a0 = (local_a0, own_a0, other_a0)
    normed0, qkv0 = ln_qkv(hidden0, mods, weights_a0, 0)
    qkv0, own_u0, z_d0 = sync(qkv0, own_u0, z_d0)
    corner_u0 = corner_stage(own_u0)
    own_d0 = sides_stage(jnp.stack(others(z_d0, z)))
    z_a1 = lax.all_gather(local_a1[0, 0], "head")
    attended0 = attn_fwd(qkv0, base_s, fc, spatial)
    attended0, corner_u0, own_d0, z_a1 = sync(attended0, corner_u0, own_d0, z_a1)
    corner_d0 = corner_stage(own_d0)
    own_u0 = joined(own_u0, corner_u0)
    other_u0 = swap(own_u0, CORE)
    branch0, middle0, shifted0 = out_proj(attended0, weights_a0, hidden0, mods, 0)
    own_a1 = jnp.stack(others(z_a1, z))
    shifted0, corner_d0, other_u0, own_a1 = sync(shifted0, corner_d0, other_u0, own_a1)
    own_d0 = joined(own_d0, corner_d0)
    other_d0 = swap(own_d0, CORE)
    z_f1 = lax.all_gather(local_f1[0, 0], "head")
    shifted0, other_d0 = sync(shifted0, other_d0)
    own_a1 = cross_stage(own_a1)
    weights_f0 = (local_f0, own_u0, other_u0, own_d0, other_d0)
    pre0, feed0, hidden1 = ffn_fwd(shifted0, weights_f0, 0, middle0, mods, 0)
    hidden1, z_f1, own_a1, tables, d_out = sync(hidden1, z_f1, own_a1, tables, d_out)
    tubes1 = spatial_to_tubes(hidden1)
    own_a1 = jnp.stack(own_a1)
    other_a1 = swap(own_a1, CORE)
    own_f1 = cross_stage(jnp.stack(others(z_f1, z)))
    base_t = tube_base(tables)
    spatial_d = rows_to_spatial(d_out, odd)
    tubes1, other_a1, base_t, spatial_d = sync(tubes1, other_a1, base_t, spatial_d)
    weights_a1 = (local_a1, own_a1, other_a1)
    tubes_d = spatial_to_tubes(spatial_d)
    normed1, qkv1 = ln_qkv(tubes1, mods, weights_a1, 6)
    qkv1, own_f1 = sync(qkv1, own_f1)
    own_f1 = jnp.stack(own_f1)
    other_f1 = swap(own_f1, CORE)
    attended1 = attn_fwd(qkv1, base_t, fc, tube)
    branch1, middle1, shifted1 = out_proj(attended1, weights_a1, tubes1, mods, 6)
    shifted1, other_f1 = sync(shifted1, other_f1)
    weights_f1 = (local_f1, own_f1, other_f1, own_f1, other_f1)
    pre1, feed1, hidden2 = ffn_fwd(shifted1, weights_f1, 1, middle1, mods, 6)
    hidden2, tubes_d = sync(hidden2, tubes_d)
    live = lax.broadcasted_iota(jnp.int32, (1280, 1), 0) // 256 < fc[0]
    grad2 = jnp.where(live, tubes_d, 0)
    out_wins = exchange(jnp.where(live, hidden2, 0))
    f1_keep, f1_send, g_shift1 = ffn_bwd(grad2, pre1, shifted1, weights_f1, 1, mods, 6)
    f1_keep, f1_send, g_shift1, out_wins = sync(f1_keep, f1_send, g_shift1, out_wins)
    f1_got = swap(f1_send, CORE)
    g_mid1, g_att1, o1_keep, o1_send, sums_o1 = out_bwd(
        grad2, g_shift1, middle1, feed1, branch1, attended1, weights_a1, mods, 6
    )
    g_att1, f1_got = sync(g_att1, f1_got)
    total_f1 = sum_core(f1_keep, f1_got)
    g_att1, total_f1 = sync(g_att1, total_f1)
    got_f1 = send_cross(total_f1)
    g_proj1, g_base1 = attn_bwd(qkv1, g_att1, base_t, fc, tube)
    g_proj1, g_base1, got_f1 = sync(g_proj1, g_base1, got_f1)
    half_f1 = sum_cross(total_f1, got_f1)
    half_f1, g_proj1 = sync(half_f1, g_proj1)
    got_f1 = send_corner(half_f1)
    g_hid1a, g_hid1b, sums_q1 = qkv_back(
        g_proj1, weights_a1, tubes1, g_mid1, mods, 6, BF16, 2
    )
    g_hid1a, g_hid1b, g_proj1, out_wins, g_base1, got_f1 = sync(
        g_hid1a, g_hid1b, g_proj1, out_wins, g_base1, got_f1
    )
    grad1a = exchange(g_hid1a)
    z_f1 = sum_corner(half_f1, got_f1, z)
    a1_keep, a1_send = qkv_grad(g_proj1, normed1, o1_keep, o1_send, None)
    gt_t = jnp.einsum(
        "hjtk,rjk->htr",
        g_base1[:, :, :576].reshape(16, 64, 9, 64),
        hot_t,
        precision=HIGHEST_PRECISION,
    ).reshape(16, n_t)
    grad1a, z_f1, a1_keep, a1_send, gt_t, g_hid1b, out_wins = sync(
        grad1a, z_f1, a1_keep, a1_send, gt_t, g_hid1b, out_wins
    )
    grad1b = exchange(g_hid1b)
    total_a1 = sum_core(a1_keep, swap(a1_send, CORE))
    output = spatial_to_rows(from_quads(out_wins), odd)
    grad1b, total_a1, output, z_f1 = sync(grad1b, total_a1, output, z_f1)
    grad1 = from_quads(jnp.concatenate([grad1a, grad1b], axis=1))
    mine_f1 = sum_line(z_f1)
    got_a1 = send_plane(total_a1, (1, 2, 3))
    f0_keep, f0_send, g_shift0 = ffn_bwd(grad1, pre0, shifted0, weights_f0, 0, mods, 0)
    f0_keep, f0_send, g_shift0, mine_f1, got_a1 = sync(f0_keep, f0_send, g_shift0, mine_f1, got_a1)
    f0_got = swap(f0_send, CORE)
    mine_a1 = sum_line(sum_plane(total_a1, got_a1, z))
    g_mid0, g_att0, o0_keep, o0_send, sums_o0 = out_bwd(
        grad1, g_shift0, middle0, feed0, branch0, attended0, weights_a0, mods, 0
    )
    g_att0, f0_got = sync(g_att0, f0_got)
    total_f0 = sum_core(f0_keep, f0_got)
    g_att0, total_f0 = sync(g_att0, total_f0)
    got_f0 = send_cross(total_f0)
    g_proj0, g_base0 = attn_bwd(qkv0, g_att0, base_s, fc, spatial)
    gt_s = jnp.einsum(
        "hjai,bji->hab",
        g_base0[:, :, :496].reshape(16, 16, 31, 16),
        hot_s,
        precision=HIGHEST_PRECISION,
    ).reshape(16, n_s)
    a0_keep, a0_send = qkv_grad(g_proj0, normed0, o0_keep, o0_send, table_rows(gt_s, gt_t))
    a0_keep, a0_send, got_f0, mine_a1, g_proj0 = sync(a0_keep, a0_send, got_f0, mine_a1, g_proj0)
    a0_got = swap(a0_send, CORE)
    half_f0 = sum_cross(total_f0, got_f0)
    got_f0 = send_corner(half_f0)
    half_f0, got_f0, a0_got, g_proj0 = sync(half_f0, got_f0, a0_got, g_proj0)
    z_f0 = sum_corner(half_f0, got_f0, z)
    total_a0 = sum_core(a0_keep, a0_got)
    total_a0, z_f0, g_proj0 = sync(total_a0, z_f0, g_proj0)
    mine_f0 = sum_line(z_f0)
    got_a0 = send_cross(total_a0)
    grad0, sums_q0 = qkv_back(g_proj0, weights_a0, hidden0, g_mid0, mods, 0, F32, 1)
    grad0, sums_q0, got_a0 = sync(grad0, sums_q0, got_a0)
    half_a0 = sum_cross(total_a0, got_a0)
    half_a0, grad0, sums_q0 = sync(half_a0, grad0, sums_q0)
    got_a0 = send_corner(half_a0)
    own_gf1 = cross_stage(mine_f1)
    got_a0, own_gf1, mine_f0 = sync(got_a0, own_gf1, mine_f0)
    mine_a0 = sum_line(sum_corner(half_a0, got_a0, z))
    own_gf0 = cross_stage(mine_f0)
    own_gf1 = jnp.stack(own_gf1)
    other_gf1 = swap(own_gf1, CORE)
    grad_tokens = spatial_to_rows(grad0, odd)
    mod_rows = jnp.concatenate(
        [
            sums_q0[0:2], sums_o0[2:3], sums_o0[0:2], sums_o0[3:4],
            sums_q1[0:2], sums_o1[2:3], sums_o1[0:2], sums_o1[3:4],
        ],
        axis=0,
    )
    mine_a0, own_gf0, other_gf1, grad_tokens = sync(mine_a0, own_gf0, other_gf1, grad_tokens)
    mine_a = jnp.concatenate([mine_a0[:128], mine_a1, mine_a0[128:]], axis=0)
    own_ga = cross_stage(mine_a)
    own_gf0 = jnp.stack(own_gf0)
    other_gf0 = swap(own_gf0, CORE)
    mod_got = [from_z(mod_rows, 1)]
    g_feed = finish_feed(place, own_gf1, other_gf1, 1, ())
    own_ga, other_gf0, g_feed, mod_got = sync(own_ga, other_gf0, g_feed, mod_got)
    own_ga = jnp.stack(own_ga)
    other_ga = swap(own_ga, CORE)
    mod_got = mod_got + [from_z(mod_rows, 2), from_z(mod_rows, 3)]
    g_feed = finish_feed(place, own_gf0, other_gf0, 0, g_feed)
    own_ga, other_ga, g_feed, mod_got = sync(own_ga, other_ga, g_feed, mod_got)
    own_ga0 = own_ga
    g_attn = finish_attn(place, own_ga, other_ga)
    tab = jnp.concatenate(
        [lax.dynamic_slice_in_dim(own_ga0, chip ^ m, 1, axis=0) for m in range(4)], axis=0
    )
    tab = tab[:, 256:272].reshape(4, 16 * D).astype(F32)
    return (
        output,
        grad_tokens,
        (mod_rows + mod_got[0] + mod_got[1] + mod_got[2])[None],
        g_attn[0],
        g_attn[1],
        g_feed[0],
        g_feed[1],
        tab[:, :n_s],
        tab[:, D : D + n_t],
    )


def solution(mesh):
    if mesh.shape["head"] == NZ and mesh.shape["clip"] == 8:
        body = on_device_windows
    else:
        body = on_device
    return jax.shard_map(
        body,
        mesh=mesh,
        in_specs=(
            P(("clip", "head"), None),
            P(("clip", "head"), None),
            P("clip", None, None),
            P("clip"),
            P(None, None, None, "head"),
            P(None, "head", None),
            P(None, None, "head"),
            P(None, "head", None),
            P("head", None),
            P("head", None),
        ),
        out_specs=(
            P(("clip", "head"), None),
            P(("clip", "head"), None),
            P("clip", None, None),
            P(None, None, None, "head"),
            P(None, "head", None),
            P(None, None, "head"),
            P(None, "head", None),
            P("head", None),
            P("head", None),
        ),
        check_vma=False,
    )
```

```python
import jax
import jax.numpy as jnp
from jax import lax
from jax.experimental import pallas as pl
from jax.experimental.pallas import tpu as pltpu
from jax.sharding import PartitionSpec as P

HD = 64
FH = 32
FW = 32
SWIN = 16
TWIN = 8
PADF = 5


EPS = 1e-06
HIGHEST_PRECISION = lax.Precision.HIGHEST
NEGATIVE = -1e30


def layer_norm(values, shift_row, scale_row):
    average = jnp.mean(values, axis=-1, keepdims=True)
    centred = values - average
    spread = jnp.mean(centred * centred, axis=-1, keepdims=True)
    return centred * lax.rsqrt(spread + EPS) * (1.0 + scale_row) + shift_row


def gelu_tanh(values):
    return jax.nn.gelu(values, approximate=True)


def window_index(side_t, side_len):
    window_size = side_t * side_len * side_len
    places = jnp.arange(window_size, dtype=jnp.int32)
    time_pos = places // (side_len * side_len)
    height_pos = places // side_len % side_len
    width_pos = places % side_len
    span_len = 2 * side_len - 1
    return (
        (time_pos[:, None] - time_pos[None, :] + side_t - 1) * span_len * span_len
        + (height_pos[:, None] - height_pos[None, :] + side_len - 1) * span_len
        + (width_pos[:, None] - width_pos[None, :] + side_len - 1)
    )


def to_windows(values, side_t, side_len):
    tail_shape = values.shape[1:]
    frames = values.shape[0] // (FH * FW)
    shaped = values.reshape(
        (frames // side_t, side_t, FH // side_len, side_len, FW // side_len, side_len) + tail_shape
    )
    axis_order = (0, 2, 4, 1, 3, 5) + tuple(range(6, 6 + len(tail_shape)))
    shaped = shaped.transpose(axis_order)
    return shaped.reshape((-1, side_t * side_len * side_len) + tail_shape)


def from_windows(values, side_t, side_len):
    tail_shape = values.shape[2:]
    blocks_high = FH // side_len
    blocks_wide = FW // side_len
    frame_groups = values.shape[0] // (blocks_high * blocks_wide)
    shaped = values.reshape(
        (frame_groups, blocks_high, blocks_wide, side_t, side_len, side_len) + tail_shape
    )
    axis_order = (0, 3, 1, 4, 2, 5) + tuple(range(6, 6 + len(tail_shape)))
    return shaped.transpose(axis_order).reshape((frame_groups * side_t * FH * FW,) + tail_shape)


def on_device(
    tokens, d_out, modulation, frame_counts, w_qkv, w_out, w_up, w_down, table_s, table_t
):
    local_rows = tokens.shape[0]
    clip_len = PADF * FH * FW
    group_clips = modulation.shape[0]
    group_rows = group_clips * clip_len
    scale_dot = HD ** (-0.5)
    my_index = lax.axis_index("head")
    first_row = my_index * local_rows
    row_ids = first_row + jnp.arange(local_rows, dtype=jnp.int32)
    clip_slots = jnp.arange(group_clips, dtype=jnp.int32)
    row_onehot = ((row_ids // clip_len)[:, None] == clip_slots[None, :]).astype(jnp.float32)
    count_float = frame_counts.astype(jnp.float32)
    row_frames = jnp.dot(row_onehot, count_float, precision=HIGHEST_PRECISION)
    row_keep = ((row_ids % clip_len // (FH * FW)).astype(jnp.float32) < row_frames).astype(
        jnp.float32
    )[:, None]
    group_ids = jnp.arange(group_rows, dtype=jnp.int32)
    group_onehot = ((group_ids // clip_len)[:, None] == clip_slots[None, :]).astype(jnp.float32)
    group_frames = jnp.dot(group_onehot, count_float, precision=HIGHEST_PRECISION)
    group_keep = (group_ids % clip_len // (FH * FW)).astype(jnp.float32) < group_frames

    def block_shape(block_id):
        if block_id == 0:
            return (1, SWIN)
        return (PADF, TWIN)

    def mod_row(slot):
        return jnp.dot(row_onehot, modulation[:, slot, :], precision=HIGHEST_PRECISION)

    def rows_in(values):
        return lax.all_gather(values, "head", axis=0, tiled=True)

    def grads_in(values):
        return lax.all_gather(values, "head", axis=0, tiled=True)

    def rows_out(full_rows, weight):
        return lax.psum_scatter(
            jnp.dot(full_rows, weight, preferred_element_type=jnp.float32).astype(jnp.bfloat16),
            "head",
            scatter_dimension=0,
            tiled=True,
        ).astype(jnp.float32)

    def grads_out(full_rows, weight, einsum_form):
        return lax.psum_scatter(
            jnp.einsum(einsum_form, full_rows, weight, preferred_element_type=jnp.float32).astype(
                jnp.bfloat16
            ),
            "head",
            scatter_dimension=0,
            tiled=True,
        ).astype(jnp.float32)

    def rows_keep(block_id):
        if block_id == 0:
            return None
        return to_windows(group_keep[:, None], PADF, TWIN)[:, :, 0]

    def shape_windows(projected, side_t, side_len):
        head_count = projected.shape[-1] // HD
        window_size = side_t * side_len * side_len
        windows = to_windows(projected, side_t, side_len)
        return windows.reshape(windows.shape[0], window_size, 3, head_count, HD)

    def shape_grad(grad_attended, side_t, side_len):
        head_count = grad_attended.shape[-1] // HD
        window_size = side_t * side_len * side_len
        windows = to_windows(grad_attended, side_t, side_len)
        return windows.reshape(windows.shape[0], window_size, head_count, HD)

    def flat_rows(windowed, side_t, side_len):
        return from_windows(windowed, side_t, side_len)

    def logits_of(queries, key_rows, table_arg, rel_index, keep_win):
        logits = (
            jnp.einsum("wqhe,wkhe->whqk", queries, key_rows, preferred_element_type=jnp.float32)
            * scale_dot
        )
        logits = logits + table_arg[:, rel_index][None]
        if keep_win is not None:
            logits = jnp.where(keep_win[:, None, None, :], logits, NEGATIVE)
        return logits

    def attend(windows, table_arg, rel_index, keep_win):
        logits = logits_of(windows[:, :, 0], windows[:, :, 1], table_arg, rel_index, keep_win)
        row_max = jnp.max(logits, axis=-1, keepdims=True)
        exponent = jnp.exp(logits - row_max)
        row_total = jnp.sum(exponent, axis=-1, keepdims=True)
        probs = exponent / row_total
        log_total = row_max + jnp.log(row_total)
        attended = jnp.einsum(
            "whqk,wkhe->wqhe",
            probs.astype(jnp.bfloat16),
            windows[:, :, 2],
            preferred_element_type=jnp.float32,
        )
        return (attended.reshape(attended.shape[0], attended.shape[1], -1), log_total)

    def attend_back(windows, grad_windows, log_total, table_arg, rel_index, keep_win):
        queries = windows[:, :, 0]
        key_rows = windows[:, :, 1]
        value_rows = windows[:, :, 2]
        logits = logits_of(queries, key_rows, table_arg, rel_index, keep_win)
        probs = jnp.exp(logits - log_total)
        grad_probs = jnp.einsum(
            "wqhe,wkhe->whqk", grad_windows, value_rows, preferred_element_type=jnp.float32
        )
        grad_values = jnp.einsum(
            "whqk,wqhe->wkhe",
            probs.astype(jnp.bfloat16),
            grad_windows,
            preferred_element_type=jnp.float32,
        )
        grad_logits = (
            probs * (grad_probs - jnp.sum(grad_probs * probs, axis=-1, keepdims=True))
        ).astype(jnp.bfloat16)
        head_count = queries.shape[2]
        table_terms = jnp.sum(grad_logits.astype(jnp.float32), axis=0).reshape(head_count, -1)
        grad_table = jax.ops.segment_sum(
            table_terms.T, rel_index.reshape(-1), num_segments=table_arg.shape[1]
        ).T
        grad_queries = (
            jnp.einsum("whqk,wkhe->wqhe", grad_logits, key_rows, preferred_element_type=jnp.float32)
            * scale_dot
        )
        grad_keys = (
            jnp.einsum("whqk,wqhe->wkhe", grad_logits, queries, preferred_element_type=jnp.float32)
            * scale_dot
        )
        grad_stack = jnp.stack([grad_queries, grad_keys, grad_values], axis=2)
        return (
            grad_stack.reshape(grad_stack.shape[0], grad_stack.shape[1], 3, head_count * HD),
            grad_table,
        )

    def forward_block(hidden, block_id):
        side_t, side_len = block_shape(block_id)
        table_local = table_s if block_id == 0 else table_t
        rel_index = window_index(side_t, side_len)
        normed = layer_norm(hidden, mod_row(6 * block_id), mod_row(6 * block_id + 1)).astype(
            jnp.bfloat16
        )
        plan = None
        normed_in = rows_in(normed)
        qkv_use, out_use, table_use = (w_qkv[block_id], w_out[block_id], table_local)
        keep_win = rows_keep(block_id)
        projected = jnp.einsum(
            "gd,cde->gce", normed_in, qkv_use, preferred_element_type=jnp.float32
        ).astype(jnp.bfloat16)
        windows = shape_windows(projected, side_t, side_len)
        attended_win, log_total = attend(windows, table_use, rel_index, keep_win)
        attended = flat_rows(attended_win, side_t, side_len).astype(jnp.bfloat16)
        branch = rows_out(attended, out_use)
        middle = hidden + mod_row(6 * block_id + 2) * branch
        shifted = layer_norm(middle, mod_row(6 * block_id + 3), mod_row(6 * block_id + 4)).astype(
            jnp.bfloat16
        )
        up_full, down_full = (
            lax.all_gather(w_up[block_id], "head", axis=1, tiled=True),
            lax.all_gather(w_down[block_id], "head", axis=0, tiled=True),
        )
        pre_gelu = jnp.dot(shifted, up_full, preferred_element_type=jnp.float32)
        activated = gelu_tanh(pre_gelu).astype(jnp.bfloat16)
        feed_out = jnp.dot(activated, down_full, preferred_element_type=jnp.float32)
        mlp_state = (shifted, pre_gelu, activated, up_full, down_full)
        result = middle + mod_row(6 * block_id + 5) * feed_out
        attn_state = (
            normed_in,
            projected,
            log_total,
            attended,
            qkv_use,
            out_use,
            table_use,
            keep_win,
            plan,
        )
        saved_state = (hidden, attn_state, branch, middle, feed_out, mlp_state)
        return (saved_state, result)

    def backward_block(saved_state, grad_result, block_id):
        hidden, attn_state, branch, middle, feed_out, mlp_state = saved_state
        normed_in, projected, log_total, attended, qkv_use, out_use, table_use, keep_win, plan = (
            attn_state
        )
        shifted_in, pre_gelu, activated, up_weight, down_weight = mlp_state
        side_t, side_len = block_shape(block_id)
        rel_index = window_index(side_t, side_len)
        grad_feed = (grad_result * mod_row(6 * block_id + 5)).astype(jnp.bfloat16)
        grad_gate_mlp = grad_result * feed_out
        grad_down = jnp.einsum(
            "gf,gd->fd", activated, grad_feed, preferred_element_type=jnp.float32
        )
        grad_activated = jnp.einsum(
            "gd,fd->gf", grad_feed, down_weight, preferred_element_type=jnp.float32
        )
        grad_pre = jax.vjp(gelu_tanh, pre_gelu)[1](grad_activated)[0].astype(jnp.bfloat16)
        grad_up = jnp.einsum("gd,gf->df", shifted_in, grad_pre, preferred_element_type=jnp.float32)
        grad_shifted = jnp.einsum(
            "gf,df->gd", grad_pre, up_weight, preferred_element_type=jnp.float32
        )
        grad_up, grad_down = (
            lax.psum_scatter(
                grad_up.astype(jnp.bfloat16), "head", scatter_dimension=1, tiled=True
            ).astype(jnp.float32),
            lax.psum_scatter(
                grad_down.astype(jnp.bfloat16), "head", scatter_dimension=0, tiled=True
            ).astype(jnp.float32),
        )
        unused_mid, pull_second = jax.vjp(
            layer_norm, middle, mod_row(6 * block_id + 3), mod_row(6 * block_id + 4)
        )
        grad_mid_norm, grad_shift_mlp, grad_scale_mlp = pull_second(grad_shifted)
        grad_middle = grad_result + grad_mid_norm
        grad_branch = (grad_middle * mod_row(6 * block_id + 2)).astype(jnp.bfloat16)
        grad_gate_att = grad_middle * branch
        branch_in = grads_in(grad_branch)
        grad_wout = jnp.einsum("ge,gd->ed", attended, branch_in, preferred_element_type=jnp.float32)
        grad_attended = jnp.einsum(
            "gd,ed->ge", branch_in, out_use, preferred_element_type=jnp.float32
        ).astype(jnp.bfloat16)
        windows = shape_windows(projected, side_t, side_len)
        grad_windows = shape_grad(grad_attended, side_t, side_len)
        grad_stack, grad_table = attend_back(
            windows, grad_windows, log_total, table_use, rel_index, keep_win
        )
        grad_projected = flat_rows(grad_stack, side_t, side_len).astype(jnp.bfloat16)
        grad_qkv = jnp.einsum(
            "gd,gce->cde", normed_in, grad_projected, preferred_element_type=jnp.float32
        )
        grad_normed = grads_out(grad_projected, qkv_use, "gce,cde->gd")
        unused_hid, pull_first = jax.vjp(
            layer_norm, hidden, mod_row(6 * block_id), mod_row(6 * block_id + 1)
        )
        grad_hid_norm, grad_shift_att, grad_scale_att = pull_first(grad_normed)
        grad_hidden = grad_middle + grad_hid_norm
        mod_terms = jnp.stack(
            [
                grad_shift_att,
                grad_scale_att,
                grad_gate_att,
                grad_shift_mlp,
                grad_scale_mlp,
                grad_gate_mlp,
            ],
            axis=1,
        )
        grad_mods = jnp.einsum("rc,rke->cke", row_onehot, mod_terms, precision=HIGHEST_PRECISION)
        return (grad_hidden, grad_mods, (grad_qkv, grad_wout, grad_up, grad_down, grad_table))

    hidden_first = tokens.astype(jnp.float32)
    saved_first, hidden_second = forward_block(hidden_first, 0)
    saved_second, hidden_last = forward_block(hidden_second, 1)
    output = (hidden_last * row_keep).astype(jnp.bfloat16)
    grad_second, mods_second, weights_second = backward_block(
        saved_second, d_out.astype(jnp.float32) * row_keep, 1
    )
    grad_first, mods_first, weights_first = backward_block(saved_first, grad_second, 0)
    grad_modulation = lax.psum(
        jnp.concatenate([mods_first, mods_second], axis=1).astype(jnp.bfloat16), "head"
    ).astype(jnp.float32)
    summed = (
        lax.psum(
            jnp.stack([weights_first[0], weights_second[0]]).astype(jnp.bfloat16), "clip"
        ).astype(jnp.float32),
        lax.psum(
            jnp.stack([weights_first[1], weights_second[1]]).astype(jnp.bfloat16), "clip"
        ).astype(jnp.float32),
        lax.psum(
            jnp.stack([weights_first[2], weights_second[2]]).astype(jnp.bfloat16), "clip"
        ).astype(jnp.float32),
        lax.psum(
            jnp.stack([weights_first[3], weights_second[3]]).astype(jnp.bfloat16), "clip"
        ).astype(jnp.float32),
        lax.psum(weights_first[4].astype(jnp.bfloat16), "clip").astype(jnp.float32),
        lax.psum(weights_second[4].astype(jnp.bfloat16), "clip").astype(jnp.float32),
    )
    return (
        output,
        grad_first,
        grad_modulation,
        summed[0],
        summed[1],
        summed[2],
        summed[3],
        summed[4],
        summed[5],
    )


F32 = jnp.float32
BF16 = jnp.bfloat16
VMEM_LIMIT = 58 * 1024 * 1024
NZ = 4
D = 1024
HPZ = 4
CONST = pl.Buffered(1)


def dot_nn(a, b):
    return lax.dot_general(a, b, (((1,), (0,)), ((), ())), preferred_element_type=F32)


def dot_nt(a, b):
    return lax.dot_general(a, b, (((1,), (1,)), ((), ())), preferred_element_type=F32)


def dot_tn(a, b):
    return lax.dot_general(a, b, (((0,), (0,)), ((), ())), preferred_element_type=F32)


def call(kernel, name, grid, in_specs, out_specs, out_shape, scratch, flops, nbytes):
    return pl.pallas_call(
        kernel,
        name=name,
        grid=grid,
        in_specs=in_specs,
        out_specs=out_specs,
        out_shape=out_shape,
        scratch_shapes=scratch,
        compiler_params=pltpu.CompilerParams(
            dimension_semantics=("arbitrary",) * len(grid), vmem_limit_bytes=VMEM_LIMIT
        ),
        cost_estimate=pl.CostEstimate(
            flops=flops // 4, bytes_accessed=nbytes // 4, transcendentals=0
        ),
    )


def full(shape):
    return pl.BlockSpec(shape, lambda *ids: (0,) * len(shape), pipeline_mode=CONST)


def chunk_rows(i, size):
    return pl.ds(pl.multiple_of(i * size, size), size)


def ln_stats(x):
    mean = jnp.mean(x, axis=-1, keepdims=True)
    centred = x - mean
    rstd = lax.rsqrt(jnp.mean(centred * centred, axis=-1, keepdims=True) + EPS)
    return centred * rstd, rstd


def ln_back(grad, hat, rstd, scale):
    gh = grad * (1.0 + scale)
    m1 = jnp.mean(gh, axis=-1, keepdims=True)
    m2 = jnp.mean(gh * hat, axis=-1, keepdims=True)
    return rstd * (gh - m1 - hat * m2)


def piece_specs(k, row, count):
    tail = (count, D)
    return [
        pl.BlockSpec((2, 4) + tail, lambda d: (0, 0, row, 0), pipeline_mode=CONST),
        pl.BlockSpec((4, 1) + tail, lambda d: (0, jnp.maximum(d - 1, 0), row, 0)),
        pl.BlockSpec((4, 1) + tail, lambda d: (0, jnp.maximum(d - 1, 0), row, 0)),
    ]


def by_offset(d, body, local_ref, own_ref, other_ref):
    @pl.when(d == 0)
    def _():
        body(lambda m, r, n: local_ref[0, m, r : r + n, :], lambda m, r, n: local_ref[1, m, r : r + n, :])

    @pl.when(d > 0)
    def _():
        body(lambda m, r, n: own_ref[m, 0, r : r + n, :], lambda m, r, n: other_ref[m, 0, r : r + n, :])


def head_rows(own, other, row):
    parts = []
    for m in range(4):
        parts += [own(m, row, 32), other(m, row, 32)]
    return jnp.concatenate(parts, axis=0)


def pair_rows(first, second):
    return jnp.concatenate([get(m) for get in (first, second) for m in range(4)], axis=0)


def feed_specs(down_block):
    def spec(block):
        return pl.BlockSpec((4, 1, 128, D), lambda d: (0, jnp.maximum(d - 1, 0), block, 0))

    return [full((2, 4, 256, D)), spec(0), spec(0), spec(down_block), spec(down_block)]


def feed_by_offset(d, body, l_ref, wu_ref, vu_ref, wd_ref, vd_ref):
    @pl.when(d == 0)
    def _():
        body(
            lambda: pair_rows(lambda m: l_ref[0, m, 0:128], lambda m: l_ref[1, m, 0:128]),
            lambda: pair_rows(lambda m: l_ref[0, m, 128:256], lambda m: l_ref[1, m, 128:256]),
        )

    @pl.when(d > 0)
    def _():
        body(
            lambda: pair_rows(lambda m: wu_ref[m, 0], lambda m: vu_ref[m, 0]),
            lambda: pair_rows(lambda m: wd_ref[m, 0], lambda m: vd_ref[m, 0]),
        )


def ln_qkv(hidden, mods, weights, base):
    rows = hidden.shape[0]
    step = 640

    def kernel(h_ref, m_ref, l_ref, w_ref, v_ref, normed_ref, qkv_ref):
        d = pl.program_id(0)

        @pl.when(d == 0)
        def _():
            def body(i, carry):
                sl = chunk_rows(i, step)
                hat, _ = ln_stats(h_ref[sl, :].astype(F32))
                normed_ref[sl, :] = (
                    hat * (1.0 + m_ref[base + 1 : base + 2, :]) + m_ref[base : base + 1, :]
                ).astype(BF16)
                return carry

            lax.fori_loop(0, rows // step, body, 0)

        def work(own, other):
            for t in range(3):
                qkv_ref[:, t * 256 : (t + 1) * 256] = dot_nt(
                    normed_ref[...], head_rows(own, other, t * 32)
                ).astype(BF16)

        by_offset(d, work, l_ref, w_ref, v_ref)

    return call(
        kernel,
        "ln_qkv",
        (NZ,),
        [full((rows, D)), full((12, D))] + piece_specs(128, 0, 96),
        [full((rows, D)), pl.BlockSpec((rows, 768), lambda z: (0, z))],
        [jax.ShapeDtypeStruct((rows, D), BF16), jax.ShapeDtypeStruct((rows, 3 * D), BF16)],
        [],
        2 * rows * D * 3 * D,
        rows * D * 12 + 6 * D * D,
    )(hidden, mods, *weights)


def build_bias(base_ref, bias_ref, fc_ref, slides, width, lanes_step):
    rows_step = width // slides
    for h in range(HPZ):
        for s in range(slides):
            off = (slides - 1 - s) * lanes_step
            tile = base_ref[h, :, off : off + width]
            if fc_ref is not None:
                tile = jnp.where(s < fc_ref[0], tile, NEGATIVE)
            bias_ref[h, s * rows_step : (s + 1) * rows_step, :] = tile


def window_view(values, kind):
    parts, count, size = kind[0]
    return values.reshape(parts, count, size, values.shape[-1])


def attn_fwd(qkv, base, fc, kind):
    (parts, count, size), slides, lanes_step, masked = kind
    rows, width = qkv.shape[0], parts * size
    r_step, lanes = base.shape[1], base.shape[2]

    def kernel(x_ref, b_ref, fc_ref, o_ref, bias_ref):
        build_bias(b_ref, bias_ref, fc_ref if masked else None, slides, width, lanes_step)

        def one(w, carry):
            def cut(col):
                return x_ref[:, w, :, col : col + HD].reshape(width, HD)

            scores, probs = [], []
            for h in range(HPZ):
                scores.append(dot_nt(cut(256 + h * HD), cut(h * HD) * 0.125) + bias_ref[h])
            for h in range(HPZ):
                expo = jnp.exp(scores[h] - jnp.max(scores[h], axis=0, keepdims=True))
                inv = 1.0 / jnp.sum(expo, axis=0, keepdims=True)
                probs.append((expo * inv).astype(BF16))
            for h in range(HPZ):
                got = dot_tn(probs[h], cut(512 + h * HD)).astype(BF16)
                o_ref[:, w, :, h * HD : (h + 1) * HD] = got.reshape(parts, size, HD)
            return carry

        lax.fori_loop(0, count, one, 0)

    return call(
        kernel,
        "attn_fwd",
        (NZ,),
        [
            pl.BlockSpec((parts, count, size, 768), lambda z: (0, 0, 0, z)),
            pl.BlockSpec((HPZ, r_step, lanes), lambda z: (z, 0, 0)),
            pl.BlockSpec(memory_space=pltpu.SMEM),
        ],
        pl.BlockSpec((parts, count, size, 256), lambda z: (0, 0, 0, z)),
        jax.ShapeDtypeStruct((parts, count, size, D), BF16),
        [pltpu.VMEM((HPZ, width, width), F32)],
        count * 16 * width * width * HD * 16,
        rows * D * 8,
    )(window_view(qkv, kind), base, fc).reshape(rows, D)


def attn_bwd(qkv, grad_att, base, fc, kind):
    (parts, count, size), slides, lanes_step, masked = kind
    rows, width = qkv.shape[0], parts * size
    r_step, lanes = base.shape[1], base.shape[2]

    def kernel(x_ref, d_ref, b_ref, fc_ref, o_ref, gb_ref, bias_ref, acc_ref):
        build_bias(b_ref, bias_ref, fc_ref if masked else None, slides, width, lanes_step)
        acc_ref[...] = jnp.zeros_like(acc_ref)

        def one(w, carry):
            def cut(ref, col):
                return ref[:, w, :, col : col + HD].reshape(width, HD)

            def put(col, value):
                o_ref[:, w, :, col : col + HD] = value.astype(BF16).reshape(parts, size, HD)

            q = [cut(x_ref, h * HD) * 0.125 for h in range(HPZ)]
            k = [cut(x_ref, 256 + h * HD) for h in range(HPZ)]
            da = [cut(d_ref, h * HD) for h in range(HPZ)]
            score = [dot_nt(k[h], q[h]) + bias_ref[h] for h in range(HPZ)]
            dp = [dot_nt(cut(x_ref, 512 + h * HD), da[h]) for h in range(HPZ)]
            probs, dl = [], []
            for h in range(HPZ):
                expo = jnp.exp(score[h] - jnp.max(score[h], axis=0, keepdims=True))
                inv = 1.0 / jnp.sum(expo, axis=0, keepdims=True)
                p = expo * inv
                row = jnp.sum(dp[h] * p, axis=0, keepdims=True)
                g = (p * (dp[h] - row)).astype(BF16)
                acc_ref[h] += g.astype(F32)
                probs.append(p.astype(BF16))
                dl.append(g)
            for h in range(HPZ):
                put(h * HD, dot_tn(dl[h], k[h]) * 0.125)
                put(256 + h * HD, dot_nn(dl[h], q[h]))
                put(512 + h * HD, dot_nn(probs[h], da[h]))
            return carry

        lax.fori_loop(0, count, one, 0)
        gb_ref[...] = jnp.zeros_like(gb_ref)
        for h in range(HPZ):
            for s in range(slides):
                off = (slides - 1 - s) * lanes_step
                gb_ref[h, :, off : off + width] += acc_ref[h, s * r_step : (s + 1) * r_step, :]

    xspec = pl.BlockSpec((parts, count, size, 768), lambda z: (0, 0, 0, z))
    bspec = pl.BlockSpec((HPZ, r_step, lanes), lambda z: (z, 0, 0))
    proj, strips = call(
        kernel,
        "attn_bwd",
        (NZ,),
        [
            xspec,
            pl.BlockSpec((parts, count, size, 256), lambda z: (0, 0, 0, z)),
            bspec,
            pl.BlockSpec(memory_space=pltpu.SMEM),
        ],
        [xspec, bspec],
        [
            jax.ShapeDtypeStruct((parts, count, size, 3 * D), BF16),
            jax.ShapeDtypeStruct(base.shape, F32),
        ],
        [pltpu.VMEM((HPZ, width, width), F32), pltpu.VMEM((HPZ, width, width), F32)],
        count * 16 * width * width * HD * 40,
        rows * D * 16,
    )(window_view(qkv, kind), window_view(grad_att, kind), base, fc)
    return proj.reshape(rows, 3 * D), strips


def out_specs_of(row_block):
    return [
        pl.BlockSpec((2, 4, 32, D), lambda i: (0, 0, row_block, 0), pipeline_mode=CONST),
        pl.BlockSpec((4, 3, 32, D), lambda i: (0, 0, row_block, 0), pipeline_mode=CONST),
        pl.BlockSpec((4, 3, 32, D), lambda i: (0, 0, row_block, 0), pipeline_mode=CONST),
    ]


def out_rows(d, l_ref, w_ref, v_ref):
    if d == 0:
        return head_rows(
            lambda m, r, n: l_ref[0, m, :, :], lambda m, r, n: l_ref[1, m, :, :], 0
        )
    return head_rows(
        lambda m, r, n: w_ref[m, d - 1, :, :], lambda m, r, n: v_ref[m, d - 1, :, :], 0
    )


def out_proj(attended, weights, hidden, mods, base):
    rows = attended.shape[0]
    step = 256

    def kernel(a_ref, l_ref, w_ref, v_ref, h_ref, m_ref, br_ref, mid_ref, sh_ref):
        branch = jnp.zeros((step, D), F32)
        for d in range(NZ):
            branch += dot_nn(a_ref[:, d * 256 : (d + 1) * 256], out_rows(d, l_ref, w_ref, v_ref))
        br_ref[...] = branch.astype(BF16)
        middle = h_ref[...].astype(F32) + m_ref[base + 2 : base + 3, :] * branch
        mid_ref[...] = middle
        hat, _ = ln_stats(middle)
        sh_ref[...] = (
            hat * (1.0 + m_ref[base + 4 : base + 5, :]) + m_ref[base + 3 : base + 4, :]
        ).astype(BF16)

    tile = pl.BlockSpec((step, D), lambda i: (i, 0))
    return call(
        kernel,
        "out_proj",
        (rows // step,),
        [tile] + out_specs_of(3) + [tile, full((12, D))],
        [tile, tile, tile],
        [
            jax.ShapeDtypeStruct((rows, D), BF16),
            jax.ShapeDtypeStruct((rows, D), F32),
            jax.ShapeDtypeStruct((rows, D), BF16),
        ],
        [],
        2 * rows * D * D,
        rows * D * 14 + 2 * D * D,
    )(attended, *weights, hidden, mods)


GELU_C = 0.7978845608028654
GELU_A = 0.044715


def gelu_of(x):
    return 0.5 * x * (1.0 + jnp.tanh(GELU_C * (x + GELU_A * x * x * x)))


def gelu_both(x):
    x2 = x * x
    th = jnp.tanh(GELU_C * (x + GELU_A * x * x2))
    half = 0.5 * (1.0 + th)
    slope = half + 0.5 * x * (1.0 - th * th) * (GELU_C * (1.0 + 3.0 * GELU_A * x2))
    return x * half, slope


def ffn_fwd(shifted, weights, down_block, middle, mods, base):
    rows = shifted.shape[0]
    step = 640

    def kernel(x_ref, *refs):
        parts, (mid_ref, m_ref, pre_ref, feed_ref, nx_ref, acc_ref) = refs[:5], refs[5:]
        z = pl.program_id(0)

        def work(up, down):
            def body(i, carry):
                sl = chunk_rows(i, step)
                pre = dot_nt(x_ref[sl, :], up())
                pre_ref[sl, :] = pre.astype(BF16)
                part = dot_nn(gelu_of(pre).astype(BF16), down())

                @pl.when(z == 0)
                def _():
                    acc_ref[sl, :] = part

                @pl.when((z > 0) & (z < NZ - 1))
                def _():
                    acc_ref[sl, :] += part

                @pl.when(z == NZ - 1)
                def _():
                    feed = acc_ref[sl, :] + part
                    feed_ref[sl, :] = feed.astype(BF16)
                    nx_ref[sl, :] = (
                        mid_ref[sl, :] + m_ref[base + 5 : base + 6, :] * feed
                    ).astype(BF16)

                return carry

            lax.fori_loop(0, rows // step, body, 0)

        feed_by_offset(z, work, *parts)

    return call(
        kernel,
        "ffn_fwd",
        (NZ,),
        [full((rows, D))] + feed_specs(down_block) + [full((rows, D)), full((12, D))],
        [pl.BlockSpec((rows, D), lambda z: (0, z)), full((rows, D)), full((rows, D))],
        [
            jax.ShapeDtypeStruct((rows, 4 * D), BF16),
            jax.ShapeDtypeStruct((rows, D), BF16),
            jax.ShapeDtypeStruct((rows, D), BF16),
        ],
        [pltpu.VMEM((rows, D), F32)],
        16 * rows * D * D,
        rows * D * 20 + 16 * D * D,
    )(shifted, *weights, middle, mods)


def ffn_bwd(grad, pre, shifted, weights, down_block, mods, base):
    rows = grad.shape[0]
    step = 640

    def kernel(g_ref, p_ref, x_ref, *refs):
        parts, refs = refs[:5], refs[5:]
        m_ref, keep_ref, send_ref, gs_ref, gf_ref, act_ref, gp_ref = refs
        z = pl.program_id(0)

        @pl.when(z == 0)
        def _():
            def body(i, carry):
                sl = chunk_rows(i, step)
                gf_ref[sl, :] = (
                    g_ref[sl, :].astype(F32) * m_ref[base + 5 : base + 6, :]
                ).astype(BF16)
                gs_ref[sl, :] = jnp.zeros((step, D), F32)
                return carry

            lax.fori_loop(0, rows // step, body, 0)

        def work(up, down):
            def body(i, carry):
                sl = chunk_rows(i, step)
                back = dot_nt(gf_ref[sl, :], down())
                act, slope = gelu_both(p_ref[sl, :].astype(F32))
                act_ref[sl, :] = act.astype(BF16)
                gpre = (back * slope).astype(BF16)
                gp_ref[sl, :] = gpre
                part = dot_nn(gpre, up())
                gs_ref[sl, :] += part
                return carry

            lax.fori_loop(0, rows // step, body, 0)

        feed_by_offset(z, work, *parts)
        for j, out_ref in enumerate((keep_ref, send_ref)):
            cols = slice(j * 512, (j + 1) * 512)
            gd = dot_tn(act_ref[:, cols], gf_ref[...]).astype(BF16)
            gu = dot_tn(gp_ref[:, cols], x_ref[...]).astype(BF16)
            out_ref[:, 0, 0:128] = gu.reshape(4, 128, D)
            out_ref[:, 0, 128:256] = gd.reshape(4, 128, D)

    gspec = pl.BlockSpec((4, 1, 256, D), lambda z: (0, z, 0, 0))
    gshape = jax.ShapeDtypeStruct((4, NZ, 256, D), BF16)
    return call(
        kernel,
        "ffn_bwd",
        (NZ,),
        [
            full((rows, D)),
            pl.BlockSpec((rows, D), lambda z: (0, z)),
            full((rows, D)),
        ]
        + feed_specs(down_block)
        + [full((12, D))],
        [gspec, gspec, full((rows, D))],
        [gshape, gshape, jax.ShapeDtypeStruct((rows, D), F32)],
        [pltpu.VMEM((rows, D), BF16)] * 3,
        32 * rows * D * D,
        rows * D * 16 + 32 * D * D,
    )(grad, pre, shifted, *weights, mods)


def split_heads(value, keep_ref, send_ref, d, row):
    for m in range(4):
        keep_ref[m, d, row : row + 32] = value[m * 64 : m * 64 + 32]
        send_ref[m, d, row : row + 32] = value[m * 64 + 32 : m * 64 + 64]


def out_bwd(grad, grad_shifted, middle, feed, branch, attended, weights, mods, base):
    rows = grad.shape[0]
    step = 256
    steps = rows // step

    def kernel(
        g_ref, gs_ref, mid_ref, f_ref, b_ref, a_ref, l_ref, w_ref, v_ref, m_ref, gm_ref, ga_ref,
        keep_ref, send_ref, s_ref, gb_ref,
    ):
        i = pl.program_id(0)

        @pl.when(i == 0)
        def _():
            s_ref[...] = jnp.zeros_like(s_ref)

        g = g_ref[...].astype(F32)
        gs = gs_ref[...]
        hat, rstd = ln_stats(mid_ref[...])
        gm = g + ln_back(gs, hat, rstd, m_ref[base + 4 : base + 5, :])
        gm_ref[...] = gm
        s_ref[0:1, :] += jnp.sum(gs, axis=0, keepdims=True)
        s_ref[1:2, :] += jnp.sum(gs * hat, axis=0, keepdims=True)
        s_ref[2:3, :] += jnp.sum(gm * b_ref[...].astype(F32), axis=0, keepdims=True)
        s_ref[3:4, :] += jnp.sum(g * f_ref[...].astype(F32), axis=0, keepdims=True)
        gb = (gm * m_ref[base + 2 : base + 3, :]).astype(BF16)
        gb_ref[chunk_rows(i, step), :] = gb
        for d in range(NZ):
            ga_ref[:, d * 256 : (d + 1) * 256] = dot_nt(
                gb, out_rows(d, l_ref, w_ref, v_ref)
            ).astype(BF16)

        @pl.when(i == steps - 1)
        def _():
            for d in range(NZ):
                gw = dot_tn(a_ref[:, d * 256 : (d + 1) * 256], gb_ref[...]).astype(BF16)
                split_heads(gw, keep_ref, send_ref, d, 0)

    tile = pl.BlockSpec((step, D), lambda i: (i, 0))
    gshape = jax.ShapeDtypeStruct((4, NZ, 32, D), BF16)
    return call(
        kernel,
        "out_bwd",
        (steps,),
        [tile, tile, tile, tile, tile, full((rows, D))] + out_specs_of(3) + [full((12, D))],
        [tile, tile, full(gshape.shape), full(gshape.shape), full((8, D))],
        [
            jax.ShapeDtypeStruct((rows, D), F32),
            jax.ShapeDtypeStruct((rows, D), BF16),
            gshape,
            gshape,
            jax.ShapeDtypeStruct((8, D), F32),
        ],
        [pltpu.VMEM((rows, D), BF16)],
        4 * rows * D * D,
        rows * D * 24 + 4 * D * D,
    )(grad, grad_shifted, middle, feed, branch, attended, *weights, mods)


def qkv_back(grad_proj, weights, hidden, grad_middle, mods, base, out_dtype, pieces):
    rows = hidden.shape[0]
    step = 640

    cols = D // pieces

    def kernel(p_ref, l_ref, w_ref, v_ref, h_ref, gm_ref, m_ref, *refs):
        gh_refs, (s_ref, acc_ref) = refs[:pieces], refs[pieces:]
        z = pl.program_id(0)

        @pl.when(z == 0)
        def _():
            acc_ref[...] = jnp.zeros_like(acc_ref)
            s_ref[...] = jnp.zeros_like(s_ref)

        def work(own, other):
            def body(i, carry):
                sl = chunk_rows(i, step)
                rows_of = jnp.concatenate([head_rows(own, other, t * 32) for t in range(3)], axis=0)
                acc_ref[sl, :] += dot_nn(p_ref[sl, :], rows_of)
                return carry

            lax.fori_loop(0, rows // step, body, 0)

        by_offset(z, work, l_ref, w_ref, v_ref)

        @pl.when(z == NZ - 1)
        def _():
            def tail(n, carry):
                sl = chunk_rows(n, 256)
                gn = acc_ref[sl, :]
                hat, rstd = ln_stats(h_ref[sl, :].astype(F32))
                gh = gm_ref[sl, :] + ln_back(gn, hat, rstd, m_ref[base + 1 : base + 2, :])
                for i, gh_ref in enumerate(gh_refs):
                    gh_ref[sl, :] = gh[:, i * cols : (i + 1) * cols].astype(out_dtype)
                s_ref[0:1, :] += jnp.sum(gn, axis=0, keepdims=True)
                s_ref[1:2, :] += jnp.sum(gn * hat, axis=0, keepdims=True)
                return carry

            lax.fori_loop(0, rows // 256, tail, 0)

    return call(
        kernel,
        "qkv_back",
        (NZ,),
        [pl.BlockSpec((rows, 768), lambda z: (0, z))]
        + piece_specs(128, 0, 96)
        + [full((rows, D)), full((rows, D)), full((12, D))],
        [full((rows, cols))] * pieces + [full((8, D))],
        [jax.ShapeDtypeStruct((rows, cols), out_dtype)] * pieces
        + [jax.ShapeDtypeStruct((8, D), F32)],
        [pltpu.VMEM((rows, D), F32)],
        6 * rows * D * D,
        rows * D * 20 + 6 * D * D,
    )(grad_proj, *weights, hidden, grad_middle, mods)


def qkv_grad(grad_proj, normed, out_keep, out_send, table_rows):
    rows = normed.shape[0]
    k = 128 if table_rows is None else 144

    def kernel(p_ref, n_ref, ok_ref, os_ref, *rest):
        keep_ref, send_ref = rest[-2:]
        for t in range(3):
            gw = dot_tn(p_ref[:, t * 256 : (t + 1) * 256], n_ref[...]).astype(BF16)
            split_heads(gw, keep_ref, send_ref, 0, t * 32)
        keep_ref[:, :, 96:128] = ok_ref[...]
        send_ref[:, :, 96:128] = os_ref[...]
        if table_rows is not None:
            keep_ref[:, :, 128:144] = rest[0][...]
            send_ref[:, :, 128:144] = rest[0][...]

    gspec = pl.BlockSpec((4, 1, k, D), lambda z: (0, z, 0, 0))
    ospec = pl.BlockSpec((4, 1, 32, D), lambda z: (0, z, 0, 0))
    tspec = pl.BlockSpec((4, 1, 16, D), lambda z: (0, z, 0, 0))
    gshape = jax.ShapeDtypeStruct((4, NZ, k, D), BF16)
    extra = () if table_rows is None else (table_rows,)
    return call(
        kernel,
        "qkv_grad",
        (NZ,),
        [pl.BlockSpec((rows, 768), lambda z: (0, z)), full((rows, D)), ospec, ospec]
        + [tspec] * len(extra),
        [gspec, gspec],
        [gshape, gshape],
        [],
        6 * rows * D * D,
        rows * D * 8 + 8 * D * D,
    )(grad_proj, normed, out_keep, out_send, *extra)


def place_call(kernel, name, in_specs, out_specs, out_shape, scratch, nbytes, aliases):
    return pl.pallas_call(
        kernel,
        name=name,
        grid_spec=pltpu.PrefetchScalarGridSpec(
            num_scalar_prefetch=1,
            grid=(8,),
            in_specs=in_specs,
            out_specs=out_specs,
            scratch_shapes=scratch,
        ),
        out_shape=out_shape,
        input_output_aliases=aliases,
        compiler_params=pltpu.CompilerParams(
            dimension_semantics=("arbitrary",), vmem_limit_bytes=VMEM_LIMIT
        ),
        cost_estimate=pl.CostEstimate(flops=0, bytes_accessed=nbytes, transcendentals=0),
    )


def rows_at(place):
    return pl.ds(pl.multiple_of(place * 32, 32), 32)


def prep_attn(place, w_qkv, w_out, b):
    def kernel(c_ref, q_ref, o_ref, out_ref, t_ref):
        r = pl.program_id(0)

        @pl.when(r == 0)
        def _():
            for t in range(3):
                t_ref[t] = q_ref[0, t].T

        at = rows_at(c_ref[0] ^ r)
        for t in range(3):
            out_ref[0, 0, t * 32 : (t + 1) * 32, :] = t_ref[t, at, :]
        out_ref[0, 0, 96:128, :] = o_ref[0, at, :]

    return place_call(
        kernel,
        "prep_attn",
        [
            pl.BlockSpec((1, 3, D, 256), lambda r, c: (b, 0, 0, 0)),
            pl.BlockSpec((1, 256, D), lambda r, c: (b, 0, 0)),
        ],
        pl.BlockSpec((1, 1, 128, D), lambda r, c: (r % 2, r // 2, 0, 0)),
        jax.ShapeDtypeStruct((2, 4, 128, D), BF16),
        [pltpu.VMEM((3, 256, D), BF16)],
        4 * D * D,
        {},
    )(place, w_qkv, w_out)


def prep_feed(place, w_up, w_down, b):
    def kernel(c_ref, u_ref, d_ref, out_ref):
        out_ref[0, 0, 0:128, :] = u_ref[0].T
        out_ref[0, 0, 128:256, :] = d_ref[0]

    return place_call(
        kernel,
        "prep_feed",
        [
            pl.BlockSpec((1, D, 128), lambda r, c: (b, 0, c[0] ^ r)),
            pl.BlockSpec((1, 128, D), lambda r, c: (b, c[0] ^ r, 0)),
        ],
        pl.BlockSpec((1, 1, 256, D), lambda r, c: (r % 2, r // 2, 0, 0)),
        jax.ShapeDtypeStruct((2, 4, 256, D), BF16),
        [],
        8 * D * D,
        {},
    )(place, w_up, w_down)


def finish_attn(place, own, other):
    def kernel(c_ref, own_ref, oth_ref, gq_ref, go_ref, t_ref):
        r = pl.program_id(0)
        at = rows_at(c_ref[0] ^ r)

        def store(ref):
            for b in range(2):
                row = 128 * b
                for t in range(3):
                    t_ref[b, t, at, :] = ref[0, row + t * 32 : row + (t + 1) * 32, :]
                go_ref[b, at, :] = ref[0, row + 96 : row + 128, :].astype(F32)

        @pl.when(r % 2 == 0)
        def _():
            store(own_ref)

        @pl.when(r % 2 == 1)
        def _():
            store(oth_ref)

        @pl.when(r == 7)
        def _():
            for b in range(2):
                for t in range(3):
                    gq_ref[b, t] = t_ref[b, t].T.astype(F32)

    piece = pl.BlockSpec((1, 256, D), lambda r, c: (r // 2, 0, 0))
    return place_call(
        kernel,
        "finish_attn",
        [piece, piece],
        [
            pl.BlockSpec((2, 3, D, 256), lambda r, c: (0, 0, 0, 0), pipeline_mode=CONST),
            pl.BlockSpec((2, 256, D), lambda r, c: (0, 0, 0), pipeline_mode=CONST),
        ],
        [
            jax.ShapeDtypeStruct((2, 3, D, 256), F32),
            jax.ShapeDtypeStruct((2, 256, D), F32),
        ],
        [pltpu.VMEM((2, 3, 256, D), BF16)],
        12 * D * D,
        {},
    )(place, own, other)


def finish_feed(place, own, other, b, earlier):
    def kernel(c_ref, own_ref, oth_ref, *rest):
        gu_ref, gd_ref = rest[-2:]
        r = pl.program_id(0)

        def store(ref):
            gu_ref[0] = ref[0, 0:128, :].T.astype(F32)
            gd_ref[0] = ref[0, 128:256, :].astype(F32)

        @pl.when(r % 2 == 0)
        def _():
            store(own_ref)

        @pl.when(r % 2 == 1)
        def _():
            store(oth_ref)

    piece = pl.BlockSpec((1, 256, D), lambda r, c: (r // 2, 0, 0))
    anywhere = pl.BlockSpec(memory_space=pl.ANY)
    return place_call(
        kernel,
        "finish_feed",
        [piece, piece] + [anywhere] * len(earlier),
        [
            pl.BlockSpec((1, D, 128), lambda r, c: (b, 0, c[0] ^ r)),
            pl.BlockSpec((1, 128, D), lambda r, c: (b, c[0] ^ r, 0)),
        ],
        [jax.ShapeDtypeStruct((2, D, D), F32), jax.ShapeDtypeStruct((2, D, D), F32)],
        [],
        12 * D * D,
        {3 + i: i for i in range(len(earlier))},
    )(place, own, other, *earlier)


def partner(values):
    return lax.ppermute(values, "head", [(i, i ^ 1) for i in range(NZ)])


def rows_to_spatial(rows, odd):
    cols = rows.shape[1]
    whole = lax.dynamic_slice(rows, (256 * odd, 0), (1024, cols))
    part = lax.dynamic_slice(rows, (1024 * (1 - odd), 0), (256, cols)).reshape(8, 2, 16, cols)
    wins = whole.reshape(2, 16, 2, 16, cols).transpose(0, 2, 1, 3, 4).reshape(1024, cols)
    left, right = part[:, 0].reshape(128, cols), part[:, 1].reshape(128, cols)
    keep = jnp.where(odd == 0, left, right)
    got = partner(jnp.where(odd == 0, right, left))
    top, bottom = jnp.where(odd == 0, keep, got), jnp.where(odd == 0, got, keep)
    part = jnp.concatenate([top, bottom], axis=0)
    return jnp.where(
        odd == 0,
        jnp.concatenate([wins, part], axis=0),
        jnp.concatenate([part, wins], axis=0),
    )


def spatial_to_rows(wins, odd):
    cols = wins.shape[1]
    whole = lax.dynamic_slice(wins, (256 * odd, 0), (1024, cols))
    part = lax.dynamic_slice(wins, (1024 * (1 - odd), 0), (256, cols))
    whole = whole.reshape(2, 2, 16, 16, cols).transpose(0, 2, 1, 3, 4).reshape(1024, cols)
    keep = jnp.where(odd == 0, part[:128], part[128:])
    got = partner(jnp.where(odd == 0, part[128:], part[:128]))
    left, right = jnp.where(odd == 0, keep, got), jnp.where(odd == 0, got, keep)
    part = jnp.stack([left.reshape(8, 16, cols), right.reshape(8, 16, cols)], axis=1)
    part = part.reshape(256, cols)
    return jnp.where(
        odd == 0,
        jnp.concatenate([whole, part], axis=0),
        jnp.concatenate([part, whole], axis=0),
    )


def exchange(values):
    return lax.all_to_all(values, "head", 0, 0, tiled=True)


def spatial_to_tubes(wins):
    cols = wins.shape[1]
    return exchange(
        wins.reshape(5, 2, 8, 2, 8, cols).transpose(1, 3, 0, 2, 4, 5).reshape(1280, cols)
    )


def from_quads(quads):
    cols = quads.shape[1]
    return quads.reshape(2, 2, 5, 8, 8, cols).transpose(2, 0, 3, 1, 4, 5).reshape(1280, cols)


def toeplitz(side):
    span = 2 * side - 1
    b = lax.broadcasted_iota(jnp.int32, (span, side, side), 0)
    j = lax.broadcasted_iota(jnp.int32, (span, side, side), 1)
    i = lax.broadcasted_iota(jnp.int32, (span, side, side), 2)
    return (b == i - j + side - 1).astype(F32)


def toeplitz_pair(side):
    span = 2 * side - 1
    shape = (span * span, side * side, side * side)
    r = lax.broadcasted_iota(jnp.int32, shape, 0)
    j = lax.broadcasted_iota(jnp.int32, shape, 1)
    i = lax.broadcasted_iota(jnp.int32, shape, 2)
    dy = i // side - j // side + side - 1
    dx = i % side - j % side + side - 1
    return (r == dy * span + dx).astype(F32)


CORE, ROW_X, ROW_Y = 1, 2, 4


def swap(values, bit):
    return lax.ppermute(values, "clip", [(i, i ^ bit) for i in range(8)])


def from_z(values, d):
    return lax.ppermute(values, "head", [((i + d) % NZ, i) for i in range(NZ)])


def sync(*values):
    return lax.optimization_barrier(values)


def add(first, second):
    return (first.astype(F32) + second.astype(F32)).astype(BF16)


def line_stage(piece):
    return [from_z(piece, d) for d in (1, 2, 3)]


def others(by_z, z):
    return [lax.dynamic_index_in_dim(by_z, (z + d) % NZ, 0, keepdims=False) for d in (1, 2, 3)]


def cross_stage(own):
    return [own] + [swap(own, m * 2) for m in (1, 2, 3)]


def sides_stage(own):
    return [own, swap(own, ROW_X), swap(own, ROW_Y)]


def corner_stage(sides):
    half = sides[0].shape[1] // 2
    return [swap(sides[1][:, :half], ROW_Y), swap(sides[2][:, half:], ROW_X)]


def joined(sides, corner):
    return jnp.stack(sides + [jnp.concatenate(corner, axis=1)])


def sum_core(keep, got):
    return [add(keep[m], got[m]) for m in range(4)]


def send_plane(totals, offsets):
    return [swap(totals[m], m * 2) for m in offsets]


def to_places(total, z):
    twice = jnp.concatenate([total, total[: NZ - 1]], axis=0)
    return lax.dynamic_slice_in_dim(twice, (NZ - z) % NZ, NZ, axis=0)


def sum_plane(totals, got, z):
    total = totals[0].astype(F32)
    for value in got:
        total = total + value.astype(F32)
    return to_places(total.astype(BF16), z)


def send_cross(totals):
    half = totals[0].shape[1] // 2
    first = [t[:, :half] for t in totals]
    second = [t[:, half:] for t in totals]
    by_x = swap(jnp.stack([first[1], first[3]]), ROW_X)
    by_y = swap(jnp.stack([second[2], second[3]]), ROW_Y)
    return by_x, by_y


def sum_cross(totals, got):
    half = totals[0].shape[1] // 2
    by_x, by_y = got
    first = [add(totals[0][:, :half], by_x[0]), add(totals[2][:, :half], by_x[1])]
    second = [add(totals[0][:, half:], by_y[0]), add(totals[1][:, half:], by_y[1])]
    return first, second


def send_corner(halves):
    return swap(halves[0][1], ROW_Y), swap(halves[1][1], ROW_X)


def sum_corner(halves, got, z):
    first = add(halves[0][0], got[0])
    second = add(halves[1][0], got[1])
    return to_places(jnp.concatenate([first, second], axis=1), z)


def sum_line(by_z):
    return lax.psum_scatter(by_z, "head", scatter_dimension=0)


def on_device_windows(
    tokens, d_out, modulation, frame_counts, w_qkv, w_out, w_up, w_down, table_s, table_t
):
    z = lax.axis_index("head")
    c = lax.axis_index("clip")
    place = c.astype(jnp.int32).reshape(1)
    chip = c // 2
    odd = z % 2
    mods = modulation[0]
    n_s, n_t = table_s.shape[1], table_t.shape[1]
    hot_s, hot_t = toeplitz(SWIN), toeplitz_pair(TWIN)
    fc = frame_counts

    def spatial_base(tables):
        base = jnp.einsum(
            "hab,bji->hjai", tables[:, :n_s].reshape(16, 31, 31), hot_s, precision=HIGHEST_PRECISION
        ).reshape(16, 16, 496)
        return jnp.pad(base, ((0, 0), (0, 0), (0, 16)))

    def tube_base(tables):
        base = jnp.einsum(
            "htr,rjk->hjtk", tables[:, n_s:].reshape(16, 9, 225), hot_t, precision=HIGHEST_PRECISION
        ).reshape(16, 64, 576)
        return jnp.pad(base, ((0, 0), (0, 0), (0, 64)))

    def table_rows(first, second):
        first = jnp.pad(first, ((0, 0), (0, D - n_s)))
        second = jnp.pad(second, ((0, 0), (0, 15 * D - n_t)))
        values = jnp.concatenate([first, second], axis=1).astype(BF16)
        return values.reshape(NZ, 4, 16, D).transpose(1, 0, 2, 3)

    spatial = ((1, 5, 256), 16, 16, False)
    tube = ((5, 4, 64), 5, 64, True)

    local_a0 = prep_attn(place, w_qkv, w_out, 0)
    line_a0 = line_stage(local_a0[0, 0])
    table_piece = jnp.concatenate([table_s, table_t], axis=1)
    tables = [from_z(table_piece, d) for d in (1, 2)]
    local_f0 = prep_feed(place, w_up, w_down, 0)
    local_a1 = prep_attn(place, w_qkv, w_out, 1)
    local_f1 = prep_feed(place, w_up, w_down, 1)
    line_a0, local_f0, local_a1, local_f1, tables, tokens, table_piece = sync(
        line_a0, local_f0, local_a1, local_f1, tables, tokens, table_piece
    )
    own_a0 = cross_stage(jnp.stack(line_a0))
    z_u0 = lax.all_gather(local_f0[0, 0, :128], "head")
    z_d0 = lax.all_gather(local_f0[0, 0, 128:], "head")
    tables = jnp.stack([table_piece] + tables + [from_z(table_piece, 3)])
    tables = jnp.concatenate(
        [lax.dynamic_slice_in_dim(tables, chip ^ m, 1, axis=1) for m in range(4)], axis=1
    ).reshape(16, n_s + n_t)
    base_s = spatial_base(tables)
    hidden0 = rows_to_spatial(tokens, odd)
    own_a0, hidden0, tables, base_s, z_u0 = sync(own_a0, hidden0, tables, base_s, z_u0)
    own_a0 = jnp.stack(own_a0)
    other_a0 = swap(own_a0, CORE)
    own_u0 = sides_stage(jnp.stack(others(z_u0, z)))
    own_a0, other_a0 = sync(own_a0, other_a0)
    weights_a0 = (local_a0, own_a0, other_a0)
    normed0, qkv0 = ln_qkv(hidden0, mods, weights_a0, 0)
    qkv0, own_u0, z_d0 = sync(qkv0, own_u0, z_d0)
    corner_u0 = corner_stage(own_u0)
    own_d0 = sides_stage(jnp.stack(others(z_d0, z)))
    z_a1 = lax.all_gather(local_a1[0, 0], "head")
    attended0 = attn_fwd(qkv0, base_s, fc, spatial)
    attended0, corner_u0, own_d0, z_a1 = sync(attended0, corner_u0, own_d0, z_a1)
    corner_d0 = corner_stage(own_d0)
    own_u0 = joined(own_u0, corner_u0)
    other_u0 = swap(own_u0, CORE)
    branch0, middle0, shifted0 = out_proj(attended0, weights_a0, hidden0, mods, 0)
    own_a1 = jnp.stack(others(z_a1, z))
    shifted0, corner_d0, other_u0, own_a1 = sync(shifted0, corner_d0, other_u0, own_a1)
    own_d0 = joined(own_d0, corner_d0)
    other_d0 = swap(own_d0, CORE)
    z_f1 = lax.all_gather(local_f1[0, 0], "head")
    shifted0, other_d0 = sync(shifted0, other_d0)
    own_a1 = cross_stage(own_a1)
    weights_f0 = (local_f0, own_u0, other_u0, own_d0, other_d0)
    pre0, feed0, hidden1 = ffn_fwd(shifted0, weights_f0, 0, middle0, mods, 0)
    hidden1, z_f1, own_a1, tables, d_out = sync(hidden1, z_f1, own_a1, tables, d_out)
    tubes1 = spatial_to_tubes(hidden1)
    own_a1 = jnp.stack(own_a1)
    other_a1 = swap(own_a1, CORE)
    own_f1 = cross_stage(jnp.stack(others(z_f1, z)))
    base_t = tube_base(tables)
    spatial_d = rows_to_spatial(d_out, odd)
    tubes1, other_a1, base_t, spatial_d = sync(tubes1, other_a1, base_t, spatial_d)
    weights_a1 = (local_a1, own_a1, other_a1)
    tubes_d = spatial_to_tubes(spatial_d)
    normed1, qkv1 = ln_qkv(tubes1, mods, weights_a1, 6)
    qkv1, own_f1 = sync(qkv1, own_f1)
    own_f1 = jnp.stack(own_f1)
    other_f1 = swap(own_f1, CORE)
    attended1 = attn_fwd(qkv1, base_t, fc, tube)
    branch1, middle1, shifted1 = out_proj(attended1, weights_a1, tubes1, mods, 6)
    shifted1, other_f1 = sync(shifted1, other_f1)
    weights_f1 = (local_f1, own_f1, other_f1, own_f1, other_f1)
    pre1, feed1, hidden2 = ffn_fwd(shifted1, weights_f1, 1, middle1, mods, 6)
    hidden2, tubes_d = sync(hidden2, tubes_d)
    live = lax.broadcasted_iota(jnp.int32, (1280, 1), 0) // 256 < fc[0]
    grad2 = jnp.where(live, tubes_d, 0)
    out_wins = exchange(jnp.where(live, hidden2, 0))
    f1_keep, f1_send, g_shift1 = ffn_bwd(grad2, pre1, shifted1, weights_f1, 1, mods, 6)
    f1_keep, f1_send, g_shift1, out_wins = sync(f1_keep, f1_send, g_shift1, out_wins)
    f1_got = swap(f1_send, CORE)
    g_mid1, g_att1, o1_keep, o1_send, sums_o1 = out_bwd(
        grad2, g_shift1, middle1, feed1, branch1, attended1, weights_a1, mods, 6
    )
    g_att1, f1_got = sync(g_att1, f1_got)
    total_f1 = sum_core(f1_keep, f1_got)
    g_att1, total_f1 = sync(g_att1, total_f1)
    got_f1 = send_cross(total_f1)
    g_proj1, g_base1 = attn_bwd(qkv1, g_att1, base_t, fc, tube)
    g_proj1, g_base1, got_f1 = sync(g_proj1, g_base1, got_f1)
    half_f1 = sum_cross(total_f1, got_f1)
    half_f1, g_proj1 = sync(half_f1, g_proj1)
    got_f1 = send_corner(half_f1)
    g_hid1a, g_hid1b, sums_q1 = qkv_back(
        g_proj1, weights_a1, tubes1, g_mid1, mods, 6, BF16, 2
    )
    g_hid1a, g_hid1b, g_proj1, out_wins, g_base1, got_f1 = sync(
        g_hid1a, g_hid1b, g_proj1, out_wins, g_base1, got_f1
    )
    grad1a = exchange(g_hid1a)
    z_f1 = sum_corner(half_f1, got_f1, z)
    a1_keep, a1_send = qkv_grad(g_proj1, normed1, o1_keep, o1_send, None)
    gt_t = jnp.einsum(
        "hjtk,rjk->htr",
        g_base1[:, :, :576].reshape(16, 64, 9, 64),
        hot_t,
        precision=HIGHEST_PRECISION,
    ).reshape(16, n_t)
    grad1a, z_f1, a1_keep, a1_send, gt_t, g_hid1b, out_wins = sync(
        grad1a, z_f1, a1_keep, a1_send, gt_t, g_hid1b, out_wins
    )
    grad1b = exchange(g_hid1b)
    total_a1 = sum_core(a1_keep, swap(a1_send, CORE))
    output = spatial_to_rows(from_quads(out_wins), odd)
    grad1b, total_a1, output, z_f1 = sync(grad1b, total_a1, output, z_f1)
    grad1 = from_quads(jnp.concatenate([grad1a, grad1b], axis=1))
    mine_f1 = sum_line(z_f1)
    got_a1 = send_plane(total_a1, (1, 2, 3))
    f0_keep, f0_send, g_shift0 = ffn_bwd(grad1, pre0, shifted0, weights_f0, 0, mods, 0)
    f0_keep, f0_send, g_shift0, mine_f1, got_a1 = sync(f0_keep, f0_send, g_shift0, mine_f1, got_a1)
    f0_got = swap(f0_send, CORE)
    sides_f1 = sides_stage(mine_f1[None])
    mine_a1 = sum_line(sum_plane(total_a1, got_a1, z))
    g_mid0, g_att0, o0_keep, o0_send, sums_o0 = out_bwd(
        grad1, g_shift0, middle0, feed0, branch0, attended0, weights_a0, mods, 0
    )
    g_att0, f0_got, sides_f1 = sync(g_att0, f0_got, sides_f1)
    total_f0 = sum_core(f0_keep, f0_got)
    g_att0, total_f0 = sync(g_att0, total_f0)
    got_f0 = send_cross(total_f0)
    corner_f1 = corner_stage(sides_f1)
    g_proj0, g_base0 = attn_bwd(qkv0, g_att0, base_s, fc, spatial)
    gt_s = jnp.einsum(
        "hjai,bji->hab",
        g_base0[:, :, :496].reshape(16, 16, 31, 16),
        hot_s,
        precision=HIGHEST_PRECISION,
    ).reshape(16, n_s)
    a0_keep, a0_send = qkv_grad(g_proj0, normed0, o0_keep, o0_send, table_rows(gt_s, gt_t))
    a0_keep, a0_send, got_f0, corner_f1, mine_a1, g_proj0 = sync(
        a0_keep, a0_send, got_f0, corner_f1, mine_a1, g_proj0
    )
    a0_got = swap(a0_send, CORE)
    half_f0 = sum_cross(total_f0, got_f0)
    got_f0 = send_corner(half_f0)
    own_gf1 = joined(sides_f1, corner_f1).reshape(4, 256, D)
    g_feed = finish_feed(place, own_gf1, swap(own_gf1, CORE), 1, ())
    half_f0, got_f0, a0_got, g_proj0, g_feed = sync(half_f0, got_f0, a0_got, g_proj0, g_feed)
    z_f0 = sum_corner(half_f0, got_f0, z)
    total_a0 = sum_core(a0_keep, a0_got)
    total_a0, z_f0, g_proj0 = sync(total_a0, z_f0, g_proj0)
    mine_f0 = sum_line(z_f0)
    got_a0 = send_cross(total_a0)
    grad0, sums_q0 = qkv_back(g_proj0, weights_a0, hidden0, g_mid0, mods, 0, F32, 1)
    grad0, sums_q0, got_a0 = sync(grad0, sums_q0, got_a0)
    half_a0 = sum_cross(total_a0, got_a0)
    half_a0, grad0, sums_q0 = sync(half_a0, grad0, sums_q0)
    got_a0 = send_corner(half_a0)
    sides_a1 = sides_stage(mine_a1[None])
    got_a0, sides_a1, mine_f0 = sync(got_a0, sides_a1, mine_f0)
    z_a0 = sum_corner(half_a0, got_a0, z)
    z_a0, mine_f0 = sync(z_a0, mine_f0)
    mine_a0 = sum_line(z_a0)
    own_gf0 = cross_stage(mine_f0)
    corner_a1 = corner_stage(sides_a1)
    mod_rows = jnp.concatenate(
        [
            sums_q0[0:2], sums_o0[2:3], sums_o0[0:2], sums_o0[3:4],
            sums_q1[0:2], sums_o1[2:3], sums_o1[0:2], sums_o1[3:4],
        ],
        axis=0,
    )
    mine_a0, own_gf0, corner_a1, mod_rows, grad0 = sync(mine_a0, own_gf0, corner_a1, mod_rows, grad0)
    own_ga0 = cross_stage(mine_a0)
    own_gf0 = jnp.stack(own_gf0)
    grad_tokens = spatial_to_rows(grad0, odd)
    own_ga1 = joined(sides_a1, corner_a1).reshape(4, 128, D)
    g_feed = finish_feed(place, own_gf0, swap(own_gf0, CORE), 0, g_feed)
    own_ga0, g_feed, grad_tokens, mod_rows, own_ga1 = sync(
        own_ga0, g_feed, grad_tokens, mod_rows, own_ga1
    )
    own_ga0 = jnp.stack(own_ga0)
    own_ga = jnp.concatenate([own_ga0[:, :128], own_ga1, own_ga0[:, 128:]], axis=1)
    mod_got = [from_z(mod_rows, d) for d in (1, 2, 3)]
    own_ga0 = own_ga
    g_attn = finish_attn(place, own_ga, swap(own_ga, CORE))
    tab = jnp.concatenate(
        [lax.dynamic_slice_in_dim(own_ga0, chip ^ m, 1, axis=0) for m in range(4)], axis=0
    )
    tab = tab[:, 256:272].reshape(4, 16 * D).astype(F32)
    return (
        output,
        grad_tokens,
        (mod_rows + mod_got[0] + mod_got[1] + mod_got[2])[None],
        g_attn[0],
        g_attn[1],
        g_feed[0],
        g_feed[1],
        tab[:, :n_s],
        tab[:, D : D + n_t],
    )


def solution(mesh):
    if mesh.shape["head"] == NZ and mesh.shape["clip"] == 8:
        body = on_device_windows
    else:
        body = on_device
    return jax.shard_map(
        body,
        mesh=mesh,
        in_specs=(
            P(("clip", "head"), None),
            P(("clip", "head"), None),
            P("clip", None, None),
            P("clip"),
            P(None, None, None, "head"),
            P(None, "head", None),
            P(None, None, "head"),
            P(None, "head", None),
            P("head", None),
            P("head", None),
        ),
        out_specs=(
            P(("clip", "head"), None),
            P(("clip", "head"), None),
            P("clip", None, None),
            P(None, None, None, "head"),
            P(None, "head", None),
            P(None, None, "head"),
            P(None, "head", None),
            P("head", None),
            P("head", None),
        ),
        check_vma=False,
    )
```

```python
import jax
import jax.numpy as jnp
from jax import lax
from jax.experimental import pallas as pl
from jax.experimental.pallas import tpu as pltpu
from jax.sharding import PartitionSpec as P

HD = 64
FH = 32
FW = 32
SWIN = 16
TWIN = 8
PADF = 5


EPS = 1e-06
HIGHEST_PRECISION = lax.Precision.HIGHEST
NEGATIVE = -1e30


def layer_norm(values, shift_row, scale_row):
    average = jnp.mean(values, axis=-1, keepdims=True)
    centred = values - average
    spread = jnp.mean(centred * centred, axis=-1, keepdims=True)
    return centred * lax.rsqrt(spread + EPS) * (1.0 + scale_row) + shift_row


def gelu_tanh(values):
    return jax.nn.gelu(values, approximate=True)


def window_index(side_t, side_len):
    window_size = side_t * side_len * side_len
    places = jnp.arange(window_size, dtype=jnp.int32)
    time_pos = places // (side_len * side_len)
    height_pos = places // side_len % side_len
    width_pos = places % side_len
    span_len = 2 * side_len - 1
    return (
        (time_pos[:, None] - time_pos[None, :] + side_t - 1) * span_len * span_len
        + (height_pos[:, None] - height_pos[None, :] + side_len - 1) * span_len
        + (width_pos[:, None] - width_pos[None, :] + side_len - 1)
    )


def to_windows(values, side_t, side_len):
    tail_shape = values.shape[1:]
    frames = values.shape[0] // (FH * FW)
    shaped = values.reshape(
        (frames // side_t, side_t, FH // side_len, side_len, FW // side_len, side_len) + tail_shape
    )
    axis_order = (0, 2, 4, 1, 3, 5) + tuple(range(6, 6 + len(tail_shape)))
    shaped = shaped.transpose(axis_order)
    return shaped.reshape((-1, side_t * side_len * side_len) + tail_shape)


def from_windows(values, side_t, side_len):
    tail_shape = values.shape[2:]
    blocks_high = FH // side_len
    blocks_wide = FW // side_len
    frame_groups = values.shape[0] // (blocks_high * blocks_wide)
    shaped = values.reshape(
        (frame_groups, blocks_high, blocks_wide, side_t, side_len, side_len) + tail_shape
    )
    axis_order = (0, 3, 1, 4, 2, 5) + tuple(range(6, 6 + len(tail_shape)))
    return shaped.transpose(axis_order).reshape((frame_groups * side_t * FH * FW,) + tail_shape)


def on_device(
    tokens, d_out, modulation, frame_counts, w_qkv, w_out, w_up, w_down, table_s, table_t
):
    local_rows = tokens.shape[0]
    clip_len = PADF * FH * FW
    group_clips = modulation.shape[0]
    group_rows = group_clips * clip_len
    scale_dot = HD ** (-0.5)
    my_index = lax.axis_index("head")
    first_row = my_index * local_rows
    row_ids = first_row + jnp.arange(local_rows, dtype=jnp.int32)
    clip_slots = jnp.arange(group_clips, dtype=jnp.int32)
    row_onehot = ((row_ids // clip_len)[:, None] == clip_slots[None, :]).astype(jnp.float32)
    count_float = frame_counts.astype(jnp.float32)
    row_frames = jnp.dot(row_onehot, count_float, precision=HIGHEST_PRECISION)
    row_keep = ((row_ids % clip_len // (FH * FW)).astype(jnp.float32) < row_frames).astype(
        jnp.float32
    )[:, None]
    group_ids = jnp.arange(group_rows, dtype=jnp.int32)
    group_onehot = ((group_ids // clip_len)[:, None] == clip_slots[None, :]).astype(jnp.float32)
    group_frames = jnp.dot(group_onehot, count_float, precision=HIGHEST_PRECISION)
    group_keep = (group_ids % clip_len // (FH * FW)).astype(jnp.float32) < group_frames

    def block_shape(block_id):
        if block_id == 0:
            return (1, SWIN)
        return (PADF, TWIN)

    def mod_row(slot):
        return jnp.dot(row_onehot, modulation[:, slot, :], precision=HIGHEST_PRECISION)

    def rows_in(values):
        return lax.all_gather(values, "head", axis=0, tiled=True)

    def grads_in(values):
        return lax.all_gather(values, "head", axis=0, tiled=True)

    def rows_out(full_rows, weight):
        return lax.psum_scatter(
            jnp.dot(full_rows, weight, preferred_element_type=jnp.float32).astype(jnp.bfloat16),
            "head",
            scatter_dimension=0,
            tiled=True,
        ).astype(jnp.float32)

    def grads_out(full_rows, weight, einsum_form):
        return lax.psum_scatter(
            jnp.einsum(einsum_form, full_rows, weight, preferred_element_type=jnp.float32).astype(
                jnp.bfloat16
            ),
            "head",
            scatter_dimension=0,
            tiled=True,
        ).astype(jnp.float32)

    def rows_keep(block_id):
        if block_id == 0:
            return None
        return to_windows(group_keep[:, None], PADF, TWIN)[:, :, 0]

    def shape_windows(projected, side_t, side_len):
        head_count = projected.shape[-1] // HD
        window_size = side_t * side_len * side_len
        windows = to_windows(projected, side_t, side_len)
        return windows.reshape(windows.shape[0], window_size, 3, head_count, HD)

    def shape_grad(grad_attended, side_t, side_len):
        head_count = grad_attended.shape[-1] // HD
        window_size = side_t * side_len * side_len
        windows = to_windows(grad_attended, side_t, side_len)
        return windows.reshape(windows.shape[0], window_size, head_count, HD)

    def flat_rows(windowed, side_t, side_len):
        return from_windows(windowed, side_t, side_len)

    def logits_of(queries, key_rows, table_arg, rel_index, keep_win):
        logits = (
            jnp.einsum("wqhe,wkhe->whqk", queries, key_rows, preferred_element_type=jnp.float32)
            * scale_dot
        )
        logits = logits + table_arg[:, rel_index][None]
        if keep_win is not None:
            logits = jnp.where(keep_win[:, None, None, :], logits, NEGATIVE)
        return logits

    def attend(windows, table_arg, rel_index, keep_win):
        logits = logits_of(windows[:, :, 0], windows[:, :, 1], table_arg, rel_index, keep_win)
        row_max = jnp.max(logits, axis=-1, keepdims=True)
        exponent = jnp.exp(logits - row_max)
        row_total = jnp.sum(exponent, axis=-1, keepdims=True)
        probs = exponent / row_total
        log_total = row_max + jnp.log(row_total)
        attended = jnp.einsum(
            "whqk,wkhe->wqhe",
            probs.astype(jnp.bfloat16),
            windows[:, :, 2],
            preferred_element_type=jnp.float32,
        )
        return (attended.reshape(attended.shape[0], attended.shape[1], -1), log_total)

    def attend_back(windows, grad_windows, log_total, table_arg, rel_index, keep_win):
        queries = windows[:, :, 0]
        key_rows = windows[:, :, 1]
        value_rows = windows[:, :, 2]
        logits = logits_of(queries, key_rows, table_arg, rel_index, keep_win)
        probs = jnp.exp(logits - log_total)
        grad_probs = jnp.einsum(
            "wqhe,wkhe->whqk", grad_windows, value_rows, preferred_element_type=jnp.float32
        )
        grad_values = jnp.einsum(
            "whqk,wqhe->wkhe",
            probs.astype(jnp.bfloat16),
            grad_windows,
            preferred_element_type=jnp.float32,
        )
        grad_logits = (
            probs * (grad_probs - jnp.sum(grad_probs * probs, axis=-1, keepdims=True))
        ).astype(jnp.bfloat16)
        head_count = queries.shape[2]
        table_terms = jnp.sum(grad_logits.astype(jnp.float32), axis=0).reshape(head_count, -1)
        grad_table = jax.ops.segment_sum(
            table_terms.T, rel_index.reshape(-1), num_segments=table_arg.shape[1]
        ).T
        grad_queries = (
            jnp.einsum("whqk,wkhe->wqhe", grad_logits, key_rows, preferred_element_type=jnp.float32)
            * scale_dot
        )
        grad_keys = (
            jnp.einsum("whqk,wqhe->wkhe", grad_logits, queries, preferred_element_type=jnp.float32)
            * scale_dot
        )
        grad_stack = jnp.stack([grad_queries, grad_keys, grad_values], axis=2)
        return (
            grad_stack.reshape(grad_stack.shape[0], grad_stack.shape[1], 3, head_count * HD),
            grad_table,
        )

    def forward_block(hidden, block_id):
        side_t, side_len = block_shape(block_id)
        table_local = table_s if block_id == 0 else table_t
        rel_index = window_index(side_t, side_len)
        normed = layer_norm(hidden, mod_row(6 * block_id), mod_row(6 * block_id + 1)).astype(
            jnp.bfloat16
        )
        plan = None
        normed_in = rows_in(normed)
        qkv_use, out_use, table_use = (w_qkv[block_id], w_out[block_id], table_local)
        keep_win = rows_keep(block_id)
        projected = jnp.einsum(
            "gd,cde->gce", normed_in, qkv_use, preferred_element_type=jnp.float32
        ).astype(jnp.bfloat16)
        windows = shape_windows(projected, side_t, side_len)
        attended_win, log_total = attend(windows, table_use, rel_index, keep_win)
        attended = flat_rows(attended_win, side_t, side_len).astype(jnp.bfloat16)
        branch = rows_out(attended, out_use)
        middle = hidden + mod_row(6 * block_id + 2) * branch
        shifted = layer_norm(middle, mod_row(6 * block_id + 3), mod_row(6 * block_id + 4)).astype(
            jnp.bfloat16
        )
        up_full, down_full = (
            lax.all_gather(w_up[block_id], "head", axis=1, tiled=True),
            lax.all_gather(w_down[block_id], "head", axis=0, tiled=True),
        )
        pre_gelu = jnp.dot(shifted, up_full, preferred_element_type=jnp.float32)
        activated = gelu_tanh(pre_gelu).astype(jnp.bfloat16)
        feed_out = jnp.dot(activated, down_full, preferred_element_type=jnp.float32)
        mlp_state = (shifted, pre_gelu, activated, up_full, down_full)
        result = middle + mod_row(6 * block_id + 5) * feed_out
        attn_state = (
            normed_in,
            projected,
            log_total,
            attended,
            qkv_use,
            out_use,
            table_use,
            keep_win,
            plan,
        )
        saved_state = (hidden, attn_state, branch, middle, feed_out, mlp_state)
        return (saved_state, result)

    def backward_block(saved_state, grad_result, block_id):
        hidden, attn_state, branch, middle, feed_out, mlp_state = saved_state
        normed_in, projected, log_total, attended, qkv_use, out_use, table_use, keep_win, plan = (
            attn_state
        )
        shifted_in, pre_gelu, activated, up_weight, down_weight = mlp_state
        side_t, side_len = block_shape(block_id)
        rel_index = window_index(side_t, side_len)
        grad_feed = (grad_result * mod_row(6 * block_id + 5)).astype(jnp.bfloat16)
        grad_gate_mlp = grad_result * feed_out
        grad_down = jnp.einsum(
            "gf,gd->fd", activated, grad_feed, preferred_element_type=jnp.float32
        )
        grad_activated = jnp.einsum(
            "gd,fd->gf", grad_feed, down_weight, preferred_element_type=jnp.float32
        )
        grad_pre = jax.vjp(gelu_tanh, pre_gelu)[1](grad_activated)[0].astype(jnp.bfloat16)
        grad_up = jnp.einsum("gd,gf->df", shifted_in, grad_pre, preferred_element_type=jnp.float32)
        grad_shifted = jnp.einsum(
            "gf,df->gd", grad_pre, up_weight, preferred_element_type=jnp.float32
        )
        grad_up, grad_down = (
            lax.psum_scatter(
                grad_up.astype(jnp.bfloat16), "head", scatter_dimension=1, tiled=True
            ).astype(jnp.float32),
            lax.psum_scatter(
                grad_down.astype(jnp.bfloat16), "head", scatter_dimension=0, tiled=True
            ).astype(jnp.float32),
        )
        unused_mid, pull_second = jax.vjp(
            layer_norm, middle, mod_row(6 * block_id + 3), mod_row(6 * block_id + 4)
        )
        grad_mid_norm, grad_shift_mlp, grad_scale_mlp = pull_second(grad_shifted)
        grad_middle = grad_result + grad_mid_norm
        grad_branch = (grad_middle * mod_row(6 * block_id + 2)).astype(jnp.bfloat16)
        grad_gate_att = grad_middle * branch
        branch_in = grads_in(grad_branch)
        grad_wout = jnp.einsum("ge,gd->ed", attended, branch_in, preferred_element_type=jnp.float32)
        grad_attended = jnp.einsum(
            "gd,ed->ge", branch_in, out_use, preferred_element_type=jnp.float32
        ).astype(jnp.bfloat16)
        windows = shape_windows(projected, side_t, side_len)
        grad_windows = shape_grad(grad_attended, side_t, side_len)
        grad_stack, grad_table = attend_back(
            windows, grad_windows, log_total, table_use, rel_index, keep_win
        )
        grad_projected = flat_rows(grad_stack, side_t, side_len).astype(jnp.bfloat16)
        grad_qkv = jnp.einsum(
            "gd,gce->cde", normed_in, grad_projected, preferred_element_type=jnp.float32
        )
        grad_normed = grads_out(grad_projected, qkv_use, "gce,cde->gd")
        unused_hid, pull_first = jax.vjp(
            layer_norm, hidden, mod_row(6 * block_id), mod_row(6 * block_id + 1)
        )
        grad_hid_norm, grad_shift_att, grad_scale_att = pull_first(grad_normed)
        grad_hidden = grad_middle + grad_hid_norm
        mod_terms = jnp.stack(
            [
                grad_shift_att,
                grad_scale_att,
                grad_gate_att,
                grad_shift_mlp,
                grad_scale_mlp,
                grad_gate_mlp,
            ],
            axis=1,
        )
        grad_mods = jnp.einsum("rc,rke->cke", row_onehot, mod_terms, precision=HIGHEST_PRECISION)
        return (grad_hidden, grad_mods, (grad_qkv, grad_wout, grad_up, grad_down, grad_table))

    hidden_first = tokens.astype(jnp.float32)
    saved_first, hidden_second = forward_block(hidden_first, 0)
    saved_second, hidden_last = forward_block(hidden_second, 1)
    output = (hidden_last * row_keep).astype(jnp.bfloat16)
    grad_second, mods_second, weights_second = backward_block(
        saved_second, d_out.astype(jnp.float32) * row_keep, 1
    )
    grad_first, mods_first, weights_first = backward_block(saved_first, grad_second, 0)
    grad_modulation = lax.psum(
        jnp.concatenate([mods_first, mods_second], axis=1).astype(jnp.bfloat16), "head"
    ).astype(jnp.float32)
    summed = (
        lax.psum(
            jnp.stack([weights_first[0], weights_second[0]]).astype(jnp.bfloat16), "clip"
        ).astype(jnp.float32),
        lax.psum(
            jnp.stack([weights_first[1], weights_second[1]]).astype(jnp.bfloat16), "clip"
        ).astype(jnp.float32),
        lax.psum(
            jnp.stack([weights_first[2], weights_second[2]]).astype(jnp.bfloat16), "clip"
        ).astype(jnp.float32),
        lax.psum(
            jnp.stack([weights_first[3], weights_second[3]]).astype(jnp.bfloat16), "clip"
        ).astype(jnp.float32),
        lax.psum(weights_first[4].astype(jnp.bfloat16), "clip").astype(jnp.float32),
        lax.psum(weights_second[4].astype(jnp.bfloat16), "clip").astype(jnp.float32),
    )
    return (
        output,
        grad_first,
        grad_modulation,
        summed[0],
        summed[1],
        summed[2],
        summed[3],
        summed[4],
        summed[5],
    )


F32 = jnp.float32
BF16 = jnp.bfloat16
VMEM_LIMIT = 58 * 1024 * 1024
NZ = 4
D = 1024
HPZ = 4
CONST = pl.Buffered(1)


def dot_nn(a, b):
    return lax.dot_general(a, b, (((1,), (0,)), ((), ())), preferred_element_type=F32)


def dot_nt(a, b):
    return lax.dot_general(a, b, (((1,), (1,)), ((), ())), preferred_element_type=F32)


def dot_tn(a, b):
    return lax.dot_general(a, b, (((0,), (0,)), ((), ())), preferred_element_type=F32)


def call(kernel, name, grid, in_specs, out_specs, out_shape, scratch, flops, nbytes):
    return pl.pallas_call(
        kernel,
        name=name,
        grid=grid,
        in_specs=in_specs,
        out_specs=out_specs,
        out_shape=out_shape,
        scratch_shapes=scratch,
        compiler_params=pltpu.CompilerParams(
            dimension_semantics=("arbitrary",) * len(grid), vmem_limit_bytes=VMEM_LIMIT
        ),
        cost_estimate=pl.CostEstimate(
            flops=flops // 4, bytes_accessed=nbytes // 4, transcendentals=0
        ),
    )


def full(shape):
    return pl.BlockSpec(shape, lambda *ids: (0,) * len(shape), pipeline_mode=CONST)


def chunk_rows(i, size):
    return pl.ds(pl.multiple_of(i * size, size), size)


def ln_stats(x):
    mean = jnp.mean(x, axis=-1, keepdims=True)
    centred = x - mean
    rstd = lax.rsqrt(jnp.mean(centred * centred, axis=-1, keepdims=True) + EPS)
    return centred * rstd, rstd


def ln_back(grad, hat, rstd, scale):
    gh = grad * (1.0 + scale)
    m1 = jnp.mean(gh, axis=-1, keepdims=True)
    m2 = jnp.mean(gh * hat, axis=-1, keepdims=True)
    return rstd * (gh - m1 - hat * m2)


def piece_specs(k, row, count):
    tail = (count, D)
    return [
        pl.BlockSpec((2, 4) + tail, lambda d: (0, 0, row, 0), pipeline_mode=CONST),
        pl.BlockSpec((4, 1) + tail, lambda d: (0, jnp.maximum(d - 1, 0), row, 0)),
        pl.BlockSpec((4, 1) + tail, lambda d: (0, jnp.maximum(d - 1, 0), row, 0)),
    ]


def by_offset(d, body, local_ref, own_ref, other_ref):
    @pl.when(d == 0)
    def _():
        body(lambda m, r, n: local_ref[0, m, r : r + n, :], lambda m, r, n: local_ref[1, m, r : r + n, :])

    @pl.when(d > 0)
    def _():
        body(lambda m, r, n: own_ref[m, 0, r : r + n, :], lambda m, r, n: other_ref[m, 0, r : r + n, :])


def head_rows(own, other, row):
    parts = []
    for m in range(4):
        parts += [own(m, row, 32), other(m, row, 32)]
    return jnp.concatenate(parts, axis=0)


def pair_rows(first, second):
    return jnp.concatenate([get(m) for get in (first, second) for m in range(4)], axis=0)


def feed_specs(down_block):
    def spec(block):
        return pl.BlockSpec((4, 1, 128, D), lambda d: (0, jnp.maximum(d - 1, 0), block, 0))

    return [full((2, 4, 256, D)), spec(0), spec(0), spec(down_block), spec(down_block)]


def feed_by_offset(d, body, l_ref, wu_ref, vu_ref, wd_ref, vd_ref):
    @pl.when(d == 0)
    def _():
        body(
            lambda: pair_rows(lambda m: l_ref[0, m, 0:128], lambda m: l_ref[1, m, 0:128]),
            lambda: pair_rows(lambda m: l_ref[0, m, 128:256], lambda m: l_ref[1, m, 128:256]),
        )

    @pl.when(d > 0)
    def _():
        body(
            lambda: pair_rows(lambda m: wu_ref[m, 0], lambda m: vu_ref[m, 0]),
            lambda: pair_rows(lambda m: wd_ref[m, 0], lambda m: vd_ref[m, 0]),
        )


def ln_qkv(hidden, mods, weights, base):
    rows = hidden.shape[0]
    step = 640

    def kernel(h_ref, m_ref, l_ref, w_ref, v_ref, normed_ref, qkv_ref):
        d = pl.program_id(0)

        @pl.when(d == 0)
        def _():
            def body(i, carry):
                sl = chunk_rows(i, step)
                hat, _ = ln_stats(h_ref[sl, :].astype(F32))
                normed_ref[sl, :] = (
                    hat * (1.0 + m_ref[base + 1 : base + 2, :]) + m_ref[base : base + 1, :]
                ).astype(BF16)
                return carry

            lax.fori_loop(0, rows // step, body, 0)

        def work(own, other):
            for t in range(3):
                qkv_ref[:, t * 256 : (t + 1) * 256] = dot_nt(
                    normed_ref[...], head_rows(own, other, t * 32)
                ).astype(BF16)

        by_offset(d, work, l_ref, w_ref, v_ref)

    return call(
        kernel,
        "ln_qkv",
        (NZ,),
        [full((rows, D)), full((12, D))] + piece_specs(128, 0, 96),
        [full((rows, D)), pl.BlockSpec((rows, 768), lambda z: (0, z))],
        [jax.ShapeDtypeStruct((rows, D), BF16), jax.ShapeDtypeStruct((rows, 3 * D), BF16)],
        [],
        2 * rows * D * 3 * D,
        rows * D * 12 + 6 * D * D,
    )(hidden, mods, *weights)


def build_bias(base_ref, bias_ref, fc_ref, slides, width, lanes_step):
    rows_step = width // slides
    for h in range(HPZ):
        for s in range(slides):
            off = (slides - 1 - s) * lanes_step
            tile = base_ref[h, :, off : off + width]
            if fc_ref is not None:
                tile = jnp.where(s < fc_ref[0], tile, NEGATIVE)
            bias_ref[h, s * rows_step : (s + 1) * rows_step, :] = tile


def window_view(values, kind):
    parts, count, size = kind[0]
    return values.reshape(parts, count, size, values.shape[-1])


def attn_fwd(qkv, base, fc, kind):
    (parts, count, size), slides, lanes_step, masked = kind
    rows, width = qkv.shape[0], parts * size
    r_step, lanes = base.shape[1], base.shape[2]

    def kernel(x_ref, b_ref, fc_ref, o_ref, bias_ref):
        build_bias(b_ref, bias_ref, fc_ref if masked else None, slides, width, lanes_step)

        def one(w, carry):
            def cut(col):
                return x_ref[:, w, :, col : col + HD].reshape(width, HD)

            scores, probs = [], []
            for h in range(HPZ):
                scores.append(dot_nt(cut(256 + h * HD), cut(h * HD) * 0.125) + bias_ref[h])
            for h in range(HPZ):
                expo = jnp.exp(scores[h] - jnp.max(scores[h], axis=0, keepdims=True))
                inv = 1.0 / jnp.sum(expo, axis=0, keepdims=True)
                probs.append((expo * inv).astype(BF16))
            for h in range(HPZ):
                got = dot_tn(probs[h], cut(512 + h * HD)).astype(BF16)
                o_ref[:, w, :, h * HD : (h + 1) * HD] = got.reshape(parts, size, HD)
            return carry

        lax.fori_loop(0, count, one, 0)

    return call(
        kernel,
        "attn_fwd",
        (NZ,),
        [
            pl.BlockSpec((parts, count, size, 768), lambda z: (0, 0, 0, z)),
            pl.BlockSpec((HPZ, r_step, lanes), lambda z: (z, 0, 0)),
            pl.BlockSpec(memory_space=pltpu.SMEM),
        ],
        pl.BlockSpec((parts, count, size, 256), lambda z: (0, 0, 0, z)),
        jax.ShapeDtypeStruct((parts, count, size, D), BF16),
        [pltpu.VMEM((HPZ, width, width), F32)],
        count * 16 * width * width * HD * 16,
        rows * D * 8,
    )(window_view(qkv, kind), base, fc).reshape(rows, D)


def attn_bwd(qkv, grad_att, base, fc, kind):
    (parts, count, size), slides, lanes_step, masked = kind
    rows, width = qkv.shape[0], parts * size
    r_step, lanes = base.shape[1], base.shape[2]

    def kernel(x_ref, d_ref, b_ref, fc_ref, o_ref, gb_ref, bias_ref, acc_ref):
        build_bias(b_ref, bias_ref, fc_ref if masked else None, slides, width, lanes_step)
        acc_ref[...] = jnp.zeros_like(acc_ref)

        def one(w, carry):
            def cut(ref, col):
                return ref[:, w, :, col : col + HD].reshape(width, HD)

            def put(col, value):
                o_ref[:, w, :, col : col + HD] = value.astype(BF16).reshape(parts, size, HD)

            q = [cut(x_ref, h * HD) * 0.125 for h in range(HPZ)]
            k = [cut(x_ref, 256 + h * HD) for h in range(HPZ)]
            da = [cut(d_ref, h * HD) for h in range(HPZ)]
            score = [dot_nt(k[h], q[h]) + bias_ref[h] for h in range(HPZ)]
            dp = [dot_nt(cut(x_ref, 512 + h * HD), da[h]) for h in range(HPZ)]
            probs, dl = [], []
            for h in range(HPZ):
                expo = jnp.exp(score[h] - jnp.max(score[h], axis=0, keepdims=True))
                inv = 1.0 / jnp.sum(expo, axis=0, keepdims=True)
                p = expo * inv
                row = jnp.sum(dp[h] * p, axis=0, keepdims=True)
                g = (p * (dp[h] - row)).astype(BF16)
                acc_ref[h] += g.astype(F32)
                probs.append(p.astype(BF16))
                dl.append(g)
            for h in range(HPZ):
                put(h * HD, dot_tn(dl[h], k[h]) * 0.125)
                put(256 + h * HD, dot_nn(dl[h], q[h]))
                put(512 + h * HD, dot_nn(probs[h], da[h]))
            return carry

        lax.fori_loop(0, count, one, 0)
        gb_ref[...] = jnp.zeros_like(gb_ref)
        for h in range(HPZ):
            for s in range(slides):
                off = (slides - 1 - s) * lanes_step
                gb_ref[h, :, off : off + width] += acc_ref[h, s * r_step : (s + 1) * r_step, :]

    xspec = pl.BlockSpec((parts, count, size, 768), lambda z: (0, 0, 0, z))
    bspec = pl.BlockSpec((HPZ, r_step, lanes), lambda z: (z, 0, 0))
    proj, strips = call(
        kernel,
        "attn_bwd",
        (NZ,),
        [
            xspec,
            pl.BlockSpec((parts, count, size, 256), lambda z: (0, 0, 0, z)),
            bspec,
            pl.BlockSpec(memory_space=pltpu.SMEM),
        ],
        [xspec, bspec],
        [
            jax.ShapeDtypeStruct((parts, count, size, 3 * D), BF16),
            jax.ShapeDtypeStruct(base.shape, F32),
        ],
        [pltpu.VMEM((HPZ, width, width), F32), pltpu.VMEM((HPZ, width, width), F32)],
        count * 16 * width * width * HD * 40,
        rows * D * 16,
    )(window_view(qkv, kind), window_view(grad_att, kind), base, fc)
    return proj.reshape(rows, 3 * D), strips


def out_specs_of(row_block):
    return [
        pl.BlockSpec((2, 4, 32, D), lambda i: (0, 0, row_block, 0), pipeline_mode=CONST),
        pl.BlockSpec((4, 3, 32, D), lambda i: (0, 0, row_block, 0), pipeline_mode=CONST),
        pl.BlockSpec((4, 3, 32, D), lambda i: (0, 0, row_block, 0), pipeline_mode=CONST),
    ]


def out_rows(d, l_ref, w_ref, v_ref):
    if d == 0:
        return head_rows(
            lambda m, r, n: l_ref[0, m, :, :], lambda m, r, n: l_ref[1, m, :, :], 0
        )
    return head_rows(
        lambda m, r, n: w_ref[m, d - 1, :, :], lambda m, r, n: v_ref[m, d - 1, :, :], 0
    )


def out_proj(attended, weights, hidden, mods, base):
    rows = attended.shape[0]
    step = 256

    def kernel(a_ref, l_ref, w_ref, v_ref, h_ref, m_ref, br_ref, mid_ref, sh_ref):
        branch = jnp.zeros((step, D), F32)
        for d in range(NZ):
            branch += dot_nn(a_ref[:, d * 256 : (d + 1) * 256], out_rows(d, l_ref, w_ref, v_ref))
        br_ref[...] = branch.astype(BF16)
        middle = h_ref[...].astype(F32) + m_ref[base + 2 : base + 3, :] * branch
        mid_ref[...] = middle
        hat, _ = ln_stats(middle)
        sh_ref[...] = (
            hat * (1.0 + m_ref[base + 4 : base + 5, :]) + m_ref[base + 3 : base + 4, :]
        ).astype(BF16)

    tile = pl.BlockSpec((step, D), lambda i: (i, 0))
    return call(
        kernel,
        "out_proj",
        (rows // step,),
        [tile] + out_specs_of(3) + [tile, full((12, D))],
        [tile, tile, tile],
        [
            jax.ShapeDtypeStruct((rows, D), BF16),
            jax.ShapeDtypeStruct((rows, D), F32),
            jax.ShapeDtypeStruct((rows, D), BF16),
        ],
        [],
        2 * rows * D * D,
        rows * D * 14 + 2 * D * D,
    )(attended, *weights, hidden, mods)


GELU_C = 0.7978845608028654
GELU_A = 0.044715


def gelu_of(x):
    return 0.5 * x * (1.0 + jnp.tanh(GELU_C * (x + GELU_A * x * x * x)))


def gelu_both(x):
    x2 = x * x
    th = jnp.tanh(GELU_C * (x + GELU_A * x * x2))
    half = 0.5 * (1.0 + th)
    slope = half + 0.5 * x * (1.0 - th * th) * (GELU_C * (1.0 + 3.0 * GELU_A * x2))
    return x * half, slope


def ffn_fwd(shifted, weights, down_block, middle, mods, base):
    rows = shifted.shape[0]
    step = 640

    def kernel(x_ref, *refs):
        parts, (mid_ref, m_ref, pre_ref, feed_ref, nx_ref, acc_ref) = refs[:5], refs[5:]
        z = pl.program_id(0)

        def work(up, down):
            def body(i, carry):
                sl = chunk_rows(i, step)
                pre = dot_nt(x_ref[sl, :], up())
                pre_ref[sl, :] = pre.astype(BF16)
                part = dot_nn(gelu_of(pre).astype(BF16), down())

                @pl.when(z == 0)
                def _():
                    acc_ref[sl, :] = part

                @pl.when((z > 0) & (z < NZ - 1))
                def _():
                    acc_ref[sl, :] += part

                @pl.when(z == NZ - 1)
                def _():
                    feed = acc_ref[sl, :] + part
                    feed_ref[sl, :] = feed.astype(BF16)
                    nx_ref[sl, :] = (
                        mid_ref[sl, :] + m_ref[base + 5 : base + 6, :] * feed
                    ).astype(BF16)

                return carry

            lax.fori_loop(0, rows // step, body, 0)

        feed_by_offset(z, work, *parts)

    return call(
        kernel,
        "ffn_fwd",
        (NZ,),
        [full((rows, D))] + feed_specs(down_block) + [full((rows, D)), full((12, D))],
        [pl.BlockSpec((rows, D), lambda z: (0, z)), full((rows, D)), full((rows, D))],
        [
            jax.ShapeDtypeStruct((rows, 4 * D), BF16),
            jax.ShapeDtypeStruct((rows, D), BF16),
            jax.ShapeDtypeStruct((rows, D), BF16),
        ],
        [pltpu.VMEM((rows, D), F32)],
        16 * rows * D * D,
        rows * D * 20 + 16 * D * D,
    )(shifted, *weights, middle, mods)


def ffn_bwd(grad, pre, shifted, weights, down_block, mods, base):
    rows = grad.shape[0]
    step = 640

    def kernel(g_ref, p_ref, x_ref, *refs):
        parts, refs = refs[:5], refs[5:]
        m_ref, keep_ref, send_ref, gs_ref, gf_ref, act_ref, gp_ref = refs
        z = pl.program_id(0)

        @pl.when(z == 0)
        def _():
            def body(i, carry):
                sl = chunk_rows(i, step)
                gf_ref[sl, :] = (
                    g_ref[sl, :].astype(F32) * m_ref[base + 5 : base + 6, :]
                ).astype(BF16)
                gs_ref[sl, :] = jnp.zeros((step, D), F32)
                return carry

            lax.fori_loop(0, rows // step, body, 0)

        def work(up, down):
            def body(i, carry):
                sl = chunk_rows(i, step)
                back = dot_nt(gf_ref[sl, :], down())
                act, slope = gelu_both(p_ref[sl, :].astype(F32))
                act_ref[sl, :] = act.astype(BF16)
                gpre = (back * slope).astype(BF16)
                gp_ref[sl, :] = gpre
                part = dot_nn(gpre, up())
                gs_ref[sl, :] += part
                return carry

            lax.fori_loop(0, rows // step, body, 0)

        feed_by_offset(z, work, *parts)
        for j, out_ref in enumerate((keep_ref, send_ref)):
            cols = slice(j * 512, (j + 1) * 512)
            gd = dot_tn(act_ref[:, cols], gf_ref[...]).astype(BF16)
            gu = dot_tn(gp_ref[:, cols], x_ref[...]).astype(BF16)
            out_ref[:, 0, 0:128] = gu.reshape(4, 128, D)
            out_ref[:, 0, 128:256] = gd.reshape(4, 128, D)

    gspec = pl.BlockSpec((4, 1, 256, D), lambda z: (0, z, 0, 0))
    gshape = jax.ShapeDtypeStruct((4, NZ, 256, D), BF16)
    return call(
        kernel,
        "ffn_bwd",
        (NZ,),
        [
            full((rows, D)),
            pl.BlockSpec((rows, D), lambda z: (0, z)),
            full((rows, D)),
        ]
        + feed_specs(down_block)
        + [full((12, D))],
        [gspec, gspec, full((rows, D))],
        [gshape, gshape, jax.ShapeDtypeStruct((rows, D), F32)],
        [pltpu.VMEM((rows, D), BF16)] * 3,
        32 * rows * D * D,
        rows * D * 16 + 32 * D * D,
    )(grad, pre, shifted, *weights, mods)


def split_heads(value, keep_ref, send_ref, d, row):
    for m in range(4):
        keep_ref[m, d, row : row + 32] = value[m * 64 : m * 64 + 32]
        send_ref[m, d, row : row + 32] = value[m * 64 + 32 : m * 64 + 64]


def out_bwd(grad, grad_shifted, middle, feed, branch, attended, weights, mods, base):
    rows = grad.shape[0]
    step = 256
    steps = rows // step

    def kernel(
        g_ref, gs_ref, mid_ref, f_ref, b_ref, a_ref, l_ref, w_ref, v_ref, m_ref, gm_ref, ga_ref,
        keep_ref, send_ref, s_ref, gb_ref,
    ):
        i = pl.program_id(0)

        @pl.when(i == 0)
        def _():
            s_ref[...] = jnp.zeros_like(s_ref)

        g = g_ref[...].astype(F32)
        gs = gs_ref[...]
        hat, rstd = ln_stats(mid_ref[...])
        gm = g + ln_back(gs, hat, rstd, m_ref[base + 4 : base + 5, :])
        gm_ref[...] = gm
        s_ref[0:1, :] += jnp.sum(gs, axis=0, keepdims=True)
        s_ref[1:2, :] += jnp.sum(gs * hat, axis=0, keepdims=True)
        s_ref[2:3, :] += jnp.sum(gm * b_ref[...].astype(F32), axis=0, keepdims=True)
        s_ref[3:4, :] += jnp.sum(g * f_ref[...].astype(F32), axis=0, keepdims=True)
        gb = (gm * m_ref[base + 2 : base + 3, :]).astype(BF16)
        gb_ref[chunk_rows(i, step), :] = gb
        for d in range(NZ):
            ga_ref[:, d * 256 : (d + 1) * 256] = dot_nt(
                gb, out_rows(d, l_ref, w_ref, v_ref)
            ).astype(BF16)

        @pl.when(i == steps - 1)
        def _():
            for d in range(NZ):
                gw = dot_tn(a_ref[:, d * 256 : (d + 1) * 256], gb_ref[...]).astype(BF16)
                split_heads(gw, keep_ref, send_ref, d, 0)

    tile = pl.BlockSpec((step, D), lambda i: (i, 0))
    gshape = jax.ShapeDtypeStruct((4, NZ, 32, D), BF16)
    return call(
        kernel,
        "out_bwd",
        (steps,),
        [tile, tile, tile, tile, tile, full((rows, D))] + out_specs_of(3) + [full((12, D))],
        [tile, tile, full(gshape.shape), full(gshape.shape), full((8, D))],
        [
            jax.ShapeDtypeStruct((rows, D), F32),
            jax.ShapeDtypeStruct((rows, D), BF16),
            gshape,
            gshape,
            jax.ShapeDtypeStruct((8, D), F32),
        ],
        [pltpu.VMEM((rows, D), BF16)],
        4 * rows * D * D,
        rows * D * 24 + 4 * D * D,
    )(grad, grad_shifted, middle, feed, branch, attended, *weights, mods)


def qkv_back(grad_proj, weights, hidden, grad_middle, mods, base, out_dtype, pieces):
    rows = hidden.shape[0]
    step = 640

    cols = D // pieces

    def kernel(p_ref, l_ref, w_ref, v_ref, h_ref, gm_ref, m_ref, *refs):
        gh_refs, (s_ref, acc_ref) = refs[:pieces], refs[pieces:]
        z = pl.program_id(0)

        @pl.when(z == 0)
        def _():
            acc_ref[...] = jnp.zeros_like(acc_ref)
            s_ref[...] = jnp.zeros_like(s_ref)

        def work(own, other):
            def body(i, carry):
                sl = chunk_rows(i, step)
                rows_of = jnp.concatenate([head_rows(own, other, t * 32) for t in range(3)], axis=0)
                acc_ref[sl, :] += dot_nn(p_ref[sl, :], rows_of)
                return carry

            lax.fori_loop(0, rows // step, body, 0)

        by_offset(z, work, l_ref, w_ref, v_ref)

        @pl.when(z == NZ - 1)
        def _():
            def tail(n, carry):
                sl = chunk_rows(n, 256)
                gn = acc_ref[sl, :]
                hat, rstd = ln_stats(h_ref[sl, :].astype(F32))
                gh = gm_ref[sl, :] + ln_back(gn, hat, rstd, m_ref[base + 1 : base + 2, :])
                for i, gh_ref in enumerate(gh_refs):
                    gh_ref[sl, :] = gh[:, i * cols : (i + 1) * cols].astype(out_dtype)
                s_ref[0:1, :] += jnp.sum(gn, axis=0, keepdims=True)
                s_ref[1:2, :] += jnp.sum(gn * hat, axis=0, keepdims=True)
                return carry

            lax.fori_loop(0, rows // 256, tail, 0)

    return call(
        kernel,
        "qkv_back",
        (NZ,),
        [pl.BlockSpec((rows, 768), lambda z: (0, z))]
        + piece_specs(128, 0, 96)
        + [full((rows, D)), full((rows, D)), full((12, D))],
        [full((rows, cols))] * pieces + [full((8, D))],
        [jax.ShapeDtypeStruct((rows, cols), out_dtype)] * pieces
        + [jax.ShapeDtypeStruct((8, D), F32)],
        [pltpu.VMEM((rows, D), F32)],
        6 * rows * D * D,
        rows * D * 20 + 6 * D * D,
    )(grad_proj, *weights, hidden, grad_middle, mods)


def qkv_grad(grad_proj, normed, out_keep, out_send, table_rows, apart=False):
    rows = normed.shape[0]
    k = 128 if table_rows is None else 144

    def kernel(p_ref, n_ref, ok_ref, os_ref, *rest):
        if apart:
            keep_ref, send_refs = rest[-5], rest[-4:]
        else:
            keep_ref, send_ref = rest[-2:]
            send_refs = [send_ref.at[m : m + 1] for m in range(4)]
        for t in range(3):
            gw = dot_tn(p_ref[:, t * 256 : (t + 1) * 256], n_ref[...]).astype(BF16)
            for m in range(4):
                keep_ref[m, 0, t * 32 : t * 32 + 32] = gw[m * 64 : m * 64 + 32]
                send_refs[m][0, 0, t * 32 : t * 32 + 32] = gw[m * 64 + 32 : m * 64 + 64]
        keep_ref[:, :, 96:128] = ok_ref[...]
        for m in range(4):
            send_refs[m][0, :, 96:128] = os_ref[m]
        if table_rows is not None:
            keep_ref[:, :, 128:144] = rest[0][...]
            for m in range(4):
                send_refs[m][0, :, 128:144] = rest[0][m]

    gspec = pl.BlockSpec((4, 1, k, D), lambda z: (0, z, 0, 0))
    ospec = pl.BlockSpec((4, 1, 32, D), lambda z: (0, z, 0, 0))
    tspec = pl.BlockSpec((4, 1, 16, D), lambda z: (0, z, 0, 0))
    gshape = jax.ShapeDtypeStruct((4, NZ, k, D), BF16)
    extra = () if table_rows is None else (table_rows,)
    sends, send_shapes = [gspec], [gshape]
    if apart:
        sends = [pl.BlockSpec((1, 1, k, D), lambda z: (0, z, 0, 0))] * 4
        send_shapes = [jax.ShapeDtypeStruct((1, NZ, k, D), BF16)] * 4
    return call(
        kernel,
        "qkv_grad",
        (NZ,),
        [pl.BlockSpec((rows, 768), lambda z: (0, z)), full((rows, D)), ospec, ospec]
        + [tspec] * len(extra),
        [gspec] + sends,
        [gshape] + send_shapes,
        [],
        6 * rows * D * D,
        rows * D * 8 + 8 * D * D,
    )(grad_proj, normed, out_keep, out_send, *extra)


def place_call(kernel, name, in_specs, out_specs, out_shape, scratch, nbytes, aliases):
    return pl.pallas_call(
        kernel,
        name=name,
        grid_spec=pltpu.PrefetchScalarGridSpec(
            num_scalar_prefetch=1,
            grid=(8,),
            in_specs=in_specs,
            out_specs=out_specs,
            scratch_shapes=scratch,
        ),
        out_shape=out_shape,
        input_output_aliases=aliases,
        compiler_params=pltpu.CompilerParams(
            dimension_semantics=("arbitrary",), vmem_limit_bytes=VMEM_LIMIT
        ),
        cost_estimate=pl.CostEstimate(flops=0, bytes_accessed=nbytes, transcendentals=0),
    )


def rows_at(place):
    return pl.ds(pl.multiple_of(place * 32, 32), 32)


def prep_attn(place, w_qkv, w_out, b):
    def kernel(c_ref, q_ref, o_ref, out_ref, t_ref):
        r = pl.program_id(0)

        @pl.when(r == 0)
        def _():
            for t in range(3):
                t_ref[t] = q_ref[0, t].T

        at = rows_at(c_ref[0] ^ r)
        for t in range(3):
            out_ref[0, 0, t * 32 : (t + 1) * 32, :] = t_ref[t, at, :]
        out_ref[0, 0, 96:128, :] = o_ref[0, at, :]

    return place_call(
        kernel,
        "prep_attn",
        [
            pl.BlockSpec((1, 3, D, 256), lambda r, c: (b, 0, 0, 0)),
            pl.BlockSpec((1, 256, D), lambda r, c: (b, 0, 0)),
        ],
        pl.BlockSpec((1, 1, 128, D), lambda r, c: (r % 2, r // 2, 0, 0)),
        jax.ShapeDtypeStruct((2, 4, 128, D), BF16),
        [pltpu.VMEM((3, 256, D), BF16)],
        4 * D * D,
        {},
    )(place, w_qkv, w_out)


def prep_feed(place, w_up, w_down, b):
    def kernel(c_ref, u_ref, d_ref, out_ref):
        out_ref[0, 0, 0:128, :] = u_ref[0].T
        out_ref[0, 0, 128:256, :] = d_ref[0]

    return place_call(
        kernel,
        "prep_feed",
        [
            pl.BlockSpec((1, D, 128), lambda r, c: (b, 0, c[0] ^ r)),
            pl.BlockSpec((1, 128, D), lambda r, c: (b, c[0] ^ r, 0)),
        ],
        pl.BlockSpec((1, 1, 256, D), lambda r, c: (r % 2, r // 2, 0, 0)),
        jax.ShapeDtypeStruct((2, 4, 256, D), BF16),
        [],
        8 * D * D,
        {},
    )(place, w_up, w_down)


def finish_attn(place, own, other):
    def kernel(c_ref, own_ref, oth_ref, gq_ref, go_ref, t_ref):
        r = pl.program_id(0)
        at = rows_at(c_ref[0] ^ r)

        def store(ref):
            for b in range(2):
                row = 128 * b
                for t in range(3):
                    t_ref[b, t, at, :] = ref[0, row + t * 32 : row + (t + 1) * 32, :]
                go_ref[b, at, :] = ref[0, row + 96 : row + 128, :].astype(F32)

        @pl.when(r % 2 == 0)
        def _():
            store(own_ref)

        @pl.when(r % 2 == 1)
        def _():
            store(oth_ref)

        @pl.when(r == 7)
        def _():
            for b in range(2):
                for t in range(3):
                    gq_ref[b, t] = t_ref[b, t].T.astype(F32)

    piece = pl.BlockSpec((1, 256, D), lambda r, c: (r // 2, 0, 0))
    return place_call(
        kernel,
        "finish_attn",
        [piece, piece],
        [
            pl.BlockSpec((2, 3, D, 256), lambda r, c: (0, 0, 0, 0), pipeline_mode=CONST),
            pl.BlockSpec((2, 256, D), lambda r, c: (0, 0, 0), pipeline_mode=CONST),
        ],
        [
            jax.ShapeDtypeStruct((2, 3, D, 256), F32),
            jax.ShapeDtypeStruct((2, 256, D), F32),
        ],
        [pltpu.VMEM((2, 3, 256, D), BF16)],
        12 * D * D,
        {},
    )(place, own, other)


def finish_feed(place, own, other, b, earlier):
    def kernel(c_ref, own_ref, oth_ref, *rest):
        gu_ref, gd_ref = rest[-2:]
        r = pl.program_id(0)

        def store(ref):
            gu_ref[0] = ref[0, 0:128, :].T.astype(F32)
            gd_ref[0] = ref[0, 128:256, :].astype(F32)

        @pl.when(r % 2 == 0)
        def _():
            store(own_ref)

        @pl.when(r % 2 == 1)
        def _():
            store(oth_ref)

    piece = pl.BlockSpec((1, 256, D), lambda r, c: (r // 2, 0, 0))
    anywhere = pl.BlockSpec(memory_space=pl.ANY)
    return place_call(
        kernel,
        "finish_feed",
        [piece, piece] + [anywhere] * len(earlier),
        [
            pl.BlockSpec((1, D, 128), lambda r, c: (b, 0, c[0] ^ r)),
            pl.BlockSpec((1, 128, D), lambda r, c: (b, c[0] ^ r, 0)),
        ],
        [jax.ShapeDtypeStruct((2, D, D), F32), jax.ShapeDtypeStruct((2, D, D), F32)],
        [],
        12 * D * D,
        {3 + i: i for i in range(len(earlier))},
    )(place, own, other, *earlier)


def partner(values):
    return lax.ppermute(values, "head", [(i, i ^ 1) for i in range(NZ)])


def rows_to_spatial(rows, odd):
    cols = rows.shape[1]
    whole = lax.dynamic_slice(rows, (256 * odd, 0), (1024, cols))
    part = lax.dynamic_slice(rows, (1024 * (1 - odd), 0), (256, cols)).reshape(8, 2, 16, cols)
    wins = whole.reshape(2, 16, 2, 16, cols).transpose(0, 2, 1, 3, 4).reshape(1024, cols)
    left, right = part[:, 0].reshape(128, cols), part[:, 1].reshape(128, cols)
    keep = jnp.where(odd == 0, left, right)
    got = partner(jnp.where(odd == 0, right, left))
    top, bottom = jnp.where(odd == 0, keep, got), jnp.where(odd == 0, got, keep)
    part = jnp.concatenate([top, bottom], axis=0)
    return jnp.where(
        odd == 0,
        jnp.concatenate([wins, part], axis=0),
        jnp.concatenate([part, wins], axis=0),
    )


def last_window(wins, odd):
    part = lax.dynamic_slice(wins, (1024 * (1 - odd), 0), (256, wins.shape[1]))
    keep = jnp.where(odd == 0, part[:128], part[128:])
    return keep, jnp.where(odd == 0, part[128:], part[:128])


def spatial_to_rows(wins, keep, got, odd):
    cols = wins.shape[1]
    whole = lax.dynamic_slice(wins, (256 * odd, 0), (1024, cols))
    whole = whole.reshape(2, 2, 16, 16, cols).transpose(0, 2, 1, 3, 4).reshape(1024, cols)
    left, right = jnp.where(odd == 0, keep, got), jnp.where(odd == 0, got, keep)
    part = jnp.stack([left.reshape(8, 16, cols), right.reshape(8, 16, cols)], axis=1)
    part = part.reshape(256, cols)
    return jnp.where(
        odd == 0,
        jnp.concatenate([whole, part], axis=0),
        jnp.concatenate([part, whole], axis=0),
    )


def exchange(values):
    return lax.all_to_all(values, "head", 0, 0, tiled=True)


def spatial_to_tubes(wins):
    cols = wins.shape[1]
    return exchange(
        wins.reshape(5, 2, 8, 2, 8, cols).transpose(1, 3, 0, 2, 4, 5).reshape(1280, cols)
    )


def from_quads(quads):
    cols = quads.shape[1]
    return quads.reshape(2, 2, 5, 8, 8, cols).transpose(2, 0, 3, 1, 4, 5).reshape(1280, cols)


def toeplitz(side):
    span = 2 * side - 1
    b = lax.broadcasted_iota(jnp.int32, (span, side, side), 0)
    j = lax.broadcasted_iota(jnp.int32, (span, side, side), 1)
    i = lax.broadcasted_iota(jnp.int32, (span, side, side), 2)
    return (b == i - j + side - 1).astype(F32)


def toeplitz_pair(side):
    span = 2 * side - 1
    shape = (span * span, side * side, side * side)
    r = lax.broadcasted_iota(jnp.int32, shape, 0)
    j = lax.broadcasted_iota(jnp.int32, shape, 1)
    i = lax.broadcasted_iota(jnp.int32, shape, 2)
    dy = i // side - j // side + side - 1
    dx = i % side - j % side + side - 1
    return (r == dy * span + dx).astype(F32)


CORE, ROW_X, ROW_Y = 1, 2, 4


def swap(values, bit):
    return lax.ppermute(values, "clip", [(i, i ^ bit) for i in range(8)])


def from_z(values, d):
    return lax.ppermute(values, "head", [((i + d) % NZ, i) for i in range(NZ)])


def sync(*values):
    return lax.optimization_barrier(values)


def add(first, second):
    return (first.astype(F32) + second.astype(F32)).astype(BF16)


def line_stage(piece):
    return [from_z(piece, d) for d in (1, 2, 3)]


def others(by_z, z):
    return [lax.dynamic_index_in_dim(by_z, (z + d) % NZ, 0, keepdims=False) for d in (1, 2, 3)]


def cross_stage(own):
    return [own] + [swap(own, m * 2) for m in (1, 2, 3)]


def sides_stage(own):
    return [own, swap(own, ROW_X), swap(own, ROW_Y)]


def corner_stage(sides):
    half = sides[0].shape[1] // 2
    return [swap(sides[1][:, :half], ROW_Y), swap(sides[2][:, half:], ROW_X)]


def joined(sides, corner):
    return jnp.stack(sides + [jnp.concatenate(corner, axis=1)])


def sum_core(keep, got):
    return [add(keep[m], got[m].reshape(keep.shape[1:])) for m in range(4)]


def send_plane(totals, offsets):
    return [swap(totals[m], m * 2) for m in offsets]


def to_places(total, z):
    twice = jnp.concatenate([total, total[: NZ - 1]], axis=0)
    return lax.dynamic_slice_in_dim(twice, (NZ - z) % NZ, NZ, axis=0)


def sum_plane(totals, got, z):
    total = totals[0].astype(F32)
    for value in got:
        total = total + value.astype(F32)
    return to_places(total.astype(BF16), z)


def send_cross(totals):
    half = totals[0].shape[1] // 2
    first = [t[:, :half] for t in totals]
    second = [t[:, half:] for t in totals]
    by_x = swap(jnp.stack([first[1], first[3]]), ROW_X)
    by_y = swap(jnp.stack([second[2], second[3]]), ROW_Y)
    return by_x, by_y


def sum_cross(totals, got):
    half = totals[0].shape[1] // 2
    by_x, by_y = got
    first = [add(totals[0][:, :half], by_x[0]), add(totals[2][:, :half], by_x[1])]
    second = [add(totals[0][:, half:], by_y[0]), add(totals[1][:, half:], by_y[1])]
    return first, second


def send_corner(halves):
    return swap(halves[0][1], ROW_Y), swap(halves[1][1], ROW_X)


def sum_corner(halves, got, z):
    first = add(halves[0][0], got[0])
    second = add(halves[1][0], got[1])
    return to_places(jnp.concatenate([first, second], axis=1), z)


def sum_line(by_z):
    return lax.psum_scatter(by_z, "head", scatter_dimension=0)


def on_device_windows(
    tokens, d_out, modulation, frame_counts, w_qkv, w_out, w_up, w_down, table_s, table_t
):
    z = lax.axis_index("head")
    c = lax.axis_index("clip")
    place = c.astype(jnp.int32).reshape(1)
    chip = c // 2
    odd = z % 2
    mods = modulation[0]
    n_s, n_t = table_s.shape[1], table_t.shape[1]
    hot_s, hot_t = toeplitz(SWIN), toeplitz_pair(TWIN)
    fc = frame_counts

    def spatial_base(tables):
        base = jnp.einsum(
            "hab,bji->hjai", tables[:, :n_s].reshape(16, 31, 31), hot_s, precision=HIGHEST_PRECISION
        ).reshape(16, 16, 496)
        return jnp.pad(base, ((0, 0), (0, 0), (0, 16)))

    def tube_base(tables):
        base = jnp.einsum(
            "htr,rjk->hjtk", tables[:, n_s:].reshape(16, 9, 225), hot_t, precision=HIGHEST_PRECISION
        ).reshape(16, 64, 576)
        return jnp.pad(base, ((0, 0), (0, 0), (0, 64)))

    def table_rows(first, second):
        first = jnp.pad(first, ((0, 0), (0, D - n_s)))
        second = jnp.pad(second, ((0, 0), (0, 15 * D - n_t)))
        values = jnp.concatenate([first, second], axis=1).astype(BF16)
        return values.reshape(NZ, 4, 16, D).transpose(1, 0, 2, 3)

    spatial = ((1, 5, 256), 16, 16, False)
    tube = ((5, 4, 64), 5, 64, True)

    local_a0 = prep_attn(place, w_qkv, w_out, 0)
    line_a0 = line_stage(local_a0[0, 0])
    table_piece = jnp.concatenate([table_s, table_t], axis=1)
    tables = [from_z(table_piece, d) for d in (1, 2)]
    local_f0 = prep_feed(place, w_up, w_down, 0)
    local_a1 = prep_attn(place, w_qkv, w_out, 1)
    local_f1 = prep_feed(place, w_up, w_down, 1)
    line_a0, local_f0, local_a1, local_f1, tables, tokens, table_piece = sync(
        line_a0, local_f0, local_a1, local_f1, tables, tokens, table_piece
    )
    own_a0 = cross_stage(jnp.stack(line_a0))
    z_u0 = lax.all_gather(local_f0[0, 0, :128], "head")
    z_d0 = lax.all_gather(local_f0[0, 0, 128:], "head")
    tables = jnp.stack([table_piece] + tables + [from_z(table_piece, 3)])
    tables = jnp.concatenate(
        [lax.dynamic_slice_in_dim(tables, chip ^ m, 1, axis=1) for m in range(4)], axis=1
    ).reshape(16, n_s + n_t)
    base_s = spatial_base(tables)
    hidden0 = rows_to_spatial(tokens, odd)
    own_a0, hidden0, tables, base_s, z_u0 = sync(own_a0, hidden0, tables, base_s, z_u0)
    own_a0 = jnp.stack(own_a0)
    other_a0 = swap(own_a0, CORE)
    own_u0 = sides_stage(jnp.stack(others(z_u0, z)))
    own_a0, other_a0 = sync(own_a0, other_a0)
    weights_a0 = (local_a0, own_a0, other_a0)
    normed0, qkv0 = ln_qkv(hidden0, mods, weights_a0, 0)
    qkv0, own_u0, z_d0 = sync(qkv0, own_u0, z_d0)
    corner_u0 = corner_stage(own_u0)
    own_d0 = sides_stage(jnp.stack(others(z_d0, z)))
    z_a1 = lax.all_gather(local_a1[0, 0], "head")
    attended0 = attn_fwd(qkv0, base_s, fc, spatial)
    attended0, corner_u0, own_d0, z_a1 = sync(attended0, corner_u0, own_d0, z_a1)
    corner_d0 = corner_stage(own_d0)
    own_u0 = joined(own_u0, corner_u0)
    other_u0 = swap(own_u0, CORE)
    branch0, middle0, shifted0 = out_proj(attended0, weights_a0, hidden0, mods, 0)
    own_a1 = jnp.stack(others(z_a1, z))
    shifted0, corner_d0, other_u0, own_a1 = sync(shifted0, corner_d0, other_u0, own_a1)
    own_d0 = joined(own_d0, corner_d0)
    other_d0 = swap(own_d0, CORE)
    z_f1 = lax.all_gather(local_f1[0, 0], "head")
    shifted0, other_d0 = sync(shifted0, other_d0)
    own_a1 = cross_stage(own_a1)
    weights_f0 = (local_f0, own_u0, other_u0, own_d0, other_d0)
    pre0, feed0, hidden1 = ffn_fwd(shifted0, weights_f0, 0, middle0, mods, 0)
    hidden1, z_f1, own_a1, tables, d_out = sync(hidden1, z_f1, own_a1, tables, d_out)
    tubes1 = spatial_to_tubes(hidden1)
    own_a1 = jnp.stack(own_a1)
    other_a1 = swap(own_a1, CORE)
    own_f1 = cross_stage(jnp.stack(others(z_f1, z)))
    base_t = tube_base(tables)
    spatial_d = rows_to_spatial(d_out, odd)
    tubes1, other_a1, base_t, spatial_d = sync(tubes1, other_a1, base_t, spatial_d)
    weights_a1 = (local_a1, own_a1, other_a1)
    tubes_d = spatial_to_tubes(spatial_d)
    normed1, qkv1 = ln_qkv(tubes1, mods, weights_a1, 6)
    qkv1, own_f1 = sync(qkv1, own_f1)
    own_f1 = jnp.stack(own_f1)
    other_f1 = swap(own_f1, CORE)
    attended1 = attn_fwd(qkv1, base_t, fc, tube)
    branch1, middle1, shifted1 = out_proj(attended1, weights_a1, tubes1, mods, 6)
    shifted1, other_f1 = sync(shifted1, other_f1)
    weights_f1 = (local_f1, own_f1, other_f1, own_f1, other_f1)
    pre1, feed1, hidden2 = ffn_fwd(shifted1, weights_f1, 1, middle1, mods, 6)
    hidden2, tubes_d = sync(hidden2, tubes_d)
    live = lax.broadcasted_iota(jnp.int32, (1280, 1), 0) // 256 < fc[0]
    grad2 = jnp.where(live, tubes_d, 0)
    out_wins = exchange(jnp.where(live, hidden2, 0))
    f1_keep, f1_send, g_shift1 = ffn_bwd(grad2, pre1, shifted1, weights_f1, 1, mods, 6)
    f1_keep, f1_send, g_shift1, out_wins = sync(f1_keep, f1_send, g_shift1, out_wins)
    f1_got = swap(f1_send, CORE)
    g_mid1, g_att1, o1_keep, o1_send, sums_o1 = out_bwd(
        grad2, g_shift1, middle1, feed1, branch1, attended1, weights_a1, mods, 6
    )
    g_att1, f1_got = sync(g_att1, f1_got)
    total_f1 = sum_core(f1_keep, f1_got)
    g_att1, total_f1 = sync(g_att1, total_f1)
    got_f1 = send_cross(total_f1)
    g_proj1, g_base1 = attn_bwd(qkv1, g_att1, base_t, fc, tube)
    g_proj1, g_base1, got_f1 = sync(g_proj1, g_base1, got_f1)
    half_f1 = sum_cross(total_f1, got_f1)
    half_f1, g_proj1 = sync(half_f1, g_proj1)
    got_f1 = send_corner(half_f1)
    g_hid1, sums_q1 = qkv_back(g_proj1, weights_a1, tubes1, g_mid1, mods, 6, BF16, 1)
    g_hid1, g_proj1, out_wins, g_base1, got_f1 = sync(g_hid1, g_proj1, out_wins, g_base1, got_f1)
    grad1 = exchange(g_hid1)
    z_f1 = sum_corner(half_f1, got_f1, z)
    a1_keep, *a1_send = qkv_grad(g_proj1, normed1, o1_keep, o1_send, None, True)
    a1_got = [swap(v, CORE) for v in a1_send]
    gt_t = jnp.einsum(
        "hjtk,rjk->htr",
        g_base1[:, :, :576].reshape(16, 64, 9, 64),
        hot_t,
        precision=HIGHEST_PRECISION,
    ).reshape(16, n_t)
    out_wins = from_quads(out_wins)
    out_keep, out_send = last_window(out_wins, odd)
    grad1, a1_got, z_f1, gt_t, out_wins, out_keep, out_send = sync(
        grad1, a1_got, z_f1, gt_t, out_wins, out_keep, out_send
    )
    grad1 = from_quads(grad1)
    total_a1 = sum_core(a1_keep, a1_got)
    grad1, total_a1 = sync(grad1, total_a1)
    mine_f1 = sum_line(z_f1)
    out_got = partner(out_send)
    got_a1 = send_plane(total_a1, (1, 2, 3))
    f0_keep, f0_send, g_shift0 = ffn_bwd(grad1, pre0, shifted0, weights_f0, 0, mods, 0)
    f0_keep, f0_send, g_shift0, mine_f1, got_a1, out_got = sync(
        f0_keep, f0_send, g_shift0, mine_f1, got_a1, out_got
    )
    f0_got = swap(f0_send, CORE)
    sides_f1 = sides_stage(mine_f1[None])
    mine_a1 = sum_line(sum_plane(total_a1, got_a1, z))
    g_mid0, g_att0, o0_keep, o0_send, sums_o0 = out_bwd(
        grad1, g_shift0, middle0, feed0, branch0, attended0, weights_a0, mods, 0
    )
    g_att0, f0_got, sides_f1 = sync(g_att0, f0_got, sides_f1)
    total_f0 = sum_core(f0_keep, f0_got)
    g_att0, total_f0 = sync(g_att0, total_f0)
    got_f0 = send_cross(total_f0)
    corner_f1 = corner_stage(sides_f1)
    g_proj0, g_base0 = attn_bwd(qkv0, g_att0, base_s, fc, spatial)
    gt_s = jnp.einsum(
        "hjai,bji->hab",
        g_base0[:, :, :496].reshape(16, 16, 31, 16),
        hot_s,
        precision=HIGHEST_PRECISION,
    ).reshape(16, n_s)
    a0_keep, a0_send = qkv_grad(g_proj0, normed0, o0_keep, o0_send, table_rows(gt_s, gt_t))
    a0_keep, a0_send, got_f0, corner_f1, mine_a1, g_proj0 = sync(
        a0_keep, a0_send, got_f0, corner_f1, mine_a1, g_proj0
    )
    a0_got = swap(a0_send, CORE)
    half_f0 = sum_cross(total_f0, got_f0)
    got_f0 = send_corner(half_f0)
    own_gf1 = joined(sides_f1, corner_f1).reshape(4, 256, D)
    g_feed = finish_feed(place, own_gf1, swap(own_gf1, CORE), 1, ())
    half_f0, got_f0, a0_got, g_proj0, g_feed = sync(half_f0, got_f0, a0_got, g_proj0, g_feed)
    z_f0 = sum_corner(half_f0, got_f0, z)
    total_a0 = sum_core(a0_keep, a0_got)
    total_a0, z_f0, g_proj0 = sync(total_a0, z_f0, g_proj0)
    mine_f0 = sum_line(z_f0)
    got_a0 = send_cross(total_a0)
    grad0, sums_q0 = qkv_back(g_proj0, weights_a0, hidden0, g_mid0, mods, 0, F32, 1)
    grad0, sums_q0, got_a0 = sync(grad0, sums_q0, got_a0)
    half_a0 = sum_cross(total_a0, got_a0)
    half_a0, grad0, sums_q0 = sync(half_a0, grad0, sums_q0)
    got_a0 = send_corner(half_a0)
    sides_a1 = sides_stage(mine_a1[None])
    mod_rows = jnp.concatenate(
        [
            sums_q0[0:2], sums_o0[2:3], sums_o0[0:2], sums_o0[3:4],
            sums_q1[0:2], sums_o1[2:3], sums_o1[0:2], sums_o1[3:4],
        ],
        axis=0,
    )
    mod_got = partner(mod_rows)
    got_a0, sides_a1, mine_f0, mod_got, mod_rows = sync(
        got_a0, sides_a1, mine_f0, mod_got, mod_rows
    )
    z_a0 = sum_corner(half_a0, got_a0, z)
    mod_sum = mod_rows + mod_got
    z_a0, mine_f0, mod_sum = sync(z_a0, mine_f0, mod_sum)
    mine_a0 = sum_line(z_a0)
    own_gf0 = cross_stage(mine_f0)
    corner_a1 = corner_stage(sides_a1)
    output = spatial_to_rows(out_wins, out_keep, out_got, odd)
    rows_keep, rows_send = last_window(grad0, odd)
    mine_a0, own_gf0, corner_a1, rows_keep, rows_send, output = sync(
        mine_a0, own_gf0, corner_a1, rows_keep, rows_send, output
    )
    own_ga0 = cross_stage(mine_a0)
    rows_got = partner(rows_send)
    own_gf0 = jnp.stack(own_gf0)
    own_ga1 = joined(sides_a1, corner_a1).reshape(4, 128, D)
    g_feed = finish_feed(place, own_gf0, swap(own_gf0, CORE), 0, g_feed)
    own_ga0, g_feed, rows_got, own_ga1, mod_sum = sync(own_ga0, g_feed, rows_got, own_ga1, mod_sum)
    own_ga0 = jnp.stack(own_ga0)
    own_ga = jnp.concatenate([own_ga0[:, :128], own_ga1, own_ga0[:, 128:]], axis=1)
    own_ga0 = own_ga
    mod_got = lax.ppermute(mod_sum, "head", [(i, i ^ 2) for i in range(NZ)])
    grad_tokens = spatial_to_rows(grad0, rows_keep, rows_got, odd)
    g_attn = finish_attn(place, own_ga, swap(own_ga, CORE))
    tab = jnp.concatenate(
        [lax.dynamic_slice_in_dim(own_ga0, chip ^ m, 1, axis=0) for m in range(4)], axis=0
    )
    tab = tab[:, 256:272].reshape(4, 16 * D).astype(F32)
    return (
        output,
        grad_tokens,
        (mod_sum + mod_got)[None],
        g_attn[0],
        g_attn[1],
        g_feed[0],
        g_feed[1],
        tab[:, :n_s],
        tab[:, D : D + n_t],
    )


def solution(mesh):
    if mesh.shape["head"] == NZ and mesh.shape["clip"] == 8:
        body = on_device_windows
    else:
        body = on_device
    return jax.shard_map(
        body,
        mesh=mesh,
        in_specs=(
            P(("clip", "head"), None),
            P(("clip", "head"), None),
            P("clip", None, None),
            P("clip"),
            P(None, None, None, "head"),
            P(None, "head", None),
            P(None, None, "head"),
            P(None, "head", None),
            P("head", None),
            P("head", None),
        ),
        out_specs=(
            P(("clip", "head"), None),
            P(("clip", "head"), None),
            P("clip", None, None),
            P(None, None, None, "head"),
            P(None, "head", None),
            P(None, None, "head"),
            P(None, "head", None),
            P("head", None),
            P("head", None),
        ),
        check_vma=False,
    )
```

```python
import jax
import jax.numpy as jnp
from jax import lax
from jax.experimental import pallas as pl
from jax.experimental.pallas import tpu as pltpu
from jax.sharding import PartitionSpec as P

HD = 64
FH = 32
FW = 32
SWIN = 16
TWIN = 8
PADF = 5


EPS = 1e-06
HIGHEST_PRECISION = lax.Precision.HIGHEST
NEGATIVE = -1e30


def layer_norm(values, shift_row, scale_row):
    average = jnp.mean(values, axis=-1, keepdims=True)
    centred = values - average
    spread = jnp.mean(centred * centred, axis=-1, keepdims=True)
    return centred * lax.rsqrt(spread + EPS) * (1.0 + scale_row) + shift_row


def gelu_tanh(values):
    return jax.nn.gelu(values, approximate=True)


def window_index(side_t, side_len):
    window_size = side_t * side_len * side_len
    places = jnp.arange(window_size, dtype=jnp.int32)
    time_pos = places // (side_len * side_len)
    height_pos = places // side_len % side_len
    width_pos = places % side_len
    span_len = 2 * side_len - 1
    return (
        (time_pos[:, None] - time_pos[None, :] + side_t - 1) * span_len * span_len
        + (height_pos[:, None] - height_pos[None, :] + side_len - 1) * span_len
        + (width_pos[:, None] - width_pos[None, :] + side_len - 1)
    )


def to_windows(values, side_t, side_len):
    tail_shape = values.shape[1:]
    frames = values.shape[0] // (FH * FW)
    shaped = values.reshape(
        (frames // side_t, side_t, FH // side_len, side_len, FW // side_len, side_len) + tail_shape
    )
    axis_order = (0, 2, 4, 1, 3, 5) + tuple(range(6, 6 + len(tail_shape)))
    shaped = shaped.transpose(axis_order)
    return shaped.reshape((-1, side_t * side_len * side_len) + tail_shape)


def from_windows(values, side_t, side_len):
    tail_shape = values.shape[2:]
    blocks_high = FH // side_len
    blocks_wide = FW // side_len
    frame_groups = values.shape[0] // (blocks_high * blocks_wide)
    shaped = values.reshape(
        (frame_groups, blocks_high, blocks_wide, side_t, side_len, side_len) + tail_shape
    )
    axis_order = (0, 3, 1, 4, 2, 5) + tuple(range(6, 6 + len(tail_shape)))
    return shaped.transpose(axis_order).reshape((frame_groups * side_t * FH * FW,) + tail_shape)


def on_device(
    tokens, d_out, modulation, frame_counts, w_qkv, w_out, w_up, w_down, table_s, table_t
):
    local_rows = tokens.shape[0]
    clip_len = PADF * FH * FW
    group_clips = modulation.shape[0]
    group_rows = group_clips * clip_len
    scale_dot = HD ** (-0.5)
    my_index = lax.axis_index("head")
    first_row = my_index * local_rows
    row_ids = first_row + jnp.arange(local_rows, dtype=jnp.int32)
    clip_slots = jnp.arange(group_clips, dtype=jnp.int32)
    row_onehot = ((row_ids // clip_len)[:, None] == clip_slots[None, :]).astype(jnp.float32)
    count_float = frame_counts.astype(jnp.float32)
    row_frames = jnp.dot(row_onehot, count_float, precision=HIGHEST_PRECISION)
    row_keep = ((row_ids % clip_len // (FH * FW)).astype(jnp.float32) < row_frames).astype(
        jnp.float32
    )[:, None]
    group_ids = jnp.arange(group_rows, dtype=jnp.int32)
    group_onehot = ((group_ids // clip_len)[:, None] == clip_slots[None, :]).astype(jnp.float32)
    group_frames = jnp.dot(group_onehot, count_float, precision=HIGHEST_PRECISION)
    group_keep = (group_ids % clip_len // (FH * FW)).astype(jnp.float32) < group_frames

    def block_shape(block_id):
        if block_id == 0:
            return (1, SWIN)
        return (PADF, TWIN)

    def mod_row(slot):
        return jnp.dot(row_onehot, modulation[:, slot, :], precision=HIGHEST_PRECISION)

    def rows_in(values):
        return lax.all_gather(values, "head", axis=0, tiled=True)

    def grads_in(values):
        return lax.all_gather(values, "head", axis=0, tiled=True)

    def rows_out(full_rows, weight):
        return lax.psum_scatter(
            jnp.dot(full_rows, weight, preferred_element_type=jnp.float32).astype(jnp.bfloat16),
            "head",
            scatter_dimension=0,
            tiled=True,
        ).astype(jnp.float32)

    def grads_out(full_rows, weight, einsum_form):
        return lax.psum_scatter(
            jnp.einsum(einsum_form, full_rows, weight, preferred_element_type=jnp.float32).astype(
                jnp.bfloat16
            ),
            "head",
            scatter_dimension=0,
            tiled=True,
        ).astype(jnp.float32)

    def rows_keep(block_id):
        if block_id == 0:
            return None
        return to_windows(group_keep[:, None], PADF, TWIN)[:, :, 0]

    def shape_windows(projected, side_t, side_len):
        head_count = projected.shape[-1] // HD
        window_size = side_t * side_len * side_len
        windows = to_windows(projected, side_t, side_len)
        return windows.reshape(windows.shape[0], window_size, 3, head_count, HD)

    def shape_grad(grad_attended, side_t, side_len):
        head_count = grad_attended.shape[-1] // HD
        window_size = side_t * side_len * side_len
        windows = to_windows(grad_attended, side_t, side_len)
        return windows.reshape(windows.shape[0], window_size, head_count, HD)

    def flat_rows(windowed, side_t, side_len):
        return from_windows(windowed, side_t, side_len)

    def logits_of(queries, key_rows, table_arg, rel_index, keep_win):
        logits = (
            jnp.einsum("wqhe,wkhe->whqk", queries, key_rows, preferred_element_type=jnp.float32)
            * scale_dot
        )
        logits = logits + table_arg[:, rel_index][None]
        if keep_win is not None:
            logits = jnp.where(keep_win[:, None, None, :], logits, NEGATIVE)
        return logits

    def attend(windows, table_arg, rel_index, keep_win):
        logits = logits_of(windows[:, :, 0], windows[:, :, 1], table_arg, rel_index, keep_win)
        row_max = jnp.max(logits, axis=-1, keepdims=True)
        exponent = jnp.exp(logits - row_max)
        row_total = jnp.sum(exponent, axis=-1, keepdims=True)
        probs = exponent / row_total
        log_total = row_max + jnp.log(row_total)
        attended = jnp.einsum(
            "whqk,wkhe->wqhe",
            probs.astype(jnp.bfloat16),
            windows[:, :, 2],
            preferred_element_type=jnp.float32,
        )
        return (attended.reshape(attended.shape[0], attended.shape[1], -1), log_total)

    def attend_back(windows, grad_windows, log_total, table_arg, rel_index, keep_win):
        queries = windows[:, :, 0]
        key_rows = windows[:, :, 1]
        value_rows = windows[:, :, 2]
        logits = logits_of(queries, key_rows, table_arg, rel_index, keep_win)
        probs = jnp.exp(logits - log_total)
        grad_probs = jnp.einsum(
            "wqhe,wkhe->whqk", grad_windows, value_rows, preferred_element_type=jnp.float32
        )
        grad_values = jnp.einsum(
            "whqk,wqhe->wkhe",
            probs.astype(jnp.bfloat16),
            grad_windows,
            preferred_element_type=jnp.float32,
        )
        grad_logits = (
            probs * (grad_probs - jnp.sum(grad_probs * probs, axis=-1, keepdims=True))
        ).astype(jnp.bfloat16)
        head_count = queries.shape[2]
        table_terms = jnp.sum(grad_logits.astype(jnp.float32), axis=0).reshape(head_count, -1)
        grad_table = jax.ops.segment_sum(
            table_terms.T, rel_index.reshape(-1), num_segments=table_arg.shape[1]
        ).T
        grad_queries = (
            jnp.einsum("whqk,wkhe->wqhe", grad_logits, key_rows, preferred_element_type=jnp.float32)
            * scale_dot
        )
        grad_keys = (
            jnp.einsum("whqk,wqhe->wkhe", grad_logits, queries, preferred_element_type=jnp.float32)
            * scale_dot
        )
        grad_stack = jnp.stack([grad_queries, grad_keys, grad_values], axis=2)
        return (
            grad_stack.reshape(grad_stack.shape[0], grad_stack.shape[1], 3, head_count * HD),
            grad_table,
        )

    def forward_block(hidden, block_id):
        side_t, side_len = block_shape(block_id)
        table_local = table_s if block_id == 0 else table_t
        rel_index = window_index(side_t, side_len)
        normed = layer_norm(hidden, mod_row(6 * block_id), mod_row(6 * block_id + 1)).astype(
            jnp.bfloat16
        )
        plan = None
        normed_in = rows_in(normed)
        qkv_use, out_use, table_use = (w_qkv[block_id], w_out[block_id], table_local)
        keep_win = rows_keep(block_id)
        projected = jnp.einsum(
            "gd,cde->gce", normed_in, qkv_use, preferred_element_type=jnp.float32
        ).astype(jnp.bfloat16)
        windows = shape_windows(projected, side_t, side_len)
        attended_win, log_total = attend(windows, table_use, rel_index, keep_win)
        attended = flat_rows(attended_win, side_t, side_len).astype(jnp.bfloat16)
        branch = rows_out(attended, out_use)
        middle = hidden + mod_row(6 * block_id + 2) * branch
        shifted = layer_norm(middle, mod_row(6 * block_id + 3), mod_row(6 * block_id + 4)).astype(
            jnp.bfloat16
        )
        up_full, down_full = (
            lax.all_gather(w_up[block_id], "head", axis=1, tiled=True),
            lax.all_gather(w_down[block_id], "head", axis=0, tiled=True),
        )
        pre_gelu = jnp.dot(shifted, up_full, preferred_element_type=jnp.float32)
        activated = gelu_tanh(pre_gelu).astype(jnp.bfloat16)
        feed_out = jnp.dot(activated, down_full, preferred_element_type=jnp.float32)
        mlp_state = (shifted, pre_gelu, activated, up_full, down_full)
        result = middle + mod_row(6 * block_id + 5) * feed_out
        attn_state = (
            normed_in,
            projected,
            log_total,
            attended,
            qkv_use,
            out_use,
            table_use,
            keep_win,
            plan,
        )
        saved_state = (hidden, attn_state, branch, middle, feed_out, mlp_state)
        return (saved_state, result)

    def backward_block(saved_state, grad_result, block_id):
        hidden, attn_state, branch, middle, feed_out, mlp_state = saved_state
        normed_in, projected, log_total, attended, qkv_use, out_use, table_use, keep_win, plan = (
            attn_state
        )
        shifted_in, pre_gelu, activated, up_weight, down_weight = mlp_state
        side_t, side_len = block_shape(block_id)
        rel_index = window_index(side_t, side_len)
        grad_feed = (grad_result * mod_row(6 * block_id + 5)).astype(jnp.bfloat16)
        grad_gate_mlp = grad_result * feed_out
        grad_down = jnp.einsum(
            "gf,gd->fd", activated, grad_feed, preferred_element_type=jnp.float32
        )
        grad_activated = jnp.einsum(
            "gd,fd->gf", grad_feed, down_weight, preferred_element_type=jnp.float32
        )
        grad_pre = jax.vjp(gelu_tanh, pre_gelu)[1](grad_activated)[0].astype(jnp.bfloat16)
        grad_up = jnp.einsum("gd,gf->df", shifted_in, grad_pre, preferred_element_type=jnp.float32)
        grad_shifted = jnp.einsum(
            "gf,df->gd", grad_pre, up_weight, preferred_element_type=jnp.float32
        )
        grad_up, grad_down = (
            lax.psum_scatter(
                grad_up.astype(jnp.bfloat16), "head", scatter_dimension=1, tiled=True
            ).astype(jnp.float32),
            lax.psum_scatter(
                grad_down.astype(jnp.bfloat16), "head", scatter_dimension=0, tiled=True
            ).astype(jnp.float32),
        )
        unused_mid, pull_second = jax.vjp(
            layer_norm, middle, mod_row(6 * block_id + 3), mod_row(6 * block_id + 4)
        )
        grad_mid_norm, grad_shift_mlp, grad_scale_mlp = pull_second(grad_shifted)
        grad_middle = grad_result + grad_mid_norm
        grad_branch = (grad_middle * mod_row(6 * block_id + 2)).astype(jnp.bfloat16)
        grad_gate_att = grad_middle * branch
        branch_in = grads_in(grad_branch)
        grad_wout = jnp.einsum("ge,gd->ed", attended, branch_in, preferred_element_type=jnp.float32)
        grad_attended = jnp.einsum(
            "gd,ed->ge", branch_in, out_use, preferred_element_type=jnp.float32
        ).astype(jnp.bfloat16)
        windows = shape_windows(projected, side_t, side_len)
        grad_windows = shape_grad(grad_attended, side_t, side_len)
        grad_stack, grad_table = attend_back(
            windows, grad_windows, log_total, table_use, rel_index, keep_win
        )
        grad_projected = flat_rows(grad_stack, side_t, side_len).astype(jnp.bfloat16)
        grad_qkv = jnp.einsum(
            "gd,gce->cde", normed_in, grad_projected, preferred_element_type=jnp.float32
        )
        grad_normed = grads_out(grad_projected, qkv_use, "gce,cde->gd")
        unused_hid, pull_first = jax.vjp(
            layer_norm, hidden, mod_row(6 * block_id), mod_row(6 * block_id + 1)
        )
        grad_hid_norm, grad_shift_att, grad_scale_att = pull_first(grad_normed)
        grad_hidden = grad_middle + grad_hid_norm
        mod_terms = jnp.stack(
            [
                grad_shift_att,
                grad_scale_att,
                grad_gate_att,
                grad_shift_mlp,
                grad_scale_mlp,
                grad_gate_mlp,
            ],
            axis=1,
        )
        grad_mods = jnp.einsum("rc,rke->cke", row_onehot, mod_terms, precision=HIGHEST_PRECISION)
        return (grad_hidden, grad_mods, (grad_qkv, grad_wout, grad_up, grad_down, grad_table))

    hidden_first = tokens.astype(jnp.float32)
    saved_first, hidden_second = forward_block(hidden_first, 0)
    saved_second, hidden_last = forward_block(hidden_second, 1)
    output = (hidden_last * row_keep).astype(jnp.bfloat16)
    grad_second, mods_second, weights_second = backward_block(
        saved_second, d_out.astype(jnp.float32) * row_keep, 1
    )
    grad_first, mods_first, weights_first = backward_block(saved_first, grad_second, 0)
    grad_modulation = lax.psum(
        jnp.concatenate([mods_first, mods_second], axis=1).astype(jnp.bfloat16), "head"
    ).astype(jnp.float32)
    summed = (
        lax.psum(
            jnp.stack([weights_first[0], weights_second[0]]).astype(jnp.bfloat16), "clip"
        ).astype(jnp.float32),
        lax.psum(
            jnp.stack([weights_first[1], weights_second[1]]).astype(jnp.bfloat16), "clip"
        ).astype(jnp.float32),
        lax.psum(
            jnp.stack([weights_first[2], weights_second[2]]).astype(jnp.bfloat16), "clip"
        ).astype(jnp.float32),
        lax.psum(
            jnp.stack([weights_first[3], weights_second[3]]).astype(jnp.bfloat16), "clip"
        ).astype(jnp.float32),
        lax.psum(weights_first[4].astype(jnp.bfloat16), "clip").astype(jnp.float32),
        lax.psum(weights_second[4].astype(jnp.bfloat16), "clip").astype(jnp.float32),
    )
    return (
        output,
        grad_first,
        grad_modulation,
        summed[0],
        summed[1],
        summed[2],
        summed[3],
        summed[4],
        summed[5],
    )


F32 = jnp.float32
BF16 = jnp.bfloat16
VMEM_LIMIT = 58 * 1024 * 1024
NZ = 4
D = 1024
HPZ = 4
CONST = pl.Buffered(1)


def dot_nn(a, b):
    return lax.dot_general(a, b, (((1,), (0,)), ((), ())), preferred_element_type=F32)


def dot_nt(a, b):
    return lax.dot_general(a, b, (((1,), (1,)), ((), ())), preferred_element_type=F32)


def dot_tn(a, b):
    return lax.dot_general(a, b, (((0,), (0,)), ((), ())), preferred_element_type=F32)


def call(kernel, name, grid, in_specs, out_specs, out_shape, scratch, flops, nbytes):
    return pl.pallas_call(
        kernel,
        name=name,
        grid=grid,
        in_specs=in_specs,
        out_specs=out_specs,
        out_shape=out_shape,
        scratch_shapes=scratch,
        compiler_params=pltpu.CompilerParams(
            dimension_semantics=("arbitrary",) * len(grid), vmem_limit_bytes=VMEM_LIMIT
        ),
        cost_estimate=pl.CostEstimate(
            flops=flops // 4, bytes_accessed=nbytes // 4, transcendentals=0
        ),
    )


def full(shape):
    return pl.BlockSpec(shape, lambda *ids: (0,) * len(shape), pipeline_mode=CONST)


def chunk_rows(i, size):
    return pl.ds(pl.multiple_of(i * size, size), size)


def ln_stats(x):
    mean = jnp.mean(x, axis=-1, keepdims=True)
    centred = x - mean
    rstd = lax.rsqrt(jnp.mean(centred * centred, axis=-1, keepdims=True) + EPS)
    return centred * rstd, rstd


def ln_back(grad, hat, rstd, scale):
    gh = grad * (1.0 + scale)
    m1 = jnp.mean(gh, axis=-1, keepdims=True)
    m2 = jnp.mean(gh * hat, axis=-1, keepdims=True)
    return rstd * (gh - m1 - hat * m2)


def piece_specs(k, row, count):
    tail = (count, D)
    return [
        pl.BlockSpec((2, 4) + tail, lambda d: (0, 0, row, 0), pipeline_mode=CONST),
        pl.BlockSpec((4, 1) + tail, lambda d: (0, jnp.maximum(d - 1, 0), row, 0)),
        pl.BlockSpec((4, 1) + tail, lambda d: (0, jnp.maximum(d - 1, 0), row, 0)),
    ]


def by_offset(d, body, local_ref, own_ref, other_ref):
    @pl.when(d == 0)
    def _():
        body(lambda m, r, n: local_ref[0, m, r : r + n, :], lambda m, r, n: local_ref[1, m, r : r + n, :])

    @pl.when(d > 0)
    def _():
        body(lambda m, r, n: own_ref[m, 0, r : r + n, :], lambda m, r, n: other_ref[m, 0, r : r + n, :])


def head_rows(own, other, row):
    parts = []
    for m in range(4):
        parts += [own(m, row, 32), other(m, row, 32)]
    return jnp.concatenate(parts, axis=0)


def pair_rows(first, second):
    return jnp.concatenate([get(m) for get in (first, second) for m in range(4)], axis=0)


def feed_specs(down_block):
    def spec(block):
        return pl.BlockSpec((4, 1, 128, D), lambda d: (0, jnp.maximum(d - 1, 0), block, 0))

    return [full((2, 4, 256, D)), spec(0), spec(0), spec(down_block), spec(down_block)]


def feed_by_offset(d, body, l_ref, wu_ref, vu_ref, wd_ref, vd_ref):
    @pl.when(d == 0)
    def _():
        body(
            lambda: pair_rows(lambda m: l_ref[0, m, 0:128], lambda m: l_ref[1, m, 0:128]),
            lambda: pair_rows(lambda m: l_ref[0, m, 128:256], lambda m: l_ref[1, m, 128:256]),
        )

    @pl.when(d > 0)
    def _():
        body(
            lambda: pair_rows(lambda m: wu_ref[m, 0], lambda m: vu_ref[m, 0]),
            lambda: pair_rows(lambda m: wd_ref[m, 0], lambda m: vd_ref[m, 0]),
        )


def ln_qkv(hidden, mods, weights, base):
    rows = hidden.shape[0]
    step = 640

    def kernel(h_ref, m_ref, l_ref, w_ref, v_ref, normed_ref, qkv_ref):
        d = pl.program_id(0)

        @pl.when(d == 0)
        def _():
            def body(i, carry):
                sl = chunk_rows(i, step)
                hat, _ = ln_stats(h_ref[sl, :].astype(F32))
                normed_ref[sl, :] = (
                    hat * (1.0 + m_ref[base + 1 : base + 2, :]) + m_ref[base : base + 1, :]
                ).astype(BF16)
                return carry

            lax.fori_loop(0, rows // step, body, 0)

        def work(own, other):
            for t in range(3):
                qkv_ref[:, t * 256 : (t + 1) * 256] = dot_nt(
                    normed_ref[...], head_rows(own, other, t * 32)
                ).astype(BF16)

        by_offset(d, work, l_ref, w_ref, v_ref)

    return call(
        kernel,
        "ln_qkv",
        (NZ,),
        [full((rows, D)), full((12, D))] + piece_specs(128, 0, 96),
        [full((rows, D)), pl.BlockSpec((rows, 768), lambda z: (0, z))],
        [jax.ShapeDtypeStruct((rows, D), BF16), jax.ShapeDtypeStruct((rows, 3 * D), BF16)],
        [],
        2 * rows * D * 3 * D,
        rows * D * 12 + 6 * D * D,
    )(hidden, mods, *weights)


def build_bias(base_ref, bias_ref, fc_ref, slides, width, lanes_step):
    rows_step = width // slides
    for h in range(HPZ):
        for s in range(slides):
            off = (slides - 1 - s) * lanes_step
            tile = base_ref[h, :, off : off + width]
            if fc_ref is not None:
                tile = jnp.where(s < fc_ref[0], tile, NEGATIVE)
            bias_ref[h, s * rows_step : (s + 1) * rows_step, :] = tile


def window_view(values, kind):
    parts, count, size = kind[0]
    return values.reshape(parts, count, size, values.shape[-1])


def attn_fwd(qkv, base, fc, kind):
    (parts, count, size), slides, lanes_step, masked = kind
    rows, width = qkv.shape[0], parts * size
    r_step, lanes = base.shape[1], base.shape[2]

    def kernel(x_ref, b_ref, fc_ref, o_ref, bias_ref):
        build_bias(b_ref, bias_ref, fc_ref if masked else None, slides, width, lanes_step)

        def one(w, carry):
            def cut(col):
                return x_ref[:, w, :, col : col + HD].reshape(width, HD)

            scores, probs = [], []
            for h in range(HPZ):
                scores.append(dot_nt(cut(256 + h * HD), cut(h * HD) * 0.125) + bias_ref[h])
            for h in range(HPZ):
                expo = jnp.exp(scores[h] - jnp.max(scores[h], axis=0, keepdims=True))
                inv = 1.0 / jnp.sum(expo, axis=0, keepdims=True)
                probs.append((expo * inv).astype(BF16))
            for h in range(HPZ):
                got = dot_tn(probs[h], cut(512 + h * HD)).astype(BF16)
                o_ref[:, w, :, h * HD : (h + 1) * HD] = got.reshape(parts, size, HD)
            return carry

        lax.fori_loop(0, count, one, 0)

    return call(
        kernel,
        "attn_fwd",
        (NZ,),
        [
            pl.BlockSpec((parts, count, size, 768), lambda z: (0, 0, 0, z)),
            pl.BlockSpec((HPZ, r_step, lanes), lambda z: (z, 0, 0)),
            pl.BlockSpec(memory_space=pltpu.SMEM),
        ],
        pl.BlockSpec((parts, count, size, 256), lambda z: (0, 0, 0, z)),
        jax.ShapeDtypeStruct((parts, count, size, D), BF16),
        [pltpu.VMEM((HPZ, width, width), F32)],
        count * 16 * width * width * HD * 16,
        rows * D * 8,
    )(window_view(qkv, kind), base, fc).reshape(rows, D)


def attn_bwd(qkv, grad_att, base, fc, kind):
    (parts, count, size), slides, lanes_step, masked = kind
    rows, width = qkv.shape[0], parts * size
    r_step, lanes = base.shape[1], base.shape[2]

    def kernel(x_ref, d_ref, b_ref, fc_ref, o_ref, gb_ref, bias_ref, acc_ref):
        build_bias(b_ref, bias_ref, fc_ref if masked else None, slides, width, lanes_step)
        acc_ref[...] = jnp.zeros_like(acc_ref)

        def one(w, carry):
            def cut(ref, col):
                return ref[:, w, :, col : col + HD].reshape(width, HD)

            def put(col, value):
                o_ref[:, w, :, col : col + HD] = value.astype(BF16).reshape(parts, size, HD)

            q = [cut(x_ref, h * HD) * 0.125 for h in range(HPZ)]
            k = [cut(x_ref, 256 + h * HD) for h in range(HPZ)]
            da = [cut(d_ref, h * HD) for h in range(HPZ)]
            score = [dot_nt(k[h], q[h]) + bias_ref[h] for h in range(HPZ)]
            dp = [dot_nt(cut(x_ref, 512 + h * HD), da[h]) for h in range(HPZ)]
            probs, dl = [], []
            for h in range(HPZ):
                expo = jnp.exp(score[h] - jnp.max(score[h], axis=0, keepdims=True))
                inv = 1.0 / jnp.sum(expo, axis=0, keepdims=True)
                p = expo * inv
                row = jnp.sum(dp[h] * p, axis=0, keepdims=True)
                g = (p * (dp[h] - row)).astype(BF16)
                acc_ref[h] += g.astype(F32)
                probs.append(p.astype(BF16))
                dl.append(g)
            for h in range(HPZ):
                put(h * HD, dot_tn(dl[h], k[h]) * 0.125)
                put(256 + h * HD, dot_nn(dl[h], q[h]))
                put(512 + h * HD, dot_nn(probs[h], da[h]))
            return carry

        lax.fori_loop(0, count, one, 0)
        gb_ref[...] = jnp.zeros_like(gb_ref)
        for h in range(HPZ):
            for s in range(slides):
                off = (slides - 1 - s) * lanes_step
                gb_ref[h, :, off : off + width] += acc_ref[h, s * r_step : (s + 1) * r_step, :]

    xspec = pl.BlockSpec((parts, count, size, 768), lambda z: (0, 0, 0, z))
    bspec = pl.BlockSpec((HPZ, r_step, lanes), lambda z: (z, 0, 0))
    proj, strips = call(
        kernel,
        "attn_bwd",
        (NZ,),
        [
            xspec,
            pl.BlockSpec((parts, count, size, 256), lambda z: (0, 0, 0, z)),
            bspec,
            pl.BlockSpec(memory_space=pltpu.SMEM),
        ],
        [xspec, bspec],
        [
            jax.ShapeDtypeStruct((parts, count, size, 3 * D), BF16),
            jax.ShapeDtypeStruct(base.shape, F32),
        ],
        [pltpu.VMEM((HPZ, width, width), F32), pltpu.VMEM((HPZ, width, width), F32)],
        count * 16 * width * width * HD * 40,
        rows * D * 16,
    )(window_view(qkv, kind), window_view(grad_att, kind), base, fc)
    return proj.reshape(rows, 3 * D), strips


def out_specs_of(row_block):
    return [
        pl.BlockSpec((2, 4, 32, D), lambda i: (0, 0, row_block, 0), pipeline_mode=CONST),
        pl.BlockSpec((4, 3, 32, D), lambda i: (0, 0, row_block, 0), pipeline_mode=CONST),
        pl.BlockSpec((4, 3, 32, D), lambda i: (0, 0, row_block, 0), pipeline_mode=CONST),
    ]


def out_rows(d, l_ref, w_ref, v_ref):
    if d == 0:
        return head_rows(
            lambda m, r, n: l_ref[0, m, :, :], lambda m, r, n: l_ref[1, m, :, :], 0
        )
    return head_rows(
        lambda m, r, n: w_ref[m, d - 1, :, :], lambda m, r, n: v_ref[m, d - 1, :, :], 0
    )


def out_proj(attended, weights, hidden, mods, base):
    rows = attended.shape[0]
    step = 256

    def kernel(a_ref, l_ref, w_ref, v_ref, h_ref, m_ref, br_ref, mid_ref, sh_ref):
        branch = jnp.zeros((step, D), F32)
        for d in range(NZ):
            branch += dot_nn(a_ref[:, d * 256 : (d + 1) * 256], out_rows(d, l_ref, w_ref, v_ref))
        br_ref[...] = branch.astype(BF16)
        middle = h_ref[...].astype(F32) + m_ref[base + 2 : base + 3, :] * branch
        mid_ref[...] = middle
        hat, _ = ln_stats(middle)
        sh_ref[...] = (
            hat * (1.0 + m_ref[base + 4 : base + 5, :]) + m_ref[base + 3 : base + 4, :]
        ).astype(BF16)

    tile = pl.BlockSpec((step, D), lambda i: (i, 0))
    return call(
        kernel,
        "out_proj",
        (rows // step,),
        [tile] + out_specs_of(3) + [tile, full((12, D))],
        [tile, tile, tile],
        [
            jax.ShapeDtypeStruct((rows, D), BF16),
            jax.ShapeDtypeStruct((rows, D), F32),
            jax.ShapeDtypeStruct((rows, D), BF16),
        ],
        [],
        2 * rows * D * D,
        rows * D * 14 + 2 * D * D,
    )(attended, *weights, hidden, mods)


GELU_C = 0.7978845608028654
GELU_A = 0.044715


def gelu_of(x):
    return 0.5 * x * (1.0 + jnp.tanh(GELU_C * (x + GELU_A * x * x * x)))


def gelu_both(x):
    x2 = x * x
    th = jnp.tanh(GELU_C * (x + GELU_A * x * x2))
    half = 0.5 * (1.0 + th)
    slope = half + 0.5 * x * (1.0 - th * th) * (GELU_C * (1.0 + 3.0 * GELU_A * x2))
    return x * half, slope


def ffn_fwd(shifted, weights, down_block, middle, mods, base):
    rows = shifted.shape[0]
    step = 640

    def kernel(x_ref, *refs):
        parts, (mid_ref, m_ref, pre_ref, feed_ref, nx_ref, acc_ref) = refs[:5], refs[5:]
        z = pl.program_id(0)

        def work(up, down):
            def body(i, carry):
                sl = chunk_rows(i, step)
                pre = dot_nt(x_ref[sl, :], up())
                pre_ref[sl, :] = pre.astype(BF16)
                part = dot_nn(gelu_of(pre).astype(BF16), down())

                @pl.when(z == 0)
                def _():
                    acc_ref[sl, :] = part

                @pl.when((z > 0) & (z < NZ - 1))
                def _():
                    acc_ref[sl, :] += part

                @pl.when(z == NZ - 1)
                def _():
                    feed = acc_ref[sl, :] + part
                    feed_ref[sl, :] = feed.astype(BF16)
                    nx_ref[sl, :] = (
                        mid_ref[sl, :] + m_ref[base + 5 : base + 6, :] * feed
                    ).astype(BF16)

                return carry

            lax.fori_loop(0, rows // step, body, 0)

        feed_by_offset(z, work, *parts)

    return call(
        kernel,
        "ffn_fwd",
        (NZ,),
        [full((rows, D))] + feed_specs(down_block) + [full((rows, D)), full((12, D))],
        [pl.BlockSpec((rows, D), lambda z: (0, z)), full((rows, D)), full((rows, D))],
        [
            jax.ShapeDtypeStruct((rows, 4 * D), BF16),
            jax.ShapeDtypeStruct((rows, D), BF16),
            jax.ShapeDtypeStruct((rows, D), BF16),
        ],
        [pltpu.VMEM((rows, D), F32)],
        16 * rows * D * D,
        rows * D * 20 + 16 * D * D,
    )(shifted, *weights, middle, mods)


def ffn_bwd(grad, pre, shifted, weights, down_block, mods, base):
    rows = grad.shape[0]
    step = 640

    def kernel(g_ref, p_ref, x_ref, *refs):
        parts, refs = refs[:5], refs[5:]
        m_ref, keep_ref, send_ref, gs_ref, gf_ref, act_ref, gp_ref = refs
        z = pl.program_id(0)

        @pl.when(z == 0)
        def _():
            def body(i, carry):
                sl = chunk_rows(i, step)
                gf_ref[sl, :] = (
                    g_ref[sl, :].astype(F32) * m_ref[base + 5 : base + 6, :]
                ).astype(BF16)
                gs_ref[sl, :] = jnp.zeros((step, D), F32)
                return carry

            lax.fori_loop(0, rows // step, body, 0)

        def work(up, down):
            def body(i, carry):
                sl = chunk_rows(i, step)
                back = dot_nt(gf_ref[sl, :], down())
                act, slope = gelu_both(p_ref[sl, :].astype(F32))
                act_ref[sl, :] = act.astype(BF16)
                gpre = (back * slope).astype(BF16)
                gp_ref[sl, :] = gpre
                part = dot_nn(gpre, up())
                gs_ref[sl, :] += part
                return carry

            lax.fori_loop(0, rows // step, body, 0)

        feed_by_offset(z, work, *parts)
        for j, out_ref in enumerate((keep_ref, send_ref)):
            cols = slice(j * 512, (j + 1) * 512)
            gd = dot_tn(act_ref[:, cols], gf_ref[...]).astype(BF16)
            gu = dot_tn(gp_ref[:, cols], x_ref[...]).astype(BF16)
            out_ref[:, 0, 0:128] = gu.reshape(4, 128, D)
            out_ref[:, 0, 128:256] = gd.reshape(4, 128, D)

    gspec = pl.BlockSpec((4, 1, 256, D), lambda z: (0, z, 0, 0))
    gshape = jax.ShapeDtypeStruct((4, NZ, 256, D), BF16)
    return call(
        kernel,
        "ffn_bwd",
        (NZ,),
        [
            full((rows, D)),
            pl.BlockSpec((rows, D), lambda z: (0, z)),
            full((rows, D)),
        ]
        + feed_specs(down_block)
        + [full((12, D))],
        [gspec, gspec, full((rows, D))],
        [gshape, gshape, jax.ShapeDtypeStruct((rows, D), F32)],
        [pltpu.VMEM((rows, D), BF16)] * 3,
        32 * rows * D * D,
        rows * D * 16 + 32 * D * D,
    )(grad, pre, shifted, *weights, mods)


def split_heads(value, keep_ref, send_ref, d, row):
    for m in range(4):
        keep_ref[m, d, row : row + 32] = value[m * 64 : m * 64 + 32]
        send_ref[m, d, row : row + 32] = value[m * 64 + 32 : m * 64 + 64]


def out_bwd(grad, grad_shifted, middle, feed, branch, attended, weights, mods, base):
    rows = grad.shape[0]
    step = 256
    steps = rows // step

    def kernel(
        g_ref, gs_ref, mid_ref, f_ref, b_ref, a_ref, l_ref, w_ref, v_ref, m_ref, gm_ref, ga_ref,
        keep_ref, send_ref, s_ref, gb_ref,
    ):
        i = pl.program_id(0)

        @pl.when(i == 0)
        def _():
            s_ref[...] = jnp.zeros_like(s_ref)

        g = g_ref[...].astype(F32)
        gs = gs_ref[...]
        hat, rstd = ln_stats(mid_ref[...])
        gm = g + ln_back(gs, hat, rstd, m_ref[base + 4 : base + 5, :])
        gm_ref[...] = gm
        s_ref[0:1, :] += jnp.sum(gs, axis=0, keepdims=True)
        s_ref[1:2, :] += jnp.sum(gs * hat, axis=0, keepdims=True)
        s_ref[2:3, :] += jnp.sum(gm * b_ref[...].astype(F32), axis=0, keepdims=True)
        s_ref[3:4, :] += jnp.sum(g * f_ref[...].astype(F32), axis=0, keepdims=True)
        gb = (gm * m_ref[base + 2 : base + 3, :]).astype(BF16)
        gb_ref[chunk_rows(i, step), :] = gb
        for d in range(NZ):
            ga_ref[:, d * 256 : (d + 1) * 256] = dot_nt(
                gb, out_rows(d, l_ref, w_ref, v_ref)
            ).astype(BF16)

        @pl.when(i == steps - 1)
        def _():
            for d in range(NZ):
                gw = dot_tn(a_ref[:, d * 256 : (d + 1) * 256], gb_ref[...]).astype(BF16)
                split_heads(gw, keep_ref, send_ref, d, 0)

    tile = pl.BlockSpec((step, D), lambda i: (i, 0))
    gshape = jax.ShapeDtypeStruct((4, NZ, 32, D), BF16)
    return call(
        kernel,
        "out_bwd",
        (steps,),
        [tile, tile, tile, tile, tile, full((rows, D))] + out_specs_of(3) + [full((12, D))],
        [tile, tile, full(gshape.shape), full(gshape.shape), full((8, D))],
        [
            jax.ShapeDtypeStruct((rows, D), F32),
            jax.ShapeDtypeStruct((rows, D), BF16),
            gshape,
            gshape,
            jax.ShapeDtypeStruct((8, D), F32),
        ],
        [pltpu.VMEM((rows, D), BF16)],
        4 * rows * D * D,
        rows * D * 24 + 4 * D * D,
    )(grad, grad_shifted, middle, feed, branch, attended, *weights, mods)


def qkv_back(grad_proj, weights, hidden, grad_middle, mods, base, out_dtype, pieces):
    rows = hidden.shape[0]
    step = 640

    cols = D // pieces

    def kernel(p_ref, l_ref, w_ref, v_ref, h_ref, gm_ref, m_ref, *refs):
        gh_refs, (s_ref, acc_ref) = refs[:pieces], refs[pieces:]
        z = pl.program_id(0)

        @pl.when(z == 0)
        def _():
            acc_ref[...] = jnp.zeros_like(acc_ref)
            s_ref[...] = jnp.zeros_like(s_ref)

        def work(own, other):
            def body(i, carry):
                sl = chunk_rows(i, step)
                rows_of = jnp.concatenate([head_rows(own, other, t * 32) for t in range(3)], axis=0)
                acc_ref[sl, :] += dot_nn(p_ref[sl, :], rows_of)
                return carry

            lax.fori_loop(0, rows // step, body, 0)

        by_offset(z, work, l_ref, w_ref, v_ref)

        @pl.when(z == NZ - 1)
        def _():
            def tail(n, carry):
                sl = chunk_rows(n, 256)
                gn = acc_ref[sl, :]
                hat, rstd = ln_stats(h_ref[sl, :].astype(F32))
                gh = gm_ref[sl, :] + ln_back(gn, hat, rstd, m_ref[base + 1 : base + 2, :])
                for i, gh_ref in enumerate(gh_refs):
                    gh_ref[sl, :] = gh[:, i * cols : (i + 1) * cols].astype(out_dtype)
                s_ref[0:1, :] += jnp.sum(gn, axis=0, keepdims=True)
                s_ref[1:2, :] += jnp.sum(gn * hat, axis=0, keepdims=True)
                return carry

            lax.fori_loop(0, rows // 256, tail, 0)

    return call(
        kernel,
        "qkv_back",
        (NZ,),
        [pl.BlockSpec((rows, 768), lambda z: (0, z))]
        + piece_specs(128, 0, 96)
        + [full((rows, D)), full((rows, D)), full((12, D))],
        [full((rows, cols))] * pieces + [full((8, D))],
        [jax.ShapeDtypeStruct((rows, cols), out_dtype)] * pieces
        + [jax.ShapeDtypeStruct((8, D), F32)],
        [pltpu.VMEM((rows, D), F32)],
        6 * rows * D * D,
        rows * D * 20 + 6 * D * D,
    )(grad_proj, *weights, hidden, grad_middle, mods)


def qkv_grad(grad_proj, normed, out_keep, out_send, apart):
    rows = normed.shape[0]
    k = 128

    def kernel(p_ref, n_ref, ok_ref, os_ref, *rest):
        if apart:
            keep_ref, send_refs = rest[-5], rest[-4:]
        else:
            keep_ref, send_ref = rest[-2:]
            send_refs = [send_ref.at[m : m + 1] for m in range(4)]
        for t in range(3):
            gw = dot_tn(p_ref[:, t * 256 : (t + 1) * 256], n_ref[...]).astype(BF16)
            for m in range(4):
                keep_ref[m, 0, t * 32 : t * 32 + 32] = gw[m * 64 : m * 64 + 32]
                send_refs[m][0, 0, t * 32 : t * 32 + 32] = gw[m * 64 + 32 : m * 64 + 64]
        keep_ref[:, :, 96:128] = ok_ref[...]
        for m in range(4):
            send_refs[m][0, :, 96:128] = os_ref[m]

    gspec = pl.BlockSpec((4, 1, k, D), lambda z: (0, z, 0, 0))
    ospec = pl.BlockSpec((4, 1, 32, D), lambda z: (0, z, 0, 0))
    gshape = jax.ShapeDtypeStruct((4, NZ, k, D), BF16)
    sends, send_shapes = [gspec], [gshape]
    if apart:
        sends = [pl.BlockSpec((1, 1, k, D), lambda z: (0, z, 0, 0))] * 4
        send_shapes = [jax.ShapeDtypeStruct((1, NZ, k, D), BF16)] * 4
    return call(
        kernel,
        "qkv_grad",
        (NZ,),
        [pl.BlockSpec((rows, 768), lambda z: (0, z)), full((rows, D)), ospec, ospec],
        [gspec] + sends,
        [gshape] + send_shapes,
        [],
        6 * rows * D * D,
        rows * D * 8 + 8 * D * D,
    )(grad_proj, normed, out_keep, out_send)


def place_call(kernel, name, in_specs, out_specs, out_shape, scratch, nbytes, aliases):
    return pl.pallas_call(
        kernel,
        name=name,
        grid_spec=pltpu.PrefetchScalarGridSpec(
            num_scalar_prefetch=1,
            grid=(8,),
            in_specs=in_specs,
            out_specs=out_specs,
            scratch_shapes=scratch,
        ),
        out_shape=out_shape,
        input_output_aliases=aliases,
        compiler_params=pltpu.CompilerParams(
            dimension_semantics=("arbitrary",), vmem_limit_bytes=VMEM_LIMIT
        ),
        cost_estimate=pl.CostEstimate(flops=0, bytes_accessed=nbytes, transcendentals=0),
    )


def rows_at(place):
    return pl.ds(pl.multiple_of(place * 32, 32), 32)


def prep_attn(place, w_qkv, w_out, b):
    def kernel(c_ref, q_ref, o_ref, out_ref, t_ref):
        r = pl.program_id(0)

        @pl.when(r == 0)
        def _():
            for t in range(3):
                t_ref[t] = q_ref[0, t].T

        at = rows_at(c_ref[0] ^ r)
        for t in range(3):
            out_ref[0, 0, t * 32 : (t + 1) * 32, :] = t_ref[t, at, :]
        out_ref[0, 0, 96:128, :] = o_ref[0, at, :]

    return place_call(
        kernel,
        "prep_attn",
        [
            pl.BlockSpec((1, 3, D, 256), lambda r, c: (b, 0, 0, 0)),
            pl.BlockSpec((1, 256, D), lambda r, c: (b, 0, 0)),
        ],
        pl.BlockSpec((1, 1, 128, D), lambda r, c: (r % 2, r // 2, 0, 0)),
        jax.ShapeDtypeStruct((2, 4, 128, D), BF16),
        [pltpu.VMEM((3, 256, D), BF16)],
        4 * D * D,
        {},
    )(place, w_qkv, w_out)


def prep_feed(place, w_up, w_down, b):
    def kernel(c_ref, u_ref, d_ref, out_ref):
        out_ref[0, 0, 0:128, :] = u_ref[0].T
        out_ref[0, 0, 128:256, :] = d_ref[0]

    return place_call(
        kernel,
        "prep_feed",
        [
            pl.BlockSpec((1, D, 128), lambda r, c: (b, 0, c[0] ^ r)),
            pl.BlockSpec((1, 128, D), lambda r, c: (b, c[0] ^ r, 0)),
        ],
        pl.BlockSpec((1, 1, 256, D), lambda r, c: (r % 2, r // 2, 0, 0)),
        jax.ShapeDtypeStruct((2, 4, 256, D), BF16),
        [],
        8 * D * D,
        {},
    )(place, w_up, w_down)


def finish_attn(place, own, other):
    def kernel(c_ref, own_ref, oth_ref, gq_ref, go_ref, t_ref):
        r = pl.program_id(0)
        at = rows_at(c_ref[0] ^ r)

        def store(ref):
            for b in range(2):
                row = 128 * b
                for t in range(3):
                    t_ref[b, t, at, :] = ref[0, row + t * 32 : row + (t + 1) * 32, :]
                go_ref[b, at, :] = ref[0, row + 96 : row + 128, :].astype(F32)

        @pl.when(r % 2 == 0)
        def _():
            store(own_ref)

        @pl.when(r % 2 == 1)
        def _():
            store(oth_ref)

        @pl.when(r == 7)
        def _():
            for b in range(2):
                for t in range(3):
                    gq_ref[b, t] = t_ref[b, t].T.astype(F32)

    piece = pl.BlockSpec((1, 256, D), lambda r, c: (r // 2, 0, 0))
    return place_call(
        kernel,
        "finish_attn",
        [piece, piece],
        [
            pl.BlockSpec((2, 3, D, 256), lambda r, c: (0, 0, 0, 0), pipeline_mode=CONST),
            pl.BlockSpec((2, 256, D), lambda r, c: (0, 0, 0), pipeline_mode=CONST),
        ],
        [
            jax.ShapeDtypeStruct((2, 3, D, 256), F32),
            jax.ShapeDtypeStruct((2, 256, D), F32),
        ],
        [pltpu.VMEM((2, 3, 256, D), BF16)],
        12 * D * D,
        {},
    )(place, own, other)


def finish_feed(place, own, other, b, earlier):
    def kernel(c_ref, own_ref, oth_ref, *rest):
        gu_ref, gd_ref = rest[-2:]
        r = pl.program_id(0)

        def store(ref):
            gu_ref[0] = ref[0, 0:128, :].T.astype(F32)
            gd_ref[0] = ref[0, 128:256, :].astype(F32)

        @pl.when(r % 2 == 0)
        def _():
            store(own_ref)

        @pl.when(r % 2 == 1)
        def _():
            store(oth_ref)

    piece = pl.BlockSpec((1, 256, D), lambda r, c: (r // 2, 0, 0))
    anywhere = pl.BlockSpec(memory_space=pl.ANY)
    return place_call(
        kernel,
        "finish_feed",
        [piece, piece] + [anywhere] * len(earlier),
        [
            pl.BlockSpec((1, D, 128), lambda r, c: (b, 0, c[0] ^ r)),
            pl.BlockSpec((1, 128, D), lambda r, c: (b, c[0] ^ r, 0)),
        ],
        [jax.ShapeDtypeStruct((2, D, D), F32), jax.ShapeDtypeStruct((2, D, D), F32)],
        [],
        12 * D * D,
        {3 + i: i for i in range(len(earlier))},
    )(place, own, other, *earlier)


def partner(values):
    return lax.ppermute(values, "head", [(i, i ^ 1) for i in range(NZ)])


def rows_to_spatial(rows, odd):
    cols = rows.shape[1]
    whole = lax.dynamic_slice(rows, (256 * odd, 0), (1024, cols))
    part = lax.dynamic_slice(rows, (1024 * (1 - odd), 0), (256, cols)).reshape(8, 2, 16, cols)
    wins = whole.reshape(2, 16, 2, 16, cols).transpose(0, 2, 1, 3, 4).reshape(1024, cols)
    left, right = part[:, 0].reshape(128, cols), part[:, 1].reshape(128, cols)
    keep = jnp.where(odd == 0, left, right)
    got = partner(jnp.where(odd == 0, right, left))
    top, bottom = jnp.where(odd == 0, keep, got), jnp.where(odd == 0, got, keep)
    part = jnp.concatenate([top, bottom], axis=0)
    return jnp.where(
        odd == 0,
        jnp.concatenate([wins, part], axis=0),
        jnp.concatenate([part, wins], axis=0),
    )


def last_window(wins, odd):
    part = lax.dynamic_slice(wins, (1024 * (1 - odd), 0), (256, wins.shape[1]))
    keep = jnp.where(odd == 0, part[:128], part[128:])
    return keep, jnp.where(odd == 0, part[128:], part[:128])


def whole_windows(wins, odd):
    cols = wins.shape[1]
    whole = lax.dynamic_slice(wins, (256 * odd, 0), (1024, cols))
    return whole.reshape(2, 2, 16, 16, cols).transpose(0, 2, 1, 3, 4).reshape(1024, cols)


def spatial_to_rows(whole, keep, got, odd):
    cols = whole.shape[1]
    left, right = jnp.where(odd == 0, keep, got), jnp.where(odd == 0, got, keep)
    part = jnp.stack([left.reshape(8, 16, cols), right.reshape(8, 16, cols)], axis=1)
    part = part.reshape(256, cols)
    return jnp.where(
        odd == 0,
        jnp.concatenate([whole, part], axis=0),
        jnp.concatenate([part, whole], axis=0),
    )


def exchange(values):
    return lax.all_to_all(values, "head", 0, 0, tiled=True)


def spatial_to_tubes(wins):
    cols = wins.shape[1]
    return exchange(
        wins.reshape(5, 2, 8, 2, 8, cols).transpose(1, 3, 0, 2, 4, 5).reshape(1280, cols)
    )


def from_quads(quads):
    cols = quads.shape[1]
    return quads.reshape(2, 2, 5, 8, 8, cols).transpose(2, 0, 3, 1, 4, 5).reshape(1280, cols)


def toeplitz(side):
    span = 2 * side - 1
    b = lax.broadcasted_iota(jnp.int32, (span, side, side), 0)
    j = lax.broadcasted_iota(jnp.int32, (span, side, side), 1)
    i = lax.broadcasted_iota(jnp.int32, (span, side, side), 2)
    return (b == i - j + side - 1).astype(F32)


def toeplitz_pair(side):
    span = 2 * side - 1
    shape = (span * span, side * side, side * side)
    r = lax.broadcasted_iota(jnp.int32, shape, 0)
    j = lax.broadcasted_iota(jnp.int32, shape, 1)
    i = lax.broadcasted_iota(jnp.int32, shape, 2)
    dy = i // side - j // side + side - 1
    dx = i % side - j % side + side - 1
    return (r == dy * span + dx).astype(F32)


CORE, ROW_X, ROW_Y = 1, 2, 4


def swap(values, bit):
    return lax.ppermute(values, "clip", [(i, i ^ bit) for i in range(8)])


def from_z(values, d):
    return lax.ppermute(values, "head", [((i + d) % NZ, i) for i in range(NZ)])


def sync(*values):
    return lax.optimization_barrier(values)


def add(first, second):
    return (first.astype(F32) + second.astype(F32)).astype(BF16)


def line_stage(piece):
    return [from_z(piece, d) for d in (1, 2, 3)]


def others(by_z, z):
    return [lax.dynamic_index_in_dim(by_z, (z + d) % NZ, 0, keepdims=False) for d in (1, 2, 3)]


def cross_stage(own):
    return [own] + [swap(own, m * 2) for m in (1, 2, 3)]


def sides_stage(own):
    return [own, swap(own, ROW_X), swap(own, ROW_Y)]


def corner_stage(sides):
    half = sides[0].shape[1] // 2
    return [swap(sides[1][:, :half], ROW_Y), swap(sides[2][:, half:], ROW_X)]


def joined(sides, corner):
    return jnp.stack(sides + [jnp.concatenate(corner, axis=1)])


def sum_core(keep, got):
    return [add(keep[m], got[m].reshape(keep.shape[1:])) for m in range(4)]


def send_plane(totals, offsets):
    return [swap(totals[m], m * 2) for m in offsets]


def to_places(total, z):
    twice = jnp.concatenate([total, total[: NZ - 1]], axis=0)
    return lax.dynamic_slice_in_dim(twice, (NZ - z) % NZ, NZ, axis=0)


def sum_plane(totals, got, z):
    total = totals[0].astype(F32)
    for value in got:
        total = total + value.astype(F32)
    return to_places(total.astype(BF16), z)


def send_cross(totals):
    half = totals[0].shape[1] // 2
    first = [t[:, :half] for t in totals]
    second = [t[:, half:] for t in totals]
    by_x = swap(jnp.stack([first[1], first[3]]), ROW_X)
    by_y = swap(jnp.stack([second[2], second[3]]), ROW_Y)
    return by_x, by_y


def sum_cross(totals, got):
    half = totals[0].shape[1] // 2
    by_x, by_y = got
    first = [add(totals[0][:, :half], by_x[0]), add(totals[2][:, :half], by_x[1])]
    second = [add(totals[0][:, half:], by_y[0]), add(totals[1][:, half:], by_y[1])]
    return first, second


def send_corner(halves):
    return swap(halves[0][1], ROW_Y), swap(halves[1][1], ROW_X)


def sum_corner(halves, got, z):
    first = add(halves[0][0], got[0])
    second = add(halves[1][0], got[1])
    return to_places(jnp.concatenate([first, second], axis=1), z)


def sum_line(by_z):
    return lax.psum_scatter(by_z, "head", scatter_dimension=0)


def on_device_windows(
    tokens, d_out, modulation, frame_counts, w_qkv, w_out, w_up, w_down, table_s, table_t
):
    z = lax.axis_index("head")
    c = lax.axis_index("clip")
    place = c.astype(jnp.int32).reshape(1)
    chip = c // 2
    odd = z % 2
    mods = modulation[0]
    n_s, n_t = table_s.shape[1], table_t.shape[1]
    hot_s, hot_t = toeplitz(SWIN), toeplitz_pair(TWIN)
    fc = frame_counts

    def spatial_base(tables):
        base = jnp.einsum(
            "hab,bji->hjai", tables[:, :n_s].reshape(16, 31, 31), hot_s, precision=HIGHEST_PRECISION
        ).reshape(16, 16, 496)
        return jnp.pad(base, ((0, 0), (0, 0), (0, 16)))

    def tube_base(tables):
        base = jnp.einsum(
            "htr,rjk->hjtk", tables[:, n_s:].reshape(16, 9, 225), hot_t, precision=HIGHEST_PRECISION
        ).reshape(16, 64, 576)
        return jnp.pad(base, ((0, 0), (0, 0), (0, 64)))

    def table_rows(first, second):
        first = jnp.pad(first, ((0, 0), (0, D - n_s)))
        second = jnp.pad(second, ((0, 0), (0, 15 * D - n_t)))
        values = jnp.concatenate([first, second], axis=1).astype(BF16)
        return values.reshape(NZ, 4, 16, D).transpose(1, 0, 2, 3)

    spatial = ((1, 5, 256), 16, 16, False)
    tube = ((5, 4, 64), 5, 64, True)

    local_a0 = prep_attn(place, w_qkv, w_out, 0)
    line_a0 = line_stage(local_a0[0, 0])
    table_piece = jnp.concatenate([table_s, table_t], axis=1)
    tables = [from_z(table_piece, d) for d in (1, 2)]
    local_f0 = prep_feed(place, w_up, w_down, 0)
    local_a1 = prep_attn(place, w_qkv, w_out, 1)
    local_f1 = prep_feed(place, w_up, w_down, 1)
    line_a0, local_f0, local_a1, local_f1, tables, tokens, table_piece = sync(
        line_a0, local_f0, local_a1, local_f1, tables, tokens, table_piece
    )
    own_a0 = cross_stage(jnp.stack(line_a0))
    z_u0 = lax.all_gather(local_f0[0, 0, :128], "head")
    z_d0 = lax.all_gather(local_f0[0, 0, 128:], "head")
    tables = jnp.stack([table_piece] + tables + [from_z(table_piece, 3)])
    tables = jnp.concatenate(
        [lax.dynamic_slice_in_dim(tables, chip ^ m, 1, axis=1) for m in range(4)], axis=1
    ).reshape(16, n_s + n_t)
    base_s = spatial_base(tables)
    hidden0 = rows_to_spatial(tokens, odd)
    own_a0, hidden0, tables, base_s, z_u0 = sync(own_a0, hidden0, tables, base_s, z_u0)
    own_a0 = jnp.stack(own_a0)
    other_a0 = swap(own_a0, CORE)
    own_u0 = sides_stage(jnp.stack(others(z_u0, z)))
    own_a0, other_a0 = sync(own_a0, other_a0)
    weights_a0 = (local_a0, own_a0, other_a0)
    normed0, qkv0 = ln_qkv(hidden0, mods, weights_a0, 0)
    qkv0, own_u0, z_d0 = sync(qkv0, own_u0, z_d0)
    corner_u0 = corner_stage(own_u0)
    own_d0 = sides_stage(jnp.stack(others(z_d0, z)))
    z_a1 = lax.all_gather(local_a1[0, 0], "head")
    attended0 = attn_fwd(qkv0, base_s, fc, spatial)
    attended0, corner_u0, own_d0, z_a1 = sync(attended0, corner_u0, own_d0, z_a1)
    corner_d0 = corner_stage(own_d0)
    own_u0 = joined(own_u0, corner_u0)
    other_u0 = swap(own_u0, CORE)
    branch0, middle0, shifted0 = out_proj(attended0, weights_a0, hidden0, mods, 0)
    own_a1 = jnp.stack(others(z_a1, z))
    shifted0, corner_d0, other_u0, own_a1 = sync(shifted0, corner_d0, other_u0, own_a1)
    own_d0 = joined(own_d0, corner_d0)
    other_d0 = swap(own_d0, CORE)
    z_f1 = lax.all_gather(local_f1[0, 0], "head")
    shifted0, other_d0 = sync(shifted0, other_d0)
    own_a1 = cross_stage(own_a1)
    weights_f0 = (local_f0, own_u0, other_u0, own_d0, other_d0)
    pre0, feed0, hidden1 = ffn_fwd(shifted0, weights_f0, 0, middle0, mods, 0)
    hidden1, z_f1, own_a1, tables, d_out = sync(hidden1, z_f1, own_a1, tables, d_out)
    tubes1 = spatial_to_tubes(hidden1)
    own_a1 = jnp.stack(own_a1)
    other_a1 = swap(own_a1, CORE)
    own_f1 = cross_stage(jnp.stack(others(z_f1, z)))
    base_t = tube_base(tables)
    spatial_d = rows_to_spatial(d_out, odd)
    tubes1, other_a1, base_t, spatial_d = sync(tubes1, other_a1, base_t, spatial_d)
    weights_a1 = (local_a1, own_a1, other_a1)
    tubes_d = spatial_to_tubes(spatial_d)
    normed1, qkv1 = ln_qkv(tubes1, mods, weights_a1, 6)
    qkv1, own_f1 = sync(qkv1, own_f1)
    own_f1 = jnp.stack(own_f1)
    other_f1 = swap(own_f1, CORE)
    attended1 = attn_fwd(qkv1, base_t, fc, tube)
    branch1, middle1, shifted1 = out_proj(attended1, weights_a1, tubes1, mods, 6)
    shifted1, other_f1 = sync(shifted1, other_f1)
    weights_f1 = (local_f1, own_f1, other_f1, own_f1, other_f1)
    pre1, feed1, hidden2 = ffn_fwd(shifted1, weights_f1, 1, middle1, mods, 6)
    hidden2, tubes_d = sync(hidden2, tubes_d)
    live = lax.broadcasted_iota(jnp.int32, (1280, 1), 0) // 256 < fc[0]
    grad2 = jnp.where(live, tubes_d, 0)
    out_wins = exchange(jnp.where(live, hidden2, 0))
    f1_keep, f1_send, g_shift1 = ffn_bwd(grad2, pre1, shifted1, weights_f1, 1, mods, 6)
    f1_keep, f1_send, g_shift1, out_wins = sync(f1_keep, f1_send, g_shift1, out_wins)
    f1_got = swap(f1_send, CORE)
    g_mid1, g_att1, o1_keep, o1_send, sums_o1 = out_bwd(
        grad2, g_shift1, middle1, feed1, branch1, attended1, weights_a1, mods, 6
    )
    g_att1, f1_got = sync(g_att1, f1_got)
    total_f1 = sum_core(f1_keep, f1_got)
    g_att1, total_f1 = sync(g_att1, total_f1)
    got_f1 = send_cross(total_f1)
    g_proj1, g_base1 = attn_bwd(qkv1, g_att1, base_t, fc, tube)
    g_proj1, g_base1, got_f1 = sync(g_proj1, g_base1, got_f1)
    half_f1 = sum_cross(total_f1, got_f1)
    half_f1, g_proj1 = sync(half_f1, g_proj1)
    got_f1 = send_corner(half_f1)
    g_hid1, sums_q1 = qkv_back(g_proj1, weights_a1, tubes1, g_mid1, mods, 6, BF16, 1)
    g_hid1, g_proj1, out_wins, g_base1, got_f1 = sync(g_hid1, g_proj1, out_wins, g_base1, got_f1)
    grad1 = exchange(g_hid1)
    z_f1 = sum_corner(half_f1, got_f1, z)
    a1_keep, *a1_send = qkv_grad(g_proj1, normed1, o1_keep, o1_send, True)
    a1_got = [swap(v, CORE) for v in a1_send]
    gt_t = jnp.einsum(
        "hjtk,rjk->htr",
        g_base1[:, :, :576].reshape(16, 64, 9, 64),
        hot_t,
        precision=HIGHEST_PRECISION,
    ).reshape(16, n_t)
    out_wins = from_quads(out_wins)
    out_keep, out_send = last_window(out_wins, odd)
    total_a1 = sum_core(a1_keep, a1_got)
    grad1, total_a1, z_f1, gt_t, out_wins, out_keep, out_send = sync(
        grad1, total_a1, z_f1, gt_t, out_wins, out_keep, out_send
    )
    grad1 = from_quads(grad1)
    mine_f1 = sum_line(z_f1)
    out_got = partner(out_send)
    got_a1 = send_plane(total_a1, (1, 2, 3))
    f0_keep, f0_send, g_shift0 = ffn_bwd(grad1, pre0, shifted0, weights_f0, 0, mods, 0)
    f0_keep, f0_send, g_shift0, mine_f1, got_a1, out_got = sync(
        f0_keep, f0_send, g_shift0, mine_f1, got_a1, out_got
    )
    f0_got = swap(f0_send, CORE)
    sides_f1 = sides_stage(mine_f1[None])
    mine_a1 = sum_line(sum_plane(total_a1, got_a1, z))
    g_mid0, g_att0, o0_keep, o0_send, sums_o0 = out_bwd(
        grad1, g_shift0, middle0, feed0, branch0, attended0, weights_a0, mods, 0
    )
    g_att0, f0_got, sides_f1 = sync(g_att0, f0_got, sides_f1)
    total_f0 = sum_core(f0_keep, f0_got)
    g_att0, total_f0 = sync(g_att0, total_f0)
    got_f0 = send_cross(total_f0)
    corner_f1 = corner_stage(sides_f1)
    g_proj0, g_base0 = attn_bwd(qkv0, g_att0, base_s, fc, spatial)
    a0_keep, a0_send = qkv_grad(g_proj0, normed0, o0_keep, o0_send, False)
    a0_keep, a0_send, got_f0, corner_f1, mine_a1, g_proj0, g_base0 = sync(
        a0_keep, a0_send, got_f0, corner_f1, mine_a1, g_proj0, g_base0
    )
    a0_got = swap(a0_send, CORE)
    half_f0 = sum_cross(total_f0, got_f0)
    half_f0, g_base0, sides_f1, corner_f1 = sync(half_f0, g_base0, sides_f1, corner_f1)
    got_f0 = send_corner(half_f0)
    own_gf1 = joined(sides_f1, corner_f1).reshape(4, 256, D)
    g_feed = finish_feed(place, own_gf1, swap(own_gf1, CORE), 1, ())
    gt_s = jnp.einsum(
        "hjai,bji->hab",
        g_base0[:, :, :496].reshape(16, 16, 31, 16),
        hot_s,
        precision=HIGHEST_PRECISION,
    ).reshape(16, n_s)
    gt = table_rows(gt_s, gt_t)
    half_f0, got_f0, a0_got, g_proj0, g_feed, gt = sync(
        half_f0, got_f0, a0_got, g_proj0, g_feed, gt
    )
    z_f0 = sum_corner(half_f0, got_f0, z)
    total_a0 = sum_core(a0_keep, a0_got)
    total_a0 = [jnp.concatenate([total_a0[m], gt[m]], axis=1) for m in range(4)]
    total_a0, z_f0, g_proj0 = sync(total_a0, z_f0, g_proj0)
    mine_f0 = sum_line(z_f0)
    got_a0 = send_cross(total_a0)
    grad0, sums_q0 = qkv_back(g_proj0, weights_a0, hidden0, g_mid0, mods, 0, F32, 1)
    sides_a1 = sides_stage(mine_a1[None])
    grad0, sums_q0, got_a0, sides_a1 = sync(grad0, sums_q0, got_a0, sides_a1)
    half_a0 = sum_cross(total_a0, got_a0)
    half_a0, grad0, sums_q0 = sync(half_a0, grad0, sums_q0)
    got_a0 = send_corner(half_a0)
    corner_a1 = corner_stage(sides_a1)
    mod_rows = jnp.concatenate(
        [
            sums_q0[0:2], sums_o0[2:3], sums_o0[0:2], sums_o0[3:4],
            sums_q1[0:2], sums_o1[2:3], sums_o1[0:2], sums_o1[3:4],
        ],
        axis=0,
    )
    mod_got = partner(mod_rows)
    got_a0, corner_a1, mine_f0, mod_got, mod_rows = sync(
        got_a0, corner_a1, mine_f0, mod_got, mod_rows
    )
    z_a0 = sum_corner(half_a0, got_a0, z)
    mod_sum = mod_rows + mod_got
    z_a0, mine_f0, mod_sum = sync(z_a0, mine_f0, mod_sum)
    mine_a0 = sum_line(z_a0)
    own_gf0 = cross_stage(mine_f0)
    own_ga1 = joined(sides_a1, corner_a1).reshape(4, 128, D)
    rows_whole = whole_windows(grad0, odd)
    output = spatial_to_rows(whole_windows(out_wins, odd), out_keep, out_got, odd)
    rows_keep, rows_send = last_window(grad0, odd)
    mine_a0, own_gf0, own_ga1, rows_keep, rows_send, rows_whole, output = sync(
        mine_a0, own_gf0, own_ga1, rows_keep, rows_send, rows_whole, output
    )
    own_ga0 = cross_stage(mine_a0)
    rows_got = partner(rows_send)
    own_gf0 = jnp.stack(own_gf0)
    g_feed = finish_feed(place, own_gf0, swap(own_gf0, CORE), 0, g_feed)
    own_ga0, g_feed, rows_got, own_ga1, mod_sum = sync(own_ga0, g_feed, rows_got, own_ga1, mod_sum)
    own_ga0 = jnp.stack(own_ga0)
    own_ga = jnp.concatenate([own_ga0[:, :128], own_ga1, own_ga0[:, 128:]], axis=1)
    mod_got = lax.ppermute(mod_sum, "head", [(i, i ^ 2) for i in range(NZ)])
    grad_tokens = spatial_to_rows(rows_whole, rows_keep, rows_got, odd)
    other_ga = swap(own_ga, CORE)
    g_attn = finish_attn(place, own_ga, other_ga)
    tab = own_ga[:, 256:272].astype(F32) + other_ga[:, 256:272].astype(F32)
    tab = jnp.concatenate(
        [lax.dynamic_slice_in_dim(tab, chip ^ m, 1, axis=0) for m in range(4)], axis=0
    )
    tab = tab.reshape(4, 16 * D)
    return (
        output,
        grad_tokens,
        (mod_sum + mod_got)[None],
        g_attn[0],
        g_attn[1],
        g_feed[0],
        g_feed[1],
        tab[:, :n_s],
        tab[:, D : D + n_t],
    )


def solution(mesh):
    if mesh.shape["head"] == NZ and mesh.shape["clip"] == 8:
        body = on_device_windows
    else:
        body = on_device
    return jax.shard_map(
        body,
        mesh=mesh,
        in_specs=(
            P(("clip", "head"), None),
            P(("clip", "head"), None),
            P("clip", None, None),
            P("clip"),
            P(None, None, None, "head"),
            P(None, "head", None),
            P(None, None, "head"),
            P(None, "head", None),
            P("head", None),
            P("head", None),
        ),
        out_specs=(
            P(("clip", "head"), None),
            P(("clip", "head"), None),
            P("clip", None, None),
            P(None, None, None, "head"),
            P(None, "head", None),
            P(None, None, "head"),
            P(None, "head", None),
            P("head", None),
            P("head", None),
        ),
        check_vma=False,
    )
```

```python
import jax
import jax.numpy as jnp
from jax import lax
from jax.experimental import pallas as pl
from jax.experimental.pallas import tpu as pltpu
from jax.sharding import PartitionSpec as P

HD = 64
FH = 32
FW = 32
SWIN = 16
TWIN = 8
PADF = 5


EPS = 1e-06
HIGHEST_PRECISION = lax.Precision.HIGHEST
NEGATIVE = -1e30


def layer_norm(values, shift_row, scale_row):
    average = jnp.mean(values, axis=-1, keepdims=True)
    centred = values - average
    spread = jnp.mean(centred * centred, axis=-1, keepdims=True)
    return centred * lax.rsqrt(spread + EPS) * (1.0 + scale_row) + shift_row


def gelu_tanh(values):
    return jax.nn.gelu(values, approximate=True)


def window_index(side_t, side_len):
    window_size = side_t * side_len * side_len
    places = jnp.arange(window_size, dtype=jnp.int32)
    time_pos = places // (side_len * side_len)
    height_pos = places // side_len % side_len
    width_pos = places % side_len
    span_len = 2 * side_len - 1
    return (
        (time_pos[:, None] - time_pos[None, :] + side_t - 1) * span_len * span_len
        + (height_pos[:, None] - height_pos[None, :] + side_len - 1) * span_len
        + (width_pos[:, None] - width_pos[None, :] + side_len - 1)
    )


def to_windows(values, side_t, side_len):
    tail_shape = values.shape[1:]
    frames = values.shape[0] // (FH * FW)
    shaped = values.reshape(
        (frames // side_t, side_t, FH // side_len, side_len, FW // side_len, side_len) + tail_shape
    )
    axis_order = (0, 2, 4, 1, 3, 5) + tuple(range(6, 6 + len(tail_shape)))
    shaped = shaped.transpose(axis_order)
    return shaped.reshape((-1, side_t * side_len * side_len) + tail_shape)


def from_windows(values, side_t, side_len):
    tail_shape = values.shape[2:]
    blocks_high = FH // side_len
    blocks_wide = FW // side_len
    frame_groups = values.shape[0] // (blocks_high * blocks_wide)
    shaped = values.reshape(
        (frame_groups, blocks_high, blocks_wide, side_t, side_len, side_len) + tail_shape
    )
    axis_order = (0, 3, 1, 4, 2, 5) + tuple(range(6, 6 + len(tail_shape)))
    return shaped.transpose(axis_order).reshape((frame_groups * side_t * FH * FW,) + tail_shape)


def on_device(
    tokens, d_out, modulation, frame_counts, w_qkv, w_out, w_up, w_down, table_s, table_t
):
    local_rows = tokens.shape[0]
    clip_len = PADF * FH * FW
    group_clips = modulation.shape[0]
    group_rows = group_clips * clip_len
    scale_dot = HD ** (-0.5)
    my_index = lax.axis_index("head")
    first_row = my_index * local_rows
    row_ids = first_row + jnp.arange(local_rows, dtype=jnp.int32)
    clip_slots = jnp.arange(group_clips, dtype=jnp.int32)
    row_onehot = ((row_ids // clip_len)[:, None] == clip_slots[None, :]).astype(jnp.float32)
    count_float = frame_counts.astype(jnp.float32)
    row_frames = jnp.dot(row_onehot, count_float, precision=HIGHEST_PRECISION)
    row_keep = ((row_ids % clip_len // (FH * FW)).astype(jnp.float32) < row_frames).astype(
        jnp.float32
    )[:, None]
    group_ids = jnp.arange(group_rows, dtype=jnp.int32)
    group_onehot = ((group_ids // clip_len)[:, None] == clip_slots[None, :]).astype(jnp.float32)
    group_frames = jnp.dot(group_onehot, count_float, precision=HIGHEST_PRECISION)
    group_keep = (group_ids % clip_len // (FH * FW)).astype(jnp.float32) < group_frames

    def block_shape(block_id):
        if block_id == 0:
            return (1, SWIN)
        return (PADF, TWIN)

    def mod_row(slot):
        return jnp.dot(row_onehot, modulation[:, slot, :], precision=HIGHEST_PRECISION)

    def rows_in(values):
        return lax.all_gather(values, "head", axis=0, tiled=True)

    def grads_in(values):
        return lax.all_gather(values, "head", axis=0, tiled=True)

    def rows_out(full_rows, weight):
        return lax.psum_scatter(
            jnp.dot(full_rows, weight, preferred_element_type=jnp.float32).astype(jnp.bfloat16),
            "head",
            scatter_dimension=0,
            tiled=True,
        ).astype(jnp.float32)

    def grads_out(full_rows, weight, einsum_form):
        return lax.psum_scatter(
            jnp.einsum(einsum_form, full_rows, weight, preferred_element_type=jnp.float32).astype(
                jnp.bfloat16
            ),
            "head",
            scatter_dimension=0,
            tiled=True,
        ).astype(jnp.float32)

    def rows_keep(block_id):
        if block_id == 0:
            return None
        return to_windows(group_keep[:, None], PADF, TWIN)[:, :, 0]

    def shape_windows(projected, side_t, side_len):
        head_count = projected.shape[-1] // HD
        window_size = side_t * side_len * side_len
        windows = to_windows(projected, side_t, side_len)
        return windows.reshape(windows.shape[0], window_size, 3, head_count, HD)

    def shape_grad(grad_attended, side_t, side_len):
        head_count = grad_attended.shape[-1] // HD
        window_size = side_t * side_len * side_len
        windows = to_windows(grad_attended, side_t, side_len)
        return windows.reshape(windows.shape[0], window_size, head_count, HD)

    def flat_rows(windowed, side_t, side_len):
        return from_windows(windowed, side_t, side_len)

    def logits_of(queries, key_rows, table_arg, rel_index, keep_win):
        logits = (
            jnp.einsum("wqhe,wkhe->whqk", queries, key_rows, preferred_element_type=jnp.float32)
            * scale_dot
        )
        logits = logits + table_arg[:, rel_index][None]
        if keep_win is not None:
            logits = jnp.where(keep_win[:, None, None, :], logits, NEGATIVE)
        return logits

    def attend(windows, table_arg, rel_index, keep_win):
        logits = logits_of(windows[:, :, 0], windows[:, :, 1], table_arg, rel_index, keep_win)
        row_max = jnp.max(logits, axis=-1, keepdims=True)
        exponent = jnp.exp(logits - row_max)
        row_total = jnp.sum(exponent, axis=-1, keepdims=True)
        probs = exponent / row_total
        log_total = row_max + jnp.log(row_total)
        attended = jnp.einsum(
            "whqk,wkhe->wqhe",
            probs.astype(jnp.bfloat16),
            windows[:, :, 2],
            preferred_element_type=jnp.float32,
        )
        return (attended.reshape(attended.shape[0], attended.shape[1], -1), log_total)

    def attend_back(windows, grad_windows, log_total, table_arg, rel_index, keep_win):
        queries = windows[:, :, 0]
        key_rows = windows[:, :, 1]
        value_rows = windows[:, :, 2]
        logits = logits_of(queries, key_rows, table_arg, rel_index, keep_win)
        probs = jnp.exp(logits - log_total)
        grad_probs = jnp.einsum(
            "wqhe,wkhe->whqk", grad_windows, value_rows, preferred_element_type=jnp.float32
        )
        grad_values = jnp.einsum(
            "whqk,wqhe->wkhe",
            probs.astype(jnp.bfloat16),
            grad_windows,
            preferred_element_type=jnp.float32,
        )
        grad_logits = (
            probs * (grad_probs - jnp.sum(grad_probs * probs, axis=-1, keepdims=True))
        ).astype(jnp.bfloat16)
        head_count = queries.shape[2]
        table_terms = jnp.sum(grad_logits.astype(jnp.float32), axis=0).reshape(head_count, -1)
        grad_table = jax.ops.segment_sum(
            table_terms.T, rel_index.reshape(-1), num_segments=table_arg.shape[1]
        ).T
        grad_queries = (
            jnp.einsum("whqk,wkhe->wqhe", grad_logits, key_rows, preferred_element_type=jnp.float32)
            * scale_dot
        )
        grad_keys = (
            jnp.einsum("whqk,wqhe->wkhe", grad_logits, queries, preferred_element_type=jnp.float32)
            * scale_dot
        )
        grad_stack = jnp.stack([grad_queries, grad_keys, grad_values], axis=2)
        return (
            grad_stack.reshape(grad_stack.shape[0], grad_stack.shape[1], 3, head_count * HD),
            grad_table,
        )

    def forward_block(hidden, block_id):
        side_t, side_len = block_shape(block_id)
        table_local = table_s if block_id == 0 else table_t
        rel_index = window_index(side_t, side_len)
        normed = layer_norm(hidden, mod_row(6 * block_id), mod_row(6 * block_id + 1)).astype(
            jnp.bfloat16
        )
        plan = None
        normed_in = rows_in(normed)
        qkv_use, out_use, table_use = (w_qkv[block_id], w_out[block_id], table_local)
        keep_win = rows_keep(block_id)
        projected = jnp.einsum(
            "gd,cde->gce", normed_in, qkv_use, preferred_element_type=jnp.float32
        ).astype(jnp.bfloat16)
        windows = shape_windows(projected, side_t, side_len)
        attended_win, log_total = attend(windows, table_use, rel_index, keep_win)
        attended = flat_rows(attended_win, side_t, side_len).astype(jnp.bfloat16)
        branch = rows_out(attended, out_use)
        middle = hidden + mod_row(6 * block_id + 2) * branch
        shifted = layer_norm(middle, mod_row(6 * block_id + 3), mod_row(6 * block_id + 4)).astype(
            jnp.bfloat16
        )
        up_full, down_full = (
            lax.all_gather(w_up[block_id], "head", axis=1, tiled=True),
            lax.all_gather(w_down[block_id], "head", axis=0, tiled=True),
        )
        pre_gelu = jnp.dot(shifted, up_full, preferred_element_type=jnp.float32)
        activated = gelu_tanh(pre_gelu).astype(jnp.bfloat16)
        feed_out = jnp.dot(activated, down_full, preferred_element_type=jnp.float32)
        mlp_state = (shifted, pre_gelu, activated, up_full, down_full)
        result = middle + mod_row(6 * block_id + 5) * feed_out
        attn_state = (
            normed_in,
            projected,
            log_total,
            attended,
            qkv_use,
            out_use,
            table_use,
            keep_win,
            plan,
        )
        saved_state = (hidden, attn_state, branch, middle, feed_out, mlp_state)
        return (saved_state, result)

    def backward_block(saved_state, grad_result, block_id):
        hidden, attn_state, branch, middle, feed_out, mlp_state = saved_state
        normed_in, projected, log_total, attended, qkv_use, out_use, table_use, keep_win, plan = (
            attn_state
        )
        shifted_in, pre_gelu, activated, up_weight, down_weight = mlp_state
        side_t, side_len = block_shape(block_id)
        rel_index = window_index(side_t, side_len)
        grad_feed = (grad_result * mod_row(6 * block_id + 5)).astype(jnp.bfloat16)
        grad_gate_mlp = grad_result * feed_out
        grad_down = jnp.einsum(
            "gf,gd->fd", activated, grad_feed, preferred_element_type=jnp.float32
        )
        grad_activated = jnp.einsum(
            "gd,fd->gf", grad_feed, down_weight, preferred_element_type=jnp.float32
        )
        grad_pre = jax.vjp(gelu_tanh, pre_gelu)[1](grad_activated)[0].astype(jnp.bfloat16)
        grad_up = jnp.einsum("gd,gf->df", shifted_in, grad_pre, preferred_element_type=jnp.float32)
        grad_shifted = jnp.einsum(
            "gf,df->gd", grad_pre, up_weight, preferred_element_type=jnp.float32
        )
        grad_up, grad_down = (
            lax.psum_scatter(
                grad_up.astype(jnp.bfloat16), "head", scatter_dimension=1, tiled=True
            ).astype(jnp.float32),
            lax.psum_scatter(
                grad_down.astype(jnp.bfloat16), "head", scatter_dimension=0, tiled=True
            ).astype(jnp.float32),
        )
        unused_mid, pull_second = jax.vjp(
            layer_norm, middle, mod_row(6 * block_id + 3), mod_row(6 * block_id + 4)
        )
        grad_mid_norm, grad_shift_mlp, grad_scale_mlp = pull_second(grad_shifted)
        grad_middle = grad_result + grad_mid_norm
        grad_branch = (grad_middle * mod_row(6 * block_id + 2)).astype(jnp.bfloat16)
        grad_gate_att = grad_middle * branch
        branch_in = grads_in(grad_branch)
        grad_wout = jnp.einsum("ge,gd->ed", attended, branch_in, preferred_element_type=jnp.float32)
        grad_attended = jnp.einsum(
            "gd,ed->ge", branch_in, out_use, preferred_element_type=jnp.float32
        ).astype(jnp.bfloat16)
        windows = shape_windows(projected, side_t, side_len)
        grad_windows = shape_grad(grad_attended, side_t, side_len)
        grad_stack, grad_table = attend_back(
            windows, grad_windows, log_total, table_use, rel_index, keep_win
        )
        grad_projected = flat_rows(grad_stack, side_t, side_len).astype(jnp.bfloat16)
        grad_qkv = jnp.einsum(
            "gd,gce->cde", normed_in, grad_projected, preferred_element_type=jnp.float32
        )
        grad_normed = grads_out(grad_projected, qkv_use, "gce,cde->gd")
        unused_hid, pull_first = jax.vjp(
            layer_norm, hidden, mod_row(6 * block_id), mod_row(6 * block_id + 1)
        )
        grad_hid_norm, grad_shift_att, grad_scale_att = pull_first(grad_normed)
        grad_hidden = grad_middle + grad_hid_norm
        mod_terms = jnp.stack(
            [
                grad_shift_att,
                grad_scale_att,
                grad_gate_att,
                grad_shift_mlp,
                grad_scale_mlp,
                grad_gate_mlp,
            ],
            axis=1,
        )
        grad_mods = jnp.einsum("rc,rke->cke", row_onehot, mod_terms, precision=HIGHEST_PRECISION)
        return (grad_hidden, grad_mods, (grad_qkv, grad_wout, grad_up, grad_down, grad_table))

    hidden_first = tokens.astype(jnp.float32)
    saved_first, hidden_second = forward_block(hidden_first, 0)
    saved_second, hidden_last = forward_block(hidden_second, 1)
    output = (hidden_last * row_keep).astype(jnp.bfloat16)
    grad_second, mods_second, weights_second = backward_block(
        saved_second, d_out.astype(jnp.float32) * row_keep, 1
    )
    grad_first, mods_first, weights_first = backward_block(saved_first, grad_second, 0)
    grad_modulation = lax.psum(
        jnp.concatenate([mods_first, mods_second], axis=1).astype(jnp.bfloat16), "head"
    ).astype(jnp.float32)
    summed = (
        lax.psum(
            jnp.stack([weights_first[0], weights_second[0]]).astype(jnp.bfloat16), "clip"
        ).astype(jnp.float32),
        lax.psum(
            jnp.stack([weights_first[1], weights_second[1]]).astype(jnp.bfloat16), "clip"
        ).astype(jnp.float32),
        lax.psum(
            jnp.stack([weights_first[2], weights_second[2]]).astype(jnp.bfloat16), "clip"
        ).astype(jnp.float32),
        lax.psum(
            jnp.stack([weights_first[3], weights_second[3]]).astype(jnp.bfloat16), "clip"
        ).astype(jnp.float32),
        lax.psum(weights_first[4].astype(jnp.bfloat16), "clip").astype(jnp.float32),
        lax.psum(weights_second[4].astype(jnp.bfloat16), "clip").astype(jnp.float32),
    )
    return (
        output,
        grad_first,
        grad_modulation,
        summed[0],
        summed[1],
        summed[2],
        summed[3],
        summed[4],
        summed[5],
    )


F32 = jnp.float32
BF16 = jnp.bfloat16
VMEM_LIMIT = 58 * 1024 * 1024
NZ = 4
D = 1024
HPZ = 4
CONST = pl.Buffered(1)


def dot_nn(a, b):
    return lax.dot_general(a, b, (((1,), (0,)), ((), ())), preferred_element_type=F32)


def dot_nt(a, b):
    return lax.dot_general(a, b, (((1,), (1,)), ((), ())), preferred_element_type=F32)


def dot_tn(a, b):
    return lax.dot_general(a, b, (((0,), (0,)), ((), ())), preferred_element_type=F32)


def call(kernel, name, grid, in_specs, out_specs, out_shape, scratch, flops, nbytes):
    return pl.pallas_call(
        kernel,
        name=name,
        grid=grid,
        in_specs=in_specs,
        out_specs=out_specs,
        out_shape=out_shape,
        scratch_shapes=scratch,
        compiler_params=pltpu.CompilerParams(
            dimension_semantics=("arbitrary",) * len(grid), vmem_limit_bytes=VMEM_LIMIT
        ),
        cost_estimate=pl.CostEstimate(
            flops=flops // 4, bytes_accessed=nbytes // 4, transcendentals=0
        ),
    )


def full(shape):
    return pl.BlockSpec(shape, lambda *ids: (0,) * len(shape), pipeline_mode=CONST)


ANYWHERE = pl.BlockSpec(memory_space=pl.ANY)


def chunk_rows(i, size):
    return pl.ds(pl.multiple_of(i * size, size), size)


def ln_stats(x):
    mean = jnp.mean(x, axis=-1, keepdims=True)
    centred = x - mean
    rstd = lax.rsqrt(jnp.mean(centred * centred, axis=-1, keepdims=True) + EPS)
    return centred * rstd, rstd


def ln_back(grad, hat, rstd, scale):
    gh = grad * (1.0 + scale)
    m1 = jnp.mean(gh, axis=-1, keepdims=True)
    m2 = jnp.mean(gh * hat, axis=-1, keepdims=True)
    return rstd * (gh - m1 - hat * m2)


def piece_specs(k, row, count):
    tail = (count, D)
    return [
        pl.BlockSpec((2, 4) + tail, lambda d: (0, 0, row, 0), pipeline_mode=CONST),
        pl.BlockSpec((4, 1) + tail, lambda d: (0, jnp.maximum(d - 1, 0), row, 0)),
        pl.BlockSpec((4, 1) + tail, lambda d: (0, jnp.maximum(d - 1, 0), row, 0)),
    ]


def by_offset(d, body, local_ref, own_ref, other_ref):
    @pl.when(d == 0)
    def _():
        body(lambda m, r, n: local_ref[0, m, r : r + n, :], lambda m, r, n: local_ref[1, m, r : r + n, :])

    @pl.when(d > 0)
    def _():
        body(lambda m, r, n: own_ref[m, 0, r : r + n, :], lambda m, r, n: other_ref[m, 0, r : r + n, :])


def head_rows(own, other, row):
    parts = []
    for m in range(4):
        parts += [own(m, row, 32), other(m, row, 32)]
    return jnp.concatenate(parts, axis=0)


def pair_rows(first, second):
    return jnp.concatenate([get(m) for get in (first, second) for m in range(4)], axis=0)


def feed_specs(down_block):
    def spec(block):
        return pl.BlockSpec((4, 1, 128, D), lambda d: (0, jnp.maximum(d - 1, 0), block, 0))

    return [full((2, 4, 256, D)), spec(0), spec(0), spec(down_block), spec(down_block)]


def feed_by_offset(d, body, l_ref, wu_ref, vu_ref, wd_ref, vd_ref):
    @pl.when(d == 0)
    def _():
        body(
            lambda: pair_rows(lambda m: l_ref[0, m, 0:128], lambda m: l_ref[1, m, 0:128]),
            lambda: pair_rows(lambda m: l_ref[0, m, 128:256], lambda m: l_ref[1, m, 128:256]),
        )

    @pl.when(d > 0)
    def _():
        body(
            lambda: pair_rows(lambda m: wu_ref[m, 0], lambda m: vu_ref[m, 0]),
            lambda: pair_rows(lambda m: wd_ref[m, 0], lambda m: vd_ref[m, 0]),
        )


def ln_qkv(hidden, mods, weights, base):
    rows = hidden.shape[0]
    step = 640

    def kernel(h_ref, m_ref, l_ref, w_ref, v_ref, normed_ref, qkv_ref):
        d = pl.program_id(0)

        @pl.when(d == 0)
        def _():
            def body(i, carry):
                sl = chunk_rows(i, step)
                hat, _ = ln_stats(h_ref[sl, :].astype(F32))
                normed_ref[sl, :] = (
                    hat * (1.0 + m_ref[base + 1 : base + 2, :]) + m_ref[base : base + 1, :]
                ).astype(BF16)
                return carry

            lax.fori_loop(0, rows // step, body, 0)

        def work(own, other):
            for t in range(3):
                qkv_ref[:, t * 256 : (t + 1) * 256] = dot_nt(
                    normed_ref[...], head_rows(own, other, t * 32)
                ).astype(BF16)

        by_offset(d, work, l_ref, w_ref, v_ref)

    return call(
        kernel,
        "ln_qkv",
        (NZ,),
        [full((rows, D)), full((12, D))] + piece_specs(128, 0, 96),
        [full((rows, D)), pl.BlockSpec((rows, 768), lambda z: (0, z))],
        [jax.ShapeDtypeStruct((rows, D), BF16), jax.ShapeDtypeStruct((rows, 3 * D), BF16)],
        [],
        2 * rows * D * 3 * D,
        rows * D * 12 + 6 * D * D,
    )(hidden, mods, *weights)


def build_bias(base_ref, bias_ref, fc_ref, slides, width, lanes_step):
    rows_step = width // slides
    for h in range(HPZ):
        for s in range(slides):
            off = (slides - 1 - s) * lanes_step
            tile = base_ref[h, :, off : off + width]
            if fc_ref is not None:
                tile = jnp.where(s < fc_ref[0], tile, NEGATIVE)
            bias_ref[h, s * rows_step : (s + 1) * rows_step, :] = tile


def window_view(values, kind):
    parts, count, size = kind[0]
    return values.reshape(parts, count, size, values.shape[-1])


def attn_fwd(qkv, base, fc, kind):
    (parts, count, size), slides, lanes_step, masked = kind
    rows, width = qkv.shape[0], parts * size
    r_step, lanes = base.shape[1], base.shape[2]

    def kernel(x_ref, b_ref, fc_ref, o_ref, bias_ref):
        build_bias(b_ref, bias_ref, fc_ref if masked else None, slides, width, lanes_step)

        def one(w, carry):
            def cut(col):
                return x_ref[:, w, :, col : col + HD].reshape(width, HD)

            scores, probs = [], []
            for h in range(HPZ):
                scores.append(dot_nt(cut(256 + h * HD), cut(h * HD) * 0.125) + bias_ref[h])
            for h in range(HPZ):
                expo = jnp.exp(scores[h] - jnp.max(scores[h], axis=0, keepdims=True))
                inv = 1.0 / jnp.sum(expo, axis=0, keepdims=True)
                probs.append((expo * inv).astype(BF16))
            for h in range(HPZ):
                got = dot_tn(probs[h], cut(512 + h * HD)).astype(BF16)
                o_ref[:, w, :, h * HD : (h + 1) * HD] = got.reshape(parts, size, HD)
            return carry

        lax.fori_loop(0, count, one, 0)

    return call(
        kernel,
        "attn_fwd",
        (NZ,),
        [
            pl.BlockSpec((parts, count, size, 768), lambda z: (0, 0, 0, z)),
            pl.BlockSpec((HPZ, r_step, lanes), lambda z: (z, 0, 0)),
            pl.BlockSpec(memory_space=pltpu.SMEM),
        ],
        pl.BlockSpec((parts, count, size, 256), lambda z: (0, 0, 0, z)),
        jax.ShapeDtypeStruct((parts, count, size, D), BF16),
        [pltpu.VMEM((HPZ, width, width), F32)],
        count * 16 * width * width * HD * 16,
        rows * D * 8,
    )(window_view(qkv, kind), base, fc).reshape(rows, D)


def attn_bwd(qkv, grad_att, base, fc, kind):
    (parts, count, size), slides, lanes_step, masked = kind
    rows, width = qkv.shape[0], parts * size
    r_step, lanes = base.shape[1], base.shape[2]

    def kernel(x_ref, d_ref, b_ref, fc_ref, o_ref, gb_ref, bias_ref, acc_ref):
        build_bias(b_ref, bias_ref, fc_ref if masked else None, slides, width, lanes_step)
        acc_ref[...] = jnp.zeros_like(acc_ref)

        def one(w, carry):
            def cut(ref, col):
                return ref[:, w, :, col : col + HD].reshape(width, HD)

            def put(col, value):
                o_ref[:, w, :, col : col + HD] = value.astype(BF16).reshape(parts, size, HD)

            q = [cut(x_ref, h * HD) * 0.125 for h in range(HPZ)]
            k = [cut(x_ref, 256 + h * HD) for h in range(HPZ)]
            da = [cut(d_ref, h * HD) for h in range(HPZ)]
            score = [dot_nt(k[h], q[h]) + bias_ref[h] for h in range(HPZ)]
            dp = [dot_nt(cut(x_ref, 512 + h * HD), da[h]) for h in range(HPZ)]
            probs, dl = [], []
            for h in range(HPZ):
                expo = jnp.exp(score[h] - jnp.max(score[h], axis=0, keepdims=True))
                inv = 1.0 / jnp.sum(expo, axis=0, keepdims=True)
                p = expo * inv
                row = jnp.sum(dp[h] * p, axis=0, keepdims=True)
                g = (p * (dp[h] - row)).astype(BF16)
                acc_ref[h] += g.astype(F32)
                probs.append(p.astype(BF16))
                dl.append(g)
            for h in range(HPZ):
                put(h * HD, dot_tn(dl[h], k[h]) * 0.125)
                put(256 + h * HD, dot_nn(dl[h], q[h]))
                put(512 + h * HD, dot_nn(probs[h], da[h]))
            return carry

        lax.fori_loop(0, count, one, 0)
        gb_ref[...] = jnp.zeros_like(gb_ref)
        for h in range(HPZ):
            for s in range(slides):
                off = (slides - 1 - s) * lanes_step
                gb_ref[h, :, off : off + width] += acc_ref[h, s * r_step : (s + 1) * r_step, :]

    xspec = pl.BlockSpec((parts, count, size, 768), lambda z: (0, 0, 0, z))
    bspec = pl.BlockSpec((HPZ, r_step, lanes), lambda z: (z, 0, 0))
    proj, strips = call(
        kernel,
        "attn_bwd",
        (NZ,),
        [
            xspec,
            pl.BlockSpec((parts, count, size, 256), lambda z: (0, 0, 0, z)),
            bspec,
            pl.BlockSpec(memory_space=pltpu.SMEM),
        ],
        [xspec, bspec],
        [
            jax.ShapeDtypeStruct((parts, count, size, 3 * D), BF16),
            jax.ShapeDtypeStruct(base.shape, F32),
        ],
        [pltpu.VMEM((HPZ, width, width), F32), pltpu.VMEM((HPZ, width, width), F32)],
        count * 16 * width * width * HD * 40,
        rows * D * 16,
    )(window_view(qkv, kind), window_view(grad_att, kind), base, fc)
    return proj.reshape(rows, 3 * D), strips


def out_specs_of(row_block):
    return [
        pl.BlockSpec((2, 4, 32, D), lambda i: (0, 0, row_block, 0), pipeline_mode=CONST),
        pl.BlockSpec((4, 3, 32, D), lambda i: (0, 0, row_block, 0), pipeline_mode=CONST),
        pl.BlockSpec((4, 3, 32, D), lambda i: (0, 0, row_block, 0), pipeline_mode=CONST),
    ]


def out_rows(d, l_ref, w_ref, v_ref):
    if d == 0:
        return head_rows(
            lambda m, r, n: l_ref[0, m, :, :], lambda m, r, n: l_ref[1, m, :, :], 0
        )
    return head_rows(
        lambda m, r, n: w_ref[m, d - 1, :, :], lambda m, r, n: v_ref[m, d - 1, :, :], 0
    )


def out_proj(attended, weights, hidden, mods, base):
    rows = attended.shape[0]
    step = 256

    def kernel(a_ref, l_ref, w_ref, v_ref, h_ref, m_ref, br_ref, mid_ref, sh_ref):
        branch = jnp.zeros((step, D), F32)
        for d in range(NZ):
            branch += dot_nn(a_ref[:, d * 256 : (d + 1) * 256], out_rows(d, l_ref, w_ref, v_ref))
        br_ref[...] = branch.astype(BF16)
        middle = h_ref[...].astype(F32) + m_ref[base + 2 : base + 3, :] * branch
        mid_ref[...] = middle
        hat, _ = ln_stats(middle)
        sh_ref[...] = (
            hat * (1.0 + m_ref[base + 4 : base + 5, :]) + m_ref[base + 3 : base + 4, :]
        ).astype(BF16)

    tile = pl.BlockSpec((step, D), lambda i: (i, 0))
    return call(
        kernel,
        "out_proj",
        (rows // step,),
        [tile] + out_specs_of(3) + [tile, full((12, D))],
        [tile, tile, tile],
        [
            jax.ShapeDtypeStruct((rows, D), BF16),
            jax.ShapeDtypeStruct((rows, D), F32),
            jax.ShapeDtypeStruct((rows, D), BF16),
        ],
        [],
        2 * rows * D * D,
        rows * D * 14 + 2 * D * D,
    )(attended, *weights, hidden, mods)


GELU_C = 0.7978845608028654
GELU_A = 0.044715


def gelu_of(x):
    return 0.5 * x * (1.0 + jnp.tanh(GELU_C * (x + GELU_A * x * x * x)))


def gelu_both(x):
    x2 = x * x
    th = jnp.tanh(GELU_C * (x + GELU_A * x * x2))
    half = 0.5 * (1.0 + th)
    slope = half + 0.5 * x * (1.0 - th * th) * (GELU_C * (1.0 + 3.0 * GELU_A * x2))
    return x * half, slope


def ffn_fwd(shifted, weights, down_block, middle, mods, base):
    rows = shifted.shape[0]
    step = 640

    def kernel(x_ref, *refs):
        parts, refs = refs[:5], refs[5:]
        mid_ref, m_ref, pre_ref, feed_ref, nx_ref, acc_ref, mid_late, sem = refs
        z = pl.program_id(0)
        copy = pltpu.make_async_copy(mid_ref, mid_late, sem)

        @pl.when(z == 0)
        def _():
            copy.start()

        @pl.when(z == NZ - 1)
        def _():
            copy.wait()

        def work(up, down):
            def body(i, carry):
                sl = chunk_rows(i, step)
                pre = dot_nt(x_ref[sl, :], up())
                pre_ref[sl, :] = pre.astype(BF16)
                part = dot_nn(gelu_of(pre).astype(BF16), down())

                @pl.when(z == 0)
                def _():
                    acc_ref[sl, :] = part

                @pl.when((z > 0) & (z < NZ - 1))
                def _():
                    acc_ref[sl, :] += part

                @pl.when(z == NZ - 1)
                def _():
                    feed = acc_ref[sl, :] + part
                    feed_ref[sl, :] = feed.astype(BF16)
                    nx_ref[sl, :] = (
                        mid_late[sl, :] + m_ref[base + 5 : base + 6, :] * feed
                    ).astype(BF16)

                return carry

            lax.fori_loop(0, rows // step, body, 0)

        feed_by_offset(z, work, *parts)

    return call(
        kernel,
        "ffn_fwd",
        (NZ,),
        [full((rows, D))] + feed_specs(down_block) + [ANYWHERE, full((12, D))],
        [pl.BlockSpec((rows, D), lambda z: (0, z)), full((rows, D)), full((rows, D))],
        [
            jax.ShapeDtypeStruct((rows, 4 * D), BF16),
            jax.ShapeDtypeStruct((rows, D), BF16),
            jax.ShapeDtypeStruct((rows, D), BF16),
        ],
        [
            pltpu.VMEM((rows, D), F32),
            pltpu.VMEM((rows, D), F32),
            pltpu.SemaphoreType.DMA,
        ],
        16 * rows * D * D,
        rows * D * 20 + 16 * D * D,
    )(shifted, *weights, middle, mods)


def ffn_bwd(grad, pre, shifted, weights, down_block, mods, base):
    rows = grad.shape[0]
    step = 640

    def kernel(g_ref, p_ref, x_ref, *refs):
        parts, refs = refs[:5], refs[5:]
        m_ref, keep_ref, send_ref, gs_ref, gf_ref, act_ref, gp_ref, x_late, sem = refs
        z = pl.program_id(0)
        copy = pltpu.make_async_copy(x_ref, x_late, sem)

        @pl.when(z == 0)
        def _():
            copy.start()

            def body(i, carry):
                sl = chunk_rows(i, step)
                gf_ref[sl, :] = (
                    g_ref[sl, :].astype(F32) * m_ref[base + 5 : base + 6, :]
                ).astype(BF16)
                gs_ref[sl, :] = jnp.zeros((step, D), F32)
                return carry

            lax.fori_loop(0, rows // step, body, 0)

        def work(up, down):
            def body(i, carry):
                sl = chunk_rows(i, step)
                back = dot_nt(gf_ref[sl, :], down())
                act, slope = gelu_both(p_ref[sl, :].astype(F32))
                act_ref[sl, :] = act.astype(BF16)
                gpre = (back * slope).astype(BF16)
                gp_ref[sl, :] = gpre
                part = dot_nn(gpre, up())
                gs_ref[sl, :] += part
                return carry

            lax.fori_loop(0, rows // step, body, 0)

        feed_by_offset(z, work, *parts)

        @pl.when(z == 0)
        def _():
            copy.wait()

        for j, out_ref in enumerate((keep_ref, send_ref)):
            cols = slice(j * 512, (j + 1) * 512)
            gd = dot_tn(act_ref[:, cols], gf_ref[...]).astype(BF16)
            gu = dot_tn(gp_ref[:, cols], x_late[...]).astype(BF16)
            out_ref[:, 0, 0:128] = gu.reshape(4, 128, D)
            out_ref[:, 0, 128:256] = gd.reshape(4, 128, D)

    gspec = pl.BlockSpec((4, 1, 256, D), lambda z: (0, z, 0, 0))
    gshape = jax.ShapeDtypeStruct((4, NZ, 256, D), BF16)
    return call(
        kernel,
        "ffn_bwd",
        (NZ,),
        [
            full((rows, D)),
            pl.BlockSpec((rows, D), lambda z: (0, z)),
            ANYWHERE,
        ]
        + feed_specs(down_block)
        + [full((12, D))],
        [gspec, gspec, full((rows, D))],
        [gshape, gshape, jax.ShapeDtypeStruct((rows, D), F32)],
        [pltpu.VMEM((rows, D), BF16)] * 4 + [pltpu.SemaphoreType.DMA],
        32 * rows * D * D,
        rows * D * 16 + 32 * D * D,
    )(grad, pre, shifted, *weights, mods)


def split_heads(value, keep_ref, send_ref, d, row):
    for m in range(4):
        keep_ref[m, d, row : row + 32] = value[m * 64 : m * 64 + 32]
        send_ref[m, d, row : row + 32] = value[m * 64 + 32 : m * 64 + 64]


def out_bwd(grad, grad_shifted, middle, feed, branch, attended, weights, mods, base):
    rows = grad.shape[0]
    step = 256
    steps = rows // step

    def kernel(
        g_ref, gs_ref, mid_ref, f_ref, b_ref, a_ref, l_ref, w_ref, v_ref, m_ref, gm_ref, ga_ref,
        keep_ref, send_ref, s_ref, gb_ref, a_late, sem,
    ):
        i = pl.program_id(0)
        copy = pltpu.make_async_copy(a_ref, a_late, sem)

        @pl.when(i == 0)
        def _():
            copy.start()
            s_ref[...] = jnp.zeros_like(s_ref)

        g = g_ref[...].astype(F32)
        gs = gs_ref[...]
        hat, rstd = ln_stats(mid_ref[...])
        gm = g + ln_back(gs, hat, rstd, m_ref[base + 4 : base + 5, :])
        gm_ref[...] = gm
        s_ref[0:1, :] += jnp.sum(gs, axis=0, keepdims=True)
        s_ref[1:2, :] += jnp.sum(gs * hat, axis=0, keepdims=True)
        s_ref[2:3, :] += jnp.sum(gm * b_ref[...].astype(F32), axis=0, keepdims=True)
        s_ref[3:4, :] += jnp.sum(g * f_ref[...].astype(F32), axis=0, keepdims=True)
        gb = (gm * m_ref[base + 2 : base + 3, :]).astype(BF16)
        gb_ref[chunk_rows(i, step), :] = gb
        for d in range(NZ):
            ga_ref[:, d * 256 : (d + 1) * 256] = dot_nt(
                gb, out_rows(d, l_ref, w_ref, v_ref)
            ).astype(BF16)

        @pl.when(i == steps - 1)
        def _():
            copy.wait()
            for d in range(NZ):
                gw = dot_tn(a_late[:, d * 256 : (d + 1) * 256], gb_ref[...]).astype(BF16)
                split_heads(gw, keep_ref, send_ref, d, 0)

    tile = pl.BlockSpec((step, D), lambda i: (i, 0))
    gshape = jax.ShapeDtypeStruct((4, NZ, 32, D), BF16)
    return call(
        kernel,
        "out_bwd",
        (steps,),
        [tile, tile, tile, tile, tile, ANYWHERE] + out_specs_of(3) + [full((12, D))],
        [tile, tile, full(gshape.shape), full(gshape.shape), full((8, D))],
        [
            jax.ShapeDtypeStruct((rows, D), F32),
            jax.ShapeDtypeStruct((rows, D), BF16),
            gshape,
            gshape,
            jax.ShapeDtypeStruct((8, D), F32),
        ],
        [
            pltpu.VMEM((rows, D), BF16),
            pltpu.VMEM((rows, D), BF16),
            pltpu.SemaphoreType.DMA,
        ],
        4 * rows * D * D,
        rows * D * 24 + 4 * D * D,
    )(grad, grad_shifted, middle, feed, branch, attended, *weights, mods)


def qkv_back(grad_proj, weights, hidden, grad_middle, mods, base, out_dtype, pieces):
    rows = hidden.shape[0]
    step = 640

    cols = D // pieces

    def kernel(p_ref, l_ref, w_ref, v_ref, h_ref, gm_ref, m_ref, *refs):
        gh_refs, (s_ref, acc_ref, h_late, gm_late, sems) = refs[:pieces], refs[pieces:]
        copies = [
            pltpu.make_async_copy(h_ref, h_late, sems.at[0]),
            pltpu.make_async_copy(gm_ref, gm_late, sems.at[1]),
        ]
        z = pl.program_id(0)

        @pl.when(z == 0)
        def _():
            for copy in copies:
                copy.start()
            acc_ref[...] = jnp.zeros_like(acc_ref)
            s_ref[...] = jnp.zeros_like(s_ref)

        def work(own, other):
            def body(i, carry):
                sl = chunk_rows(i, step)
                rows_of = jnp.concatenate([head_rows(own, other, t * 32) for t in range(3)], axis=0)
                acc_ref[sl, :] += dot_nn(p_ref[sl, :], rows_of)
                return carry

            lax.fori_loop(0, rows // step, body, 0)

        by_offset(z, work, l_ref, w_ref, v_ref)

        @pl.when(z == NZ - 1)
        def _():
            for copy in copies:
                copy.wait()

            def tail(n, carry):
                sl = chunk_rows(n, 256)
                gn = acc_ref[sl, :]
                hat, rstd = ln_stats(h_late[sl, :].astype(F32))
                gh = gm_late[sl, :] + ln_back(gn, hat, rstd, m_ref[base + 1 : base + 2, :])
                for i, gh_ref in enumerate(gh_refs):
                    gh_ref[sl, :] = gh[:, i * cols : (i + 1) * cols].astype(out_dtype)
                s_ref[0:1, :] += jnp.sum(gn, axis=0, keepdims=True)
                s_ref[1:2, :] += jnp.sum(gn * hat, axis=0, keepdims=True)
                return carry

            lax.fori_loop(0, rows // 256, tail, 0)

    return call(
        kernel,
        "qkv_back",
        (NZ,),
        [pl.BlockSpec((rows, 768), lambda z: (0, z))]
        + piece_specs(128, 0, 96)
        + [ANYWHERE, ANYWHERE, full((12, D))],
        [full((rows, cols))] * pieces + [full((8, D))],
        [jax.ShapeDtypeStruct((rows, cols), out_dtype)] * pieces
        + [jax.ShapeDtypeStruct((8, D), F32)],
        [
            pltpu.VMEM((rows, D), F32),
            pltpu.VMEM((rows, D), hidden.dtype),
            pltpu.VMEM((rows, D), F32),
            pltpu.SemaphoreType.DMA((2,)),
        ],
        6 * rows * D * D,
        rows * D * 20 + 6 * D * D,
    )(grad_proj, *weights, hidden, grad_middle, mods)


def qkv_grad(grad_proj, normed, out_keep, out_send, apart):
    rows = normed.shape[0]
    k = 128

    def kernel(p_ref, n_ref, ok_ref, os_ref, *rest):
        if apart:
            keep_ref, send_refs = rest[-5], rest[-4:]
        else:
            keep_ref, send_ref = rest[-2:]
            send_refs = [send_ref.at[m : m + 1] for m in range(4)]
        for t in range(3):
            gw = dot_tn(p_ref[:, t * 256 : (t + 1) * 256], n_ref[...]).astype(BF16)
            for m in range(4):
                keep_ref[m, 0, t * 32 : t * 32 + 32] = gw[m * 64 : m * 64 + 32]
                send_refs[m][0, 0, t * 32 : t * 32 + 32] = gw[m * 64 + 32 : m * 64 + 64]
        keep_ref[:, :, 96:128] = ok_ref[...]
        for m in range(4):
            send_refs[m][0, :, 96:128] = os_ref[m]

    gspec = pl.BlockSpec((4, 1, k, D), lambda z: (0, z, 0, 0))
    ospec = pl.BlockSpec((4, 1, 32, D), lambda z: (0, z, 0, 0))
    gshape = jax.ShapeDtypeStruct((4, NZ, k, D), BF16)
    sends, send_shapes = [gspec], [gshape]
    if apart:
        sends = [pl.BlockSpec((1, 1, k, D), lambda z: (0, z, 0, 0))] * 4
        send_shapes = [jax.ShapeDtypeStruct((1, NZ, k, D), BF16)] * 4
    return call(
        kernel,
        "qkv_grad",
        (NZ,),
        [pl.BlockSpec((rows, 768), lambda z: (0, z)), full((rows, D)), ospec, ospec],
        [gspec] + sends,
        [gshape] + send_shapes,
        [],
        6 * rows * D * D,
        rows * D * 8 + 8 * D * D,
    )(grad_proj, normed, out_keep, out_send)


def place_call(kernel, name, in_specs, out_specs, out_shape, scratch, nbytes, aliases):
    return pl.pallas_call(
        kernel,
        name=name,
        grid_spec=pltpu.PrefetchScalarGridSpec(
            num_scalar_prefetch=1,
            grid=(8,),
            in_specs=in_specs,
            out_specs=out_specs,
            scratch_shapes=scratch,
        ),
        out_shape=out_shape,
        input_output_aliases=aliases,
        compiler_params=pltpu.CompilerParams(
            dimension_semantics=("arbitrary",), vmem_limit_bytes=VMEM_LIMIT
        ),
        cost_estimate=pl.CostEstimate(flops=0, bytes_accessed=nbytes // 64, transcendentals=0),
    )


def rows_at(place):
    return pl.ds(pl.multiple_of(place * 32, 32), 32)


def prep_attn(place, w_qkv, w_out, b):
    def kernel(c_ref, q_ref, o_ref, out_ref, t_ref):
        r = pl.program_id(0)

        @pl.when(r == 0)
        def _():
            for t in range(3):
                t_ref[t] = q_ref[0, t].T

        at = rows_at(c_ref[0] ^ r)
        for t in range(3):
            out_ref[0, 0, t * 32 : (t + 1) * 32, :] = t_ref[t, at, :]
        out_ref[0, 0, 96:128, :] = o_ref[0, at, :]

    return place_call(
        kernel,
        "prep_attn",
        [
            pl.BlockSpec((1, 3, D, 256), lambda r, c: (b, 0, 0, 0)),
            pl.BlockSpec((1, 256, D), lambda r, c: (b, 0, 0)),
        ],
        pl.BlockSpec((1, 1, 128, D), lambda r, c: (r % 2, r // 2, 0, 0)),
        jax.ShapeDtypeStruct((2, 4, 128, D), BF16),
        [pltpu.VMEM((3, 256, D), BF16)],
        4 * D * D,
        {},
    )(place, w_qkv, w_out)


def prep_feed(place, w_up, w_down, b):
    def kernel(c_ref, u_ref, d_ref, out_ref):
        out_ref[0, 0, 0:128, :] = u_ref[0].T
        out_ref[0, 0, 128:256, :] = d_ref[0]

    return place_call(
        kernel,
        "prep_feed",
        [
            pl.BlockSpec((1, D, 128), lambda r, c: (b, 0, c[0] ^ r)),
            pl.BlockSpec((1, 128, D), lambda r, c: (b, c[0] ^ r, 0)),
        ],
        pl.BlockSpec((1, 1, 256, D), lambda r, c: (r % 2, r // 2, 0, 0)),
        jax.ShapeDtypeStruct((2, 4, 256, D), BF16),
        [],
        8 * D * D,
        {},
    )(place, w_up, w_down)


def finish_attn(place, own, other):
    def kernel(c_ref, own_ref, oth_ref, gq_ref, go_ref, t_ref):
        r = pl.program_id(0)
        at = rows_at(c_ref[0] ^ r)

        def store(ref):
            for b in range(2):
                row = 128 * b
                for t in range(3):
                    t_ref[b, t, at, :] = ref[0, row + t * 32 : row + (t + 1) * 32, :]
                go_ref[b, at, :] = ref[0, row + 96 : row + 128, :].astype(F32)

        @pl.when(r % 2 == 0)
        def _():
            store(own_ref)

        @pl.when(r % 2 == 1)
        def _():
            store(oth_ref)

        @pl.when(r == 7)
        def _():
            for b in range(2):
                for t in range(3):
                    gq_ref[b, t] = t_ref[b, t].T.astype(F32)

    piece = pl.BlockSpec((1, 256, D), lambda r, c: (r // 2, 0, 0))
    return place_call(
        kernel,
        "finish_attn",
        [piece, piece],
        [
            pl.BlockSpec((2, 3, D, 256), lambda r, c: (0, 0, 0, 0), pipeline_mode=CONST),
            pl.BlockSpec((2, 256, D), lambda r, c: (0, 0, 0), pipeline_mode=CONST),
        ],
        [
            jax.ShapeDtypeStruct((2, 3, D, 256), F32),
            jax.ShapeDtypeStruct((2, 256, D), F32),
        ],
        [pltpu.VMEM((2, 3, 256, D), BF16)],
        12 * D * D,
        {},
    )(place, own, other)


def finish_feed(place, own, other, b, earlier):
    def kernel(c_ref, own_ref, oth_ref, *rest):
        gu_ref, gd_ref = rest[-2:]
        r = pl.program_id(0)

        def store(ref):
            gu_ref[0] = ref[0, 0:128, :].T.astype(F32)
            gd_ref[0] = ref[0, 128:256, :].astype(F32)

        @pl.when(r % 2 == 0)
        def _():
            store(own_ref)

        @pl.when(r % 2 == 1)
        def _():
            store(oth_ref)

    piece = pl.BlockSpec((1, 256, D), lambda r, c: (r // 2, 0, 0))
    anywhere = pl.BlockSpec(memory_space=pl.ANY)
    return place_call(
        kernel,
        "finish_feed",
        [piece, piece] + [anywhere] * len(earlier),
        [
            pl.BlockSpec((1, D, 128), lambda r, c: (b, 0, c[0] ^ r)),
            pl.BlockSpec((1, 128, D), lambda r, c: (b, c[0] ^ r, 0)),
        ],
        [jax.ShapeDtypeStruct((2, D, D), F32), jax.ShapeDtypeStruct((2, D, D), F32)],
        [],
        12 * D * D,
        {3 + i: i for i in range(len(earlier))},
    )(place, own, other, *earlier)


def partner(values):
    return lax.ppermute(values, "head", [(i, i ^ 1) for i in range(NZ)])


def rows_to_spatial(rows, odd):
    cols = rows.shape[1]
    whole = lax.dynamic_slice(rows, (256 * odd, 0), (1024, cols))
    part = lax.dynamic_slice(rows, (1024 * (1 - odd), 0), (256, cols)).reshape(8, 2, 16, cols)
    wins = whole.reshape(2, 16, 2, 16, cols).transpose(0, 2, 1, 3, 4).reshape(1024, cols)
    left, right = part[:, 0].reshape(128, cols), part[:, 1].reshape(128, cols)
    keep = jnp.where(odd == 0, left, right)
    got = partner(jnp.where(odd == 0, right, left))
    top, bottom = jnp.where(odd == 0, keep, got), jnp.where(odd == 0, got, keep)
    part = jnp.concatenate([top, bottom], axis=0)
    return jnp.where(
        odd == 0,
        jnp.concatenate([wins, part], axis=0),
        jnp.concatenate([part, wins], axis=0),
    )


def last_window(wins, odd):
    part = lax.dynamic_slice(wins, (1024 * (1 - odd), 0), (256, wins.shape[1]))
    keep = jnp.where(odd == 0, part[:128], part[128:])
    return keep, jnp.where(odd == 0, part[128:], part[:128])


def whole_windows(wins, odd):
    cols = wins.shape[1]
    whole = lax.dynamic_slice(wins, (256 * odd, 0), (1024, cols))
    return whole.reshape(2, 2, 16, 16, cols).transpose(0, 2, 1, 3, 4).reshape(1024, cols)


def spatial_to_rows(whole, keep, got, odd):
    cols = whole.shape[1]
    left, right = jnp.where(odd == 0, keep, got), jnp.where(odd == 0, got, keep)
    part = jnp.stack([left.reshape(8, 16, cols), right.reshape(8, 16, cols)], axis=1)
    part = part.reshape(256, cols)
    return jnp.where(
        odd == 0,
        jnp.concatenate([whole, part], axis=0),
        jnp.concatenate([part, whole], axis=0),
    )


def exchange(values):
    return lax.all_to_all(values, "head", 0, 0, tiled=True)


def spatial_to_tubes(wins):
    cols = wins.shape[1]
    return exchange(
        wins.reshape(5, 2, 8, 2, 8, cols).transpose(1, 3, 0, 2, 4, 5).reshape(1280, cols)
    )


def from_quads(quads):
    cols = quads.shape[1]
    return quads.reshape(2, 2, 5, 8, 8, cols).transpose(2, 0, 3, 1, 4, 5).reshape(1280, cols)


def toeplitz(side):
    span = 2 * side - 1
    b = lax.broadcasted_iota(jnp.int32, (span, side, side), 0)
    j = lax.broadcasted_iota(jnp.int32, (span, side, side), 1)
    i = lax.broadcasted_iota(jnp.int32, (span, side, side), 2)
    return (b == i - j + side - 1).astype(F32)


def toeplitz_pair(side):
    span = 2 * side - 1
    shape = (span * span, side * side, side * side)
    r = lax.broadcasted_iota(jnp.int32, shape, 0)
    j = lax.broadcasted_iota(jnp.int32, shape, 1)
    i = lax.broadcasted_iota(jnp.int32, shape, 2)
    dy = i // side - j // side + side - 1
    dx = i % side - j % side + side - 1
    return (r == dy * span + dx).astype(F32)


CORE, ROW_X, ROW_Y = 1, 2, 4


def swap(values, bit):
    return lax.ppermute(values, "clip", [(i, i ^ bit) for i in range(8)])


def from_z(values, d):
    return lax.ppermute(values, "head", [((i + d) % NZ, i) for i in range(NZ)])


def sync(*values):
    return lax.optimization_barrier(values)


def add(first, second):
    return (first.astype(F32) + second.astype(F32)).astype(BF16)


def line_stage(piece):
    return [from_z(piece, d) for d in (1, 2, 3)]


def others(by_z, z):
    return [lax.dynamic_index_in_dim(by_z, (z + d) % NZ, 0, keepdims=False) for d in (1, 2, 3)]


def cross_stage(own):
    return [own] + [swap(own, m * 2) for m in (1, 2, 3)]


def sides_stage(own):
    return [own, swap(own, ROW_X), swap(own, ROW_Y)]


def corner_stage(sides):
    half = sides[0].shape[1] // 2
    return [swap(sides[1][:, :half], ROW_Y), swap(sides[2][:, half:], ROW_X)]


def joined(sides, corner):
    return jnp.stack(sides + [jnp.concatenate(corner, axis=1)])


def sum_core(keep, got):
    return [add(keep[m], got[m].reshape(keep.shape[1:])) for m in range(4)]


def send_plane(totals, offsets):
    return [swap(totals[m], m * 2) for m in offsets]


def to_places(total, z):
    twice = jnp.concatenate([total, total[: NZ - 1]], axis=0)
    return lax.dynamic_slice_in_dim(twice, (NZ - z) % NZ, NZ, axis=0)


def sum_plane(totals, got, z):
    total = totals[0].astype(F32)
    for value in got:
        total = total + value.astype(F32)
    return to_places(total.astype(BF16), z)


def send_cross(totals):
    half = totals[0].shape[1] // 2
    first = [t[:, :half] for t in totals]
    second = [t[:, half:] for t in totals]
    by_x = swap(jnp.stack([first[1], first[3]]), ROW_X)
    by_y = swap(jnp.stack([second[2], second[3]]), ROW_Y)
    return by_x, by_y


def sum_cross(totals, got):
    half = totals[0].shape[1] // 2
    by_x, by_y = got
    first = [add(totals[0][:, :half], by_x[0]), add(totals[2][:, :half], by_x[1])]
    second = [add(totals[0][:, half:], by_y[0]), add(totals[1][:, half:], by_y[1])]
    return first, second


def send_corner(halves):
    return swap(halves[0][1], ROW_Y), swap(halves[1][1], ROW_X)


def sum_corner(halves, got, z):
    first = add(halves[0][0], got[0])
    second = add(halves[1][0], got[1])
    return to_places(jnp.concatenate([first, second], axis=1), z)


def sum_line(by_z):
    return lax.psum_scatter(by_z, "head", scatter_dimension=0)


def on_device_windows(
    tokens, d_out, modulation, frame_counts, w_qkv, w_out, w_up, w_down, table_s, table_t
):
    z = lax.axis_index("head")
    c = lax.axis_index("clip")
    place = c.astype(jnp.int32).reshape(1)
    chip = c // 2
    odd = z % 2
    mods = modulation[0]
    n_s, n_t = table_s.shape[1], table_t.shape[1]
    hot_s, hot_t = toeplitz(SWIN), toeplitz_pair(TWIN)
    fc = frame_counts

    def spatial_base(tables):
        base = jnp.einsum(
            "hab,bji->hjai", tables[:, :n_s].reshape(16, 31, 31), hot_s, precision=HIGHEST_PRECISION
        ).reshape(16, 16, 496)
        return jnp.pad(base, ((0, 0), (0, 0), (0, 16)))

    def tube_base(tables):
        base = jnp.einsum(
            "htr,rjk->hjtk", tables[:, n_s:].reshape(16, 9, 225), hot_t, precision=HIGHEST_PRECISION
        ).reshape(16, 64, 576)
        return jnp.pad(base, ((0, 0), (0, 0), (0, 64)))

    def table_rows(first, second):
        first = jnp.pad(first, ((0, 0), (0, D - n_s)))
        second = jnp.pad(second, ((0, 0), (0, 15 * D - n_t)))
        values = jnp.concatenate([first, second], axis=1).astype(BF16)
        return values.reshape(NZ, 4, 16, D).transpose(1, 0, 2, 3)

    spatial = ((1, 5, 256), 16, 16, False)
    tube = ((5, 4, 64), 5, 64, True)

    local_a0 = prep_attn(place, w_qkv, w_out, 0)
    line_a0 = line_stage(local_a0[0, 0])
    table_piece = jnp.concatenate([table_s, table_t], axis=1)
    tables = [from_z(table_piece, d) for d in (1, 2)]
    local_f0 = prep_feed(place, w_up, w_down, 0)
    local_a1 = prep_attn(place, w_qkv, w_out, 1)
    local_f1 = prep_feed(place, w_up, w_down, 1)
    line_a0, local_f0, local_a1, local_f1, tables, tokens, table_piece = sync(
        line_a0, local_f0, local_a1, local_f1, tables, tokens, table_piece
    )
    own_a0 = cross_stage(jnp.stack(line_a0))
    z_u0 = lax.all_gather(local_f0[0, 0, :128], "head")
    z_d0 = lax.all_gather(local_f0[0, 0, 128:], "head")
    tables = jnp.stack([table_piece] + tables + [from_z(table_piece, 3)])
    tables = jnp.concatenate(
        [lax.dynamic_slice_in_dim(tables, chip ^ m, 1, axis=1) for m in range(4)], axis=1
    ).reshape(16, n_s + n_t)
    base_s = spatial_base(tables)
    hidden0 = rows_to_spatial(tokens, odd)
    own_a0, hidden0, tables, base_s, z_u0 = sync(own_a0, hidden0, tables, base_s, z_u0)
    own_a0 = jnp.stack(own_a0)
    other_a0 = swap(own_a0, CORE)
    own_u0 = sides_stage(jnp.stack(others(z_u0, z)))
    own_a0, other_a0 = sync(own_a0, other_a0)
    weights_a0 = (local_a0, own_a0, other_a0)
    normed0, qkv0 = ln_qkv(hidden0, mods, weights_a0, 0)
    qkv0, own_u0, z_d0 = sync(qkv0, own_u0, z_d0)
    corner_u0 = corner_stage(own_u0)
    own_d0 = sides_stage(jnp.stack(others(z_d0, z)))
    z_a1 = lax.all_gather(local_a1[0, 0], "head")
    attended0 = attn_fwd(qkv0, base_s, fc, spatial)
    attended0, corner_u0, own_d0, z_a1 = sync(attended0, corner_u0, own_d0, z_a1)
    corner_d0 = corner_stage(own_d0)
    own_u0 = joined(own_u0, corner_u0)
    other_u0 = swap(own_u0, CORE)
    branch0, middle0, shifted0 = out_proj(attended0, weights_a0, hidden0, mods, 0)
    own_a1 = jnp.stack(others(z_a1, z))
    shifted0, corner_d0, other_u0, own_a1 = sync(shifted0, corner_d0, other_u0, own_a1)
    own_d0 = joined(own_d0, corner_d0)
    other_d0 = swap(own_d0, CORE)
    z_f1 = lax.all_gather(local_f1[0, 0], "head")
    shifted0, other_d0 = sync(shifted0, other_d0)
    own_a1 = cross_stage(own_a1)
    weights_f0 = (local_f0, own_u0, other_u0, own_d0, other_d0)
    pre0, feed0, hidden1 = ffn_fwd(shifted0, weights_f0, 0, middle0, mods, 0)
    hidden1, z_f1, own_a1, tables, d_out = sync(hidden1, z_f1, own_a1, tables, d_out)
    tubes1 = spatial_to_tubes(hidden1)
    own_a1 = jnp.stack(own_a1)
    other_a1 = swap(own_a1, CORE)
    own_f1 = cross_stage(jnp.stack(others(z_f1, z)))
    base_t = tube_base(tables)
    spatial_d = rows_to_spatial(d_out, odd)
    tubes1, other_a1, base_t, spatial_d = sync(tubes1, other_a1, base_t, spatial_d)
    weights_a1 = (local_a1, own_a1, other_a1)
    tubes_d = spatial_to_tubes(spatial_d)
    normed1, qkv1 = ln_qkv(tubes1, mods, weights_a1, 6)
    qkv1, own_f1 = sync(qkv1, own_f1)
    own_f1 = jnp.stack(own_f1)
    other_f1 = swap(own_f1, CORE)
    attended1 = attn_fwd(qkv1, base_t, fc, tube)
    branch1, middle1, shifted1 = out_proj(attended1, weights_a1, tubes1, mods, 6)
    shifted1, other_f1 = sync(shifted1, other_f1)
    weights_f1 = (local_f1, own_f1, other_f1, own_f1, other_f1)
    pre1, feed1, hidden2 = ffn_fwd(shifted1, weights_f1, 1, middle1, mods, 6)
    hidden2, tubes_d = sync(hidden2, tubes_d)
    live = lax.broadcasted_iota(jnp.int32, (1280, 1), 0) // 256 < fc[0]
    grad2 = jnp.where(live, tubes_d, 0)
    out_wins = exchange(jnp.where(live, hidden2, 0))
    f1_keep, f1_send, g_shift1 = ffn_bwd(grad2, pre1, shifted1, weights_f1, 1, mods, 6)
    f1_keep, f1_send, g_shift1, out_wins = sync(f1_keep, f1_send, g_shift1, out_wins)
    f1_got = swap(f1_send, CORE)
    g_mid1, g_att1, o1_keep, o1_send, sums_o1 = out_bwd(
        grad2, g_shift1, middle1, feed1, branch1, attended1, weights_a1, mods, 6
    )
    g_att1, f1_got = sync(g_att1, f1_got)
    total_f1 = sum_core(f1_keep, f1_got)
    g_att1, total_f1 = sync(g_att1, total_f1)
    got_f1 = send_cross(total_f1)
    g_proj1, g_base1 = attn_bwd(qkv1, g_att1, base_t, fc, tube)
    g_proj1, g_base1, got_f1 = sync(g_proj1, g_base1, got_f1)
    half_f1 = sum_cross(total_f1, got_f1)
    half_f1, g_proj1 = sync(half_f1, g_proj1)
    got_f1 = send_corner(half_f1)
    g_hid1, sums_q1 = qkv_back(g_proj1, weights_a1, tubes1, g_mid1, mods, 6, BF16, 1)
    g_hid1, g_proj1, out_wins, g_base1, got_f1 = sync(g_hid1, g_proj1, out_wins, g_base1, got_f1)
    grad1 = exchange(g_hid1)
    z_f1 = sum_corner(half_f1, got_f1, z)
    a1_keep, *a1_send = qkv_grad(g_proj1, normed1, o1_keep, o1_send, True)
    a1_got = [swap(v, CORE) for v in a1_send]
    gt_t = jnp.einsum(
        "hjtk,rjk->htr",
        g_base1[:, :, :576].reshape(16, 64, 9, 64),
        hot_t,
        precision=HIGHEST_PRECISION,
    ).reshape(16, n_t)
    out_wins = from_quads(out_wins)
    out_keep, out_send = last_window(out_wins, odd)
    total_a1 = sum_core(a1_keep, a1_got)
    grad1, total_a1, z_f1, gt_t, out_wins, out_keep, out_send = sync(
        grad1, total_a1, z_f1, gt_t, out_wins, out_keep, out_send
    )
    grad1 = from_quads(grad1)
    mine_f1 = sum_line(z_f1)
    out_got = partner(out_send)
    got_a1 = send_plane(total_a1, (1, 2, 3))
    f0_keep, f0_send, g_shift0 = ffn_bwd(grad1, pre0, shifted0, weights_f0, 0, mods, 0)
    f0_keep, f0_send, g_shift0, mine_f1, got_a1, out_got = sync(
        f0_keep, f0_send, g_shift0, mine_f1, got_a1, out_got
    )
    f0_got = swap(f0_send, CORE)
    sides_f1 = sides_stage(mine_f1[None])
    mine_a1 = sum_line(sum_plane(total_a1, got_a1, z))
    g_mid0, g_att0, o0_keep, o0_send, sums_o0 = out_bwd(
        grad1, g_shift0, middle0, feed0, branch0, attended0, weights_a0, mods, 0
    )
    g_att0, f0_got, sides_f1 = sync(g_att0, f0_got, sides_f1)
    total_f0 = sum_core(f0_keep, f0_got)
    g_att0, total_f0 = sync(g_att0, total_f0)
    got_f0 = send_cross(total_f0)
    corner_f1 = corner_stage(sides_f1)
    g_proj0, g_base0 = attn_bwd(qkv0, g_att0, base_s, fc, spatial)
    a0_keep, a0_send = qkv_grad(g_proj0, normed0, o0_keep, o0_send, False)
    a0_keep, a0_send, got_f0, corner_f1, mine_a1, g_proj0, g_base0 = sync(
        a0_keep, a0_send, got_f0, corner_f1, mine_a1, g_proj0, g_base0
    )
    a0_got = swap(a0_send, CORE)
    half_f0 = sum_cross(total_f0, got_f0)
    early_rows = jnp.concatenate(
        [
            sums_o0[2:3], sums_o0[0:2], sums_o0[3:4],
            sums_q1[0:2], sums_o1[2:3], sums_o1[0:2], sums_o1[3:4],
        ],
        axis=0,
    )
    half_f0, early_rows = sync(half_f0, early_rows)
    got_f0 = send_corner(half_f0)
    early_got = partner(early_rows)
    early_got, g_base0, sides_f1, corner_f1 = sync(early_got, g_base0, sides_f1, corner_f1)
    own_gf1 = joined(sides_f1, corner_f1).reshape(4, 256, D)
    g_feed = finish_feed(place, own_gf1, swap(own_gf1, CORE), 1, ())
    gt_s = jnp.einsum(
        "hjai,bji->hab",
        g_base0[:, :, :496].reshape(16, 16, 31, 16),
        hot_s,
        precision=HIGHEST_PRECISION,
    ).reshape(16, n_s)
    gt = table_rows(gt_s, gt_t)
    half_f0, got_f0, a0_got, g_proj0, g_feed, gt = sync(
        half_f0, got_f0, a0_got, g_proj0, g_feed, gt
    )
    z_f0 = sum_corner(half_f0, got_f0, z)
    total_a0 = sum_core(a0_keep, a0_got)
    total_a0 = [jnp.concatenate([total_a0[m], gt[m]], axis=1) for m in range(4)]
    total_a0, z_f0, g_proj0 = sync(total_a0, z_f0, g_proj0)
    mine_f0 = sum_line(z_f0)
    got_a0 = send_cross(total_a0)
    grad0, sums_q0 = qkv_back(g_proj0, weights_a0, hidden0, g_mid0, mods, 0, F32, 1)
    sides_a1 = sides_stage(mine_a1[None])
    grad0, sums_q0, got_a0, sides_a1 = sync(grad0, sums_q0, got_a0, sides_a1)
    half_a0 = sum_cross(total_a0, got_a0)
    half_a0, grad0, sums_q0 = sync(half_a0, grad0, sums_q0)
    got_a0 = send_corner(half_a0)
    corner_a1 = corner_stage(sides_a1)
    mod_rows = sums_q0[0:2]
    mod_got = partner(mod_rows)
    got_a0, corner_a1, mine_f0, mod_got, mod_rows = sync(
        got_a0, corner_a1, mine_f0, mod_got, mod_rows
    )
    z_a0 = sum_corner(half_a0, got_a0, z)
    mod_sum = jnp.concatenate([mod_rows + mod_got, early_rows + early_got], axis=0)
    z_a0, mine_f0, mod_sum = sync(z_a0, mine_f0, mod_sum)
    mine_a0 = sum_line(z_a0)
    own_gf0 = cross_stage(mine_f0)
    own_ga1 = joined(sides_a1, corner_a1).reshape(4, 128, D)
    rows_whole = whole_windows(grad0, odd)
    output = spatial_to_rows(whole_windows(out_wins, odd), out_keep, out_got, odd)
    rows_keep, rows_send = last_window(grad0, odd)
    mine_a0, own_gf0, own_ga1, rows_keep, rows_send, rows_whole, output = sync(
        mine_a0, own_gf0, own_ga1, rows_keep, rows_send, rows_whole, output
    )
    own_ga0 = cross_stage(mine_a0)
    rows_got = partner(rows_send)
    own_gf0 = jnp.stack(own_gf0)
    g_feed = finish_feed(place, own_gf0, swap(own_gf0, CORE), 0, g_feed)
    own_ga0, g_feed, rows_got, own_ga1, mod_sum = sync(own_ga0, g_feed, rows_got, own_ga1, mod_sum)
    own_ga0 = jnp.stack(own_ga0)
    own_ga = jnp.concatenate([own_ga0[:, :128], own_ga1, own_ga0[:, 128:]], axis=1)
    mod_got = lax.ppermute(mod_sum, "head", [(i, i ^ 2) for i in range(NZ)])
    grad_tokens = spatial_to_rows(rows_whole, rows_keep, rows_got, odd)
    other_ga = swap(own_ga, CORE)
    g_attn = finish_attn(place, own_ga, other_ga)
    tab = own_ga[:, 256:272].astype(F32) + other_ga[:, 256:272].astype(F32)
    tab = jnp.concatenate(
        [lax.dynamic_slice_in_dim(tab, chip ^ m, 1, axis=0) for m in range(4)], axis=0
    )
    tab = tab.reshape(4, 16 * D)
    return (
        output,
        grad_tokens,
        (mod_sum + mod_got)[None],
        g_attn[0],
        g_attn[1],
        g_feed[0],
        g_feed[1],
        tab[:, :n_s],
        tab[:, D : D + n_t],
    )


def solution(mesh):
    if mesh.shape["head"] == NZ and mesh.shape["clip"] == 8:
        body = on_device_windows
    else:
        body = on_device
    return jax.shard_map(
        body,
        mesh=mesh,
        in_specs=(
            P(("clip", "head"), None),
            P(("clip", "head"), None),
            P("clip", None, None),
            P("clip"),
            P(None, None, None, "head"),
            P(None, "head", None),
            P(None, None, "head"),
            P(None, "head", None),
            P("head", None),
            P("head", None),
        ),
        out_specs=(
            P(("clip", "head"), None),
            P(("clip", "head"), None),
            P("clip", None, None),
            P(None, None, None, "head"),
            P(None, "head", None),
            P(None, None, "head"),
            P(None, "head", None),
            P("head", None),
            P("head", None),
        ),
        check_vma=False,
    )
```

```python
import jax
import jax.numpy as jnp
from jax import lax
from jax.experimental import pallas as pl
from jax.experimental.pallas import tpu as pltpu
from jax.sharding import PartitionSpec as P

HD = 64
FH = 32
FW = 32
SWIN = 16
TWIN = 8
PADF = 5


EPS = 1e-06
HIGHEST_PRECISION = lax.Precision.HIGHEST
NEGATIVE = -1e30


def layer_norm(values, shift_row, scale_row):
    average = jnp.mean(values, axis=-1, keepdims=True)
    centred = values - average
    spread = jnp.mean(centred * centred, axis=-1, keepdims=True)
    return centred * lax.rsqrt(spread + EPS) * (1.0 + scale_row) + shift_row


def gelu_tanh(values):
    return jax.nn.gelu(values, approximate=True)


def window_index(side_t, side_len):
    window_size = side_t * side_len * side_len
    places = jnp.arange(window_size, dtype=jnp.int32)
    time_pos = places // (side_len * side_len)
    height_pos = places // side_len % side_len
    width_pos = places % side_len
    span_len = 2 * side_len - 1
    return (
        (time_pos[:, None] - time_pos[None, :] + side_t - 1) * span_len * span_len
        + (height_pos[:, None] - height_pos[None, :] + side_len - 1) * span_len
        + (width_pos[:, None] - width_pos[None, :] + side_len - 1)
    )


def to_windows(values, side_t, side_len):
    tail_shape = values.shape[1:]
    frames = values.shape[0] // (FH * FW)
    shaped = values.reshape(
        (frames // side_t, side_t, FH // side_len, side_len, FW // side_len, side_len) + tail_shape
    )
    axis_order = (0, 2, 4, 1, 3, 5) + tuple(range(6, 6 + len(tail_shape)))
    shaped = shaped.transpose(axis_order)
    return shaped.reshape((-1, side_t * side_len * side_len) + tail_shape)


def from_windows(values, side_t, side_len):
    tail_shape = values.shape[2:]
    blocks_high = FH // side_len
    blocks_wide = FW // side_len
    frame_groups = values.shape[0] // (blocks_high * blocks_wide)
    shaped = values.reshape(
        (frame_groups, blocks_high, blocks_wide, side_t, side_len, side_len) + tail_shape
    )
    axis_order = (0, 3, 1, 4, 2, 5) + tuple(range(6, 6 + len(tail_shape)))
    return shaped.transpose(axis_order).reshape((frame_groups * side_t * FH * FW,) + tail_shape)


def on_device(
    tokens, d_out, modulation, frame_counts, w_qkv, w_out, w_up, w_down, table_s, table_t
):
    local_rows = tokens.shape[0]
    clip_len = PADF * FH * FW
    group_clips = modulation.shape[0]
    group_rows = group_clips * clip_len
    scale_dot = HD ** (-0.5)
    my_index = lax.axis_index("head")
    first_row = my_index * local_rows
    row_ids = first_row + jnp.arange(local_rows, dtype=jnp.int32)
    clip_slots = jnp.arange(group_clips, dtype=jnp.int32)
    row_onehot = ((row_ids // clip_len)[:, None] == clip_slots[None, :]).astype(jnp.float32)
    count_float = frame_counts.astype(jnp.float32)
    row_frames = jnp.dot(row_onehot, count_float, precision=HIGHEST_PRECISION)
    row_keep = ((row_ids % clip_len // (FH * FW)).astype(jnp.float32) < row_frames).astype(
        jnp.float32
    )[:, None]
    group_ids = jnp.arange(group_rows, dtype=jnp.int32)
    group_onehot = ((group_ids // clip_len)[:, None] == clip_slots[None, :]).astype(jnp.float32)
    group_frames = jnp.dot(group_onehot, count_float, precision=HIGHEST_PRECISION)
    group_keep = (group_ids % clip_len // (FH * FW)).astype(jnp.float32) < group_frames

    def block_shape(block_id):
        if block_id == 0:
            return (1, SWIN)
        return (PADF, TWIN)

    def mod_row(slot):
        return jnp.dot(row_onehot, modulation[:, slot, :], precision=HIGHEST_PRECISION)

    def rows_in(values):
        return lax.all_gather(values, "head", axis=0, tiled=True)

    def grads_in(values):
        return lax.all_gather(values, "head", axis=0, tiled=True)

    def rows_out(full_rows, weight):
        return lax.psum_scatter(
            jnp.dot(full_rows, weight, preferred_element_type=jnp.float32).astype(jnp.bfloat16),
            "head",
            scatter_dimension=0,
            tiled=True,
        ).astype(jnp.float32)

    def grads_out(full_rows, weight, einsum_form):
        return lax.psum_scatter(
            jnp.einsum(einsum_form, full_rows, weight, preferred_element_type=jnp.float32).astype(
                jnp.bfloat16
            ),
            "head",
            scatter_dimension=0,
            tiled=True,
        ).astype(jnp.float32)

    def rows_keep(block_id):
        if block_id == 0:
            return None
        return to_windows(group_keep[:, None], PADF, TWIN)[:, :, 0]

    def shape_windows(projected, side_t, side_len):
        head_count = projected.shape[-1] // HD
        window_size = side_t * side_len * side_len
        windows = to_windows(projected, side_t, side_len)
        return windows.reshape(windows.shape[0], window_size, 3, head_count, HD)

    def shape_grad(grad_attended, side_t, side_len):
        head_count = grad_attended.shape[-1] // HD
        window_size = side_t * side_len * side_len
        windows = to_windows(grad_attended, side_t, side_len)
        return windows.reshape(windows.shape[0], window_size, head_count, HD)

    def flat_rows(windowed, side_t, side_len):
        return from_windows(windowed, side_t, side_len)

    def logits_of(queries, key_rows, table_arg, rel_index, keep_win):
        logits = (
            jnp.einsum("wqhe,wkhe->whqk", queries, key_rows, preferred_element_type=jnp.float32)
            * scale_dot
        )
        logits = logits + table_arg[:, rel_index][None]
        if keep_win is not None:
            logits = jnp.where(keep_win[:, None, None, :], logits, NEGATIVE)
        return logits

    def attend(windows, table_arg, rel_index, keep_win):
        logits = logits_of(windows[:, :, 0], windows[:, :, 1], table_arg, rel_index, keep_win)
        row_max = jnp.max(logits, axis=-1, keepdims=True)
        exponent = jnp.exp(logits - row_max)
        row_total = jnp.sum(exponent, axis=-1, keepdims=True)
        probs = exponent / row_total
        log_total = row_max + jnp.log(row_total)
        attended = jnp.einsum(
            "whqk,wkhe->wqhe",
            probs.astype(jnp.bfloat16),
            windows[:, :, 2],
            preferred_element_type=jnp.float32,
        )
        return (attended.reshape(attended.shape[0], attended.shape[1], -1), log_total)

    def attend_back(windows, grad_windows, log_total, table_arg, rel_index, keep_win):
        queries = windows[:, :, 0]
        key_rows = windows[:, :, 1]
        value_rows = windows[:, :, 2]
        logits = logits_of(queries, key_rows, table_arg, rel_index, keep_win)
        probs = jnp.exp(logits - log_total)
        grad_probs = jnp.einsum(
            "wqhe,wkhe->whqk", grad_windows, value_rows, preferred_element_type=jnp.float32
        )
        grad_values = jnp.einsum(
            "whqk,wqhe->wkhe",
            probs.astype(jnp.bfloat16),
            grad_windows,
            preferred_element_type=jnp.float32,
        )
        grad_logits = (
            probs * (grad_probs - jnp.sum(grad_probs * probs, axis=-1, keepdims=True))
        ).astype(jnp.bfloat16)
        head_count = queries.shape[2]
        table_terms = jnp.sum(grad_logits.astype(jnp.float32), axis=0).reshape(head_count, -1)
        grad_table = jax.ops.segment_sum(
            table_terms.T, rel_index.reshape(-1), num_segments=table_arg.shape[1]
        ).T
        grad_queries = (
            jnp.einsum("whqk,wkhe->wqhe", grad_logits, key_rows, preferred_element_type=jnp.float32)
            * scale_dot
        )
        grad_keys = (
            jnp.einsum("whqk,wqhe->wkhe", grad_logits, queries, preferred_element_type=jnp.float32)
            * scale_dot
        )
        grad_stack = jnp.stack([grad_queries, grad_keys, grad_values], axis=2)
        return (
            grad_stack.reshape(grad_stack.shape[0], grad_stack.shape[1], 3, head_count * HD),
            grad_table,
        )

    def forward_block(hidden, block_id):
        side_t, side_len = block_shape(block_id)
        table_local = table_s if block_id == 0 else table_t
        rel_index = window_index(side_t, side_len)
        normed = layer_norm(hidden, mod_row(6 * block_id), mod_row(6 * block_id + 1)).astype(
            jnp.bfloat16
        )
        plan = None
        normed_in = rows_in(normed)
        qkv_use, out_use, table_use = (w_qkv[block_id], w_out[block_id], table_local)
        keep_win = rows_keep(block_id)
        projected = jnp.einsum(
            "gd,cde->gce", normed_in, qkv_use, preferred_element_type=jnp.float32
        ).astype(jnp.bfloat16)
        windows = shape_windows(projected, side_t, side_len)
        attended_win, log_total = attend(windows, table_use, rel_index, keep_win)
        attended = flat_rows(attended_win, side_t, side_len).astype(jnp.bfloat16)
        branch = rows_out(attended, out_use)
        middle = hidden + mod_row(6 * block_id + 2) * branch
        shifted = layer_norm(middle, mod_row(6 * block_id + 3), mod_row(6 * block_id + 4)).astype(
            jnp.bfloat16
        )
        up_full, down_full = (
            lax.all_gather(w_up[block_id], "head", axis=1, tiled=True),
            lax.all_gather(w_down[block_id], "head", axis=0, tiled=True),
        )
        pre_gelu = jnp.dot(shifted, up_full, preferred_element_type=jnp.float32)
        activated = gelu_tanh(pre_gelu).astype(jnp.bfloat16)
        feed_out = jnp.dot(activated, down_full, preferred_element_type=jnp.float32)
        mlp_state = (shifted, pre_gelu, activated, up_full, down_full)
        result = middle + mod_row(6 * block_id + 5) * feed_out
        attn_state = (
            normed_in,
            projected,
            log_total,
            attended,
            qkv_use,
            out_use,
            table_use,
            keep_win,
            plan,
        )
        saved_state = (hidden, attn_state, branch, middle, feed_out, mlp_state)
        return (saved_state, result)

    def backward_block(saved_state, grad_result, block_id):
        hidden, attn_state, branch, middle, feed_out, mlp_state = saved_state
        normed_in, projected, log_total, attended, qkv_use, out_use, table_use, keep_win, plan = (
            attn_state
        )
        shifted_in, pre_gelu, activated, up_weight, down_weight = mlp_state
        side_t, side_len = block_shape(block_id)
        rel_index = window_index(side_t, side_len)
        grad_feed = (grad_result * mod_row(6 * block_id + 5)).astype(jnp.bfloat16)
        grad_gate_mlp = grad_result * feed_out
        grad_down = jnp.einsum(
            "gf,gd->fd", activated, grad_feed, preferred_element_type=jnp.float32
        )
        grad_activated = jnp.einsum(
            "gd,fd->gf", grad_feed, down_weight, preferred_element_type=jnp.float32
        )
        grad_pre = jax.vjp(gelu_tanh, pre_gelu)[1](grad_activated)[0].astype(jnp.bfloat16)
        grad_up = jnp.einsum("gd,gf->df", shifted_in, grad_pre, preferred_element_type=jnp.float32)
        grad_shifted = jnp.einsum(
            "gf,df->gd", grad_pre, up_weight, preferred_element_type=jnp.float32
        )
        grad_up, grad_down = (
            lax.psum_scatter(
                grad_up.astype(jnp.bfloat16), "head", scatter_dimension=1, tiled=True
            ).astype(jnp.float32),
            lax.psum_scatter(
                grad_down.astype(jnp.bfloat16), "head", scatter_dimension=0, tiled=True
            ).astype(jnp.float32),
        )
        unused_mid, pull_second = jax.vjp(
            layer_norm, middle, mod_row(6 * block_id + 3), mod_row(6 * block_id + 4)
        )
        grad_mid_norm, grad_shift_mlp, grad_scale_mlp = pull_second(grad_shifted)
        grad_middle = grad_result + grad_mid_norm
        grad_branch = (grad_middle * mod_row(6 * block_id + 2)).astype(jnp.bfloat16)
        grad_gate_att = grad_middle * branch
        branch_in = grads_in(grad_branch)
        grad_wout = jnp.einsum("ge,gd->ed", attended, branch_in, preferred_element_type=jnp.float32)
        grad_attended = jnp.einsum(
            "gd,ed->ge", branch_in, out_use, preferred_element_type=jnp.float32
        ).astype(jnp.bfloat16)
        windows = shape_windows(projected, side_t, side_len)
        grad_windows = shape_grad(grad_attended, side_t, side_len)
        grad_stack, grad_table = attend_back(
            windows, grad_windows, log_total, table_use, rel_index, keep_win
        )
        grad_projected = flat_rows(grad_stack, side_t, side_len).astype(jnp.bfloat16)
        grad_qkv = jnp.einsum(
            "gd,gce->cde", normed_in, grad_projected, preferred_element_type=jnp.float32
        )
        grad_normed = grads_out(grad_projected, qkv_use, "gce,cde->gd")
        unused_hid, pull_first = jax.vjp(
            layer_norm, hidden, mod_row(6 * block_id), mod_row(6 * block_id + 1)
        )
        grad_hid_norm, grad_shift_att, grad_scale_att = pull_first(grad_normed)
        grad_hidden = grad_middle + grad_hid_norm
        mod_terms = jnp.stack(
            [
                grad_shift_att,
                grad_scale_att,
                grad_gate_att,
                grad_shift_mlp,
                grad_scale_mlp,
                grad_gate_mlp,
            ],
            axis=1,
        )
        grad_mods = jnp.einsum("rc,rke->cke", row_onehot, mod_terms, precision=HIGHEST_PRECISION)
        return (grad_hidden, grad_mods, (grad_qkv, grad_wout, grad_up, grad_down, grad_table))

    hidden_first = tokens.astype(jnp.float32)
    saved_first, hidden_second = forward_block(hidden_first, 0)
    saved_second, hidden_last = forward_block(hidden_second, 1)
    output = (hidden_last * row_keep).astype(jnp.bfloat16)
    grad_second, mods_second, weights_second = backward_block(
        saved_second, d_out.astype(jnp.float32) * row_keep, 1
    )
    grad_first, mods_first, weights_first = backward_block(saved_first, grad_second, 0)
    grad_modulation = lax.psum(
        jnp.concatenate([mods_first, mods_second], axis=1).astype(jnp.bfloat16), "head"
    ).astype(jnp.float32)
    summed = (
        lax.psum(
            jnp.stack([weights_first[0], weights_second[0]]).astype(jnp.bfloat16), "clip"
        ).astype(jnp.float32),
        lax.psum(
            jnp.stack([weights_first[1], weights_second[1]]).astype(jnp.bfloat16), "clip"
        ).astype(jnp.float32),
        lax.psum(
            jnp.stack([weights_first[2], weights_second[2]]).astype(jnp.bfloat16), "clip"
        ).astype(jnp.float32),
        lax.psum(
            jnp.stack([weights_first[3], weights_second[3]]).astype(jnp.bfloat16), "clip"
        ).astype(jnp.float32),
        lax.psum(weights_first[4].astype(jnp.bfloat16), "clip").astype(jnp.float32),
        lax.psum(weights_second[4].astype(jnp.bfloat16), "clip").astype(jnp.float32),
    )
    return (
        output,
        grad_first,
        grad_modulation,
        summed[0],
        summed[1],
        summed[2],
        summed[3],
        summed[4],
        summed[5],
    )


F32 = jnp.float32
BF16 = jnp.bfloat16
VMEM_LIMIT = 58 * 1024 * 1024
NZ = 4
D = 1024
HPZ = 4
CONST = pl.Buffered(1)


def dot_nn(a, b):
    return lax.dot_general(a, b, (((1,), (0,)), ((), ())), preferred_element_type=F32)


def dot_nt(a, b):
    return lax.dot_general(a, b, (((1,), (1,)), ((), ())), preferred_element_type=F32)


def dot_tn(a, b):
    return lax.dot_general(a, b, (((0,), (0,)), ((), ())), preferred_element_type=F32)


def call(kernel, name, grid, in_specs, out_specs, out_shape, scratch, flops, nbytes):
    return pl.pallas_call(
        kernel,
        name=name,
        grid=grid,
        in_specs=in_specs,
        out_specs=out_specs,
        out_shape=out_shape,
        scratch_shapes=scratch,
        compiler_params=pltpu.CompilerParams(
            dimension_semantics=("arbitrary",) * len(grid), vmem_limit_bytes=VMEM_LIMIT
        ),
        cost_estimate=pl.CostEstimate(
            flops=flops // 4, bytes_accessed=nbytes // 4, transcendentals=0
        ),
    )


def full(shape):
    return pl.BlockSpec(shape, lambda *ids: (0,) * len(shape), pipeline_mode=CONST)


ANYWHERE = pl.BlockSpec(memory_space=pl.ANY)


def chunk_rows(i, size):
    return pl.ds(pl.multiple_of(i * size, size), size)


def ln_stats(x):
    mean = jnp.mean(x, axis=-1, keepdims=True)
    centred = x - mean
    rstd = lax.rsqrt(jnp.mean(centred * centred, axis=-1, keepdims=True) + EPS)
    return centred * rstd, rstd


def ln_back(grad, hat, rstd, scale):
    gh = grad * (1.0 + scale)
    m1 = jnp.mean(gh, axis=-1, keepdims=True)
    m2 = jnp.mean(gh * hat, axis=-1, keepdims=True)
    return rstd * (gh - m1 - hat * m2)


def piece_specs(k, row, count):
    tail = (count, D)
    return [
        pl.BlockSpec((2, 4) + tail, lambda d: (0, 0, row, 0), pipeline_mode=CONST),
        pl.BlockSpec((4, 1) + tail, lambda d: (0, jnp.maximum(d - 1, 0), row, 0)),
        pl.BlockSpec((4, 1) + tail, lambda d: (0, jnp.maximum(d - 1, 0), row, 0)),
    ]


def by_offset(d, body, local_ref, own_ref, other_ref):
    @pl.when(d == 0)
    def _():
        body(lambda m, r, n: local_ref[0, m, r : r + n, :], lambda m, r, n: local_ref[1, m, r : r + n, :])

    @pl.when(d > 0)
    def _():
        body(lambda m, r, n: own_ref[m, 0, r : r + n, :], lambda m, r, n: other_ref[m, 0, r : r + n, :])


def head_rows(own, other, row):
    parts = []
    for m in range(4):
        parts += [own(m, row, 32), other(m, row, 32)]
    return jnp.concatenate(parts, axis=0)


def pair_rows(first, second):
    return jnp.concatenate([get(m) for get in (first, second) for m in range(4)], axis=0)


def feed_specs(down_block):
    def spec(block):
        return pl.BlockSpec((4, 1, 128, D), lambda d: (0, jnp.maximum(d - 1, 0), block, 0))

    return [full((2, 4, 256, D)), spec(0), spec(0), spec(down_block), spec(down_block)]


def feed_by_offset(d, body, l_ref, wu_ref, vu_ref, wd_ref, vd_ref):
    @pl.when(d == 0)
    def _():
        body(
            lambda: pair_rows(lambda m: l_ref[0, m, 0:128], lambda m: l_ref[1, m, 0:128]),
            lambda: pair_rows(lambda m: l_ref[0, m, 128:256], lambda m: l_ref[1, m, 128:256]),
        )

    @pl.when(d > 0)
    def _():
        body(
            lambda: pair_rows(lambda m: wu_ref[m, 0], lambda m: vu_ref[m, 0]),
            lambda: pair_rows(lambda m: wd_ref[m, 0], lambda m: vd_ref[m, 0]),
        )


def ln_qkv(hidden, mods, weights, base):
    rows = hidden.shape[0]
    step = 640

    def kernel(h_ref, m_ref, l_ref, w_ref, v_ref, normed_ref, qkv_ref):
        d = pl.program_id(0)

        @pl.when(d == 0)
        def _():
            def body(i, carry):
                sl = chunk_rows(i, step)
                hat, _ = ln_stats(h_ref[sl, :].astype(F32))
                normed_ref[sl, :] = (
                    hat * (1.0 + m_ref[base + 1 : base + 2, :]) + m_ref[base : base + 1, :]
                ).astype(BF16)
                return carry

            lax.fori_loop(0, rows // step, body, 0)

        def work(own, other):
            for t in range(3):
                qkv_ref[:, t * 256 : (t + 1) * 256] = dot_nt(
                    normed_ref[...], head_rows(own, other, t * 32)
                ).astype(BF16)

        by_offset(d, work, l_ref, w_ref, v_ref)

    return call(
        kernel,
        "ln_qkv",
        (NZ,),
        [full((rows, D)), full((12, D))] + piece_specs(128, 0, 96),
        [full((rows, D)), pl.BlockSpec((rows, 768), lambda z: (0, z))],
        [jax.ShapeDtypeStruct((rows, D), BF16), jax.ShapeDtypeStruct((rows, 3 * D), BF16)],
        [],
        2 * rows * D * 3 * D,
        rows * D * 12 + 6 * D * D,
    )(hidden, mods, *weights)


def build_bias(base_ref, bias_ref, fc_ref, slides, width, lanes_step):
    rows_step = width // slides
    for h in range(HPZ):
        for s in range(slides):
            off = (slides - 1 - s) * lanes_step
            tile = base_ref[h, :, off : off + width]
            if fc_ref is not None:
                tile = jnp.where(s < fc_ref[0], tile, NEGATIVE)
            bias_ref[h, s * rows_step : (s + 1) * rows_step, :] = tile


def window_view(values, kind):
    parts, count, size = kind[0]
    return values.reshape(parts, count, size, values.shape[-1])


def attn_fwd(qkv, base, fc, kind):
    (parts, count, size), slides, lanes_step, masked = kind
    rows, width = qkv.shape[0], parts * size
    r_step, lanes = base.shape[1], base.shape[2]

    def kernel(x_ref, b_ref, fc_ref, o_ref, bias_ref):
        build_bias(b_ref, bias_ref, fc_ref if masked else None, slides, width, lanes_step)

        def one(w, carry):
            def cut(col):
                return x_ref[:, w, :, col : col + HD].reshape(width, HD)

            scores, probs = [], []
            for h in range(HPZ):
                scores.append(dot_nt(cut(256 + h * HD), cut(h * HD) * 0.125) + bias_ref[h])
            for h in range(HPZ):
                expo = jnp.exp(scores[h] - jnp.max(scores[h], axis=0, keepdims=True))
                inv = 1.0 / jnp.sum(expo, axis=0, keepdims=True)
                probs.append((expo * inv).astype(BF16))
            for h in range(HPZ):
                got = dot_tn(probs[h], cut(512 + h * HD)).astype(BF16)
                o_ref[:, w, :, h * HD : (h + 1) * HD] = got.reshape(parts, size, HD)
            return carry

        lax.fori_loop(0, count, one, 0)

    return call(
        kernel,
        "attn_fwd",
        (NZ,),
        [
            pl.BlockSpec((parts, count, size, 768), lambda z: (0, 0, 0, z)),
            pl.BlockSpec((HPZ, r_step, lanes), lambda z: (z, 0, 0)),
            pl.BlockSpec(memory_space=pltpu.SMEM),
        ],
        pl.BlockSpec((parts, count, size, 256), lambda z: (0, 0, 0, z)),
        jax.ShapeDtypeStruct((parts, count, size, D), BF16),
        [pltpu.VMEM((HPZ, width, width), F32)],
        count * 16 * width * width * HD * 16,
        rows * D * 8,
    )(window_view(qkv, kind), base, fc).reshape(rows, D)


def attn_bwd(qkv, grad_att, base, fc, kind):
    (parts, count, size), slides, lanes_step, masked = kind
    rows, width = qkv.shape[0], parts * size
    r_step, lanes = base.shape[1], base.shape[2]

    def kernel(x_ref, d_ref, b_ref, fc_ref, o_ref, gb_ref, bias_ref, acc_ref):
        build_bias(b_ref, bias_ref, fc_ref if masked else None, slides, width, lanes_step)
        acc_ref[...] = jnp.zeros_like(acc_ref)

        def one(w, carry):
            def cut(ref, col):
                return ref[:, w, :, col : col + HD].reshape(width, HD)

            def put(col, value):
                o_ref[:, w, :, col : col + HD] = value.astype(BF16).reshape(parts, size, HD)

            q = [cut(x_ref, h * HD) * 0.125 for h in range(HPZ)]
            k = [cut(x_ref, 256 + h * HD) for h in range(HPZ)]
            da = [cut(d_ref, h * HD) for h in range(HPZ)]
            score = [dot_nt(k[h], q[h]) + bias_ref[h] for h in range(HPZ)]
            dp = [dot_nt(cut(x_ref, 512 + h * HD), da[h]) for h in range(HPZ)]
            probs, dl = [], []
            for h in range(HPZ):
                expo = jnp.exp(score[h] - jnp.max(score[h], axis=0, keepdims=True))
                inv = 1.0 / jnp.sum(expo, axis=0, keepdims=True)
                p = expo * inv
                row = jnp.sum(dp[h] * p, axis=0, keepdims=True)
                g = (p * (dp[h] - row)).astype(BF16)
                acc_ref[h] += g.astype(F32)
                probs.append(p.astype(BF16))
                dl.append(g)
            for h in range(HPZ):
                put(h * HD, dot_tn(dl[h], k[h]) * 0.125)
                put(256 + h * HD, dot_nn(dl[h], q[h]))
                put(512 + h * HD, dot_nn(probs[h], da[h]))
            return carry

        lax.fori_loop(0, count, one, 0)
        gb_ref[...] = jnp.zeros_like(gb_ref)
        for h in range(HPZ):
            for s in range(slides):
                off = (slides - 1 - s) * lanes_step
                gb_ref[h, :, off : off + width] += acc_ref[h, s * r_step : (s + 1) * r_step, :]

    xspec = pl.BlockSpec((parts, count, size, 768), lambda z: (0, 0, 0, z))
    bspec = pl.BlockSpec((HPZ, r_step, lanes), lambda z: (z, 0, 0))
    proj, strips = call(
        kernel,
        "attn_bwd",
        (NZ,),
        [
            xspec,
            pl.BlockSpec((parts, count, size, 256), lambda z: (0, 0, 0, z)),
            bspec,
            pl.BlockSpec(memory_space=pltpu.SMEM),
        ],
        [xspec, bspec],
        [
            jax.ShapeDtypeStruct((parts, count, size, 3 * D), BF16),
            jax.ShapeDtypeStruct(base.shape, F32),
        ],
        [pltpu.VMEM((HPZ, width, width), F32), pltpu.VMEM((HPZ, width, width), F32)],
        count * 16 * width * width * HD * 40,
        rows * D * 16,
    )(window_view(qkv, kind), window_view(grad_att, kind), base, fc)
    return proj.reshape(rows, 3 * D), strips


def out_specs_of(row_block):
    return [
        pl.BlockSpec((2, 4, 32, D), lambda i: (0, 0, row_block, 0), pipeline_mode=CONST),
        pl.BlockSpec((4, 3, 32, D), lambda i: (0, 0, row_block, 0), pipeline_mode=CONST),
        pl.BlockSpec((4, 3, 32, D), lambda i: (0, 0, row_block, 0), pipeline_mode=CONST),
    ]


def out_rows(d, l_ref, w_ref, v_ref):
    if d == 0:
        return head_rows(
            lambda m, r, n: l_ref[0, m, :, :], lambda m, r, n: l_ref[1, m, :, :], 0
        )
    return head_rows(
        lambda m, r, n: w_ref[m, d - 1, :, :], lambda m, r, n: v_ref[m, d - 1, :, :], 0
    )


def out_proj(attended, weights, hidden, mods, base):
    rows = attended.shape[0]
    step = 256

    def kernel(a_ref, l_ref, w_ref, v_ref, h_ref, m_ref, br_ref, mid_ref, sh_ref):
        branch = jnp.zeros((step, D), F32)
        for d in range(NZ):
            branch += dot_nn(a_ref[:, d * 256 : (d + 1) * 256], out_rows(d, l_ref, w_ref, v_ref))
        br_ref[...] = branch.astype(BF16)
        middle = h_ref[...].astype(F32) + m_ref[base + 2 : base + 3, :] * branch
        mid_ref[...] = middle
        hat, _ = ln_stats(middle)
        sh_ref[...] = (
            hat * (1.0 + m_ref[base + 4 : base + 5, :]) + m_ref[base + 3 : base + 4, :]
        ).astype(BF16)

    tile = pl.BlockSpec((step, D), lambda i: (i, 0))
    return call(
        kernel,
        "out_proj",
        (rows // step,),
        [tile] + out_specs_of(3) + [tile, full((12, D))],
        [tile, tile, tile],
        [
            jax.ShapeDtypeStruct((rows, D), BF16),
            jax.ShapeDtypeStruct((rows, D), F32),
            jax.ShapeDtypeStruct((rows, D), BF16),
        ],
        [],
        2 * rows * D * D,
        rows * D * 14 + 2 * D * D,
    )(attended, *weights, hidden, mods)


GELU_C = 0.7978845608028654
GELU_A = 0.044715


def gelu_of(x):
    return 0.5 * x * (1.0 + jnp.tanh(GELU_C * (x + GELU_A * x * x * x)))


def gelu_both(x):
    x2 = x * x
    th = jnp.tanh(GELU_C * (x + GELU_A * x * x2))
    half = 0.5 * (1.0 + th)
    slope = half + 0.5 * x * (1.0 - th * th) * (GELU_C * (1.0 + 3.0 * GELU_A * x2))
    return x * half, slope


def ffn_fwd(shifted, weights, down_block, middle, mods, base):
    rows = shifted.shape[0]
    step = 640

    def kernel(x_ref, *refs):
        parts, refs = refs[:5], refs[5:]
        mid_ref, m_ref, pre_ref, feed_ref, nx_ref, acc_ref, mid_late, sem = refs
        z = pl.program_id(0)
        copy = pltpu.make_async_copy(mid_ref, mid_late, sem)

        @pl.when(z == 0)
        def _():
            copy.start()

        @pl.when(z == NZ - 1)
        def _():
            copy.wait()

        def work(up, down):
            def body(i, carry):
                sl = chunk_rows(i, step)
                pre = dot_nt(x_ref[sl, :], up())
                pre_ref[sl, :] = pre.astype(BF16)
                part = dot_nn(gelu_of(pre).astype(BF16), down())

                @pl.when(z == 0)
                def _():
                    acc_ref[sl, :] = part

                @pl.when((z > 0) & (z < NZ - 1))
                def _():
                    acc_ref[sl, :] += part

                @pl.when(z == NZ - 1)
                def _():
                    feed = acc_ref[sl, :] + part
                    feed_ref[sl, :] = feed.astype(BF16)
                    nx_ref[sl, :] = (
                        mid_late[sl, :] + m_ref[base + 5 : base + 6, :] * feed
                    ).astype(BF16)

                return carry

            lax.fori_loop(0, rows // step, body, 0)

        feed_by_offset(z, work, *parts)

    return call(
        kernel,
        "ffn_fwd",
        (NZ,),
        [full((rows, D))] + feed_specs(down_block) + [ANYWHERE, full((12, D))],
        [pl.BlockSpec((rows, D), lambda z: (0, z)), full((rows, D)), full((rows, D))],
        [
            jax.ShapeDtypeStruct((rows, 4 * D), BF16),
            jax.ShapeDtypeStruct((rows, D), BF16),
            jax.ShapeDtypeStruct((rows, D), BF16),
        ],
        [
            pltpu.VMEM((rows, D), F32),
            pltpu.VMEM((rows, D), F32),
            pltpu.SemaphoreType.DMA,
        ],
        16 * rows * D * D,
        rows * D * 20 + 16 * D * D,
    )(shifted, *weights, middle, mods)


def ffn_bwd(grad, pre, shifted, weights, down_block, mods, base):
    rows = grad.shape[0]
    step = 640

    def kernel(g_ref, p_ref, x_ref, *refs):
        parts, refs = refs[:5], refs[5:]
        m_ref, keep_ref, send_ref, gs_ref, gf_ref, act_ref, gp_ref, x_late, sem = refs
        z = pl.program_id(0)
        copy = pltpu.make_async_copy(x_ref, x_late, sem)

        @pl.when(z == 0)
        def _():
            copy.start()

            def body(i, carry):
                sl = chunk_rows(i, step)
                gf_ref[sl, :] = (
                    g_ref[sl, :].astype(F32) * m_ref[base + 5 : base + 6, :]
                ).astype(BF16)
                gs_ref[sl, :] = jnp.zeros((step, D), F32)
                return carry

            lax.fori_loop(0, rows // step, body, 0)

        def work(up, down):
            def body(i, carry):
                sl = chunk_rows(i, step)
                back = dot_nt(gf_ref[sl, :], down())
                act, slope = gelu_both(p_ref[sl, :].astype(F32))
                act_ref[sl, :] = act.astype(BF16)
                gpre = (back * slope).astype(BF16)
                gp_ref[sl, :] = gpre
                part = dot_nn(gpre, up())
                gs_ref[sl, :] += part
                return carry

            lax.fori_loop(0, rows // step, body, 0)

        feed_by_offset(z, work, *parts)

        @pl.when(z == 0)
        def _():
            copy.wait()

        for j, out_ref in enumerate((keep_ref, send_ref)):
            cols = slice(j * 512, (j + 1) * 512)
            gd = dot_tn(act_ref[:, cols], gf_ref[...]).astype(BF16)
            gu = dot_tn(gp_ref[:, cols], x_late[...]).astype(BF16)
            out_ref[:, 0, 0:128] = gu.reshape(4, 128, D)
            out_ref[:, 0, 128:256] = gd.reshape(4, 128, D)

    gspec = pl.BlockSpec((4, 1, 256, D), lambda z: (0, z, 0, 0))
    gshape = jax.ShapeDtypeStruct((4, NZ, 256, D), BF16)
    return call(
        kernel,
        "ffn_bwd",
        (NZ,),
        [
            full((rows, D)),
            pl.BlockSpec((rows, D), lambda z: (0, z)),
            ANYWHERE,
        ]
        + feed_specs(down_block)
        + [full((12, D))],
        [gspec, gspec, full((rows, D))],
        [gshape, gshape, jax.ShapeDtypeStruct((rows, D), F32)],
        [pltpu.VMEM((rows, D), BF16)] * 4 + [pltpu.SemaphoreType.DMA],
        32 * rows * D * D,
        rows * D * 16 + 32 * D * D,
    )(grad, pre, shifted, *weights, mods)


def split_heads(value, keep_ref, send_ref, d, row):
    for m in range(4):
        keep_ref[m, d, row : row + 32] = value[m * 64 : m * 64 + 32]
        send_ref[m, d, row : row + 32] = value[m * 64 + 32 : m * 64 + 64]


def out_bwd(grad, grad_shifted, middle, feed, branch, attended, weights, mods, base):
    rows = grad.shape[0]
    step = 256
    steps = rows // step

    def kernel(
        g_ref, gs_ref, mid_ref, f_ref, b_ref, a_ref, l_ref, w_ref, v_ref, m_ref, gm_ref, ga_ref,
        keep_ref, send_ref, s_ref, gb_ref, a_late, sem,
    ):
        i = pl.program_id(0)
        copy = pltpu.make_async_copy(a_ref, a_late, sem)

        @pl.when(i == 0)
        def _():
            copy.start()
            s_ref[...] = jnp.zeros_like(s_ref)

        g = g_ref[...].astype(F32)
        gs = gs_ref[...]
        hat, rstd = ln_stats(mid_ref[...])
        gm = g + ln_back(gs, hat, rstd, m_ref[base + 4 : base + 5, :])
        gm_ref[...] = gm
        s_ref[0:1, :] += jnp.sum(gs, axis=0, keepdims=True)
        s_ref[1:2, :] += jnp.sum(gs * hat, axis=0, keepdims=True)
        s_ref[2:3, :] += jnp.sum(gm * b_ref[...].astype(F32), axis=0, keepdims=True)
        s_ref[3:4, :] += jnp.sum(g * f_ref[...].astype(F32), axis=0, keepdims=True)
        gb = (gm * m_ref[base + 2 : base + 3, :]).astype(BF16)
        gb_ref[chunk_rows(i, step), :] = gb
        for d in range(NZ):
            ga_ref[:, d * 256 : (d + 1) * 256] = dot_nt(
                gb, out_rows(d, l_ref, w_ref, v_ref)
            ).astype(BF16)

        @pl.when(i == steps - 1)
        def _():
            copy.wait()
            for d in range(NZ):
                gw = dot_tn(a_late[:, d * 256 : (d + 1) * 256], gb_ref[...]).astype(BF16)
                split_heads(gw, keep_ref, send_ref, d, 0)

    tile = pl.BlockSpec((step, D), lambda i: (i, 0))
    gshape = jax.ShapeDtypeStruct((4, NZ, 32, D), BF16)
    return call(
        kernel,
        "out_bwd",
        (steps,),
        [tile, tile, tile, tile, tile, ANYWHERE] + out_specs_of(3) + [full((12, D))],
        [tile, tile, full(gshape.shape), full(gshape.shape), full((8, D))],
        [
            jax.ShapeDtypeStruct((rows, D), F32),
            jax.ShapeDtypeStruct((rows, D), BF16),
            gshape,
            gshape,
            jax.ShapeDtypeStruct((8, D), F32),
        ],
        [
            pltpu.VMEM((rows, D), BF16),
            pltpu.VMEM((rows, D), BF16),
            pltpu.SemaphoreType.DMA,
        ],
        4 * rows * D * D,
        rows * D * 24 + 4 * D * D,
    )(grad, grad_shifted, middle, feed, branch, attended, *weights, mods)


def qkv_back(grad_proj, weights, hidden, grad_middle, mods, base, out_dtype, pieces):
    rows = hidden.shape[0]
    step = 640

    cols = D // pieces

    def kernel(p_ref, l_ref, w_ref, v_ref, h_ref, gm_ref, m_ref, *refs):
        gh_refs, (s_ref, acc_ref, h_late, gm_late, sems) = refs[:pieces], refs[pieces:]
        copies = [
            pltpu.make_async_copy(h_ref, h_late, sems.at[0]),
            pltpu.make_async_copy(gm_ref, gm_late, sems.at[1]),
        ]
        z = pl.program_id(0)

        @pl.when(z == 0)
        def _():
            for copy in copies:
                copy.start()
            acc_ref[...] = jnp.zeros_like(acc_ref)
            s_ref[...] = jnp.zeros_like(s_ref)

        def work(own, other):
            def body(i, carry):
                sl = chunk_rows(i, step)
                rows_of = jnp.concatenate([head_rows(own, other, t * 32) for t in range(3)], axis=0)
                acc_ref[sl, :] += dot_nn(p_ref[sl, :], rows_of)
                return carry

            lax.fori_loop(0, rows // step, body, 0)

        by_offset(z, work, l_ref, w_ref, v_ref)

        @pl.when(z == NZ - 1)
        def _():
            for copy in copies:
                copy.wait()

            def tail(n, carry):
                sl = chunk_rows(n, 256)
                gn = acc_ref[sl, :]
                hat, rstd = ln_stats(h_late[sl, :].astype(F32))
                gh = gm_late[sl, :] + ln_back(gn, hat, rstd, m_ref[base + 1 : base + 2, :])
                for i, gh_ref in enumerate(gh_refs):
                    gh_ref[sl, :] = gh[:, i * cols : (i + 1) * cols].astype(out_dtype)
                s_ref[0:1, :] += jnp.sum(gn, axis=0, keepdims=True)
                s_ref[1:2, :] += jnp.sum(gn * hat, axis=0, keepdims=True)
                return carry

            lax.fori_loop(0, rows // 256, tail, 0)

    return call(
        kernel,
        "qkv_back",
        (NZ,),
        [pl.BlockSpec((rows, 768), lambda z: (0, z))]
        + piece_specs(128, 0, 96)
        + [ANYWHERE, ANYWHERE, full((12, D))],
        [full((rows, cols))] * pieces + [full((8, D))],
        [jax.ShapeDtypeStruct((rows, cols), out_dtype)] * pieces
        + [jax.ShapeDtypeStruct((8, D), F32)],
        [
            pltpu.VMEM((rows, D), F32),
            pltpu.VMEM((rows, D), hidden.dtype),
            pltpu.VMEM((rows, D), F32),
            pltpu.SemaphoreType.DMA((2,)),
        ],
        6 * rows * D * D,
        rows * D * 20 + 6 * D * D,
    )(grad_proj, *weights, hidden, grad_middle, mods)


def qkv_grad(grad_proj, normed, out_keep, out_send, apart):
    rows = normed.shape[0]
    k = 128

    def kernel(p_ref, n_ref, ok_ref, os_ref, *rest):
        if apart:
            keep_ref, send_refs = rest[-5], rest[-4:]
        else:
            keep_ref, send_ref = rest[-2:]
            send_refs = [send_ref.at[m : m + 1] for m in range(4)]
        for t in range(3):
            gw = dot_tn(p_ref[:, t * 256 : (t + 1) * 256], n_ref[...]).astype(BF16)
            for m in range(4):
                keep_ref[m, 0, t * 32 : t * 32 + 32] = gw[m * 64 : m * 64 + 32]
                send_refs[m][0, 0, t * 32 : t * 32 + 32] = gw[m * 64 + 32 : m * 64 + 64]
        keep_ref[:, :, 96:128] = ok_ref[...]
        for m in range(4):
            send_refs[m][0, :, 96:128] = os_ref[m]

    gspec = pl.BlockSpec((4, 1, k, D), lambda z: (0, z, 0, 0))
    ospec = pl.BlockSpec((4, 1, 32, D), lambda z: (0, z, 0, 0))
    gshape = jax.ShapeDtypeStruct((4, NZ, k, D), BF16)
    sends, send_shapes = [gspec], [gshape]
    if apart:
        sends = [pl.BlockSpec((1, 1, k, D), lambda z: (0, z, 0, 0))] * 4
        send_shapes = [jax.ShapeDtypeStruct((1, NZ, k, D), BF16)] * 4
    return call(
        kernel,
        "qkv_grad",
        (NZ,),
        [pl.BlockSpec((rows, 768), lambda z: (0, z)), full((rows, D)), ospec, ospec],
        [gspec] + sends,
        [gshape] + send_shapes,
        [],
        6 * rows * D * D,
        rows * D * 8 + 8 * D * D,
    )(grad_proj, normed, out_keep, out_send)


def place_call(kernel, name, in_specs, out_specs, out_shape, scratch, nbytes, aliases):
    return pl.pallas_call(
        kernel,
        name=name,
        grid_spec=pltpu.PrefetchScalarGridSpec(
            num_scalar_prefetch=1,
            grid=(8,),
            in_specs=in_specs,
            out_specs=out_specs,
            scratch_shapes=scratch,
        ),
        out_shape=out_shape,
        input_output_aliases=aliases,
        compiler_params=pltpu.CompilerParams(
            dimension_semantics=("arbitrary",), vmem_limit_bytes=VMEM_LIMIT
        ),
        cost_estimate=pl.CostEstimate(flops=0, bytes_accessed=nbytes // 64, transcendentals=0),
    )


def rows_at(place):
    return pl.ds(pl.multiple_of(place * 32, 32), 32)


def prep_attn(place, w_qkv, w_out, b):
    def kernel(c_ref, q_ref, o_ref, out_ref, t_ref):
        r = pl.program_id(0)

        @pl.when(r == 0)
        def _():
            for t in range(3):
                t_ref[t] = q_ref[0, t].T

        at = rows_at(c_ref[0] ^ r)
        for t in range(3):
            out_ref[0, 0, t * 32 : (t + 1) * 32, :] = t_ref[t, at, :]
        out_ref[0, 0, 96:128, :] = o_ref[0, at, :]

    return place_call(
        kernel,
        "prep_attn",
        [
            pl.BlockSpec((1, 3, D, 256), lambda r, c: (b, 0, 0, 0)),
            pl.BlockSpec((1, 256, D), lambda r, c: (b, 0, 0)),
        ],
        pl.BlockSpec((1, 1, 128, D), lambda r, c: (r % 2, r // 2, 0, 0)),
        jax.ShapeDtypeStruct((2, 4, 128, D), BF16),
        [pltpu.VMEM((3, 256, D), BF16)],
        4 * D * D,
        {},
    )(place, w_qkv, w_out)


def prep_feed(place, w_up, w_down, b):
    def kernel(c_ref, u_ref, d_ref, out_ref):
        out_ref[0, 0, 0:128, :] = u_ref[0].T
        out_ref[0, 0, 128:256, :] = d_ref[0]

    return place_call(
        kernel,
        "prep_feed",
        [
            pl.BlockSpec((1, D, 128), lambda r, c: (b, 0, c[0] ^ r)),
            pl.BlockSpec((1, 128, D), lambda r, c: (b, c[0] ^ r, 0)),
        ],
        pl.BlockSpec((1, 1, 256, D), lambda r, c: (r % 2, r // 2, 0, 0)),
        jax.ShapeDtypeStruct((2, 4, 256, D), BF16),
        [],
        8 * D * D,
        {},
    )(place, w_up, w_down)


def finish_attn(place, own, other):
    def kernel(c_ref, own_ref, oth_ref, gq_ref, go_ref, t_ref):
        r = pl.program_id(0)
        at = rows_at(c_ref[0] ^ r)

        def store(ref):
            for b in range(2):
                row = 128 * b
                for t in range(3):
                    t_ref[b, t, at, :] = ref[0, row + t * 32 : row + (t + 1) * 32, :]
                go_ref[b, at, :] = ref[0, row + 96 : row + 128, :].astype(F32)

        @pl.when(r % 2 == 0)
        def _():
            store(own_ref)

        @pl.when(r % 2 == 1)
        def _():
            store(oth_ref)

        @pl.when(r == 7)
        def _():
            for b in range(2):
                for t in range(3):
                    gq_ref[b, t] = t_ref[b, t].T.astype(F32)

    piece = pl.BlockSpec((1, 256, D), lambda r, c: (r // 2, 0, 0))
    return place_call(
        kernel,
        "finish_attn",
        [piece, piece],
        [
            pl.BlockSpec((2, 3, D, 256), lambda r, c: (0, 0, 0, 0), pipeline_mode=CONST),
            pl.BlockSpec((2, 256, D), lambda r, c: (0, 0, 0), pipeline_mode=CONST),
        ],
        [
            jax.ShapeDtypeStruct((2, 3, D, 256), F32),
            jax.ShapeDtypeStruct((2, 256, D), F32),
        ],
        [pltpu.VMEM((2, 3, 256, D), BF16)],
        12 * D * D,
        {},
    )(place, own, other)


def finish_feed(place, own, other, b, earlier):
    def kernel(c_ref, own_ref, oth_ref, *rest):
        gu_ref, gd_ref = rest[-2:]
        r = pl.program_id(0)

        def store(ref):
            gu_ref[0] = ref[0, 0:128, :].T.astype(F32)
            gd_ref[0] = ref[0, 128:256, :].astype(F32)

        @pl.when(r % 2 == 0)
        def _():
            store(own_ref)

        @pl.when(r % 2 == 1)
        def _():
            store(oth_ref)

    piece = pl.BlockSpec((1, 256, D), lambda r, c: (r // 2, 0, 0))
    anywhere = pl.BlockSpec(memory_space=pl.ANY)
    return place_call(
        kernel,
        "finish_feed",
        [piece, piece] + [anywhere] * len(earlier),
        [
            pl.BlockSpec((1, D, 128), lambda r, c: (b, 0, c[0] ^ r)),
            pl.BlockSpec((1, 128, D), lambda r, c: (b, c[0] ^ r, 0)),
        ],
        [jax.ShapeDtypeStruct((2, D, D), F32), jax.ShapeDtypeStruct((2, D, D), F32)],
        [],
        12 * D * D,
        {3 + i: i for i in range(len(earlier))},
    )(place, own, other, *earlier)


def partner(values):
    return lax.ppermute(values, "head", [(i, i ^ 1) for i in range(NZ)])


def rows_to_spatial(rows, odd):
    cols = rows.shape[1]
    whole = lax.dynamic_slice(rows, (256 * odd, 0), (1024, cols))
    part = lax.dynamic_slice(rows, (1024 * (1 - odd), 0), (256, cols)).reshape(8, 2, 16, cols)
    wins = whole.reshape(2, 16, 2, 16, cols).transpose(0, 2, 1, 3, 4).reshape(1024, cols)
    left, right = part[:, 0].reshape(128, cols), part[:, 1].reshape(128, cols)
    keep = jnp.where(odd == 0, left, right)
    got = partner(jnp.where(odd == 0, right, left))
    top, bottom = jnp.where(odd == 0, keep, got), jnp.where(odd == 0, got, keep)
    part = jnp.concatenate([top, bottom], axis=0)
    return jnp.where(
        odd == 0,
        jnp.concatenate([wins, part], axis=0),
        jnp.concatenate([part, wins], axis=0),
    )


def last_window(wins, odd):
    part = lax.dynamic_slice(wins, (1024 * (1 - odd), 0), (256, wins.shape[1]))
    keep = jnp.where(odd == 0, part[:128], part[128:])
    return keep, jnp.where(odd == 0, part[128:], part[:128])


def whole_windows(wins, odd):
    cols = wins.shape[1]
    whole = lax.dynamic_slice(wins, (256 * odd, 0), (1024, cols))
    return whole.reshape(2, 2, 16, 16, cols).transpose(0, 2, 1, 3, 4).reshape(1024, cols)


def spatial_to_rows(whole, keep, got, odd):
    cols = whole.shape[1]
    left, right = jnp.where(odd == 0, keep, got), jnp.where(odd == 0, got, keep)
    part = jnp.stack([left.reshape(8, 16, cols), right.reshape(8, 16, cols)], axis=1)
    part = part.reshape(256, cols)
    return jnp.where(
        odd == 0,
        jnp.concatenate([whole, part], axis=0),
        jnp.concatenate([part, whole], axis=0),
    )


def exchange(values):
    return lax.all_to_all(values, "head", 0, 0, tiled=True)


def to_quads(wins):
    cols = wins.shape[1]
    return wins.reshape(5, 2, 8, 2, 8, cols).transpose(1, 3, 0, 2, 4, 5).reshape(1280, cols)


def spatial_to_tubes(wins):
    return exchange(to_quads(wins))


def from_quads(quads):
    cols = quads.shape[1]
    return quads.reshape(2, 2, 5, 8, 8, cols).transpose(2, 0, 3, 1, 4, 5).reshape(1280, cols)


def toeplitz(side):
    span = 2 * side - 1
    b = lax.broadcasted_iota(jnp.int32, (span, side, side), 0)
    j = lax.broadcasted_iota(jnp.int32, (span, side, side), 1)
    i = lax.broadcasted_iota(jnp.int32, (span, side, side), 2)
    return (b == i - j + side - 1).astype(F32)


def toeplitz_pair(side):
    span = 2 * side - 1
    shape = (span * span, side * side, side * side)
    r = lax.broadcasted_iota(jnp.int32, shape, 0)
    j = lax.broadcasted_iota(jnp.int32, shape, 1)
    i = lax.broadcasted_iota(jnp.int32, shape, 2)
    dy = i // side - j // side + side - 1
    dx = i % side - j % side + side - 1
    return (r == dy * span + dx).astype(F32)


CORE, ROW_X, ROW_Y = 1, 2, 4


def swap(values, bit):
    return lax.ppermute(values, "clip", [(i, i ^ bit) for i in range(8)])


def from_z(values, d):
    return lax.ppermute(values, "head", [((i + d) % NZ, i) for i in range(NZ)])


def sync(*values):
    return lax.optimization_barrier(values)


def add(first, second):
    return (first.astype(F32) + second.astype(F32)).astype(BF16)


def line_stage(piece):
    return [from_z(piece, d) for d in (1, 2, 3)]


def others(by_z, z):
    return [lax.dynamic_index_in_dim(by_z, (z + d) % NZ, 0, keepdims=False) for d in (1, 2, 3)]


def cross_stage(own):
    return [own] + [swap(own, m * 2) for m in (1, 2, 3)]


def sides_stage(own):
    return [own, swap(own, ROW_X), swap(own, ROW_Y)]


def corner_stage(sides):
    half = sides[0].shape[1] // 2
    return [swap(sides[1][:, :half], ROW_Y), swap(sides[2][:, half:], ROW_X)]


def joined(sides, corner):
    return jnp.stack(sides + [jnp.concatenate(corner, axis=1)])


def sum_core(keep, got):
    return [add(keep[m], got[m].reshape(keep.shape[1:])) for m in range(4)]


def send_plane(totals, offsets):
    return [swap(totals[m], m * 2) for m in offsets]


def to_places(total, z):
    twice = jnp.concatenate([total, total[: NZ - 1]], axis=0)
    return lax.dynamic_slice_in_dim(twice, (NZ - z) % NZ, NZ, axis=0)


def sum_plane(totals, got, z):
    total = totals[0].astype(F32)
    for value in got:
        total = total + value.astype(F32)
    return to_places(total.astype(BF16), z)


def send_cross(totals):
    half = totals[0].shape[1] // 2
    first = [t[:, :half] for t in totals]
    second = [t[:, half:] for t in totals]
    by_x = swap(jnp.stack([first[1], first[3]]), ROW_X)
    by_y = swap(jnp.stack([second[2], second[3]]), ROW_Y)
    return by_x, by_y


def sum_cross(totals, got):
    half = totals[0].shape[1] // 2
    by_x, by_y = got
    first = [add(totals[0][:, :half], by_x[0]), add(totals[2][:, :half], by_x[1])]
    second = [add(totals[0][:, half:], by_y[0]), add(totals[1][:, half:], by_y[1])]
    return first, second


def send_corner(halves):
    return swap(halves[0][1], ROW_Y), swap(halves[1][1], ROW_X)


def sum_corner(halves, got, z):
    first = add(halves[0][0], got[0])
    second = add(halves[1][0], got[1])
    return to_places(jnp.concatenate([first, second], axis=1), z)


def sum_line(by_z):
    return lax.psum_scatter(by_z, "head", scatter_dimension=0)


def on_device_windows(
    tokens, d_out, modulation, frame_counts, w_qkv, w_out, w_up, w_down, table_s, table_t
):
    z = lax.axis_index("head")
    c = lax.axis_index("clip")
    place = c.astype(jnp.int32).reshape(1)
    chip = c // 2
    odd = z % 2
    mods = modulation[0]
    n_s, n_t = table_s.shape[1], table_t.shape[1]
    hot_s, hot_t = toeplitz(SWIN), toeplitz_pair(TWIN)
    fc = frame_counts

    def spatial_base(tables):
        base = jnp.einsum(
            "hab,bji->hjai", tables[:, :n_s].reshape(16, 31, 31), hot_s, precision=HIGHEST_PRECISION
        ).reshape(16, 16, 496)
        return jnp.pad(base, ((0, 0), (0, 0), (0, 16)))

    def tube_base(tables):
        base = jnp.einsum(
            "htr,rjk->hjtk", tables[:, n_s:].reshape(16, 9, 225), hot_t, precision=HIGHEST_PRECISION
        ).reshape(16, 64, 576)
        return jnp.pad(base, ((0, 0), (0, 0), (0, 64)))

    def table_rows(first, second):
        first = jnp.pad(first, ((0, 0), (0, D - n_s)))
        second = jnp.pad(second, ((0, 0), (0, 15 * D - n_t)))
        values = jnp.concatenate([first, second], axis=1).astype(BF16)
        return values.reshape(NZ, 4, 16, D).transpose(1, 0, 2, 3)

    spatial = ((1, 5, 256), 16, 16, False)
    tube = ((5, 4, 64), 5, 64, True)

    local_a0 = prep_attn(place, w_qkv, w_out, 0)
    line_a0 = line_stage(local_a0[0, 0])
    table_piece = jnp.concatenate([table_s, table_t], axis=1)
    tables = [from_z(table_piece, d) for d in (1, 2)]
    local_f0 = prep_feed(place, w_up, w_down, 0)
    local_a1 = prep_attn(place, w_qkv, w_out, 1)
    local_f1 = prep_feed(place, w_up, w_down, 1)
    line_a0, local_f0, local_a1, local_f1, tables, tokens, table_piece = sync(
        line_a0, local_f0, local_a1, local_f1, tables, tokens, table_piece
    )
    own_a0 = cross_stage(jnp.stack(line_a0))
    z_u0 = lax.all_gather(local_f0[0, 0, :128], "head")
    z_d0 = lax.all_gather(local_f0[0, 0, 128:], "head")
    tables = jnp.stack([table_piece] + tables + [from_z(table_piece, 3)])
    tables = jnp.concatenate(
        [lax.dynamic_slice_in_dim(tables, chip ^ m, 1, axis=1) for m in range(4)], axis=1
    ).reshape(16, n_s + n_t)
    base_s = spatial_base(tables)
    hidden0 = rows_to_spatial(tokens, odd)
    own_a0, hidden0, tables, base_s, z_u0 = sync(own_a0, hidden0, tables, base_s, z_u0)
    own_a0 = jnp.stack(own_a0)
    other_a0 = swap(own_a0, CORE)
    own_u0 = sides_stage(jnp.stack(others(z_u0, z)))
    own_a0, other_a0 = sync(own_a0, other_a0)
    weights_a0 = (local_a0, own_a0, other_a0)
    normed0, qkv0 = ln_qkv(hidden0, mods, weights_a0, 0)
    qkv0, own_u0, z_d0 = sync(qkv0, own_u0, z_d0)
    corner_u0 = corner_stage(own_u0)
    own_d0 = sides_stage(jnp.stack(others(z_d0, z)))
    z_a1 = lax.all_gather(local_a1[0, 0], "head")
    attended0 = attn_fwd(qkv0, base_s, fc, spatial)
    attended0, corner_u0, own_d0, z_a1 = sync(attended0, corner_u0, own_d0, z_a1)
    corner_d0 = corner_stage(own_d0)
    own_u0 = joined(own_u0, corner_u0)
    other_u0 = swap(own_u0, CORE)
    branch0, middle0, shifted0 = out_proj(attended0, weights_a0, hidden0, mods, 0)
    own_a1 = jnp.stack(others(z_a1, z))
    shifted0, corner_d0, other_u0, own_a1 = sync(shifted0, corner_d0, other_u0, own_a1)
    own_d0 = joined(own_d0, corner_d0)
    other_d0 = swap(own_d0, CORE)
    z_f1 = lax.all_gather(local_f1[0, 0], "head")
    shifted0, other_d0 = sync(shifted0, other_d0)
    own_a1 = cross_stage(own_a1)
    weights_f0 = (local_f0, own_u0, other_u0, own_d0, other_d0)
    pre0, feed0, hidden1 = ffn_fwd(shifted0, weights_f0, 0, middle0, mods, 0)
    quads1 = to_quads(hidden1)
    quads1, own_a1 = sync(quads1, own_a1)
    tubes1 = exchange(quads1)
    quads1, z_f1, tables, d_out = sync(quads1, z_f1, tables, d_out)
    own_a1 = jnp.stack(own_a1)
    other_a1 = swap(own_a1, CORE)
    own_f1 = cross_stage(jnp.stack(others(z_f1, z)))
    base_t = tube_base(tables)
    spatial_d = rows_to_spatial(d_out, odd)
    tubes1, other_a1, base_t, spatial_d = sync(tubes1, other_a1, base_t, spatial_d)
    weights_a1 = (local_a1, own_a1, other_a1)
    tubes_d = spatial_to_tubes(spatial_d)
    normed1, qkv1 = ln_qkv(tubes1, mods, weights_a1, 6)
    qkv1, own_f1 = sync(qkv1, own_f1)
    own_f1 = jnp.stack(own_f1)
    other_f1 = swap(own_f1, CORE)
    attended1 = attn_fwd(qkv1, base_t, fc, tube)
    branch1, middle1, shifted1 = out_proj(attended1, weights_a1, tubes1, mods, 6)
    shifted1, other_f1 = sync(shifted1, other_f1)
    weights_f1 = (local_f1, own_f1, other_f1, own_f1, other_f1)
    pre1, feed1, hidden2 = ffn_fwd(shifted1, weights_f1, 1, middle1, mods, 6)
    hidden2, tubes_d = sync(hidden2, tubes_d)
    live = lax.broadcasted_iota(jnp.int32, (1280, 1), 0) // 256 < fc[0]
    grad2 = jnp.where(live, tubes_d, 0)
    out_wins = exchange(jnp.where(live, hidden2, 0))
    f1_keep, f1_send, g_shift1 = ffn_bwd(grad2, pre1, shifted1, weights_f1, 1, mods, 6)
    f1_keep, f1_send, g_shift1, out_wins = sync(f1_keep, f1_send, g_shift1, out_wins)
    f1_got = swap(f1_send, CORE)
    g_mid1, g_att1, o1_keep, o1_send, sums_o1 = out_bwd(
        grad2, g_shift1, middle1, feed1, branch1, attended1, weights_a1, mods, 6
    )
    g_att1, f1_got = sync(g_att1, f1_got)
    total_f1 = sum_core(f1_keep, f1_got)
    g_att1, total_f1 = sync(g_att1, total_f1)
    got_f1 = send_cross(total_f1)
    g_proj1, g_base1 = attn_bwd(qkv1, g_att1, base_t, fc, tube)
    g_proj1, g_base1, got_f1 = sync(g_proj1, g_base1, got_f1)
    half_f1 = sum_cross(total_f1, got_f1)
    half_f1, g_proj1 = sync(half_f1, g_proj1)
    got_f1 = send_corner(half_f1)
    g_hid1, sums_q1 = qkv_back(g_proj1, weights_a1, tubes1, g_mid1, mods, 6, BF16, 1)
    g_hid1, g_proj1, out_wins, g_base1, got_f1 = sync(g_hid1, g_proj1, out_wins, g_base1, got_f1)
    grad1 = exchange(g_hid1)
    z_f1 = sum_corner(half_f1, got_f1, z)
    a1_keep, *a1_send = qkv_grad(g_proj1, normed1, o1_keep, o1_send, True)
    a1_got = [swap(v, CORE) for v in a1_send]
    gt_t = jnp.einsum(
        "hjtk,rjk->htr",
        g_base1[:, :, :576].reshape(16, 64, 9, 64),
        hot_t,
        precision=HIGHEST_PRECISION,
    ).reshape(16, n_t)
    out_wins = from_quads(out_wins)
    out_keep, out_send = last_window(out_wins, odd)
    total_a1 = sum_core(a1_keep, a1_got)
    grad1, total_a1, z_f1, gt_t, out_wins, out_keep, out_send = sync(
        grad1, total_a1, z_f1, gt_t, out_wins, out_keep, out_send
    )
    grad1 = from_quads(grad1)
    mine_f1 = sum_line(z_f1)
    out_got = partner(out_send)
    got_a1 = send_plane(total_a1, (1, 2, 3))
    f0_keep, f0_send, g_shift0 = ffn_bwd(grad1, pre0, shifted0, weights_f0, 0, mods, 0)
    f0_keep, f0_send, g_shift0, mine_f1, got_a1, out_got = sync(
        f0_keep, f0_send, g_shift0, mine_f1, got_a1, out_got
    )
    f0_got = swap(f0_send, CORE)
    sides_f1 = sides_stage(mine_f1[None])
    mine_a1 = sum_line(sum_plane(total_a1, got_a1, z))
    g_mid0, g_att0, o0_keep, o0_send, sums_o0 = out_bwd(
        grad1, g_shift0, middle0, feed0, branch0, attended0, weights_a0, mods, 0
    )
    g_att0, f0_got, sides_f1 = sync(g_att0, f0_got, sides_f1)
    total_f0 = sum_core(f0_keep, f0_got)
    g_att0, total_f0 = sync(g_att0, total_f0)
    got_f0 = send_cross(total_f0)
    corner_f1 = corner_stage(sides_f1)
    g_proj0, g_base0 = attn_bwd(qkv0, g_att0, base_s, fc, spatial)
    a0_keep, a0_send = qkv_grad(g_proj0, normed0, o0_keep, o0_send, False)
    a0_keep, a0_send, got_f0, corner_f1, mine_a1, g_proj0, g_base0 = sync(
        a0_keep, a0_send, got_f0, corner_f1, mine_a1, g_proj0, g_base0
    )
    a0_got = swap(a0_send, CORE)
    half_f0 = sum_cross(total_f0, got_f0)
    early_rows = jnp.concatenate(
        [
            sums_o0[2:3], sums_o0[0:2], sums_o0[3:4],
            sums_q1[0:2], sums_o1[2:3], sums_o1[0:2], sums_o1[3:4],
        ],
        axis=0,
    )
    half_f0, early_rows = sync(half_f0, early_rows)
    got_f0 = send_corner(half_f0)
    early_got = partner(early_rows)
    early_got, g_base0, sides_f1, corner_f1 = sync(early_got, g_base0, sides_f1, corner_f1)
    own_gf1 = joined(sides_f1, corner_f1).reshape(4, 256, D)
    g_feed = finish_feed(place, own_gf1, swap(own_gf1, CORE), 1, ())
    gt_s = jnp.einsum(
        "hjai,bji->hab",
        g_base0[:, :, :496].reshape(16, 16, 31, 16),
        hot_s,
        precision=HIGHEST_PRECISION,
    ).reshape(16, n_s)
    gt = table_rows(gt_s, gt_t)
    half_f0, got_f0, a0_got, g_proj0, g_feed, gt = sync(
        half_f0, got_f0, a0_got, g_proj0, g_feed, gt
    )
    z_f0 = sum_corner(half_f0, got_f0, z)
    total_a0 = sum_core(a0_keep, a0_got)
    total_a0 = [jnp.concatenate([total_a0[m], gt[m]], axis=1) for m in range(4)]
    total_a0, z_f0, g_proj0 = sync(total_a0, z_f0, g_proj0)
    mine_f0 = sum_line(z_f0)
    got_a0 = send_cross(total_a0)
    grad0, sums_q0 = qkv_back(g_proj0, weights_a0, hidden0, g_mid0, mods, 0, F32, 1)
    grad0, sums_q0, got_a0 = sync(grad0, sums_q0, got_a0)
    half_a0 = sum_cross(total_a0, got_a0)
    half_a0, grad0, sums_q0 = sync(half_a0, grad0, sums_q0)
    got_a0 = send_corner(half_a0)
    sides_a1 = sides_stage(mine_a1[None])
    mod_rows = sums_q0[0:2]
    mod_got = partner(mod_rows)
    got_a0, sides_a1, mine_f0, mod_got, mod_rows = sync(
        got_a0, sides_a1, mine_f0, mod_got, mod_rows
    )
    z_a0 = sum_corner(half_a0, got_a0, z)
    mod_sum = jnp.concatenate([mod_rows + mod_got, early_rows + early_got], axis=0)
    z_a0, mine_f0, mod_sum = sync(z_a0, mine_f0, mod_sum)
    mine_a0 = sum_line(z_a0)
    own_gf0 = cross_stage(mine_f0)
    corner_a1 = corner_stage(sides_a1)
    rows_whole = whole_windows(grad0, odd)
    output = spatial_to_rows(whole_windows(out_wins, odd), out_keep, out_got, odd)
    rows_keep, rows_send = last_window(grad0, odd)
    mine_a0, own_gf0, corner_a1, rows_keep, rows_send, rows_whole, output = sync(
        mine_a0, own_gf0, corner_a1, rows_keep, rows_send, rows_whole, output
    )
    own_ga1 = joined(sides_a1, corner_a1).reshape(4, 128, D)
    own_ga0 = cross_stage(mine_a0)
    rows_got = partner(rows_send)
    own_gf0 = jnp.stack(own_gf0)
    g_feed = finish_feed(place, own_gf0, swap(own_gf0, CORE), 0, g_feed)
    own_ga0, g_feed, rows_got, own_ga1, mod_sum = sync(own_ga0, g_feed, rows_got, own_ga1, mod_sum)
    own_ga0 = jnp.stack(own_ga0)
    own_ga = jnp.concatenate([own_ga0[:, :128], own_ga1, own_ga0[:, 128:]], axis=1)
    mod_got = lax.ppermute(mod_sum, "head", [(i, i ^ 2) for i in range(NZ)])
    grad_tokens = spatial_to_rows(rows_whole, rows_keep, rows_got, odd)
    other_ga = swap(own_ga, CORE)
    g_attn = finish_attn(place, own_ga, other_ga)
    tab = own_ga[:, 256:272].astype(F32) + other_ga[:, 256:272].astype(F32)
    tab = jnp.concatenate(
        [lax.dynamic_slice_in_dim(tab, chip ^ m, 1, axis=0) for m in range(4)], axis=0
    )
    tab = tab.reshape(4, 16 * D)
    return (
        output,
        grad_tokens,
        (mod_sum + mod_got)[None],
        g_attn[0],
        g_attn[1],
        g_feed[0],
        g_feed[1],
        tab[:, :n_s],
        tab[:, D : D + n_t],
    )


def solution(mesh):
    if mesh.shape["head"] == NZ and mesh.shape["clip"] == 8:
        body = on_device_windows
    else:
        body = on_device
    return jax.shard_map(
        body,
        mesh=mesh,
        in_specs=(
            P(("clip", "head"), None),
            P(("clip", "head"), None),
            P("clip", None, None),
            P("clip"),
            P(None, None, None, "head"),
            P(None, "head", None),
            P(None, None, "head"),
            P(None, "head", None),
            P("head", None),
            P("head", None),
        ),
        out_specs=(
            P(("clip", "head"), None),
            P(("clip", "head"), None),
            P("clip", None, None),
            P(None, None, None, "head"),
            P(None, "head", None),
            P(None, None, "head"),
            P(None, "head", None),
            P("head", None),
            P("head", None),
        ),
        check_vma=False,
    )
```
